32 devices in a mesh: dp: 4 (over z), context: 2 (over core), tensor: 4 (over y, x).
Axes of the slice: x: 2, y: 2, z: 4, core: 2. Of those that a mesh axis runs over, the one named last changes fastest.
Arguments:
- tokens: bfloat16 [12, 2048, 768], P('dp', ('context', 'tensor')), may hold values from -6 to 6
- segments: int32 [12, 2048], P('dp'), may hold values from 0 to 7, never falling along the last dimension, each value on 1 to 1792 neighbouring positions
- w_qkv: bfloat16 [768, 3, 768], P('dp', None, 'tensor'), may hold values from -0.21875 to 0.21875
- w_out: bfloat16 [768, 768], P('tensor', 'dp'), may hold values from -1.5 to 1.5
- w_in: bfloat16 [768, 3072], P('dp', 'tensor'), may hold values from -0.21875 to 0.21875
- w_back: bfloat16 [3072, 768], P('tensor', 'dp'), may hold values from -0.109375 to 0.109375
- gain_attn: bfloat16 [768], P('dp'), may hold values from 0.25 to 1.75
- gain_mlp: bfloat16 [768], P('dp'), may hold values from 0.25 to 1.75
- cotangent: bfloat16 [12, 2048, 768], P('dp', ('context', 'tensor')), may hold values from -6 to 6
Outputs:
- output: bfloat16 [12, 2048, 768], P('dp', ('context', 'tensor'))
- grad_tokens: bfloat16 [12, 2048, 768], P('dp', ('context', 'tensor'))
- grad_w_qkv: float32 [768, 3, 768], P('dp', None, 'tensor')
- grad_w_out: float32 [768, 768], P('tensor', 'dp')
- grad_w_in: float32 [768, 3072], P('dp', 'tensor')
- grad_w_back: float32 [3072, 768], P('tensor', 'dp')
- grad_gain_attn: float32 [768], P('dp')
- grad_gain_mlp: float32 [768], P('dp')
The draws below stay inside these ranges and needn't reach their ends.
Inputs may be any that keep to these rules, and one draw needn't show every extreme that they name: `segments`: within a sequence the numbers never fall; a document holds 1 to 1792 bytes, and some document holds exactly 1792.
All inputs are finite; a program needn't handle non-finite values.
Results may differ from the reference program's by a relative error of at most 0.02.
Values may be sent and summed in bfloat16 or wider, within the bound.
A program may use at most 192 MiB of HBM per device.

```python
import math
import jax
import jax.numpy as jnp
import numpy as np
from jax import lax

D = 768
H = 12
HD = 64
FF = 3072
WIN = 1536
L = 2048
QB = 512
SEG_COUNT = 8
SEG_MOST = 1792
B = 12


def level_of(stream_key, shape, pieces, low, top_value):
    level = 1.0
    for dim, blocks in pieces:
        draws = jax.random.uniform(jax.random.fold_in(jax.random.fold_in(stream_key, 6), dim), (blocks,), jnp.float32, low / len(pieces), top_value / len(pieces))
        level = level * jnp.repeat(jnp.exp(draws), shape[dim] // blocks).reshape((-1,) + (1,) * (len(shape) - 1 - dim))
    return level


def length_profile(amount, total, reach, lean):
    portions = [(1 << 20) // math.isqrt(grade ** lean) + 1 for grade in range(2, amount + 1)]
    spare, given = total - reach - (amount - 1), [1] * (amount - 1)
    while spare > 0:
        movable = [i for i in range(amount - 1) if given[i] < reach]
        pool, remaining = sum([portions[i] for i in movable]), spare
        for i in movable:
            addition = min(reach - given[i], max(1, remaining * portions[i] // pool), spare)
            given[i] = given[i] + addition
            spare = spare - addition
    return np.array([reach] + given)


def ragged(own_key, number_of, total, reach, skew):
    if number_of == 2:
        one = jax.random.randint(own_key, (), max(1, total - reach), min(reach, total - 1) + 1)
        return jnp.stack([one, total - one])
    sizes = jnp.asarray(length_profile(number_of, total, reach, skew), jnp.int32)
    couples = (number_of - 1) // 2
    donor, taker = sizes[1:1 + 2 * couples:2], sizes[2:2 + 2 * couples:2]
    slack = jnp.minimum(donor - 1, reach - taker)
    shifted = jax.random.randint(jax.random.fold_in(own_key, 1), (couples,), 0, 1 << 20) % (slack + 1)
    sizes = sizes.at[1:1 + 2 * couples:2].set(donor - shifted).at[2:2 + 2 * couples:2].set(taker + shifted)
    return sizes[jax.random.permutation(jax.random.fold_in(own_key, 2), number_of)]


def normal_values(stream_key, shape, scale, bound, pieces=(), held_as=jnp.bfloat16):
    loudness = level_of(stream_key, shape, pieces, -0.22, 0.18) if pieces else 1.0
    entries = jax.random.normal(stream_key, shape, jnp.float32) * scale * loudness
    return jnp.minimum(jnp.maximum(entries, -bound), bound).astype(held_as)


def setup_inputs(seed: int = 0) -> dict:
    streams_of = jax.random.split(jax.random.key(seed), 10)
    return {
        "tokens": normal_values(streams_of[0], (B, L, D), 1.0, 6.0, ((0, 4), (1, 8))),
        "segments": jax.vmap(lambda own: jnp.searchsorted(jnp.cumsum(ragged(own, SEG_COUNT, L, SEG_MOST, 2)), jnp.arange(L), side="right"))(jax.random.split(streams_of[1], B)).reshape((B, L)).astype(jnp.int32),
        "w_qkv": normal_values(streams_of[2], (D, 3, D), D ** -0.5, 0.21875, ((0, 4), (2, 4))),
        "w_out": normal_values(streams_of[3], (D, D), 16 ** -0.5, 1.5, ((0, 4), (1, 4))),
        "w_in": normal_values(streams_of[4], (D, FF), D ** -0.5, 0.21875, ((0, 4), (1, 4))),
        "w_back": normal_values(streams_of[5], (FF, D), FF ** -0.5, 0.109375, ((0, 4), (1, 4))),
        "gain_attn": jnp.clip(1.0 + 0.15 * jax.random.normal(streams_of[6], (D,), jnp.float32), 0.25, 1.75).astype(jnp.bfloat16),
        "gain_mlp": jnp.clip(1.0 + 0.15 * jax.random.normal(streams_of[7], (D,), jnp.float32), 0.25, 1.75).astype(jnp.bfloat16),
        "cotangent": normal_values(streams_of[8], (B, L, D), 1.0, 6.0, ((0, 4), (1, 8))),
    }


epsilon = 1e-06

@jax.custom_vjp
def low(v):
    return lax.optimization_barrier(v.astype(jnp.bfloat16)).astype(jnp.float32)

@jax.custom_vjp
def low_back(v):
    return v

def low_keep(v):
    return (low(v), None)

def low_pass(kept, grad):
    return (grad,)

def back_keep(v):
    return (v, None)

def back_low(kept, grad):
    return (low(grad),)
low.defvjp(low_keep, low_pass)
low_back.defvjp(back_keep, back_low)

def rms_norm(values, gain):
    return values * lax.rsqrt(lax.optimization_barrier(jnp.mean(values * values, axis=-1, keepdims=True)) + epsilon) * gain

def reference(tokens, segments, w_qkv, w_out, w_in, w_back, gain_attn, gain_mlp, cotangent):
    highest = lax.Precision.HIGHEST
    score_scale = 1.0 / math.sqrt(HD)
    weights = (w_qkv.astype(jnp.float32), w_out.astype(jnp.float32), w_in.astype(jnp.float32), w_back.astype(jnp.float32), gain_attn.astype(jnp.float32), gain_mlp.astype(jnp.float32))

    def per_sequence(running, sequence_item):
        token_row, doc_ids, cotan_row = sequence_item

        def block_layer(inputs, w_attn, w_proj, w_up, w_down, gain_first, gain_second):
            normed_one = low(rms_norm(inputs, gain_first))
            projected = low(low_back(jnp.dot(normed_one, w_attn.reshape(D, 3 * D), precision=highest)))
            projected = projected.reshape(L, 3, H, HD)
            queries = projected[:, 0]
            keys_all = projected[:, 1]
            values_all = projected[:, 2]
            key_pos = jnp.arange(L, dtype=jnp.int32)

            def attend_block(query_block, query_start):
                query_pos = query_start + jnp.arange(QB, dtype=jnp.int32)
                query_seg = lax.dynamic_slice_in_dim(doc_ids, query_start, QB, 0)
                scores = low_back(jnp.einsum('qhd,khd->hqk', query_block, keys_all, precision=highest) * score_scale)
                allowed = (key_pos[None, :] <= query_pos[:, None]) & (query_pos[:, None] - key_pos[None, :] < WIN) & (query_seg[:, None] == doc_ids[None, :])
                scores = jnp.where(allowed[None], scores, -1e+30)
                row_max = lax.optimization_barrier(jnp.max(scores, axis=-1, keepdims=True))
                exponent = jnp.exp(scores - row_max)
                soft = exponent / lax.optimization_barrier(jnp.sum(exponent, axis=-1, keepdims=True))
                return jnp.einsum('hqk,khd->qhd', low(soft), values_all, precision=highest)
            attend_saved = jax.checkpoint(attend_block)

            def attend_pair(pair):
                return attend_saved(pair[0], pair[1])
            starts = (jnp.arange(L // QB, dtype=jnp.int32) * QB).astype(jnp.int32)
            attended = lax.map(attend_pair, (queries.reshape(L // QB, QB, H, HD), starts)).reshape(L, D)
            attended = low(low_back(attended))
            middle = inputs + low_back(jnp.dot(attended, w_proj, precision=highest))
            normed_two = low(rms_norm(middle, gain_second))
            hidden_pre = low_back(jnp.dot(normed_two, w_up, precision=highest))
            activated = low(jax.nn.gelu(hidden_pre, approximate=True))
            branch = low_back(jnp.dot(activated, w_down, precision=highest))
            return middle + branch
        result, pullback = jax.vjp(block_layer, token_row.astype(jnp.float32), *weights)
        gradients = pullback(cotan_row.astype(jnp.float32))
        running = tuple((left + right for left, right in zip(running, gradients[1:])))
        return (running, (result.astype(jnp.bfloat16), gradients[0].astype(jnp.bfloat16)))
    zeros_init = tuple((jnp.zeros(w.shape, jnp.float32) for w in weights))
    running, (outputs, grad_inputs) = lax.scan(per_sequence, zeros_init, (tokens, segments, cotangent))
    return (outputs, grad_inputs, running[0], running[1], running[2], running[3], running[4], running[5])
```

```python
import functools
import math

import jax
import jax.numpy as jnp
from jax import lax
from jax.experimental import pallas as pl
from jax.experimental.pallas import tpu as pltpu
from jax.sharding import PartitionSpec as P

HD = 64
WIN = 1536
QB = 256
CHUNK = 128
NEG = -1e30
epsilon = 1e-06
low = jnp.bfloat16
full = jnp.float32


def dot(left, right, dims):
    return lax.dot_general(left, right, (dims, ((), ())), preferred_element_type=full)


def nn(left, right):
    return dot(left, right, ((1,), (0,)))


def nt(left, right):
    return dot(left, right, ((1,), (1,)))


def tn(left, right):
    return dot(left, right, ((0,), (0,)))


def across(array, axis, by):
    return lax.ppermute(array, axis, [(i, i ^ by) for i in range(lax.axis_size(axis))])


def gather_tensor(array, axis):
    half = array.shape[axis] // 2
    one = lax.slice_in_dim(array, 0, half, axis=axis)
    two = lax.slice_in_dim(array, half, 2 * half, axis=axis)
    one_x, two_y = across(one, "tensor", 1), across(two, "tensor", 2)
    one_y, one_d = across(one, "tensor", 2), across(one_x, "tensor", 2)
    two_x, two_d = across(two, "tensor", 1), across(two_y, "tensor", 1)
    join = lambda a, b: jnp.concatenate([a, b], axis=axis)
    return [array, join(one_x, two_x), join(one_y, two_y), join(one_d, two_d)]


def scatter_tensor(parts, axis):
    half = parts[0].shape[axis] // 2
    one = [lax.slice_in_dim(p, 0, half, axis=axis) for p in parts]
    two = [lax.slice_in_dim(p, half, 2 * half, axis=axis) for p in parts]

    def reduce(p, first, second):
        sent = jnp.stack([p[first], p[first ^ second]]).astype(low)
        got = across(sent, "tensor", first).astype(full)
        mine, theirs = p[0] + got[0], p[second] + got[1]
        return mine + across(theirs.astype(low), "tensor", second).astype(full)

    return jnp.concatenate([reduce(one, 1, 2), reduce(two, 2, 1)], axis=axis)


UNITS = 5


def unit_block(part):
    return lambda u, c: (jnp.where(u < 3, part * 3 + u, 9 + part * 2 + (u - 3)), 0, 0)


def attend_kernel(c_ref, qm, km, vm, qt, kt, vt, lo_ref, om, ot, lse_ref, of_ref, qs, ks, vs, ss):
    c = c_ref[0]
    length = lo_ref.shape[2]
    half = length // 2
    for place, q, k, v in ((c, qm, km, vm), (1 - c, qt, kt, vt)):
        off = pl.multiple_of(place * half, half)
        qs[:, pl.ds(off, half)] = q[0] * low(0.125)
        vs[:, pl.ds(off, half)] = v[0]
        ks[pl.ds(off, half), :] = k[0].T
    for start in range(0, length, QB):
        stop = start + QB
        q = qs[:, start:stop]
        lo = lo_ref[0, :, start:stop]
        first = max(0, start - WIN)
        most = jnp.full((8, QB), NEG, full)
        for at in range(first, stop, CHUNK):
            s = nn(ks[at : at + CHUNK, :], q)
            key_pos = at + lax.broadcasted_iota(jnp.int32, (CHUNK, QB), 0)
            allowed = key_pos >= lo
            if at + CHUNK - 1 > start:
                allowed &= key_pos <= start + lax.broadcasted_iota(jnp.int32, (CHUNK, QB), 1)
            s = jnp.where(allowed, s, NEG)
            ss[at - first : at - first + CHUNK, :] = s
            most = jnp.maximum(most, jnp.max(s.reshape(CHUNK // 8, 8, QB), axis=0))
        most = jnp.max(most, axis=0, keepdims=True)
        total = jnp.zeros((8, QB), full)
        acc = jnp.zeros((HD, QB), full)
        for at in range(first, stop, CHUNK):
            p = jnp.exp(ss[at - first : at - first + CHUNK, :] - most)
            total += jnp.sum(p.reshape(CHUNK // 8, 8, QB), axis=0)
            acc += nn(vs[:, at : at + CHUNK], p.astype(low))
        total = jnp.sum(total, axis=0, keepdims=True)
        lse_ref[0, :, start:stop] = most + jnp.log(total)
        of_ref[0, :, start:stop] = acc * (1.0 / total)
    om[0] = of_ref[0, :, pl.ds(pl.multiple_of(c * half, half), half)].astype(low)
    ot[0] = of_ref[0, :, pl.ds(pl.multiple_of((1 - c) * half, half), half)].astype(low)


def attend(c, mine, theirs, lo):
    length = lo.shape[2]
    half = length // 2
    part = lambda p: pl.BlockSpec((1, HD, half), unit_block(p))
    unit = lambda rows, n: pl.BlockSpec((1, rows, n), lambda u, c: (u, 0, 0))
    return pl.pallas_call(
        attend_kernel,
        grid_spec=pltpu.PrefetchScalarGridSpec(
            num_scalar_prefetch=1,
            grid=(UNITS,),
            in_specs=[part(0), part(1), part(2)] * 2
            + [pl.BlockSpec((1, 1, length), lambda u, c: (u // 3, 0, 0))],
            out_specs=[unit(HD, half), unit(HD, half), unit(1, length), unit(HD, length)],
            scratch_shapes=[
                pltpu.VMEM((HD, length), low),
                pltpu.VMEM((length, HD), low),
                pltpu.VMEM((HD, length), low),
                pltpu.VMEM((WIN + QB, QB), full),
            ],
        ),
        out_shape=[jax.ShapeDtypeStruct((UNITS, HD, half), low)] * 2
        + [
            jax.ShapeDtypeStruct((UNITS, 1, length), full),
            jax.ShapeDtypeStruct((UNITS, HD, length), full),
        ],
        compiler_params=pltpu.CompilerParams(vmem_limit_bytes=40 << 20),
        cost_estimate=pl.CostEstimate(
            flops=UNITS * 18 * 2 * 256 * 1024 * 128, bytes_accessed=20 << 20, transcendentals=0
        ),
        name="attend",
    )(c, mine, mine, mine, theirs, theirs, theirs, lo)


def attend_back_kernel(
    c_ref, qm, km, vm, gm, qt, kt, vt, gt, lo_ref, lse_ref, of_ref, dm, dt,
    qs, ks, kts, vs, gs, grow, qrow, delta, dqs, dks, dvs,
):
    c = c_ref[0]
    length = lo_ref.shape[2]
    half = length // 2
    for place, q, k, v, g in ((c, qm, km, vm, gm), (1 - c, qt, kt, vt, gt)):
        off = pl.multiple_of(place * half, half)
        scaled = q[0] * low(0.125)
        qs[:, pl.ds(off, half)] = scaled
        kts[:, pl.ds(off, half)] = k[0]
        gs[:, pl.ds(off, half)] = g[0]
        ks[pl.ds(off, half), :] = k[0].T
        vs[pl.ds(off, half), :] = v[0].T
        grow[pl.ds(off, half), :] = g[0].T
        qrow[pl.ds(off, half), :] = scaled.T
        delta[:, pl.ds(off, half)] = jnp.sum(
            g[0].astype(full) * of_ref[0, :, pl.ds(off, half)], axis=0, keepdims=True
        )
    dqs[...] = jnp.zeros_like(dqs)
    for key_start in range(0, length, QB):
        rows = slice(key_start, key_start + QB)
        k, v, key_t = ks[rows, :], vs[rows, :], kts[:, rows]
        dk = jnp.zeros((QB, HD), full)
        dv = jnp.zeros((QB, HD), full)
        key_pos = key_start + lax.broadcasted_iota(jnp.int32, (QB, QB), 0)
        for start in range(key_start, min(key_start + WIN + QB, length), QB):
            cols = slice(start, start + QB)
            s = nn(k, qs[:, cols]) - lse_ref[0, :, cols]
            allowed = key_pos >= lo_ref[0, :, cols]
            if start == key_start:
                allowed &= key_pos <= start + lax.broadcasted_iota(jnp.int32, (QB, QB), 1)
            p = jnp.exp(jnp.where(allowed, s, NEG))
            dp = nn(v, gs[:, cols])
            ds = (p * (dp - delta[:, cols])).astype(low)
            dv += nn(p.astype(low), grow[cols, :])
            dk += nn(ds, qrow[cols, :])
            dqs[:, cols] += nn(key_t, ds)
        dks[:, rows] = dk.T.astype(low)
        dvs[:, rows] = dv.T.astype(low)
    for ref, place in ((dm, c), (dt, 1 - c)):
        off = pl.ds(pl.multiple_of(place * half, half), half)
        ref[0, 0] = (dqs[:, off] * 0.125).astype(low)
        ref[0, 1] = dks[:, off]
        ref[0, 2] = dvs[:, off]


def attend_back(c, mine, theirs, grad_mine, grad_theirs, lo, lse, attended):
    length = lo.shape[2]
    half = length // 2
    part = lambda p: pl.BlockSpec((1, HD, half), unit_block(p))
    unit = lambda rows, n: pl.BlockSpec((1, rows, n), lambda u, c: (u, 0, 0))
    wide, tall = pltpu.VMEM((HD, length), low), pltpu.VMEM((length, HD), low)
    return pl.pallas_call(
        attend_back_kernel,
        grid_spec=pltpu.PrefetchScalarGridSpec(
            num_scalar_prefetch=1,
            grid=(UNITS,),
            in_specs=[part(0), part(1), part(2), unit(HD, half)] * 2
            + [
                pl.BlockSpec((1, 1, length), lambda u, c: (u // 3, 0, 0)),
                unit(1, length),
                unit(HD, length),
            ],
            out_specs=[pl.BlockSpec((1, 3, HD, half), lambda u, c: (u, 0, 0, 0))] * 2,
            scratch_shapes=[
                wide, tall, wide, tall, wide, tall, tall,
                pltpu.VMEM((1, length), full), pltpu.VMEM((HD, length), full), wide, wide,
            ],
        ),
        out_shape=[jax.ShapeDtypeStruct((UNITS, 3, HD, half), low)] * 2,
        compiler_params=pltpu.CompilerParams(vmem_limit_bytes=40 << 20),
        cost_estimate=pl.CostEstimate(
            flops=UNITS * 18 * 5 * 256 * 1024 * 128, bytes_accessed=30 << 20, transcendentals=0
        ),
        name="attend_back",
    )(c, mine, mine, mine, grad_mine, theirs, theirs, theirs, grad_theirs, lo, lse, attended)


def gelu_and_slope(v):
    k0 = math.sqrt(2.0 / math.pi)
    square = v * v
    th = jnp.tanh(k0 * v * (1.0 + 0.044715 * square))
    slope = 0.5 * (1.0 + th) + 0.5 * v * (1.0 - th * th) * k0 * (1.0 + 3.0 * 0.044715 * square)
    return 0.5 * v * (1.0 + th), slope


def per_device(tokens, segments, w_qkv, w_out, w_in, w_back, gain_attn, gain_mlp, cotangent):
    sequences, own, width = tokens.shape
    assert lax.axis_size("tensor") == 4 and lax.axis_size("context") == 2 and sequences == 3
    c, t, d = lax.axis_index("context"), lax.axis_index("tensor"), lax.axis_index("dp")
    span = 4 * own
    length = segments.shape[1]
    shard = w_qkv.shape[0]
    local = w_qkv.shape[2]
    heads = local // HD
    hidden = w_in.shape[1] // 2
    rows = sequences * own

    blocks = gather_tensor(tokens, 1)
    cot_theirs = across(cotangent, "context", 1)
    w_attn = lax.all_gather(w_qkv.reshape(shard, 3 * local), "dp", axis=0, tiled=True)
    gains = lax.all_gather(jnp.stack([gain_attn, gain_mlp], axis=1), "dp", axis=0, tiled=True)
    gain_first, gain_second = gains[:, 0].astype(full), gains[:, 1].astype(full)
    up_own = lax.dynamic_slice_in_dim(w_in, c * hidden, hidden, 1)
    down_own = lax.dynamic_slice_in_dim(w_back, c * hidden, hidden, 0).T
    up_down = jnp.stack(gather_tensor(jnp.stack([up_own, down_own]), 1), axis=1)
    up_down = lax.all_gather(up_down, "dp", axis=2, tiled=True)
    w_up, w_down = up_down[0], up_down[1]
    w_proj = jnp.stack(gather_tensor(w_out.T, 0), axis=0)
    w_proj = lax.all_gather(w_proj, "dp", axis=1, tiled=True)

    lo = jnp.zeros((sequences, length), jnp.int32)
    for value in range(8):
        before = jnp.sum((segments < value).astype(jnp.int32), axis=1, keepdims=True)
        lo = jnp.where(segments == value, before, lo)
    lo = jnp.maximum(lo, jnp.arange(length, dtype=jnp.int32)[None] - (WIN - 1))
    lo = jnp.stack([jnp.where(c == 0, lo[0], lo[2]), lo[1]])[:, None]

    stacked = jnp.stack(blocks)
    in_order = lambda s: [lax.dynamic_index_in_dim(s, t ^ p, 0, False) for p in range(4)]
    all_tokens = jnp.stack(in_order(stacked), axis=1).reshape(sequences * span, width)

    def inverse(v):
        return lax.rsqrt(jnp.mean(v * v, axis=-1, keepdims=True) + epsilon)

    wide_tokens = all_tokens.astype(full)
    normed_one = (wide_tokens * inverse(wide_tokens) * gain_first).astype(low)
    projected = dot(w_attn, normed_one, ((0,), (1,))).astype(low)

    def units(array, parts, core):
        block = array.reshape(parts, heads, HD, sequences * span)
        whole = lax.dynamic_slice_in_dim(block, 2 * core * span, span, 3)
        shared = lax.dynamic_slice_in_dim(block[..., span : 2 * span], core, 2, 1)
        whole, shared = (a.reshape(-1, HD, span) for a in (whole, shared))
        return jnp.concatenate([whole, shared], axis=0)

    def rejoin(mine, theirs):
        first = jnp.where(c == 0, mine[:3], theirs[:3])
        last = jnp.where(c == 0, theirs[:3], mine[:3])
        shared = jnp.where(
            c == 0,
            jnp.concatenate([mine[3:5], theirs[4:5]]),
            jnp.concatenate([theirs[3:4], mine[3:5]]),
        )
        return jnp.stack([first, shared, last])

    core = c.reshape(1).astype(jnp.int32)
    qkv_mine = units(projected, 3, c)
    qkv_theirs = across(units(projected, 3, 1 - c), "context", 1)
    out_mine, out_sent, log_totals, out_full = attend(core, qkv_mine, qkv_theirs, lo)
    heads_out = rejoin(out_mine, across(out_sent, "context", 1))
    heads_out = heads_out.reshape(sequences, local, span)

    def to_owner(array, by):
        piece = lax.dynamic_slice_in_dim(array, (t ^ by) * own, own, 2)
        return across(piece, "tensor", by) if by else piece

    attended = jnp.stack([to_owner(heads_out, r) for r in range(4)])
    attended = attended.transpose(0, 2, 1, 3).reshape(4 * local, rows)

    proj_rows = w_proj.transpose(0, 2, 1).reshape(4 * local, width)
    inputs = tokens.astype(full).reshape(rows, width)
    middle = inputs + tn(attended, proj_rows)
    inv_two = inverse(middle)
    normed_two = (middle * inv_two * gain_second).astype(low)

    both = jnp.concatenate([normed_two, across(normed_two, "context", 1)], axis=0)
    cot = cotangent.reshape(rows, width)
    both_cot = jnp.concatenate([cot, cot_theirs.reshape(rows, width)], axis=0)
    up = w_up.transpose(1, 0, 2).reshape(width, 4 * hidden)
    down = w_down.transpose(1, 0, 2).reshape(width, 4 * hidden)
    hidden_pre = nn(both, up)
    active, slope = gelu_and_slope(hidden_pre)
    active = active.astype(low)
    grad_hidden = (nn(both_cot, down) * slope).astype(low)
    branch = nt(active, down)
    back = nt(grad_hidden, up)
    crossed = across(back[rows:].astype(low), "context", 1).astype(full)
    grad_norm_two = back[:rows] + crossed
    crossed = across(branch[rows:].astype(low), "context", 1).astype(full)
    result = (middle + branch[:rows] + crossed).astype(low)
    grad_down = tn(both_cot, active)
    grad_up = tn(both, grad_hidden)

    def norm_back(r, gain, v, inv):
        rg = r * gain
        return inv * (rg - v * (inv * inv * jnp.mean(rg * v, axis=-1, keepdims=True)))

    grad_middle = cot.astype(full) + norm_back(grad_norm_two, gain_second, middle, inv_two)
    grad_low = grad_middle.astype(low)
    grad_proj = nn(attended, grad_low)
    grad_att = nt(proj_rows, grad_low).astype(low).reshape(4, local, sequences, own)
    grad_heads = jnp.stack([across(grad_att[r], "tensor", r) if r else grad_att[0] for r in range(4)])
    grad_heads = jnp.stack(in_order(grad_heads), axis=2).reshape(local, sequences * span)
    g_mine = units(grad_heads, 1, c)
    g_theirs = across(units(grad_heads, 1, 1 - c), "context", 1)
    d_mine, d_sent = attend_back(core, qkv_mine, qkv_theirs, g_mine, g_theirs, lo, log_totals, out_full)
    grad_projected = rejoin(d_mine, across(d_sent, "context", 1))
    grad_projected = grad_projected.transpose(2, 1, 3, 0, 4).reshape(3 * local, sequences * span)
    grad_attn = nn(grad_projected, normed_one)
    spread = dot(grad_projected, w_attn, ((0,), (1,))).reshape(sequences, 4, own, width)
    spread = [lax.dynamic_index_in_dim(spread, t ^ r, 1, False) for r in range(4)]
    grad_norm_one = scatter_tensor(spread, 1).reshape(rows, width)
    inv_one = inverse(inputs)
    grad_input = grad_middle + norm_back(grad_norm_one, gain_first, inputs, inv_one)

    def scatter_dp(array, axis):
        return lax.psum_scatter(array.astype(low), "dp", scatter_dimension=axis, tiled=True)

    def swap_halves(mine, axis):
        theirs = across(mine, "context", 1)
        return jnp.where(
            c == 0,
            jnp.concatenate([mine, theirs], axis=axis),
            jnp.concatenate([theirs, mine], axis=axis),
        )

    def half_sum(array, axis):
        size = array.shape[axis] // 2
        mine = lax.dynamic_slice_in_dim(array, c * size, size, axis)
        sent = lax.dynamic_slice_in_dim(array, (1 - c) * size, size, axis)
        return mine + across(sent.astype(low), "context", 1).astype(full)

    up_down = jnp.stack([grad_up, grad_down]).reshape(2, width, 4, hidden)
    up_down = scatter_tensor([up_down[:, :, r] for r in range(4)], 1)
    up_down = scatter_dp(up_down, 1)
    own_up = swap_halves(up_down[0], 1).astype(full)
    own_down = swap_halves(up_down[1].T, 0).astype(full)
    proj = half_sum(grad_proj.reshape(4, local, width), 1)
    proj = scatter_dp(scatter_tensor([proj[r] for r in range(4)], 0), 1)
    own_proj = swap_halves(proj, 0).astype(full)
    attn = scatter_dp(half_sum(grad_attn, 0), 1).T
    own_attn = swap_halves(attn, 1).astype(full)

    def gain_grad(weight, grad, gain):
        part = jnp.sum(weight.astype(full) * grad, axis=1)
        return lax.psum(part, "tensor") / gain.astype(full)

    own_gain_attn = gain_grad(w_qkv.reshape(shard, 3 * local), own_attn, gain_attn)
    own_gain_mlp = gain_grad(w_in, own_up, gain_mlp)
    return (
        result.reshape(sequences, own, width),
        grad_input.astype(low).reshape(sequences, own, width),
        own_attn.reshape(shard, 3, local),
        own_proj,
        own_up,
        own_down,
        own_gain_attn,
        own_gain_mlp,
    )


def solution(mesh):
    return jax.shard_map(
        per_device,
        mesh=mesh,
        in_specs=(
            P("dp", ("context", "tensor"), None),
            P("dp", None),
            P("dp", None, "tensor"),
            P("tensor", "dp"),
            P("dp", "tensor"),
            P("tensor", "dp"),
            P("dp"),
            P("dp"),
            P("dp", ("context", "tensor"), None),
        ),
        out_specs=(
            P("dp", ("context", "tensor"), None),
            P("dp", ("context", "tensor"), None),
            P("dp", None, "tensor"),
            P("tensor", "dp"),
            P("dp", "tensor"),
            P("tensor", "dp"),
            P("dp"),
            P("dp"),
        ),
        check_vma=False,
    )
```

```python
import functools
import math

import jax
import jax.numpy as jnp
from jax import lax
from jax.experimental import pallas as pl
from jax.experimental.pallas import tpu as pltpu
from jax.sharding import PartitionSpec as P

HD = 64
WIN = 1536
QB = 256
CHUNK = 128
NEG = -1e30
epsilon = 1e-06
low = jnp.bfloat16
full = jnp.float32


def dot(left, right, dims):
    return lax.dot_general(left, right, (dims, ((), ())), preferred_element_type=full)


def nn(left, right):
    return dot(left, right, ((1,), (0,)))


def nt(left, right):
    return dot(left, right, ((1,), (1,)))


def tn(left, right):
    return dot(left, right, ((0,), (0,)))


def across(array, axis, by):
    return lax.ppermute(array, axis, [(i, i ^ by) for i in range(lax.axis_size(axis))])


def gather_tensor(array, axis):
    half = array.shape[axis] // 2
    one = lax.slice_in_dim(array, 0, half, axis=axis)
    two = lax.slice_in_dim(array, half, 2 * half, axis=axis)
    one_x, two_y = across(one, "tensor", 1), across(two, "tensor", 2)
    one_y, one_d = across(one, "tensor", 2), across(one_x, "tensor", 2)
    two_x, two_d = across(two, "tensor", 1), across(two_y, "tensor", 1)
    join = lambda a, b: jnp.concatenate([a, b], axis=axis)
    return [array, join(one_x, two_x), join(one_y, two_y), join(one_d, two_d)]


def scatter_tensor(parts, axis):
    half = parts[0].shape[axis] // 2
    one = [lax.slice_in_dim(p, 0, half, axis=axis) for p in parts]
    two = [lax.slice_in_dim(p, half, 2 * half, axis=axis) for p in parts]

    def reduce(p, first, second):
        sent = jnp.stack([p[first], p[first ^ second]]).astype(low)
        got = across(sent, "tensor", first).astype(full)
        mine, theirs = p[0] + got[0], p[second] + got[1]
        return mine + across(theirs.astype(low), "tensor", second).astype(full)

    return jnp.concatenate([reduce(one, 1, 2), reduce(two, 2, 1)], axis=axis)


def gather_dp(array, axis):
    n = lax.axis_size("dp")
    if n != 4:
        return lax.all_gather(array, "dp", axis=axis, tiled=True)
    parts = jnp.stack([across(array, "dp", r) if r else array for r in range(n)])
    d = lax.axis_index("dp")
    return jnp.concatenate(
        [lax.dynamic_index_in_dim(parts, d ^ p, 0, False) for p in range(n)], axis=axis
    )


UNITS = 5


def unit_block(part):
    return lambda u, c: (jnp.where(u < 3, part * 3 + u, 9 + part * 2 + (u - 3)), 0, 0)


def attend_kernel(c_ref, qm, km, vm, qt, kt, vt, lo_ref, om, ot, lse_ref, of_ref, qs, ks, vs, ss):
    c = c_ref[0]
    length = lo_ref.shape[2]
    half = length // 2
    for place, q, k, v in ((c, qm, km, vm), (1 - c, qt, kt, vt)):
        off = pl.multiple_of(place * half, half)
        qs[:, pl.ds(off, half)] = q[0] * low(0.125)
        vs[:, pl.ds(off, half)] = v[0]
        ks[pl.ds(off, half), :] = k[0].T
    for start in range(0, length, QB):
        stop = start + QB
        q = qs[:, start:stop]
        lo = lo_ref[0, :, start:stop]
        first = max(0, start - WIN)
        most = jnp.full((8, QB), NEG, full)
        for at in range(first, stop, CHUNK):
            s = nn(ks[at : at + CHUNK, :], q)
            key_pos = at + lax.broadcasted_iota(jnp.int32, (CHUNK, QB), 0)
            allowed = key_pos >= lo
            if at + CHUNK - 1 > start:
                allowed &= key_pos <= start + lax.broadcasted_iota(jnp.int32, (CHUNK, QB), 1)
            s = jnp.where(allowed, s, NEG)
            ss[at - first : at - first + CHUNK, :] = s
            most = jnp.maximum(most, jnp.max(s.reshape(CHUNK // 8, 8, QB), axis=0))
        most = jnp.max(most, axis=0, keepdims=True)
        total = jnp.zeros((8, QB), full)
        acc = jnp.zeros((HD, QB), full)
        for at in range(first, stop, CHUNK):
            p = jnp.exp(ss[at - first : at - first + CHUNK, :] - most)
            total += jnp.sum(p.reshape(CHUNK // 8, 8, QB), axis=0)
            acc += nn(vs[:, at : at + CHUNK], p.astype(low))
        total = jnp.sum(total, axis=0, keepdims=True)
        lse_ref[0, :, start:stop] = most + jnp.log(total)
        of_ref[0, :, start:stop] = acc * (1.0 / total)
    om[0] = of_ref[0, :, pl.ds(pl.multiple_of(c * half, half), half)].astype(low)
    ot[0] = of_ref[0, :, pl.ds(pl.multiple_of((1 - c) * half, half), half)].astype(low)


def attend(c, mine, theirs, lo):
    length = lo.shape[2]
    half = length // 2
    part = lambda p: pl.BlockSpec((1, HD, half), unit_block(p))
    unit = lambda rows, n: pl.BlockSpec((1, rows, n), lambda u, c: (u, 0, 0))
    return pl.pallas_call(
        attend_kernel,
        grid_spec=pltpu.PrefetchScalarGridSpec(
            num_scalar_prefetch=1,
            grid=(UNITS,),
            in_specs=[part(0), part(1), part(2)] * 2
            + [pl.BlockSpec((1, 1, length), lambda u, c: (u // 3, 0, 0))],
            out_specs=[unit(HD, half), unit(HD, half), unit(1, length), unit(HD, length)],
            scratch_shapes=[
                pltpu.VMEM((HD, length), low),
                pltpu.VMEM((length, HD), low),
                pltpu.VMEM((HD, length), low),
                pltpu.VMEM((WIN + QB, QB), full),
            ],
        ),
        out_shape=[jax.ShapeDtypeStruct((UNITS, HD, half), low)] * 2
        + [
            jax.ShapeDtypeStruct((UNITS, 1, length), full),
            jax.ShapeDtypeStruct((UNITS, HD, length), full),
        ],
        compiler_params=pltpu.CompilerParams(vmem_limit_bytes=40 << 20),
        cost_estimate=pl.CostEstimate(
            flops=UNITS * 18 * 2 * 256 * 1024 * 128, bytes_accessed=20 << 20, transcendentals=0
        ),
        name="attend",
    )(c, mine, mine, mine, theirs, theirs, theirs, lo)


def attend_back_kernel(
    c_ref, qm, km, vm, gm, qt, kt, vt, gt, lo_ref, lse_ref, of_ref, dm, dt,
    qs, ks, kts, vs, gs, grow, qrow, delta, dqs, dks, dvs,
):
    c = c_ref[0]
    length = lo_ref.shape[2]
    half = length // 2
    for place, q, k, v, g in ((c, qm, km, vm, gm), (1 - c, qt, kt, vt, gt)):
        off = pl.multiple_of(place * half, half)
        scaled = q[0] * low(0.125)
        qs[:, pl.ds(off, half)] = scaled
        kts[:, pl.ds(off, half)] = k[0]
        gs[:, pl.ds(off, half)] = g[0]
        ks[pl.ds(off, half), :] = k[0].T
        vs[pl.ds(off, half), :] = v[0].T
        grow[pl.ds(off, half), :] = g[0].T
        qrow[pl.ds(off, half), :] = scaled.T
        delta[:, pl.ds(off, half)] = jnp.sum(
            g[0].astype(full) * of_ref[0, :, pl.ds(off, half)], axis=0, keepdims=True
        )
    dqs[...] = jnp.zeros_like(dqs)
    for key_start in range(0, length, QB):
        rows = slice(key_start, key_start + QB)
        k, v, key_t = ks[rows, :], vs[rows, :], kts[:, rows]
        dk = jnp.zeros((QB, HD), full)
        dv = jnp.zeros((QB, HD), full)
        key_pos = key_start + lax.broadcasted_iota(jnp.int32, (QB, QB), 0)
        for start in range(key_start, min(key_start + WIN + QB, length), QB):
            cols = slice(start, start + QB)
            s = nn(k, qs[:, cols]) - lse_ref[0, :, cols]
            allowed = key_pos >= lo_ref[0, :, cols]
            if start == key_start:
                allowed &= key_pos <= start + lax.broadcasted_iota(jnp.int32, (QB, QB), 1)
            p = jnp.exp(jnp.where(allowed, s, NEG))
            dp = nn(v, gs[:, cols])
            ds = (p * (dp - delta[:, cols])).astype(low)
            dv += nn(p.astype(low), grow[cols, :])
            dk += nn(ds, qrow[cols, :])
            dqs[:, cols] += nn(key_t, ds)
        dks[:, rows] = dk.T.astype(low)
        dvs[:, rows] = dv.T.astype(low)
    for ref, place in ((dm, c), (dt, 1 - c)):
        off = pl.ds(pl.multiple_of(place * half, half), half)
        ref[0, 0] = (dqs[:, off] * 0.125).astype(low)
        ref[0, 1] = dks[:, off]
        ref[0, 2] = dvs[:, off]


def attend_back(c, mine, theirs, grad_mine, grad_theirs, lo, lse, attended):
    length = lo.shape[2]
    half = length // 2
    part = lambda p: pl.BlockSpec((1, HD, half), unit_block(p))
    unit = lambda rows, n: pl.BlockSpec((1, rows, n), lambda u, c: (u, 0, 0))
    wide, tall = pltpu.VMEM((HD, length), low), pltpu.VMEM((length, HD), low)
    return pl.pallas_call(
        attend_back_kernel,
        grid_spec=pltpu.PrefetchScalarGridSpec(
            num_scalar_prefetch=1,
            grid=(UNITS,),
            in_specs=[part(0), part(1), part(2), unit(HD, half)] * 2
            + [
                pl.BlockSpec((1, 1, length), lambda u, c: (u // 3, 0, 0)),
                unit(1, length),
                unit(HD, length),
            ],
            out_specs=[pl.BlockSpec((1, 3, HD, half), lambda u, c: (u, 0, 0, 0))] * 2,
            scratch_shapes=[
                wide, tall, wide, tall, wide, tall, tall,
                pltpu.VMEM((1, length), full), pltpu.VMEM((HD, length), full), wide, wide,
            ],
        ),
        out_shape=[jax.ShapeDtypeStruct((UNITS, 3, HD, half), low)] * 2,
        compiler_params=pltpu.CompilerParams(vmem_limit_bytes=40 << 20),
        cost_estimate=pl.CostEstimate(
            flops=UNITS * 18 * 5 * 256 * 1024 * 128, bytes_accessed=30 << 20, transcendentals=0
        ),
        name="attend_back",
    )(c, mine, mine, mine, grad_mine, theirs, theirs, theirs, grad_theirs, lo, lse, attended)


def gelu_and_slope(v):
    k0 = math.sqrt(2.0 / math.pi)
    square = v * v
    th = jnp.tanh(v * (k0 + (k0 * 0.044715) * square))
    half = 0.5 + 0.5 * th
    slope = half + (v * half) * ((1.0 - th) * (k0 + (3.0 * 0.044715 * k0) * square))
    return v * half, slope


def feed_kernel(
    xm, xt, gm, gt, up_ref, down_ref, om, ot, bm, bt, dup, ddown,
    x, g, x_t, g_t, up, down, act, gh, out, back, pre, ga,
):
    rows, width = xm.shape
    n = up_ref.shape[2]
    blocks = 2 * rows // QB

    @pl.when(pl.program_id(0) == 0)
    def _():
        for i, (a, b) in enumerate(((xm, gm), (xt, gt))):
            part = slice(i * rows, (i + 1) * rows)
            x[part, :] = a[...]
            g[part, :] = b[...]
            x_t[:, part] = a[...].T
            g_t[:, part] = b[...].T
        out[...] = jnp.zeros_like(out)
        back[...] = jnp.zeros_like(back)

    for i in range(2):
        up[:, i * n : (i + 1) * n] = up_ref[i]
        down[:, i * n : (i + 1) * n] = down_ref[i]

    def first(i):
        part = slice(i * QB, (i + 1) * QB)
        pre[i % 2] = nn(x[part, :], up[...])
        ga[i % 2] = nn(g[part, :], down[...])

    def second(i):
        part = slice(i * QB, (i + 1) * QB)
        a, slope = gelu_and_slope(pre[i % 2])
        act[part, :] = a.astype(low)
        gh[part, :] = (ga[i % 2] * slope).astype(low)

    def third(i):
        part = slice(i * QB, (i + 1) * QB)
        out[part, :] += nt(act[part, :], down[...])
        back[part, :] += nt(gh[part, :], up[...])

    first(0)
    for i in range(blocks):
        if i + 1 < blocks:
            first(i + 1)
        second(i)
        if i > 0:
            third(i - 1)
    third(blocks - 1)
    for m in range(0, width, QB):
        part = slice(m, m + QB)
        u = nn(x_t[part, :], gh[...]).astype(low)
        v = nn(g_t[part, :], act[...]).astype(low)
        for i in range(2):
            dup[i, part, :] = u[:, i * n : (i + 1) * n]
            ddown[i, part, :] = v[:, i * n : (i + 1) * n]

    @pl.when(pl.program_id(0) == pl.num_programs(0) - 1)
    def _():
        om[...] = out[:rows, :]
        ot[...] = out[rows:, :].astype(low)
        bm[...] = back[:rows, :]
        bt[...] = back[rows:, :].astype(low)


def feed(xm, xt, gm, gt, up, down):
    rows, width = xm.shape
    pieces, _, n = up.shape
    whole = pl.BlockSpec((rows, width), lambda j: (0, 0))
    weight = pl.BlockSpec((2, width, n), lambda j: (j, 0, 0))
    shape = jax.ShapeDtypeStruct
    return pl.pallas_call(
        feed_kernel,
        grid=(pieces // 2,),
        in_specs=[whole] * 4 + [weight] * 2,
        out_specs=[whole] * 4 + [weight] * 2,
        out_shape=[shape((rows, width), kind) for kind in (full, low, full, low)]
        + [shape(up.shape, low)] * 2,
        scratch_shapes=[pltpu.VMEM((2 * rows, width), low)] * 2
        + [pltpu.VMEM((width, 2 * rows), low)] * 2
        + [pltpu.VMEM((width, 2 * n), low)] * 2
        + [pltpu.VMEM((2 * rows, 2 * n), low)] * 2
        + [pltpu.VMEM((2 * rows, width), full)] * 2
        + [pltpu.VMEM((2, QB, 2 * n), full)] * 2,
        compiler_params=pltpu.CompilerParams(vmem_limit_bytes=60 << 20),
        cost_estimate=pl.CostEstimate(
            flops=6 * 2 * 2 * rows * width * pieces * n, bytes_accessed=20 << 20, transcendentals=0
        ),
        name="feed",
    )(xm, xt, gm, gt, up, down)


def per_device(tokens, segments, w_qkv, w_out, w_in, w_back, gain_attn, gain_mlp, cotangent):
    sequences, own, width = tokens.shape
    assert lax.axis_size("tensor") == 4 and lax.axis_size("context") == 2 and sequences == 3
    c, t, d = lax.axis_index("context"), lax.axis_index("tensor"), lax.axis_index("dp")
    span = 4 * own
    length = segments.shape[1]
    shard = w_qkv.shape[0]
    local = w_qkv.shape[2]
    heads = local // HD
    hidden = w_in.shape[1] // 2
    rows = sequences * own

    blocks = gather_tensor(tokens, 1)
    cot_theirs = across(cotangent, "context", 1)
    w_attn = gather_dp(w_qkv.reshape(shard, 3 * local), 0)
    gains = gather_dp(jnp.stack([gain_attn, gain_mlp], axis=1), 0)
    gain_first, gain_second = gains[:, 0].astype(full), gains[:, 1].astype(full)
    up_own = lax.dynamic_slice_in_dim(w_in, c * hidden, hidden, 1)
    down_own = lax.dynamic_slice_in_dim(w_back, c * hidden, hidden, 0).T
    up_down = jnp.stack(gather_tensor(jnp.stack([up_own, down_own]), 1), axis=1)
    up_down = gather_dp(up_down, 2)
    w_up, w_down = up_down[0], up_down[1]
    w_proj = jnp.stack(gather_tensor(w_out.T, 0), axis=0)
    w_proj = gather_dp(w_proj, 1)

    lo = jnp.zeros((sequences, length), jnp.int32)
    for value in range(8):
        before = jnp.sum((segments < value).astype(jnp.int32), axis=1, keepdims=True)
        lo = jnp.where(segments == value, before, lo)
    lo = jnp.maximum(lo, jnp.arange(length, dtype=jnp.int32)[None] - (WIN - 1))
    lo = jnp.stack([jnp.where(c == 0, lo[0], lo[2]), lo[1]])[:, None]

    stacked = jnp.stack(blocks)
    in_order = lambda s: [lax.dynamic_index_in_dim(s, t ^ p, 0, False) for p in range(4)]
    all_tokens = jnp.stack(in_order(stacked), axis=1).reshape(sequences * span, width)

    def inverse(v):
        return lax.rsqrt(jnp.mean(v * v, axis=-1, keepdims=True) + epsilon)

    wide_tokens = all_tokens.astype(full)
    normed_one = (wide_tokens * inverse(wide_tokens) * gain_first).astype(low)
    projected = dot(w_attn, normed_one, ((0,), (1,))).astype(low)

    def units(array, parts, core):
        block = array.reshape(parts, heads, HD, sequences * span)
        whole = lax.dynamic_slice_in_dim(block, 2 * core * span, span, 3)
        shared = lax.dynamic_slice_in_dim(block[..., span : 2 * span], core, 2, 1)
        whole, shared = (a.reshape(-1, HD, span) for a in (whole, shared))
        return jnp.concatenate([whole, shared], axis=0)

    def rejoin(mine, theirs):
        first = jnp.where(c == 0, mine[:3], theirs[:3])
        last = jnp.where(c == 0, theirs[:3], mine[:3])
        shared = jnp.where(
            c == 0,
            jnp.concatenate([mine[3:5], theirs[4:5]]),
            jnp.concatenate([theirs[3:4], mine[3:5]]),
        )
        return jnp.stack([first, shared, last])

    core = c.reshape(1).astype(jnp.int32)
    qkv_mine = units(projected, 3, c)
    qkv_theirs = across(units(projected, 3, 1 - c), "context", 1)
    out_mine, out_sent, log_totals, out_full = attend(core, qkv_mine, qkv_theirs, lo)
    heads_out = rejoin(out_mine, across(out_sent, "context", 1))
    heads_out = heads_out.reshape(sequences, local, span)

    def to_owner(array, by):
        piece = lax.dynamic_slice_in_dim(array, (t ^ by) * own, own, 2)
        return across(piece, "tensor", by) if by else piece

    attended = jnp.stack([to_owner(heads_out, r) for r in range(4)])
    attended = attended.transpose(0, 2, 1, 3).reshape(4 * local, rows)

    proj_rows = w_proj.transpose(0, 2, 1).reshape(4 * local, width)
    inputs = tokens.astype(full).reshape(rows, width)
    middle = inputs + tn(attended, proj_rows)
    inv_two = inverse(middle)
    normed_two = (middle * inv_two * gain_second).astype(low)

    cot = cotangent.reshape(rows, width)
    branch, branch_sent, back, back_sent, grad_up, grad_down = feed(
        normed_two, across(normed_two, "context", 1), cot, cot_theirs.reshape(rows, width), w_up, w_down
    )
    grad_norm_two = back + across(back_sent, "context", 1).astype(full)
    result = (middle + branch + across(branch_sent, "context", 1).astype(full)).astype(low)

    def norm_back(r, gain, v, inv):
        rg = r * gain
        return inv * (rg - v * (inv * inv * jnp.mean(rg * v, axis=-1, keepdims=True)))

    grad_middle = cot.astype(full) + norm_back(grad_norm_two, gain_second, middle, inv_two)
    grad_low = grad_middle.astype(low)
    grad_proj = nn(attended, grad_low)
    grad_att = nt(proj_rows, grad_low).astype(low).reshape(4, local, sequences, own)
    grad_heads = jnp.stack([across(grad_att[r], "tensor", r) if r else grad_att[0] for r in range(4)])
    grad_heads = jnp.stack(in_order(grad_heads), axis=2).reshape(local, sequences * span)
    g_mine = units(grad_heads, 1, c)
    g_theirs = across(units(grad_heads, 1, 1 - c), "context", 1)
    d_mine, d_sent = attend_back(core, qkv_mine, qkv_theirs, g_mine, g_theirs, lo, log_totals, out_full)
    grad_projected = rejoin(d_mine, across(d_sent, "context", 1))
    grad_projected = grad_projected.transpose(2, 1, 3, 0, 4).reshape(3 * local, sequences * span)
    grad_attn = nn(grad_projected, normed_one)
    spread = dot(grad_projected, w_attn, ((0,), (1,))).reshape(sequences, 4, own, width)
    spread = [lax.dynamic_index_in_dim(spread, t ^ r, 1, False) for r in range(4)]
    grad_norm_one = scatter_tensor(spread, 1).reshape(rows, width)
    inv_one = inverse(inputs)
    grad_input = grad_middle + norm_back(grad_norm_one, gain_first, inputs, inv_one)

    def scatter_dp(array, axis):
        return lax.psum_scatter(array.astype(low), "dp", scatter_dimension=axis, tiled=True)

    def swap_halves(mine, axis):
        theirs = across(mine, "context", 1)
        return jnp.where(
            c == 0,
            jnp.concatenate([mine, theirs], axis=axis),
            jnp.concatenate([theirs, mine], axis=axis),
        )

    def half_sum(array, axis):
        size = array.shape[axis] // 2
        mine = lax.dynamic_slice_in_dim(array, c * size, size, axis)
        sent = lax.dynamic_slice_in_dim(array, (1 - c) * size, size, axis)
        return mine + across(sent.astype(low), "context", 1).astype(full)

    up_down = [jnp.stack([grad_up[r], grad_down[r]]).astype(full) for r in range(4)]
    up_down = scatter_tensor(up_down, 1)
    up_down = scatter_dp(up_down, 1)
    own_up = swap_halves(up_down[0], 1).astype(full)
    own_down = swap_halves(up_down[1].T, 0).astype(full)
    proj = half_sum(grad_proj.reshape(4, local, width), 1)
    proj = scatter_dp(scatter_tensor([proj[r] for r in range(4)], 0), 1)
    own_proj = swap_halves(proj, 0).astype(full)
    attn = scatter_dp(half_sum(grad_attn, 0), 1).T
    own_attn = swap_halves(attn, 1).astype(full)

    def gain_grad(weight, grad, gain):
        part = jnp.sum(weight.astype(full) * grad, axis=1)
        return lax.psum(part, "tensor") / gain.astype(full)

    own_gain_attn = gain_grad(w_qkv.reshape(shard, 3 * local), own_attn, gain_attn)
    own_gain_mlp = gain_grad(w_in, own_up, gain_mlp)
    return (
        result.reshape(sequences, own, width),
        grad_input.astype(low).reshape(sequences, own, width),
        own_attn.reshape(shard, 3, local),
        own_proj,
        own_up,
        own_down,
        own_gain_attn,
        own_gain_mlp,
    )


def solution(mesh):
    return jax.shard_map(
        per_device,
        mesh=mesh,
        in_specs=(
            P("dp", ("context", "tensor"), None),
            P("dp", None),
            P("dp", None, "tensor"),
            P("tensor", "dp"),
            P("dp", "tensor"),
            P("tensor", "dp"),
            P("dp"),
            P("dp"),
            P("dp", ("context", "tensor"), None),
        ),
        out_specs=(
            P("dp", ("context", "tensor"), None),
            P("dp", ("context", "tensor"), None),
            P("dp", None, "tensor"),
            P("tensor", "dp"),
            P("dp", "tensor"),
            P("tensor", "dp"),
            P("dp"),
            P("dp"),
        ),
        check_vma=False,
    )
```

```python
import functools
import math

import jax
import jax.numpy as jnp
from jax import lax
from jax.experimental import pallas as pl
from jax.experimental.pallas import tpu as pltpu
from jax.sharding import PartitionSpec as P

HD = 64
WIN = 1536
QB = 256
CHUNK = 128
NEG = -1e30
epsilon = 1e-06
low = jnp.bfloat16
full = jnp.float32


def dot(left, right, dims):
    return lax.dot_general(left, right, (dims, ((), ())), preferred_element_type=full)


def nn(left, right):
    return dot(left, right, ((1,), (0,)))


def nt(left, right):
    return dot(left, right, ((1,), (1,)))


def tn(left, right):
    return dot(left, right, ((0,), (0,)))


def across(array, axis, by):
    return lax.ppermute(array, axis, [(i, i ^ by) for i in range(lax.axis_size(axis))])


def gather_tensor(array, axis):
    half = array.shape[axis] // 2
    one = lax.slice_in_dim(array, 0, half, axis=axis)
    two = lax.slice_in_dim(array, half, 2 * half, axis=axis)
    one_x, two_y = across(one, "tensor", 1), across(two, "tensor", 2)
    one_y, one_d = across(one, "tensor", 2), across(one_x, "tensor", 2)
    two_x, two_d = across(two, "tensor", 1), across(two_y, "tensor", 1)
    join = lambda a, b: jnp.concatenate([a, b], axis=axis)
    return [array, join(one_x, two_x), join(one_y, two_y), join(one_d, two_d)]


def scatter_tensor(parts, axis):
    half = parts[0].shape[axis] // 2
    one = [lax.slice_in_dim(p, 0, half, axis=axis) for p in parts]
    two = [lax.slice_in_dim(p, half, 2 * half, axis=axis) for p in parts]

    def reduce(p, first, second):
        sent = jnp.stack([p[first], p[first ^ second]]).astype(low)
        got = across(sent, "tensor", first).astype(full)
        mine, theirs = p[0] + got[0], p[second] + got[1]
        return mine + across(theirs.astype(low), "tensor", second).astype(full)

    return jnp.concatenate([reduce(one, 1, 2), reduce(two, 2, 1)], axis=axis)


def gather_dp(array, axis):
    n = lax.axis_size("dp")
    if n != 4:
        return lax.all_gather(array, "dp", axis=axis, tiled=True)
    parts = jnp.stack([across(array, "dp", r) if r else array for r in range(n)])
    d = lax.axis_index("dp")
    return jnp.concatenate(
        [lax.dynamic_index_in_dim(parts, d ^ p, 0, False) for p in range(n)], axis=axis
    )


UNITS = 5
PEERS = [(dc, r) for dc in range(2) for r in range(4)]


def place():
    return lax.axis_index("context"), lax.axis_index("tensor")


def at_peer(c, t, dc, r):
    return {"context": c ^ dc, "tensor": t ^ r}


def greet(c, t):
    barrier = pltpu.get_barrier_semaphore()
    for dc, r in PEERS[1:]:
        pl.semaphore_signal(barrier, inc=1, device_id=at_peer(c, t, dc, r))


def greeted():
    pl.semaphore_wait(pltpu.get_barrier_semaphore(), len(PEERS) - 1)


def unit_place(u, c):
    return jnp.where(u < 3, u, c + u - 3), jnp.where(u < 3, 2 * c, 1)


def sends(u, c):
    return (u != 3) | (c == 0)


def unit_block(part):
    return lambda u: (jnp.where(u < 3, part * 3 + u, 9 + part * 2 + (u - 3)), 0, 0)


def attend_kernel(
    qm, km, vm, qt, kt, vt, lo_ref, att, lse_ref, of_ref, qs, ks, vs, ss, obuf, ssem, rsem, lsem
):
    u = pl.program_id(0)
    c, t = place()
    length = lo_ref.shape[2]
    half = length // 2
    own = half // 4

    @pl.when(u == 0)
    def _():
        greet(c, t)

    for core, q, k, v in ((c, qm, km, vm), (1 - c, qt, kt, vt)):
        off = pl.multiple_of(core * half, half)
        qs[:, pl.ds(off, half)] = q[0] * low(0.125)
        vs[:, pl.ds(off, half)] = v[0]
        ks[pl.ds(off, half), :] = k[0].T
    for start in range(0, length, QB):
        stop = start + QB
        q = qs[:, start:stop]
        lo = lo_ref[0, :, start:stop]
        first = max(0, start - WIN)
        most = jnp.full((8, QB), NEG, full)
        for at in range(first, stop, CHUNK):
            s = nn(ks[at : at + CHUNK, :], q)
            key_pos = at + lax.broadcasted_iota(jnp.int32, (CHUNK, QB), 0)
            allowed = key_pos >= lo
            if at + CHUNK - 1 > start:
                allowed &= key_pos <= start + lax.broadcasted_iota(jnp.int32, (CHUNK, QB), 1)
            s = jnp.where(allowed, s, NEG)
            ss[at - first : at - first + CHUNK, :] = s
            most = jnp.maximum(most, jnp.max(s.reshape(CHUNK // 8, 8, QB), axis=0))
        most = jnp.max(most, axis=0, keepdims=True)
        total = jnp.zeros((8, QB), full)
        acc = jnp.zeros((HD, QB), full)
        for at in range(first, stop, CHUNK):
            p = jnp.exp(ss[at - first : at - first + CHUNK, :] - most)
            total += jnp.sum(p.reshape(CHUNK // 8, 8, QB), axis=0)
            acc += nn(vs[:, at : at + CHUNK], p.astype(low))
        total = jnp.sum(total, axis=0, keepdims=True)
        lse_ref[0, :, start:stop] = most + jnp.log(total)
        o = acc * (1.0 / total)
        of_ref[0, :, start:stop] = o
        obuf[u, :, start:stop] = o.astype(low)

    @pl.when(u == 0)
    def _():
        greeted()

    def move(unit, i, source_core):
        dc, r = PEERS[i]
        h, seq = unit_place(unit, source_core)
        dest = pl.multiple_of(((c ^ dc) * 4 + (t ^ r)) * own, own)
        src = obuf.at[unit, :, pl.ds(dest, own)]
        dst = att.at[
            pl.ds(pl.multiple_of((t * 3 + h) * HD, HD), HD), pl.ds(pl.multiple_of(seq * own, own), own)
        ]
        if i == 0:
            return pltpu.make_async_copy(src, dst, lsem.at[unit])
        return pltpu.make_async_remote_copy(
            src, dst, ssem.at[i - 1, unit], rsem.at[i - 1, unit], device_id=at_peer(c, t, dc, r)
        )

    @pl.when(sends(u, c))
    def _():
        for i in range(1, len(PEERS)):
            move(u, i, c).start()
        move(u, 0, c).start()

    @pl.when(u == pl.num_programs(0) - 1)
    def _():
        for unit in range(UNITS):
            for i, (dc, r) in enumerate(PEERS):

                @pl.when(sends(unit, c))
                def _():
                    if i:
                        move(unit, i, c).wait_send()
                    else:
                        move(unit, i, c).wait()

                if i:

                    @pl.when(sends(unit, c ^ dc))
                    def _():
                        move(unit, i, c ^ dc).wait_recv()


def attend(mine, theirs, lo):
    length = lo.shape[2]
    half = length // 2
    own = half // 4
    part = lambda p: pl.BlockSpec((1, HD, half), unit_block(p))
    unit = lambda rows, n: pl.BlockSpec((1, rows, n), lambda u: (u, 0, 0))
    heads = 4 * 3 * HD
    dma = pltpu.SemaphoreType.DMA
    return pl.pallas_call(
        attend_kernel,
        grid=(UNITS,),
        in_specs=[part(0), part(1), part(2)] * 2
        + [pl.BlockSpec((1, 1, length), lambda u: (u // 3, 0, 0))],
        out_specs=[pl.BlockSpec(memory_space=pl.ANY), unit(1, length), unit(HD, length)],
        scratch_shapes=[
            pltpu.VMEM((HD, length), low),
            pltpu.VMEM((length, HD), low),
            pltpu.VMEM((HD, length), low),
            pltpu.VMEM((WIN + QB, QB), full),
            pltpu.VMEM((UNITS, HD, length), low),
            dma((7, UNITS)),
            dma((7, UNITS)),
            dma((UNITS,)),
        ],
        out_shape=[
            jax.ShapeDtypeStruct((heads, 3 * own), low),
            jax.ShapeDtypeStruct((UNITS, 1, length), full),
            jax.ShapeDtypeStruct((UNITS, HD, length), full),
        ],
        compiler_params=pltpu.CompilerParams(
            vmem_limit_bytes=40 << 20, collective_id=1, has_side_effects=True
        ),
        cost_estimate=pl.CostEstimate(
            flops=UNITS * 18 * 2 * 256 * 1024 * 128, bytes_accessed=20 << 20, transcendentals=0
        ),
        name="attend",
    )(mine, mine, mine, theirs, theirs, theirs, lo)


def attend_back_kernel(
    qm, km, vm, qt, kt, vt, lo_ref, lse_ref, of_ref, norm_ref, gatt, dall, gw,
    qs, ks, kts, vs, gs, grow, qrow, delta, dqs, dbuf, gsem, grsem, glsem, ssem, rsem, lsem,
):
    u = pl.program_id(0)
    c, t = place()
    length = lo_ref.shape[2]
    half = length // 2
    own = half // 4
    groups = ((0, 3), (3, 2))

    def fetch(group, i, receiving):
        dc, r = PEERS[i]
        first, count = groups[group]
        to_c, to_t = (c ^ dc, t ^ r)
        seq = 2 * to_c if group == 0 else 1
        head = to_t * 3 + (0 if group == 0 else to_c)
        src = gatt.at[pl.ds(head, count), :, pl.ds(pl.multiple_of(seq * own, own), own)]
        dst = gs.at[pl.ds(first, count), :, pl.ds(pl.multiple_of((c * 4 + t) * own, own), own)]
        if i == 0:
            return pltpu.make_async_copy(src, dst, glsem.at[group])
        return pltpu.make_async_remote_copy(
            src, dst, gsem.at[i - 1, group], grsem.at[i - 1, group], device_id=at_peer(c, t, dc, r)
        )

    @pl.when(u == 0)
    def _():
        greet(c, t)
        gw[...] = jnp.zeros_like(gw)
        greeted()
        for group in range(2):
            for i in range(1, len(PEERS)):
                fetch(group, i, False).start()
            fetch(group, 0, False).start()

    for group in range(2):

        @pl.when(u == groups[group][0])
        def _():
            fetch(group, 0, True).wait()
            for i in range(1, len(PEERS)):
                fetch(group, i, True).wait_recv()

    for core, q, k, v in ((c, qm, km, vm), (1 - c, qt, kt, vt)):
        off = pl.multiple_of(core * half, half)
        scaled = q[0] * low(0.125)
        g = gs[u, :, pl.ds(off, half)]
        qs[:, pl.ds(off, half)] = scaled
        kts[:, pl.ds(off, half)] = k[0]
        ks[pl.ds(off, half), :] = k[0].T
        vs[pl.ds(off, half), :] = v[0].T
        grow[pl.ds(off, half), :] = g.T
        qrow[pl.ds(off, half), :] = scaled.T
        delta[:, pl.ds(off, half)] = jnp.sum(
            g.astype(full) * of_ref[0, :, pl.ds(off, half)], axis=0, keepdims=True
        )
    dqs[...] = jnp.zeros_like(dqs)
    for key_start in range(0, length, QB):
        rows = slice(key_start, key_start + QB)
        k, v, key_t = ks[rows, :], vs[rows, :], kts[:, rows]
        dk = jnp.zeros((QB, HD), full)
        dv = jnp.zeros((QB, HD), full)
        key_pos = key_start + lax.broadcasted_iota(jnp.int32, (QB, QB), 0)
        for start in range(key_start, min(key_start + WIN + QB, length), QB):
            cols = slice(start, start + QB)
            s = nn(k, qs[:, cols]) - lse_ref[0, :, cols]
            allowed = key_pos >= lo_ref[0, :, cols]
            if start == key_start:
                allowed &= key_pos <= start + lax.broadcasted_iota(jnp.int32, (QB, QB), 1)
            p = jnp.exp(jnp.where(allowed, s, NEG))
            dp = nn(v, gs[u, :, cols])
            ds = (p * (dp - delta[:, cols])).astype(low)
            dv += nn(p.astype(low), grow[cols, :])
            dk += nn(ds, qrow[cols, :])
            dqs[:, cols] += nn(key_t, ds)
        dbuf[u, 1, :, rows] = dk.T.astype(low)
        dbuf[u, 2, :, rows] = dv.T.astype(low)
    dbuf[u, 0] = (dqs[...] * 0.125).astype(low)

    def move(unit, i, source_core):
        dc, r = PEERS[i]
        h, seq = unit_place(unit, source_core)
        dest = pl.multiple_of(((c ^ dc) * 4 + (t ^ r)) * own, own)
        src = dbuf.at[unit, :, :, pl.ds(dest, own)]
        dst = dall.at[:, t * 3 + h, :, pl.ds(pl.multiple_of(seq * own, own), own)]
        if i == 0:
            return pltpu.make_async_copy(src, dst, lsem.at[unit])
        return pltpu.make_async_remote_copy(
            src, dst, ssem.at[i - 1, unit], rsem.at[i - 1, unit], device_id=at_peer(c, t, dc, r)
        )

    @pl.when(sends(u, c))
    def _():
        for i in range(1, len(PEERS)):
            move(u, i, c).start()
        move(u, 0, c).start()
        h, _ = unit_place(u, c)
        gw[h] += nn(dbuf[u].reshape(3 * HD, length), norm_ref[0])

    @pl.when(u == pl.num_programs(0) - 1)
    def _():
        for group in range(2):
            for i in range(1, len(PEERS)):
                fetch(group, i, False).wait_send()
        for unit in range(UNITS):
            for i, (dc, r) in enumerate(PEERS):

                @pl.when(sends(unit, c))
                def _():
                    if i:
                        move(unit, i, c).wait_send()
                    else:
                        move(unit, i, c).wait()

                if i:

                    @pl.when(sends(unit, c ^ dc))
                    def _():
                        move(unit, i, c ^ dc).wait_recv()


def attend_back(mine, theirs, grad_attended, lo, lse, attended, normed):
    length = lo.shape[2]
    half = length // 2
    own = half // 4
    width = normed.shape[2]
    part = lambda p: pl.BlockSpec((1, HD, half), unit_block(p))
    unit = lambda rows, n: pl.BlockSpec((1, rows, n), lambda u: (u, 0, 0))
    wide, tall = pltpu.VMEM((HD, length), low), pltpu.VMEM((length, HD), low)
    dma = pltpu.SemaphoreType.DMA
    return pl.pallas_call(
        attend_back_kernel,
        grid=(UNITS,),
        in_specs=[part(0), part(1), part(2)] * 2
        + [
            pl.BlockSpec((1, 1, length), lambda u: (u // 3, 0, 0)),
            unit(1, length),
            unit(HD, length),
            pl.BlockSpec((1, length, width), lambda u: (u // 3, 0, 0)),
            pl.BlockSpec(memory_space=pl.ANY),
        ],
        out_specs=[
            pl.BlockSpec(memory_space=pl.ANY),
            pl.BlockSpec((3, 3 * HD, width), lambda u: (0, 0, 0)),
        ],
        scratch_shapes=[
            wide, tall, wide, tall, pltpu.VMEM((UNITS, HD, length), low), tall, tall,
            pltpu.VMEM((1, length), full), pltpu.VMEM((HD, length), full),
            pltpu.VMEM((UNITS, 3, HD, length), low),
            dma((7, 2)), dma((7, 2)), dma((2,)), dma((7, UNITS)), dma((7, UNITS)), dma((UNITS,)),
        ],
        out_shape=[
            jax.ShapeDtypeStruct((3, 12, HD, 3 * own), low),
            jax.ShapeDtypeStruct((3, 3 * HD, width), full),
        ],
        compiler_params=pltpu.CompilerParams(
            vmem_limit_bytes=50 << 20, collective_id=2, has_side_effects=True
        ),
        cost_estimate=pl.CostEstimate(
            flops=UNITS * 18 * 5 * 256 * 1024 * 128, bytes_accessed=30 << 20, transcendentals=0
        ),
        name="attend_back",
    )(mine, mine, mine, theirs, theirs, theirs, lo, lse, attended, normed, grad_attended)


def gelu_and_slope(v):
    k0 = math.sqrt(2.0 / math.pi)
    square = v * v
    th = jnp.tanh(v * (k0 + (k0 * 0.044715) * square))
    half = 0.5 + 0.5 * th
    slope = half + (v * half) * ((1.0 - th) * (k0 + (3.0 * 0.044715 * k0) * square))
    return v * half, slope


def feed_kernel(
    xm, xt, gm, gt, up_ref, down_ref, om, ot, bm, bt, dup, ddown,
    x, g, x_t, g_t, up, down, act, gh, out, back, pre, ga,
):
    rows, width = xm.shape
    n = up_ref.shape[2]
    blocks = 2 * rows // QB

    @pl.when(pl.program_id(0) == 0)
    def _():
        for i, (a, b) in enumerate(((xm, gm), (xt, gt))):
            part = slice(i * rows, (i + 1) * rows)
            x[part, :] = a[...]
            g[part, :] = b[...]
            x_t[:, part] = a[...].T
            g_t[:, part] = b[...].T
        out[...] = jnp.zeros_like(out)
        back[...] = jnp.zeros_like(back)

    for i in range(2):
        up[:, i * n : (i + 1) * n] = up_ref[i]
        down[:, i * n : (i + 1) * n] = down_ref[i]

    def first(i):
        part = slice(i * QB, (i + 1) * QB)
        pre[i % 2] = nn(x[part, :], up[...])
        ga[i % 2] = nn(g[part, :], down[...])

    def second(i):
        part = slice(i * QB, (i + 1) * QB)
        a, slope = gelu_and_slope(pre[i % 2])
        act[part, :] = a.astype(low)
        gh[part, :] = (ga[i % 2] * slope).astype(low)

    def third(i):
        part = slice(i * QB, (i + 1) * QB)
        out[part, :] += nt(act[part, :], down[...])
        back[part, :] += nt(gh[part, :], up[...])

    first(0)
    for i in range(blocks):
        if i + 1 < blocks:
            first(i + 1)
        second(i)
        if i > 0:
            third(i - 1)
    third(blocks - 1)
    for m in range(0, width, QB):
        part = slice(m, m + QB)
        u = nn(x_t[part, :], gh[...]).astype(low)
        v = nn(g_t[part, :], act[...]).astype(low)
        for i in range(2):
            dup[i, part, :] = u[:, i * n : (i + 1) * n]
            ddown[i, part, :] = v[:, i * n : (i + 1) * n]

    @pl.when(pl.program_id(0) == pl.num_programs(0) - 1)
    def _():
        om[...] = out[:rows, :]
        ot[...] = out[rows:, :].astype(low)
        bm[...] = back[:rows, :]
        bt[...] = back[rows:, :].astype(low)


def feed(xm, xt, gm, gt, up, down):
    rows, width = xm.shape
    pieces, _, n = up.shape
    whole = pl.BlockSpec((rows, width), lambda j: (0, 0))
    weight = pl.BlockSpec((2, width, n), lambda j: (j, 0, 0))
    shape = jax.ShapeDtypeStruct
    return pl.pallas_call(
        feed_kernel,
        grid=(pieces // 2,),
        in_specs=[whole] * 4 + [weight] * 2,
        out_specs=[whole] * 4 + [weight] * 2,
        out_shape=[shape((rows, width), kind) for kind in (full, low, full, low)]
        + [shape(up.shape, low)] * 2,
        scratch_shapes=[pltpu.VMEM((2 * rows, width), low)] * 2
        + [pltpu.VMEM((width, 2 * rows), low)] * 2
        + [pltpu.VMEM((width, 2 * n), low)] * 2
        + [pltpu.VMEM((2 * rows, 2 * n), low)] * 2
        + [pltpu.VMEM((2 * rows, width), full)] * 2
        + [pltpu.VMEM((2, QB, 2 * n), full)] * 2,
        compiler_params=pltpu.CompilerParams(vmem_limit_bytes=60 << 20),
        cost_estimate=pl.CostEstimate(
            flops=6 * 2 * 2 * rows * width * pieces * n, bytes_accessed=20 << 20, transcendentals=0
        ),
        name="feed",
    )(xm, xt, gm, gt, up, down)


def per_device(tokens, segments, w_qkv, w_out, w_in, w_back, gain_attn, gain_mlp, cotangent):
    sequences, own, width = tokens.shape
    assert lax.axis_size("tensor") == 4 and lax.axis_size("context") == 2 and sequences == 3
    c, t, d = lax.axis_index("context"), lax.axis_index("tensor"), lax.axis_index("dp")
    span = 4 * own
    length = segments.shape[1]
    shard = w_qkv.shape[0]
    local = w_qkv.shape[2]
    heads = local // HD
    hidden = w_in.shape[1] // 2
    rows = sequences * own

    blocks = gather_tensor(tokens, 1)
    cot_theirs = across(cotangent, "context", 1)
    w_attn = gather_dp(w_qkv.reshape(shard, 3 * local), 0)
    gains = gather_dp(jnp.stack([gain_attn, gain_mlp], axis=1), 0)
    gain_first, gain_second = gains[:, 0].astype(full), gains[:, 1].astype(full)
    up_own = lax.dynamic_slice_in_dim(w_in, c * hidden, hidden, 1)
    down_own = lax.dynamic_slice_in_dim(w_back, c * hidden, hidden, 0).T
    up_down = jnp.stack(gather_tensor(jnp.stack([up_own, down_own]), 1), axis=1)
    up_down = gather_dp(up_down, 2)
    w_up, w_down = up_down[0], up_down[1]
    w_proj = jnp.stack(gather_tensor(w_out.T, 0), axis=0)
    w_proj = gather_dp(w_proj, 1)

    w_attn_all = jnp.stack(gather_tensor(w_attn.T, 0)).reshape(4, 3, local, width)
    w_attn_all = [lax.dynamic_index_in_dim(w_attn_all, t ^ p, 0, False) for p in range(4)]
    w_attn_all = jnp.stack(w_attn_all, axis=1).reshape(12 * local, width)

    lo = jnp.zeros((sequences, length), jnp.int32)
    for value in range(8):
        before = jnp.sum((segments < value).astype(jnp.int32), axis=1, keepdims=True)
        lo = jnp.where(segments == value, before, lo)
    lo = jnp.maximum(lo, jnp.arange(length, dtype=jnp.int32)[None] - (WIN - 1))
    lo = jnp.stack([jnp.where(c == 0, lo[0], lo[2]), lo[1]])[:, None]

    stacked = jnp.stack(blocks)
    in_order = lambda s: [lax.dynamic_index_in_dim(s, t ^ p, 0, False) for p in range(4)]
    all_tokens = jnp.stack(in_order(stacked), axis=1).reshape(sequences * span, width)

    def inverse(v):
        return lax.rsqrt(jnp.mean(v * v, axis=-1, keepdims=True) + epsilon)

    wide_tokens = all_tokens.astype(full)
    normed_one = (wide_tokens * inverse(wide_tokens) * gain_first).astype(low)
    projected = dot(w_attn, normed_one, ((0,), (1,))).astype(low)

    def units(array, parts, core):
        block = array.reshape(parts, heads, HD, sequences * span)
        whole = lax.dynamic_slice_in_dim(block, 2 * core * span, span, 3)
        shared = lax.dynamic_slice_in_dim(block[..., span : 2 * span], core, 2, 1)
        whole, shared = (a.reshape(-1, HD, span) for a in (whole, shared))
        return jnp.concatenate([whole, shared], axis=0)

    qkv_mine = units(projected, 3, c)
    qkv_theirs = across(units(projected, 3, 1 - c), "context", 1)
    attended, log_totals, out_full = attend(qkv_mine, qkv_theirs, lo)

    def two_sequences(core):
        whole = lax.dynamic_slice_in_dim(normed_one, 2 * core * span, span, 0)
        return jnp.stack([whole, normed_one[span : 2 * span]])

    normed_theirs = across(two_sequences(1 - c), "context", 1)
    normed_mine = two_sequences(c)
    normed_units = jnp.where(
        c == 0,
        jnp.concatenate([normed_mine, normed_theirs], axis=1),
        jnp.concatenate([normed_theirs, normed_mine], axis=1),
    )

    proj_rows = jnp.stack(in_order(w_proj.transpose(0, 2, 1))).reshape(4 * local, width)
    inputs = tokens.astype(full).reshape(rows, width)
    middle = inputs + tn(attended, proj_rows)
    inv_two = inverse(middle)
    normed_two = (middle * inv_two * gain_second).astype(low)

    cot = cotangent.reshape(rows, width)
    branch, branch_sent, back, back_sent, grad_up, grad_down = feed(
        normed_two, across(normed_two, "context", 1), cot, cot_theirs.reshape(rows, width), w_up, w_down
    )
    grad_norm_two = back + across(back_sent, "context", 1).astype(full)
    result = (middle + branch + across(branch_sent, "context", 1).astype(full)).astype(low)

    def norm_back(r, gain, v, inv):
        rg = r * gain
        return inv * (rg - v * (inv * inv * jnp.mean(rg * v, axis=-1, keepdims=True)))

    grad_middle = cot.astype(full) + norm_back(grad_norm_two, gain_second, middle, inv_two)
    grad_low = grad_middle.astype(low)
    grad_proj = nn(attended, grad_low)
    grad_att = nt(proj_rows, grad_low).astype(low).reshape(4 * heads, HD, rows)
    grad_projected, grad_attn = attend_back(
        qkv_mine, qkv_theirs, grad_att, lo, log_totals, out_full, normed_units
    )
    grad_attn = grad_attn.reshape(heads, 3, HD, width).transpose(1, 0, 2, 3).reshape(3 * local, width)
    grad_norm_one = tn(grad_projected.reshape(12 * local, rows), w_attn_all)
    inv_one = inverse(inputs)
    grad_input = grad_middle + norm_back(grad_norm_one, gain_first, inputs, inv_one)

    def scatter_dp(array, axis):
        return lax.psum_scatter(array.astype(low), "dp", scatter_dimension=axis, tiled=True)

    def swap_halves(mine, axis):
        theirs = across(mine, "context", 1)
        return jnp.where(
            c == 0,
            jnp.concatenate([mine, theirs], axis=axis),
            jnp.concatenate([theirs, mine], axis=axis),
        )

    def half_sum(array, axis):
        size = array.shape[axis] // 2
        mine = lax.dynamic_slice_in_dim(array, c * size, size, axis)
        sent = lax.dynamic_slice_in_dim(array, (1 - c) * size, size, axis)
        return mine + across(sent.astype(low), "context", 1).astype(full)

    up_down = [jnp.stack([grad_up[r], grad_down[r]]).astype(full) for r in range(4)]
    up_down = scatter_tensor(up_down, 1)
    up_down = scatter_dp(up_down, 1)
    own_up = swap_halves(up_down[0], 1).astype(full)
    own_down = swap_halves(up_down[1].T, 0).astype(full)
    proj = half_sum(grad_proj.reshape(4, local, width), 1)
    proj = [lax.dynamic_index_in_dim(proj, t ^ r, 0, False) for r in range(4)]
    proj = scatter_dp(scatter_tensor(proj, 0), 1)
    own_proj = swap_halves(proj, 0).astype(full)
    attn = scatter_dp(half_sum(grad_attn, 0), 1).T
    own_attn = swap_halves(attn, 1).astype(full)

    def gain_grad(weight, grad, gain):
        part = jnp.sum(weight.astype(full) * grad, axis=1)
        return lax.psum(part, "tensor") / gain.astype(full)

    own_gain_attn = gain_grad(w_qkv.reshape(shard, 3 * local), own_attn, gain_attn)
    own_gain_mlp = gain_grad(w_in, own_up, gain_mlp)
    return (
        result.reshape(sequences, own, width),
        grad_input.astype(low).reshape(sequences, own, width),
        own_attn.reshape(shard, 3, local),
        own_proj,
        own_up,
        own_down,
        own_gain_attn,
        own_gain_mlp,
    )


def solution(mesh):
    return jax.shard_map(
        per_device,
        mesh=mesh,
        in_specs=(
            P("dp", ("context", "tensor"), None),
            P("dp", None),
            P("dp", None, "tensor"),
            P("tensor", "dp"),
            P("dp", "tensor"),
            P("tensor", "dp"),
            P("dp"),
            P("dp"),
            P("dp", ("context", "tensor"), None),
        ),
        out_specs=(
            P("dp", ("context", "tensor"), None),
            P("dp", ("context", "tensor"), None),
            P("dp", None, "tensor"),
            P("tensor", "dp"),
            P("dp", "tensor"),
            P("tensor", "dp"),
            P("dp"),
            P("dp"),
        ),
        check_vma=False,
    )
```

```python
import functools
import math

import jax
import jax.numpy as jnp
from jax import lax
from jax.experimental import pallas as pl
from jax.experimental.pallas import tpu as pltpu
from jax.sharding import PartitionSpec as P

HD = 64
WIN = 1536
QB = 256
CHUNK = 128
NEG = -1e30
epsilon = 1e-06
low = jnp.bfloat16
full = jnp.float32


def dot(left, right, dims):
    return lax.dot_general(left, right, (dims, ((), ())), preferred_element_type=full)


def nn(left, right):
    return dot(left, right, ((1,), (0,)))


def nt(left, right):
    return dot(left, right, ((1,), (1,)))


def tn(left, right):
    return dot(left, right, ((0,), (0,)))


def across(array, axis, by):
    return lax.ppermute(array, axis, [(i, i ^ by) for i in range(lax.axis_size(axis))])


def gather_tensor(array, axis):
    half = array.shape[axis] // 2
    one = lax.slice_in_dim(array, 0, half, axis=axis)
    two = lax.slice_in_dim(array, half, 2 * half, axis=axis)
    one_x, two_y = across(one, "tensor", 1), across(two, "tensor", 2)
    one_y, one_d = across(one, "tensor", 2), across(one_x, "tensor", 2)
    two_x, two_d = across(two, "tensor", 1), across(two_y, "tensor", 1)
    join = lambda a, b: jnp.concatenate([a, b], axis=axis)
    return [array, join(one_x, two_x), join(one_y, two_y), join(one_d, two_d)]


def scatter_tensor(parts, axis):
    half = parts[0].shape[axis] // 2
    one = [lax.slice_in_dim(p, 0, half, axis=axis) for p in parts]
    two = [lax.slice_in_dim(p, half, 2 * half, axis=axis) for p in parts]

    def reduce(p, first, second):
        sent = jnp.stack([p[first], p[first ^ second]]).astype(low)
        got = across(sent, "tensor", first).astype(full)
        mine, theirs = p[0] + got[0], p[second] + got[1]
        return mine + across(theirs.astype(low), "tensor", second).astype(full)

    return jnp.concatenate([reduce(one, 1, 2), reduce(two, 2, 1)], axis=axis)


def gather_dp(array, axis):
    n = lax.axis_size("dp")
    if n != 4:
        return lax.all_gather(array, "dp", axis=axis, tiled=True)
    parts = jnp.stack([across(array, "dp", r) if r else array for r in range(n)])
    d = lax.axis_index("dp")
    return jnp.concatenate(
        [lax.dynamic_index_in_dim(parts, d ^ p, 0, False) for p in range(n)], axis=axis
    )


PEERS = [(dc, r) for dc in range(2) for r in range(4)]


def place():
    return lax.axis_index("context"), lax.axis_index("tensor")


def at_peer(c, t, dc, r):
    return {"context": c ^ dc, "tensor": t ^ r}


def greet(peers):
    for peer in peers:
        pl.semaphore_signal(pltpu.get_barrier_semaphore(), inc=1, device_id=peer)


def greeted(peers):
    pl.semaphore_wait(pltpu.get_barrier_semaphore(), len(peers))


def unit_place(u, c):
    return jnp.where(u < 3, u, c + u - 3), jnp.where(u < 3, 2 * c, 1)


def sends(u, c):
    return (u != 3) | (c == 0)


dma = pltpu.SemaphoreType.DMA
ANY = pl.BlockSpec(memory_space=pl.ANY)
shape = jax.ShapeDtypeStruct


SHARED = 768


def project_kernel(
    n, tokens, packed, up, qkv, norm, every, up_all, gain_ref,
    tok, x, w, w_t, proj, tsend, trecv, tlocal, wsend, wrecv, wlocal, osend, orecv, olocal,
):
    c, t = place()
    d = lax.axis_index("dp")
    own = tokens.shape[1]
    width = tokens.shape[2]
    span = 4 * own
    shard = packed.shape[0]
    half = own // 2
    to_x, to_y, to_core = {"tensor": t ^ 1}, {"tensor": t ^ 2}, {"context": 1 - c}
    others = [{"dp": lax.rem(d + r, n)} for r in range(1, n)]
    peers = [to_x, to_y, to_core] + others
    greet(peers)

    def local(i, s):
        return pltpu.make_async_copy(tokens.at[s], tok.at[s, t], tlocal.at[i])

    def weights(j, r):
        source, target, sem = ((packed, w, 0), (up, up_all, 1))[j]
        rows = pl.ds(pl.multiple_of(d * shard, shard), shard)
        if r == 0:
            return pltpu.make_async_copy(source, target.at[rows], wlocal.at[sem])
        return pltpu.make_async_remote_copy(
            source, target.at[rows], wsend.at[sem, r - 1], wrecv.at[sem, r - 1], device_id=others[r - 1]
        )

    order = (2 * (1 - c), 1, 2 * c)
    for i, s in enumerate(order):
        local(i, s).start()
    weights(0, 0).start()
    weights(1, 0).start()
    greeted(peers)
    for j in range(2):
        for r in range(1, n):
            weights(j, r).start()

    def hop(k, i):
        s = order[i]
        origin, rows, peer = (
            (t, slice(0, half), to_x),
            (t, slice(half, own), to_y),
            (t, slice(0, half), to_y),
            (t, slice(half, own), to_x),
            (t ^ 1, slice(0, half), to_y),
            (t ^ 2, slice(half, own), to_x),
        )[k]
        there = tok.at[s, origin, rows]
        here = tokens.at[s, rows] if k < 4 else there
        return pltpu.make_async_remote_copy(
            here, there, tsend.at[k, i], trecv.at[k, i], device_id=peer
        )

    def straight(i):
        for k in range(4):
            hop(k, i).start()

    def forward(i):
        for k in range(2):
            hop(k, i).wait_recv()
            hop(k + 4, i).start()

    units = proj.shape[1]

    def leave(i):
        out = []
        lanes = pl.ds(pl.multiple_of(c * span, span), span)
        if i != 0:
            out.append((x.at[i], norm.at[2 - i, lanes], False))
        if i != 2:
            out.append((x.at[i], norm.at[i, lanes], True))
        if i == 0:
            out.append((proj.at[0], qkv.at[pl.ds(0, units), :, lanes], True))
        if i == 2:
            out.append((proj.at[2], qkv.at[pl.ds(0, units), :, lanes], False))
        if i == 1:
            for away in (True, False):
                core = 1 - c if away else c
                for p in range(3):
                    src = proj.at[1, pl.ds(p * 3 + core, 2)]
                    out.append((src, qkv.at[pl.ds(units + 2 * p, 2), :, lanes], away))
        copies = []
        for j, (src, dst, away) in enumerate(out):
            if away:
                copies.append(
                    (away, pltpu.make_async_remote_copy(src, dst, osend.at[i, j], orecv.at[i, j], device_id=to_core))
                )
            else:
                copies.append((away, pltpu.make_async_copy(src, dst, olocal.at[i, j])))
        return copies

    def work(i):
        s = order[i]
        local(i, s).wait()
        for k in range(2, 6):
            hop(k, i).wait_recv()
        for p in range(4):
            v = tok[s, p].astype(full)
            inv = lax.rsqrt(jnp.mean(v * v, axis=-1, keepdims=True) + epsilon)
            x[i, p * own : (p + 1) * own, :] = (v * inv * gain_ref[0:1, :]).astype(low)
        for p in range(4):
            rows = slice(p * own, (p + 1) * own)
            part = nt(w_t[...], x[i, rows, :]).astype(low)
            proj[i, :, :, rows] = part.reshape(units, HD, own)
        for _, copy in leave(i):
            copy.start()

    straight(0)
    straight(1)
    forward(0)
    straight(2)
    weights(0, 0).wait()
    for r in range(1, n):
        weights(0, r).wait_recv()
    w_t[...] = w[:, : units * HD].T
    gain_ref[...] = w[:, SHARED : SHARED + 128].astype(full).T[:8]
    keep = pltpu.make_async_copy(w, every, wlocal.at[2])
    keep.start()
    forward(1)
    work(0)
    forward(2)
    work(1)
    work(2)
    keep.wait()
    weights(1, 0).wait()
    for r in range(1, n):
        weights(0, r).wait_send()
        weights(1, r).wait()
    for i in range(3):
        for k in range(6):
            hop(k, i).wait_send()
        for away, copy in leave(i):
            copy.wait()


def project(n, tokens, packed, up):
    sequences, own, width = tokens.shape
    shard, columns = packed.shape
    span = 4 * own
    return pl.pallas_call(
        functools.partial(project_kernel, n),
        in_specs=[ANY] * 3,
        out_specs=[ANY] * 4 + [pl.BlockSpec(memory_space=pltpu.VMEM)],
        out_shape=[
            shape((15, HD, 2 * span), low),
            shape((2, 2 * span, width), low),
            shape((n * shard, columns), low),
            shape((n * shard, up.shape[1]), low),
            shape((8, n * shard), full),
        ],
        scratch_shapes=[
            pltpu.VMEM((sequences, 4, own, width), low),
            pltpu.VMEM((sequences, span, width), low),
            pltpu.VMEM((n * shard, columns), low),
            pltpu.VMEM((9 * HD, width), low),
            pltpu.VMEM((sequences, 9, HD, span), low),
            dma((6, 3)), dma((6, 3)), dma((3,)),
            dma((2, n - 1)), dma((2, n - 1)), dma((3,)),
            dma((3, 8)), dma((3, 8)), dma((3, 8)),
        ],
        compiler_params=pltpu.CompilerParams(
            vmem_limit_bytes=40 << 20, collective_id=3, has_side_effects=True
        ),
        name="project",
    )(tokens, packed, up)


UNITS = 5
def unit_block(part):
    return lambda u: (jnp.where(u < 3, part * 3 + u, 9 + part * 2 + (u - 3)), 0, 0)


def attend_kernel(
    n, q_ref, k_ref, v_ref, lo_ref, every, up_part, down_own, att, lse_ref, of_ref, up, down, out_w,
    qs, ks, ss, obuf, ssem, rsem, lsem, wsend, wrecv, wlocal, zsend, zrecv,
):
    u = pl.program_id(0)
    c, t = place()
    d = lax.axis_index("dp")
    shard = down_own.shape[0]
    peers = [at_peer(c, t, dc, r) for dc, r in PEERS[1:]]

    def weight(j, r):
        rows = pl.ds(pl.multiple_of(d * shard, shard), shard)
        src, dst = (
            (down_own, down.at[t, rows]),
            (up_part, up.at[t]),
            (every.at[:, pl.ds(SHARED - 256, 256)], out_w.at[t]),
        )[j]
        if r == 0:
            return pltpu.make_async_copy(src, dst, wlocal.at[j])
        return pltpu.make_async_remote_copy(
            src, dst, wsend.at[j, r - 1], wrecv.at[j, r - 1], device_id={"tensor": t ^ r}
        )

    def shards(step, up_line):
        src = d - step if up_line else d + step
        rows = pl.ds(pl.multiple_of(jnp.clip(src, 0, n - 1) * shard, shard), shard)
        to = jnp.clip(d + 1 if up_line else d - 1, 0, n - 1)
        k = 0 if up_line else 1
        return pltpu.make_async_remote_copy(
            down.at[:, rows], down.at[:, rows], zsend.at[k, step], zrecv.at[k, step], device_id={"dp": to}
        )

    def line(step, what):
        for up_line in (True, False):
            inside = (d < n - 1) if up_line else (d > 0)
            has = (d >= step) if up_line else (d <= n - 1 - step)
            comes = (d >= step + 1) if up_line else (d <= n - 2 - step)
            if what == "recv":

                @pl.when(comes)
                def _():
                    shards(step, up_line).wait_recv()
            else:

                @pl.when(inside & has)
                def _():
                    if what == "start":
                        shards(step, up_line).start()
                    else:
                        shards(step, up_line).wait_send()
    length = lo_ref.shape[2]
    half = length // 2
    own = half // 4

    @pl.when(u == 0)
    def _():
        barrier = pltpu.get_barrier_semaphore()
        greet(peers)

        @pl.when(d > 0)
        def _():
            pl.semaphore_signal(barrier, inc=1, device_id={"dp": jnp.maximum(d - 1, 0)})

        @pl.when(d < n - 1)
        def _():
            pl.semaphore_signal(barrier, inc=1, device_id={"dp": jnp.minimum(d + 1, n - 1)})

        for j in range(3):
            weight(j, 0).start()
        ends = jnp.where(d > 0, 1, 0) + jnp.where(d < n - 1, 1, 0)
        pl.semaphore_wait(barrier, len(peers) + ends)
        for j in range(3):
            for r in range(1, 4):
                weight(j, r).start()

    qs[...] = q_ref[0] * low(0.125)
    ks[...] = k_ref[0].T
    for start in range(0, length, QB):
        stop = start + QB
        q = qs[:, start:stop]
        lo = lo_ref[0, :, start:stop]
        first = max(0, start - WIN)
        most = jnp.full((8, QB), NEG, full)
        for at in range(first, stop, CHUNK):
            s = nn(ks[at : at + CHUNK, :], q)
            key_pos = at + lax.broadcasted_iota(jnp.int32, (CHUNK, QB), 0)
            allowed = key_pos >= lo
            if at + CHUNK - 1 > start:
                allowed &= key_pos <= start + lax.broadcasted_iota(jnp.int32, (CHUNK, QB), 1)
            s = jnp.where(allowed, s, NEG)
            ss[at - first : at - first + CHUNK, :] = s
            most = jnp.maximum(most, jnp.max(s.reshape(CHUNK // 8, 8, QB), axis=0))
        most = jnp.max(most, axis=0, keepdims=True)
        total = jnp.zeros((8, QB), full)
        acc = jnp.zeros((HD, QB), full)
        for at in range(first, stop, CHUNK):
            p = jnp.exp(ss[at - first : at - first + CHUNK, :] - most)
            total += jnp.sum(p.reshape(CHUNK // 8, 8, QB), axis=0)
            acc += nn(v_ref[0, :, at : at + CHUNK], p.astype(low))
        total = jnp.sum(total, axis=0, keepdims=True)
        lse_ref[0, :, start:stop] = most + jnp.log(total)
        o = acc * (1.0 / total)
        of_ref[0, :, start:stop] = o
        obuf[u, :, start:stop] = o.astype(low)

    @pl.when(u == 0)
    def _():
        weight(0, 0).wait()
        for r in range(1, 4):
            weight(0, r).wait_recv()
        line(0, "start")

    @pl.when(u == 3)
    def _():
        if n > 2:
            line(0, "recv")
            line(1, "start")

    def move(unit, i, source_core):
        dc, r = PEERS[i]
        h, seq = unit_place(unit, source_core)
        dest = pl.multiple_of(((c ^ dc) * 4 + (t ^ r)) * own, own)
        src = obuf.at[unit, :, pl.ds(dest, own)]
        dst = att.at[
            pl.ds(pl.multiple_of((t * 3 + h) * HD, HD), HD), pl.ds(pl.multiple_of(seq * own, own), own)
        ]
        if i == 0:
            return pltpu.make_async_copy(src, dst, lsem.at[unit])
        return pltpu.make_async_remote_copy(
            src, dst, ssem.at[i - 1, unit], rsem.at[i - 1, unit], device_id=at_peer(c, t, dc, r)
        )

    @pl.when(sends(u, c))
    def _():
        for i in range(1, len(PEERS)):
            move(u, i, c).start()
        move(u, 0, c).start()

    @pl.when(u == pl.num_programs(0) - 1)
    def _():
        for step in range(2, n - 1):
            line(step - 1, "recv")
            line(step, "start")
        line(n - 2, "recv")
        for step in range(n - 1):
            line(step, "sent")
        for j in range(3):
            if j:
                weight(j, 0).wait()
            for r in range(1, 4):
                weight(j, r).wait_send()
                if j:
                    weight(j, r).wait_recv()
        for unit in range(UNITS):
            for i, (dc, r) in enumerate(PEERS):

                @pl.when(sends(unit, c))
                def _():
                    if i:
                        move(unit, i, c).wait_send()
                    else:
                        move(unit, i, c).wait()

                if i:

                    @pl.when(sends(unit, c ^ dc))
                    def _():
                        move(unit, i, c ^ dc).wait_recv()


def attend(n, qkv, lo, every, up_part, down_own):
    length = lo.shape[2]
    half = length // 2
    own = half // 4
    width, hidden = up_part.shape
    part = lambda p: pl.BlockSpec((1, HD, length), unit_block(p))
    unit = lambda rows, n: pl.BlockSpec((1, rows, n), lambda u: (u, 0, 0))
    heads = 4 * 3 * HD
    return pl.pallas_call(
        functools.partial(attend_kernel, n),
        grid=(UNITS,),
        in_specs=[part(0), part(1), part(2)]
        + [pl.BlockSpec((1, 1, length), lambda u: (u // 3, 0, 0))]
        + [ANY] * 3,
        out_specs=[ANY, unit(1, length), unit(HD, length)] + [ANY] * 3,
        scratch_shapes=[
            pltpu.VMEM((HD, length), low),
            pltpu.VMEM((length, HD), low),
            pltpu.VMEM((WIN + QB, QB), full),
            pltpu.VMEM((UNITS, HD, length), low),
            dma((7, UNITS)),
            dma((7, UNITS)),
            dma((UNITS,)),
            dma((3, 3)),
            dma((3, 3)),
            dma((3,)),
            dma((2, n - 1)),
            dma((2, n - 1)),
        ],
        out_shape=[
            jax.ShapeDtypeStruct((heads, 3 * own), low),
            jax.ShapeDtypeStruct((UNITS, 1, length), full),
            jax.ShapeDtypeStruct((UNITS, HD, length), full),
            shape((4, width, hidden), low),
            shape((4, width, hidden), low),
            shape((4, width, 256), low),
        ],
        compiler_params=pltpu.CompilerParams(
            vmem_limit_bytes=40 << 20, collective_id=1, has_side_effects=True
        ),
        cost_estimate=pl.CostEstimate(
            flops=UNITS * 18 * 2 * 256 * 1024 * 128, bytes_accessed=20 << 20, transcendentals=0
        ),
        name="attend",
    )(qkv, qkv, qkv, lo, every, up_part, down_own)


def attend_back_kernel(
    q_ref, k_ref, v_ref, lo_ref, lse_ref, of_ref, norm_ref, gatt, dall, gw,
    qs, ks, vs, gs, grow, qrow, delta, dqs, dbuf, gsem, grsem, glsem, ssem, rsem, lsem,
):
    u = pl.program_id(0)
    c, t = place()
    length = lo_ref.shape[2]
    half = length // 2
    own = half // 4
    groups = ((0, 3), (3, 2))

    def fetch(group, i, receiving):
        dc, r = PEERS[i]
        first, count = groups[group]
        to_c, to_t = (c ^ dc, t ^ r)
        seq = 2 * to_c if group == 0 else 1
        head = to_t * 3 + (0 if group == 0 else to_c)
        src = gatt.at[pl.ds(head, count), :, pl.ds(pl.multiple_of(seq * own, own), own)]
        dst = gs.at[pl.ds(first, count), :, pl.ds(pl.multiple_of((c * 4 + t) * own, own), own)]
        if i == 0:
            return pltpu.make_async_copy(src, dst, glsem.at[group])
        return pltpu.make_async_remote_copy(
            src, dst, gsem.at[i - 1, group], grsem.at[i - 1, group], device_id=at_peer(c, t, dc, r)
        )

    @pl.when(u == 0)
    def _():
        peers = [at_peer(c, t, dc, r) for dc, r in PEERS[1:]]
        greet(peers)
        gw[...] = jnp.zeros_like(gw)
        greeted(peers)
        for group in range(2):
            for i in range(1, len(PEERS)):
                fetch(group, i, False).start()
            fetch(group, 0, False).start()

    for group in range(2):

        @pl.when(u == groups[group][0])
        def _():
            fetch(group, 0, True).wait()
            for i in range(1, len(PEERS)):
                fetch(group, i, True).wait_recv()

    qs[...] = q_ref[0] * low(0.125)
    ks[...] = k_ref[0].T
    vs[...] = v_ref[0].T
    grow[...] = gs[u].T
    qrow[...] = qs[...].T
    delta[...] = jnp.sum(gs[u].astype(full) * of_ref[0], axis=0, keepdims=True)
    dqs[...] = jnp.zeros_like(dqs)
    for key_start in range(0, length, QB):
        rows = slice(key_start, key_start + QB)
        k, v, key_t = ks[rows, :], vs[rows, :], k_ref[0, :, rows]
        dk = jnp.zeros((QB, HD), full)
        dv = jnp.zeros((QB, HD), full)
        key_pos = key_start + lax.broadcasted_iota(jnp.int32, (QB, QB), 0)
        for start in range(key_start, min(key_start + WIN + QB, length), QB):
            cols = slice(start, start + QB)
            s = nn(k, qs[:, cols]) - lse_ref[0, :, cols]
            allowed = key_pos >= lo_ref[0, :, cols]
            if start == key_start:
                allowed &= key_pos <= start + lax.broadcasted_iota(jnp.int32, (QB, QB), 1)
            p = jnp.exp(jnp.where(allowed, s, NEG))
            dp = nn(v, gs[u, :, cols])
            ds = (p * (dp - delta[:, cols])).astype(low)
            dv += nn(p.astype(low), grow[cols, :])
            dk += nn(ds, qrow[cols, :])
            dqs[:, cols] += nn(key_t, ds)
        dbuf[u, 1, :, rows] = dk.T.astype(low)
        dbuf[u, 2, :, rows] = dv.T.astype(low)
    dbuf[u, 0] = (dqs[...] * 0.125).astype(low)

    def move(unit, i, source_core):
        dc, r = PEERS[i]
        h, seq = unit_place(unit, source_core)
        dest = pl.multiple_of(((c ^ dc) * 4 + (t ^ r)) * own, own)
        src = dbuf.at[unit, :, :, pl.ds(dest, own)]
        dst = dall.at[:, t * 3 + h, :, pl.ds(pl.multiple_of(seq * own, own), own)]
        if i == 0:
            return pltpu.make_async_copy(src, dst, lsem.at[unit])
        return pltpu.make_async_remote_copy(
            src, dst, ssem.at[i - 1, unit], rsem.at[i - 1, unit], device_id=at_peer(c, t, dc, r)
        )

    @pl.when(sends(u, c))
    def _():
        for i in range(1, len(PEERS)):
            move(u, i, c).start()
        move(u, 0, c).start()
        h, _ = unit_place(u, c)
        gw[h] += nn(dbuf[u].reshape(3 * HD, length), norm_ref[0])

    @pl.when(u == pl.num_programs(0) - 1)
    def _():
        for group in range(2):
            for i in range(1, len(PEERS)):
                fetch(group, i, False).wait_send()
        for unit in range(UNITS):
            for i, (dc, r) in enumerate(PEERS):

                @pl.when(sends(unit, c))
                def _():
                    if i:
                        move(unit, i, c).wait_send()
                    else:
                        move(unit, i, c).wait()

                if i:

                    @pl.when(sends(unit, c ^ dc))
                    def _():
                        move(unit, i, c ^ dc).wait_recv()


def attend_back(qkv, grad_attended, lo, lse, attended, normed):
    length = lo.shape[2]
    half = length // 2
    own = half // 4
    width = normed.shape[2]
    part = lambda p: pl.BlockSpec((1, HD, length), unit_block(p))
    unit = lambda rows, n: pl.BlockSpec((1, rows, n), lambda u: (u, 0, 0))
    wide, tall = pltpu.VMEM((HD, length), low), pltpu.VMEM((length, HD), low)
    return pl.pallas_call(
        attend_back_kernel,
        grid=(UNITS,),
        in_specs=[part(0), part(1), part(2)]
        + [
            pl.BlockSpec((1, 1, length), lambda u: (u // 3, 0, 0)),
            unit(1, length),
            unit(HD, length),
            pl.BlockSpec((1, length, width), lambda u: (u // 3, 0, 0)),
            pl.BlockSpec(memory_space=pl.ANY),
        ],
        out_specs=[
            ANY,
            pl.BlockSpec((3, 3 * HD, width), lambda u: (0, 0, 0)),
        ],
        scratch_shapes=[
            wide, tall, tall, pltpu.VMEM((UNITS, HD, length), low), tall, tall,
            pltpu.VMEM((1, length), full), pltpu.VMEM((HD, length), full),
            pltpu.VMEM((UNITS, 3, HD, length), low),
            dma((7, 2)), dma((7, 2)), dma((2,)), dma((7, UNITS)), dma((7, UNITS)), dma((UNITS,)),
        ],
        out_shape=[
            jax.ShapeDtypeStruct((3, 12, HD, 3 * own), low),
            jax.ShapeDtypeStruct((3, 3 * HD, width), full),
        ],
        compiler_params=pltpu.CompilerParams(
            vmem_limit_bytes=50 << 20, collective_id=2, has_side_effects=True
        ),
        cost_estimate=pl.CostEstimate(
            flops=UNITS * 18 * 5 * 256 * 1024 * 128, bytes_accessed=30 << 20, transcendentals=0
        ),
        name="attend_back",
    )(qkv, qkv, qkv, lo, lse, attended, normed, grad_attended)


def gelu_and_slope(v):
    k0 = math.sqrt(2.0 / math.pi)
    square = v * v
    th = jnp.tanh(v * (k0 + (k0 * 0.044715) * square))
    half = 0.5 + 0.5 * th
    slope = half + (v * half) * ((1.0 - th) * (k0 + (3.0 * 0.044715 * k0) * square))
    return v * half, slope


def feed_kernel(
    xm, xt, gm, gt, up_ref, down_ref, om, ot, bm, bt, dup, ddown,
    x, g, x_t, g_t, up, down, act, gh, out, back, pre, ga,
):
    rows, width = xm.shape
    n = up_ref.shape[2]
    blocks = 2 * rows // QB

    @pl.when(pl.program_id(0) == 0)
    def _():
        for i, (a, b) in enumerate(((xm, gm), (xt, gt))):
            part = slice(i * rows, (i + 1) * rows)
            x[part, :] = a[...]
            g[part, :] = b[...]
            x_t[:, part] = a[...].T
            g_t[:, part] = b[...].T
        out[...] = jnp.zeros_like(out)
        back[...] = jnp.zeros_like(back)

    for i in range(2):
        up[:, i * n : (i + 1) * n] = up_ref[i]
        down[:, i * n : (i + 1) * n] = down_ref[i]

    def first(i):
        part = slice(i * QB, (i + 1) * QB)
        pre[i % 2] = nn(x[part, :], up[...])
        ga[i % 2] = nn(g[part, :], down[...])

    def second(i):
        part = slice(i * QB, (i + 1) * QB)
        a, slope = gelu_and_slope(pre[i % 2])
        act[part, :] = a.astype(low)
        gh[part, :] = (ga[i % 2] * slope).astype(low)

    def third(i):
        part = slice(i * QB, (i + 1) * QB)
        out[part, :] += nt(act[part, :], down[...])
        back[part, :] += nt(gh[part, :], up[...])

    first(0)
    for i in range(blocks):
        if i + 1 < blocks:
            first(i + 1)
        second(i)
        if i > 0:
            third(i - 1)
    third(blocks - 1)
    for m in range(0, width, QB):
        part = slice(m, m + QB)
        u = nn(x_t[part, :], gh[...]).astype(low)
        v = nn(g_t[part, :], act[...]).astype(low)
        for i in range(2):
            dup[i, part, :] = u[:, i * n : (i + 1) * n]
            ddown[i, part, :] = v[:, i * n : (i + 1) * n]

    @pl.when(pl.program_id(0) == pl.num_programs(0) - 1)
    def _():
        om[...] = out[:rows, :]
        ot[...] = out[rows:, :].astype(low)
        bm[...] = back[:rows, :]
        bt[...] = back[rows:, :].astype(low)


def feed(xm, xt, gm, gt, up, down):
    rows, width = xm.shape
    pieces, _, n = up.shape
    whole = pl.BlockSpec((rows, width), lambda j: (0, 0))
    weight = pl.BlockSpec((2, width, n), lambda j: (j, 0, 0))
    shape = jax.ShapeDtypeStruct
    return pl.pallas_call(
        feed_kernel,
        grid=(pieces // 2,),
        in_specs=[whole] * 4 + [weight] * 2,
        out_specs=[whole] * 4 + [weight] * 2,
        out_shape=[shape((rows, width), kind) for kind in (full, low, full, low)]
        + [shape(up.shape, low)] * 2,
        scratch_shapes=[pltpu.VMEM((2 * rows, width), low)] * 2
        + [pltpu.VMEM((width, 2 * rows), low)] * 2
        + [pltpu.VMEM((width, 2 * n), low)] * 2
        + [pltpu.VMEM((2 * rows, 2 * n), low)] * 2
        + [pltpu.VMEM((2 * rows, width), full)] * 2
        + [pltpu.VMEM((2, QB, 2 * n), full)] * 2,
        compiler_params=pltpu.CompilerParams(vmem_limit_bytes=60 << 20),
        cost_estimate=pl.CostEstimate(
            flops=6 * 2 * 2 * rows * width * pieces * n, bytes_accessed=20 << 20, transcendentals=0
        ),
        name="feed",
    )(xm, xt, gm, gt, up, down)


def per_device(tokens, segments, w_qkv, w_out, w_in, w_back, gain_attn, gain_mlp, cotangent):
    sequences, own, width = tokens.shape
    assert lax.axis_size("tensor") == 4 and lax.axis_size("context") == 2 and sequences == 3
    c, t, d = lax.axis_index("context"), lax.axis_index("tensor"), lax.axis_index("dp")
    span = 4 * own
    length = segments.shape[1]
    shard = w_qkv.shape[0]
    local = w_qkv.shape[2]
    heads = local // HD
    hidden = w_in.shape[1] // 2
    rows = sequences * own

    up_own = lax.dynamic_slice_in_dim(w_in, c * hidden, hidden, 1)
    down_own = lax.dynamic_slice_in_dim(w_back, c * hidden, hidden, 0).T
    pad = jnp.zeros((shard, 126), low)
    packed = [w_qkv.reshape(shard, 3 * local), w_out.T, gain_attn[:, None], gain_mlp[:, None], pad]
    packed = jnp.concatenate(packed, axis=1)
    n = lax.axis_size("dp")
    qkv, normed_units, every, up_part, gains = project(n, tokens, packed, up_own)
    gain_first, gain_second = gains[0], gains[1]
    cot_theirs = across(cotangent, "context", 1)

    lo = jnp.zeros((sequences, length), jnp.int32)
    for value in range(8):
        before = jnp.sum((segments < value).astype(jnp.int32), axis=1, keepdims=True)
        lo = jnp.where(segments == value, before, lo)
    lo = jnp.maximum(lo, jnp.arange(length, dtype=jnp.int32)[None] - (WIN - 1))
    lo = jnp.stack([jnp.where(c == 0, lo[0], lo[2]), lo[1]])[:, None]

    def inverse(v):
        return lax.rsqrt(jnp.mean(v * v, axis=-1, keepdims=True) + epsilon)

    attended, log_totals, out_full, w_up, w_down, w_proj = attend(
        n, qkv, lo, every, up_part, down_own
    )
    w_attn_all = jnp.stack(gather_tensor(every[:, : 3 * local].T, 0)).reshape(4, 3, local, width)
    w_attn_all = [lax.dynamic_index_in_dim(w_attn_all, t ^ p, 0, False) for p in range(4)]
    w_attn_all = jnp.stack(w_attn_all, axis=1).reshape(12 * local, width)
    proj_rows = w_proj[:, :, 256 - local :].transpose(0, 2, 1).reshape(4 * local, width)
    inputs = tokens.astype(full).reshape(rows, width)
    middle = inputs + tn(attended, proj_rows)
    inv_two = inverse(middle)
    normed_two = (middle * inv_two * gain_second).astype(low)

    cot = cotangent.reshape(rows, width)
    branch, branch_sent, back, back_sent, grad_up, grad_down = feed(
        normed_two, across(normed_two, "context", 1), cot, cot_theirs.reshape(rows, width), w_up, w_down
    )
    grad_norm_two = back + across(back_sent, "context", 1).astype(full)
    result = (middle + branch + across(branch_sent, "context", 1).astype(full)).astype(low)

    def norm_back(r, gain, v, inv):
        rg = r * gain
        return inv * (rg - v * (inv * inv * jnp.mean(rg * v, axis=-1, keepdims=True)))

    grad_middle = cot.astype(full) + norm_back(grad_norm_two, gain_second, middle, inv_two)
    grad_low = grad_middle.astype(low)
    grad_proj = nn(attended, grad_low)
    grad_att = nt(proj_rows, grad_low).astype(low).reshape(4 * heads, HD, rows)
    grad_projected, grad_attn = attend_back(
        qkv, grad_att, lo, log_totals, out_full, normed_units
    )
    grad_attn = grad_attn.reshape(heads, 3, HD, width).transpose(1, 0, 2, 3).reshape(3 * local, width)
    grad_norm_one = tn(grad_projected.reshape(12 * local, rows), w_attn_all)
    inv_one = inverse(inputs)
    grad_input = grad_middle + norm_back(grad_norm_one, gain_first, inputs, inv_one)

    def scatter_dp(array, axis):
        return lax.psum_scatter(array.astype(low), "dp", scatter_dimension=axis, tiled=True)

    def swap_halves(mine, axis):
        theirs = across(mine, "context", 1)
        return jnp.where(
            c == 0,
            jnp.concatenate([mine, theirs], axis=axis),
            jnp.concatenate([theirs, mine], axis=axis),
        )

    def half_sum(array, axis):
        size = array.shape[axis] // 2
        mine = lax.dynamic_slice_in_dim(array, c * size, size, axis)
        sent = lax.dynamic_slice_in_dim(array, (1 - c) * size, size, axis)
        return mine + across(sent.astype(low), "context", 1).astype(full)

    up_down = jnp.stack([grad_up, grad_down], axis=1).astype(full)
    up_down = [lax.dynamic_index_in_dim(up_down, t ^ r, 0, False) for r in range(4)]
    up_down = scatter_tensor(up_down, 1)
    up_down = scatter_dp(up_down, 1)
    own_up = swap_halves(up_down[0], 1).astype(full)
    own_down = swap_halves(up_down[1].T, 0).astype(full)
    proj = half_sum(grad_proj.reshape(4, local, width), 1)
    proj = [lax.dynamic_index_in_dim(proj, t ^ r, 0, False) for r in range(4)]
    proj = scatter_dp(scatter_tensor(proj, 0), 1)
    own_proj = swap_halves(proj, 0).astype(full)
    attn = scatter_dp(half_sum(grad_attn, 0), 1).T
    own_attn = swap_halves(attn, 1).astype(full)

    def gain_grad(weight, grad, gain):
        part = jnp.sum(weight.astype(full) * grad, axis=1)
        return lax.psum(part, "tensor") / gain.astype(full)

    own_gain_attn = gain_grad(w_qkv.reshape(shard, 3 * local), own_attn, gain_attn)
    own_gain_mlp = gain_grad(w_in, own_up, gain_mlp)
    return (
        result.reshape(sequences, own, width),
        grad_input.astype(low).reshape(sequences, own, width),
        own_attn.reshape(shard, 3, local),
        own_proj,
        own_up,
        own_down,
        own_gain_attn,
        own_gain_mlp,
    )


def solution(mesh):
    return jax.shard_map(
        per_device,
        mesh=mesh,
        in_specs=(
            P("dp", ("context", "tensor"), None),
            P("dp", None),
            P("dp", None, "tensor"),
            P("tensor", "dp"),
            P("dp", "tensor"),
            P("tensor", "dp"),
            P("dp"),
            P("dp"),
            P("dp", ("context", "tensor"), None),
        ),
        out_specs=(
            P("dp", ("context", "tensor"), None),
            P("dp", ("context", "tensor"), None),
            P("dp", None, "tensor"),
            P("tensor", "dp"),
            P("dp", "tensor"),
            P("tensor", "dp"),
            P("dp"),
            P("dp"),
        ),
        check_vma=False,
    )
```

```python
import functools
import math

import jax
import jax.numpy as jnp
from jax import lax
from jax.experimental import pallas as pl
from jax.experimental.pallas import tpu as pltpu
from jax.sharding import PartitionSpec as P

HD = 64
WIN = 1536
QB = 256
CHUNK = 128
NEG = -1e30
epsilon = 1e-06
low = jnp.bfloat16
full = jnp.float32


def dot(left, right, dims):
    return lax.dot_general(left, right, (dims, ((), ())), preferred_element_type=full)


def nn(left, right):
    return dot(left, right, ((1,), (0,)))


def nt(left, right):
    return dot(left, right, ((1,), (1,)))


def tn(left, right):
    return dot(left, right, ((0,), (0,)))


def across(array, axis, by):
    return lax.ppermute(array, axis, [(i, i ^ by) for i in range(lax.axis_size(axis))])


def gather_tensor(array, axis):
    half = array.shape[axis] // 2
    one = lax.slice_in_dim(array, 0, half, axis=axis)
    two = lax.slice_in_dim(array, half, 2 * half, axis=axis)
    one_x, two_y = across(one, "tensor", 1), across(two, "tensor", 2)
    one_y, one_d = across(one, "tensor", 2), across(one_x, "tensor", 2)
    two_x, two_d = across(two, "tensor", 1), across(two_y, "tensor", 1)
    join = lambda a, b: jnp.concatenate([a, b], axis=axis)
    return [array, join(one_x, two_x), join(one_y, two_y), join(one_d, two_d)]


PEERS = [(dc, r) for dc in range(2) for r in range(4)]


def place():
    return lax.axis_index("context"), lax.axis_index("tensor")


def at_peer(c, t, dc, r):
    return {"context": c ^ dc, "tensor": t ^ r}


def greet(peers):
    for peer in peers:
        pl.semaphore_signal(pltpu.get_barrier_semaphore(), inc=1, device_id=peer)


def greeted(peers):
    pl.semaphore_wait(pltpu.get_barrier_semaphore(), len(peers))


def unit_place(u, c):
    return jnp.where(u < 3, u, c + u - 3), jnp.where(u < 3, 2 * c, 1)


def sends(u, c):
    return (u != 3) | (c == 0)


dma = pltpu.SemaphoreType.DMA
ANY = pl.BlockSpec(memory_space=pl.ANY)
shape = jax.ShapeDtypeStruct


SHARED = 768


def project_kernel(
    n, tokens, packed, up, qkv, norm, every, up_all, gain_ref,
    tok, x, w, w_t, proj, tsend, trecv, tlocal, wsend, wrecv, wlocal, osend, orecv, olocal,
):
    c, t = place()
    d = lax.axis_index("dp")
    own = tokens.shape[1]
    width = tokens.shape[2]
    span = 4 * own
    shard = packed.shape[0]
    half = own // 2
    to_x, to_y, to_core = {"tensor": t ^ 1}, {"tensor": t ^ 2}, {"context": 1 - c}
    others = [{"dp": lax.rem(d + r, n)} for r in range(1, n)]
    peers = [to_x, to_y, to_core] + others
    greet(peers)

    def local(i, s):
        return pltpu.make_async_copy(tokens.at[s], tok.at[s, t], tlocal.at[i])

    def weights(j, r):
        source, target, sem = ((packed, w, 0), (up, up_all, 1))[j]
        rows = pl.ds(pl.multiple_of(d * shard, shard), shard)
        if r == 0:
            return pltpu.make_async_copy(source, target.at[rows], wlocal.at[sem])
        return pltpu.make_async_remote_copy(
            source, target.at[rows], wsend.at[sem, r - 1], wrecv.at[sem, r - 1], device_id=others[r - 1]
        )

    order = (2 * (1 - c), 1, 2 * c)
    for i, s in enumerate(order):
        local(i, s).start()
    weights(0, 0).start()
    weights(1, 0).start()
    greeted(peers)
    for j in range(2):
        for r in range(1, n):
            weights(j, r).start()

    def hop(k, i):
        s = order[i]
        origin, rows, peer = (
            (t, slice(0, half), to_x),
            (t, slice(half, own), to_y),
            (t, slice(0, half), to_y),
            (t, slice(half, own), to_x),
            (t ^ 1, slice(0, half), to_y),
            (t ^ 2, slice(half, own), to_x),
        )[k]
        there = tok.at[s, origin, rows]
        here = tokens.at[s, rows] if k < 4 else there
        return pltpu.make_async_remote_copy(
            here, there, tsend.at[k, i], trecv.at[k, i], device_id=peer
        )

    def straight(i):
        for k in range(4):
            hop(k, i).start()

    def forward(i):
        for k in range(2):
            hop(k, i).wait_recv()
            hop(k + 4, i).start()

    units = proj.shape[1]

    def leave(i):
        out = []
        lanes = pl.ds(pl.multiple_of(c * span, span), span)
        if i != 0:
            out.append((x.at[i], norm.at[2 - i, lanes], False))
        if i != 2:
            out.append((x.at[i], norm.at[i, lanes], True))
        if i == 0:
            out.append((proj.at[0], qkv.at[pl.ds(0, units), :, lanes], True))
        if i == 2:
            out.append((proj.at[2], qkv.at[pl.ds(0, units), :, lanes], False))
        if i == 1:
            for away in (True, False):
                core = 1 - c if away else c
                for p in range(3):
                    src = proj.at[1, pl.ds(p * 3 + core, 2)]
                    out.append((src, qkv.at[pl.ds(units + 2 * p, 2), :, lanes], away))
        copies = []
        for j, (src, dst, away) in enumerate(out):
            if away:
                copies.append(
                    (away, pltpu.make_async_remote_copy(src, dst, osend.at[i, j], orecv.at[i, j], device_id=to_core))
                )
            else:
                copies.append((away, pltpu.make_async_copy(src, dst, olocal.at[i, j])))
        return copies

    def work(i):
        s = order[i]
        local(i, s).wait()
        for k in range(2, 6):
            hop(k, i).wait_recv()
        for p in range(4):
            v = tok[s, p].astype(full)
            inv = lax.rsqrt(jnp.mean(v * v, axis=-1, keepdims=True) + epsilon)
            x[i, p * own : (p + 1) * own, :] = (v * inv * gain_ref[0:1, :]).astype(low)
        for p in range(4):
            rows = slice(p * own, (p + 1) * own)
            part = nt(w_t[...], x[i, rows, :]).astype(low)
            proj[i, :, :, rows] = part.reshape(units, HD, own)
        for _, copy in leave(i):
            copy.start()

    straight(0)
    straight(1)
    forward(0)
    straight(2)
    weights(0, 0).wait()
    for r in range(1, n):
        weights(0, r).wait_recv()
    w_t[...] = w[:, : units * HD].T
    gain_ref[...] = w[:, SHARED : SHARED + 128].astype(full).T[:8]
    keep = pltpu.make_async_copy(w, every, wlocal.at[2])
    keep.start()
    forward(1)
    work(0)
    forward(2)
    work(1)
    work(2)
    keep.wait()
    weights(1, 0).wait()
    for r in range(1, n):
        weights(0, r).wait_send()
        weights(1, r).wait()
    for i in range(3):
        for k in range(6):
            hop(k, i).wait_send()
        for away, copy in leave(i):
            copy.wait()


def project(n, tokens, packed, up):
    sequences, own, width = tokens.shape
    shard, columns = packed.shape
    span = 4 * own
    return pl.pallas_call(
        functools.partial(project_kernel, n),
        in_specs=[ANY] * 3,
        out_specs=[ANY] * 4 + [pl.BlockSpec(memory_space=pltpu.VMEM)],
        out_shape=[
            shape((15, HD, 2 * span), low),
            shape((2, 2 * span, width), low),
            shape((n * shard, columns), low),
            shape((n * shard, up.shape[1]), low),
            shape((8, n * shard), full),
        ],
        scratch_shapes=[
            pltpu.VMEM((sequences, 4, own, width), low),
            pltpu.VMEM((sequences, span, width), low),
            pltpu.VMEM((n * shard, columns), low),
            pltpu.VMEM((9 * HD, width), low),
            pltpu.VMEM((sequences, 9, HD, span), low),
            dma((6, 3)), dma((6, 3)), dma((3,)),
            dma((2, n - 1)), dma((2, n - 1)), dma((3,)),
            dma((3, 8)), dma((3, 8)), dma((3, 8)),
        ],
        compiler_params=pltpu.CompilerParams(
            vmem_limit_bytes=40 << 20, collective_id=3, has_side_effects=True
        ),
        name="project",
    )(tokens, packed, up)


UNITS = 5
def unit_block(part):
    return lambda u: (jnp.where(u < 3, part * 3 + u, 9 + part * 2 + (u - 3)), 0, 0)


def attend_kernel(
    n, q_ref, k_ref, v_ref, lo_ref, every, up_part, down_own, att, lse_ref, of_ref, up, down, out_w,
    qs, ks, ss, obuf, ssem, rsem, lsem, wsend, wrecv, wlocal, zsend, zrecv,
):
    u = pl.program_id(0)
    c, t = place()
    d = lax.axis_index("dp")
    shard = down_own.shape[0]
    peers = [at_peer(c, t, dc, r) for dc, r in PEERS[1:]]

    def weight(j, r):
        rows = pl.ds(pl.multiple_of(d * shard, shard), shard)
        src, dst = (
            (down_own, down.at[t, rows]),
            (up_part, up.at[t]),
            (every.at[:, pl.ds(SHARED - 256, 256)], out_w.at[t]),
        )[j]
        if r == 0:
            return pltpu.make_async_copy(src, dst, wlocal.at[j])
        return pltpu.make_async_remote_copy(
            src, dst, wsend.at[j, r - 1], wrecv.at[j, r - 1], device_id={"tensor": t ^ r}
        )

    def shards(step, up_line):
        src = d - step if up_line else d + step
        rows = pl.ds(pl.multiple_of(jnp.clip(src, 0, n - 1) * shard, shard), shard)
        to = jnp.clip(d + 1 if up_line else d - 1, 0, n - 1)
        k = 0 if up_line else 1
        return pltpu.make_async_remote_copy(
            down.at[:, rows], down.at[:, rows], zsend.at[k, step], zrecv.at[k, step], device_id={"dp": to}
        )

    def line(step, what):
        for up_line in (True, False):
            inside = (d < n - 1) if up_line else (d > 0)
            has = (d >= step) if up_line else (d <= n - 1 - step)
            comes = (d >= step + 1) if up_line else (d <= n - 2 - step)
            if what == "recv":

                @pl.when(comes)
                def _():
                    shards(step, up_line).wait_recv()
            else:

                @pl.when(inside & has)
                def _():
                    if what == "start":
                        shards(step, up_line).start()
                    else:
                        shards(step, up_line).wait_send()
    length = lo_ref.shape[2]
    half = length // 2
    own = half // 4

    @pl.when(u == 0)
    def _():
        barrier = pltpu.get_barrier_semaphore()
        greet(peers)

        @pl.when(d > 0)
        def _():
            pl.semaphore_signal(barrier, inc=1, device_id={"dp": jnp.maximum(d - 1, 0)})

        @pl.when(d < n - 1)
        def _():
            pl.semaphore_signal(barrier, inc=1, device_id={"dp": jnp.minimum(d + 1, n - 1)})

        for j in range(3):
            weight(j, 0).start()
        ends = jnp.where(d > 0, 1, 0) + jnp.where(d < n - 1, 1, 0)
        pl.semaphore_wait(barrier, len(peers) + ends)
        for j in range(3):
            for r in range(1, 4):
                weight(j, r).start()

    qs[...] = q_ref[0] * low(0.125)
    ks[...] = k_ref[0].T
    for start in range(0, length, QB):
        stop = start + QB
        q = qs[:, start:stop]
        lo = lo_ref[0, :, start:stop]
        first = max(0, start - WIN)
        most = jnp.full((8, QB), NEG, full)
        for at in range(first, stop, CHUNK):
            s = nn(ks[at : at + CHUNK, :], q)
            key_pos = at + lax.broadcasted_iota(jnp.int32, (CHUNK, QB), 0)
            allowed = key_pos >= lo
            if at + CHUNK - 1 > start:
                allowed &= key_pos <= start + lax.broadcasted_iota(jnp.int32, (CHUNK, QB), 1)
            s = jnp.where(allowed, s, NEG)
            ss[at - first : at - first + CHUNK, :] = s
            most = jnp.maximum(most, jnp.max(s.reshape(CHUNK // 8, 8, QB), axis=0))
        most = jnp.max(most, axis=0, keepdims=True)
        total = jnp.zeros((8, QB), full)
        acc = jnp.zeros((HD, QB), full)
        for at in range(first, stop, CHUNK):
            p = jnp.exp(ss[at - first : at - first + CHUNK, :] - most)
            total += jnp.sum(p.reshape(CHUNK // 8, 8, QB), axis=0)
            acc += nn(v_ref[0, :, at : at + CHUNK], p.astype(low))
        total = jnp.sum(total, axis=0, keepdims=True)
        lse_ref[0, :, start:stop] = most + jnp.log(total)
        o = acc * (1.0 / total)
        of_ref[0, :, start:stop] = o
        obuf[u, :, start:stop] = o.astype(low)

    @pl.when(u == 0)
    def _():
        weight(0, 0).wait()
        for r in range(1, 4):
            weight(0, r).wait_recv()
        line(0, "start")

    @pl.when(u == 3)
    def _():
        if n > 2:
            line(0, "recv")
            line(1, "start")

    def move(unit, i, source_core):
        dc, r = PEERS[i]
        h, seq = unit_place(unit, source_core)
        dest = pl.multiple_of(((c ^ dc) * 4 + (t ^ r)) * own, own)
        src = obuf.at[unit, :, pl.ds(dest, own)]
        dst = att.at[
            pl.ds(pl.multiple_of((t * 3 + h) * HD, HD), HD), pl.ds(pl.multiple_of(seq * own, own), own)
        ]
        if i == 0:
            return pltpu.make_async_copy(src, dst, lsem.at[unit])
        return pltpu.make_async_remote_copy(
            src, dst, ssem.at[i - 1, unit], rsem.at[i - 1, unit], device_id=at_peer(c, t, dc, r)
        )

    @pl.when(sends(u, c))
    def _():
        for i in range(1, len(PEERS)):
            move(u, i, c).start()
        move(u, 0, c).start()

    @pl.when(u == pl.num_programs(0) - 1)
    def _():
        for step in range(2, n - 1):
            line(step - 1, "recv")
            line(step, "start")
        line(n - 2, "recv")
        for step in range(n - 1):
            line(step, "sent")
        for j in range(3):
            if j:
                weight(j, 0).wait()
            for r in range(1, 4):
                weight(j, r).wait_send()
                if j:
                    weight(j, r).wait_recv()
        for unit in range(UNITS):
            for i, (dc, r) in enumerate(PEERS):

                @pl.when(sends(unit, c))
                def _():
                    if i:
                        move(unit, i, c).wait_send()
                    else:
                        move(unit, i, c).wait()

                if i:

                    @pl.when(sends(unit, c ^ dc))
                    def _():
                        move(unit, i, c ^ dc).wait_recv()


def attend(n, qkv, lo, every, up_part, down_own):
    length = lo.shape[2]
    half = length // 2
    own = half // 4
    width, hidden = up_part.shape
    part = lambda p: pl.BlockSpec((1, HD, length), unit_block(p))
    unit = lambda rows, n: pl.BlockSpec((1, rows, n), lambda u: (u, 0, 0))
    heads = 4 * 3 * HD
    return pl.pallas_call(
        functools.partial(attend_kernel, n),
        grid=(UNITS,),
        in_specs=[part(0), part(1), part(2)]
        + [pl.BlockSpec((1, 1, length), lambda u: (u // 3, 0, 0))]
        + [ANY] * 3,
        out_specs=[ANY, unit(1, length), unit(HD, length)] + [ANY] * 3,
        scratch_shapes=[
            pltpu.VMEM((HD, length), low),
            pltpu.VMEM((length, HD), low),
            pltpu.VMEM((WIN + QB, QB), full),
            pltpu.VMEM((UNITS, HD, length), low),
            dma((7, UNITS)),
            dma((7, UNITS)),
            dma((UNITS,)),
            dma((3, 3)),
            dma((3, 3)),
            dma((3,)),
            dma((2, n - 1)),
            dma((2, n - 1)),
        ],
        out_shape=[
            jax.ShapeDtypeStruct((heads, 3 * own), low),
            jax.ShapeDtypeStruct((UNITS, 1, length), full),
            jax.ShapeDtypeStruct((UNITS, HD, length), full),
            shape((4, width, hidden), low),
            shape((4, width, hidden), low),
            shape((4, width, 256), low),
        ],
        compiler_params=pltpu.CompilerParams(
            vmem_limit_bytes=40 << 20, collective_id=1, has_side_effects=True
        ),
        cost_estimate=pl.CostEstimate(
            flops=UNITS * 18 * 2 * 256 * 1024 * 128, bytes_accessed=20 << 20, transcendentals=0
        ),
        name="attend",
    )(qkv, qkv, qkv, lo, every, up_part, down_own)


def attend_back_kernel(
    n, q_ref, k_ref, v_ref, lo_ref, lse_ref, of_ref, norm_ref, gud, gatt, gout, dall, gw_sum, zsum, osum,
    qs, ks, vs, gs, grow, qrow, delta, dqs, dbuf, gw, gwx, gwr, zr, obuf, gsem, grsem, glsem, ssem, rsem, lsem,
    zsend, zrecv, xsend, xrecv, osend, orecv, olocal,
):
    u = pl.program_id(0)
    c, t = place()
    d = lax.axis_index("dp")
    shard = gud.shape[2] // n
    peers = [at_peer(c, t, dc, r) for dc, r in PEERS[1:]]

    def rows_of(j):
        return pl.ds(pl.multiple_of(jnp.clip(j, 0, n - 1) * shard, shard), shard)

    def along(k):
        m = d if k == 0 else n - 1 - d
        to = {"dp": jnp.clip(d + 1 if k == 0 else d - 1, 0, n - 1)}
        return m, to, lambda step: (n - step + m if k == 0 else step - 1 - m)

    def pass_on(k, step, first):
        m, to, target = along(k)
        src = gud.at[:, :, rows_of(target(step))] if first else zr.at[k, max(step - 2, 0)]
        return pltpu.make_async_remote_copy(
            src, zr.at[k, step - 1], zsend.at[k, step - 1], zrecv.at[k, step - 1], device_id=to
        )

    def start_step(step):
        for k in range(2):
            m, _, target = along(k)
            if step == 1:

                @pl.when(m == 0)
                def _():
                    pass_on(k, step, True).start()

                continue

            @pl.when((m >= 1) & (step - 1 >= m))
            def _():
                pass_on(k, step - 1, False).wait_recv()

            @pl.when((m >= 1) & (m < n - 1) & (step >= m + 1))
            def _():
                rows = rows_of(target(step))
                for a in range(2):
                    for p in range(4):
                        total = zr[k, step - 2, a, p].astype(full) + gud[a, p, rows].astype(full)
                        zr[k, step - 2, a, p] = total.astype(low)
                pass_on(k, step, False).start()

            @pl.when(m == 0)
            def _():
                pass_on(k, step, True).start()

    def finish_line():
        for k in range(2):
            m, _, _ = along(k)

            @pl.when(m >= 1)
            def _():
                pass_on(k, n - 1, False).wait_recv()

            for step in range(1, n):

                @pl.when((m < n - 1) & (step >= m + 1))
                def _():
                    pass_on(k, step, False).wait_send()

        for a in range(2):
            for p in range(4):
                total = gud[a, p, rows_of(d)].astype(full)
                left, right = zr[0, n - 2, a, p].astype(full), zr[1, n - 2, a, p].astype(full)
                total += jnp.where(d > 0, left, 0.0) + jnp.where(d < n - 1, right, 0.0)
                zsum[a, p] = total.astype(low)

    part_rows = gout.shape[1] // 2

    def out_piece(i):
        dc, r = PEERS[i]
        src = gout.at[t ^ r, pl.ds(pl.multiple_of((c ^ dc) * part_rows, part_rows), part_rows)]
        if i == 0:
            return pltpu.make_async_copy(src, obuf.at[0], olocal)
        return pltpu.make_async_remote_copy(
            src, obuf.at[i], osend.at[i - 1], orecv.at[i - 1], device_id=at_peer(c, t, dc, r)
        )

    def other_core():
        return pltpu.make_async_remote_copy(
            gwx.at[1 - c], gwr, xsend, xrecv, device_id={"context": 1 - c}
        )
    length = lo_ref.shape[2]
    half = length // 2
    own = half // 4
    groups = ((0, 3), (3, 2))

    def fetch(group, i, receiving):
        dc, r = PEERS[i]
        first, count = groups[group]
        to_c, to_t = (c ^ dc, t ^ r)
        seq = 2 * to_c if group == 0 else 1
        head = to_t * 3 + (0 if group == 0 else to_c)
        src = gatt.at[pl.ds(head, count), :, pl.ds(pl.multiple_of(seq * own, own), own)]
        dst = gs.at[pl.ds(first, count), :, pl.ds(pl.multiple_of((c * 4 + t) * own, own), own)]
        if i == 0:
            return pltpu.make_async_copy(src, dst, glsem.at[group])
        return pltpu.make_async_remote_copy(
            src, dst, gsem.at[i - 1, group], grsem.at[i - 1, group], device_id=at_peer(c, t, dc, r)
        )

    @pl.when(u == 0)
    def _():
        barrier = pltpu.get_barrier_semaphore()
        greet(peers)

        @pl.when(d > 0)
        def _():
            pl.semaphore_signal(barrier, inc=1, device_id={"dp": jnp.maximum(d - 1, 0)})

        @pl.when(d < n - 1)
        def _():
            pl.semaphore_signal(barrier, inc=1, device_id={"dp": jnp.minimum(d + 1, n - 1)})

        gw[...] = jnp.zeros_like(gw)
        ends = jnp.where(d > 0, 1, 0) + jnp.where(d < n - 1, 1, 0)
        pl.semaphore_wait(barrier, len(peers) + ends)
        for group in range(2):
            for i in range(1, len(PEERS)):
                fetch(group, i, False).start()
            fetch(group, 0, False).start()
        start_step(1)
        for i in range(1, len(PEERS)):
            out_piece(i).start()
        out_piece(0).start()

    @pl.when(u == 3)
    def _():
        if n > 2:
            start_step(2)

    for group in range(2):

        @pl.when(u == groups[group][0])
        def _():
            fetch(group, 0, True).wait()
            for i in range(1, len(PEERS)):
                fetch(group, i, True).wait_recv()

    qs[...] = q_ref[0] * low(0.125)
    ks[...] = k_ref[0].T
    vs[...] = v_ref[0].T
    grow[...] = gs[u].T
    qrow[...] = qs[...].T
    delta[...] = jnp.sum(gs[u].astype(full) * of_ref[0], axis=0, keepdims=True)
    dqs[...] = jnp.zeros_like(dqs)
    for key_start in range(0, length, QB):
        rows = slice(key_start, key_start + QB)
        k, v, key_t = ks[rows, :], vs[rows, :], k_ref[0, :, rows]
        dk = jnp.zeros((QB, HD), full)
        dv = jnp.zeros((QB, HD), full)
        key_pos = key_start + lax.broadcasted_iota(jnp.int32, (QB, QB), 0)
        for start in range(key_start, min(key_start + WIN + QB, length), QB):
            cols = slice(start, start + QB)
            s = nn(k, qs[:, cols]) - lse_ref[0, :, cols]
            allowed = key_pos >= lo_ref[0, :, cols]
            if start == key_start:
                allowed &= key_pos <= start + lax.broadcasted_iota(jnp.int32, (QB, QB), 1)
            p = jnp.exp(jnp.where(allowed, s, NEG))
            dp = nn(v, gs[u, :, cols])
            ds = (p * (dp - delta[:, cols])).astype(low)
            dv += nn(p.astype(low), grow[cols, :])
            dk += nn(ds, qrow[cols, :])
            dqs[:, cols] += nn(key_t, ds)
        dbuf[u, 1, :, rows] = dk.T.astype(low)
        dbuf[u, 2, :, rows] = dv.T.astype(low)
    dbuf[u, 0] = (dqs[...] * 0.125).astype(low)

    def move(unit, i, source_core):
        dc, r = PEERS[i]
        h, seq = unit_place(unit, source_core)
        dest = pl.multiple_of(((c ^ dc) * 4 + (t ^ r)) * own, own)
        src = dbuf.at[unit, :, :, pl.ds(dest, own)]
        dst = dall.at[:, t * 3 + h, :, pl.ds(pl.multiple_of(seq * own, own), own)]
        if i == 0:
            return pltpu.make_async_copy(src, dst, lsem.at[unit])
        return pltpu.make_async_remote_copy(
            src, dst, ssem.at[i - 1, unit], rsem.at[i - 1, unit], device_id=at_peer(c, t, dc, r)
        )

    @pl.when(sends(u, c))
    def _():
        for i in range(1, len(PEERS)):
            move(u, i, c).start()
        move(u, 0, c).start()
        h, _ = unit_place(u, c)
        gw[h] += nn(dbuf[u].reshape(3 * HD, length), norm_ref[0])

    @pl.when(u == pl.num_programs(0) - 1)
    def _():
        wide_rows = [gw[h, p * HD : (p + 1) * HD, :] for p in range(3) for h in range(3)]
        gwx[0] = jnp.concatenate(wide_rows[:6], axis=0).T.astype(low)
        empty = jnp.zeros((3 * HD, gw.shape[2]), full)
        gwx[1] = jnp.concatenate(wide_rows[6:] + [empty], axis=0).T.astype(low)
        other_core().start()
        for step in range(3, n):
            start_step(step)
        out_piece(0).wait()
        for i in range(1, len(PEERS)):
            out_piece(i).wait()
        total = obuf[0].astype(full)
        for i in range(1, len(PEERS)):
            total += obuf[i].astype(full)
        osum[...] = total.astype(low)
        other_core().wait()
        gw_sum[...] = (gwx[c].astype(full) + gwr[...].astype(full)).astype(low)
        finish_line()
        for group in range(2):
            for i in range(1, len(PEERS)):
                fetch(group, i, False).wait_send()
        for unit in range(UNITS):
            for i, (dc, r) in enumerate(PEERS):

                @pl.when(sends(unit, c))
                def _():
                    if i:
                        move(unit, i, c).wait_send()
                    else:
                        move(unit, i, c).wait()

                if i:

                    @pl.when(sends(unit, c ^ dc))
                    def _():
                        move(unit, i, c ^ dc).wait_recv()


def attend_back(n, qkv, grad_attended, lo, lse, attended, normed, grad_up_down, grad_out):
    length = lo.shape[2]
    own = length // 8
    width = normed.shape[2]
    shard, hidden = grad_up_down.shape[2] // n, grad_up_down.shape[3]
    out_rows, local = grad_out.shape[1] // 2, grad_out.shape[2]
    part = lambda p: pl.BlockSpec((1, HD, length), unit_block(p))
    unit = lambda rows, m: pl.BlockSpec((1, rows, m), lambda u: (u, 0, 0))
    once = lambda dims: pl.BlockSpec(dims, lambda u: (0,) * len(dims), pipeline_mode=pl.Buffered(1))
    wide, tall = pltpu.VMEM((HD, length), low), pltpu.VMEM((length, HD), low)
    results = [(width, 2 * 3 * HD), (2, 4, shard, hidden), (out_rows, local)]
    return pl.pallas_call(
        functools.partial(attend_back_kernel, n),
        grid=(UNITS,),
        in_specs=[part(0), part(1), part(2)]
        + [
            pl.BlockSpec((1, 1, length), lambda u: (u // 3, 0, 0)),
            unit(1, length),
            unit(HD, length),
            pl.BlockSpec((1, length, width), lambda u: (u // 3, 0, 0)),
            once(grad_up_down.shape),
            ANY,
            ANY,
        ],
        out_specs=[ANY] + [once(r) for r in results],
        scratch_shapes=[
            wide, tall, tall, pltpu.VMEM((UNITS, HD, length), low), tall, tall,
            pltpu.VMEM((1, length), full), pltpu.VMEM((HD, length), full),
            pltpu.VMEM((UNITS, 3, HD, length), low), pltpu.VMEM((3, 3 * HD, width), full),
            pltpu.VMEM((2, width, 6 * HD), low), pltpu.VMEM((width, 6 * HD), low),
            pltpu.VMEM((2, n - 1, 2, 4, shard, hidden), low), pltpu.VMEM((8, out_rows, local), low),
            dma((7, 2)), dma((7, 2)), dma((2,)), dma((7, UNITS)), dma((7, UNITS)), dma((UNITS,)),
            dma((2, n - 1)), dma((2, n - 1)), dma, dma, dma((7,)), dma((7,)), dma,
        ],
        out_shape=[shape((3, 12, HD, 3 * own), low)] + [shape(r, low) for r in results],
        compiler_params=pltpu.CompilerParams(
            vmem_limit_bytes=62 << 20, collective_id=2, has_side_effects=True
        ),
        cost_estimate=pl.CostEstimate(
            flops=UNITS * 18 * 5 * 256 * 1024 * 128, bytes_accessed=30 << 20, transcendentals=0
        ),
        name="attend_back",
    )(qkv, qkv, qkv, lo, lse, attended, normed, grad_up_down, grad_attended, grad_out)


def last_kernel(
    n, dqkv, w_all, tokens, middle, gains, w_mine, up_mine, gain_mine, gw_sum, zsum, osum,
    grad_in, g_qkv, g_up, g_down, g_out, g_gain,
    rg, rw, ro, down_t, out_t, mine, sums,
    gsend, grecv, wsend, wrecv, osend, orecv, lsem, csend, crecv, ssend, srecv, clocal,
):
    c, t = place()
    d = lax.axis_index("dp")
    shard, hidden = rw.shape[2], rw.shape[3]
    cut = n // 2
    group = [at_peer(c, t, dc, r) for dc, r in PEERS[1:]]
    others = [lax.rem(d + r, n) for r in range(1, n)]
    peers = group + [{"dp": o} for o in others]
    greet(peers)

    def rows_of(j):
        return pl.ds(pl.multiple_of(j * shard, shard), shard)

    narrow = slice(0, 256)

    def qkv_piece(r, core):
        src, dst = gw_sum.at[rows_of(d if r == 0 else others[r - 1])], rg.at[r]
        if core:
            src, dst = src.at[:, narrow], dst.at[:, narrow]
        if r == 0:
            return pltpu.make_async_copy(src, dst, lsem.at[0])
        return pltpu.make_async_remote_copy(
            src, dst, gsend.at[r - 1], grecv.at[r - 1], device_id={"dp": others[r - 1]}
        )

    def each_core(what):
        for core in range(2):

            @pl.when(c == core)
            def _():
                what(core)

    def up_piece(r):
        src, dst = zsum.at[:, t ^ r], rw.at[r]
        if r == 0:
            return pltpu.make_async_copy(src, dst, lsem.at[1])
        return pltpu.make_async_remote_copy(
            src, dst, wsend.at[r - 1], wrecv.at[r - 1], device_id={"tensor": t ^ r}
        )

    mine_out = d // cut == c

    def out_piece(r):
        to = d if r == 0 else others[r - 1]
        src, dst = osum.at[rows_of(lax.rem(to, cut))], ro.at[r]
        if r == 0:
            return pltpu.make_async_copy(src, dst, lsem.at[2])
        return pltpu.make_async_remote_copy(
            src, dst, osend.at[r - 1], orecv.at[r - 1], device_id={"dp": to}
        )

    def start_all(core):
        for r in range(1, n):
            qkv_piece(r, core).start()
        qkv_piece(0, core).start()

    greeted(peers)
    each_core(start_all)
    for r in range(1, 4):
        up_piece(r).start()
    up_piece(0).start()
    for r in range(1, n):

        @pl.when(others[r - 1] // cut == c)
        def _():
            out_piece(r).start()

    @pl.when(mine_out)
    def _():
        out_piece(0).start()

    for m in range(0, tokens.shape[0], QB):
        rows = slice(m, m + QB)
        r = tn(dqkv[:, rows], w_all[...])
        v = tokens[rows, :].astype(full)
        inv = lax.rsqrt(jnp.mean(v * v, axis=-1, keepdims=True) + epsilon)
        rg_ = r * gains[0:1, :]
        grad = inv * (rg_ - v * (inv * inv * jnp.mean(rg_ * v, axis=-1, keepdims=True)))
        grad_in[rows, :] = (middle[rows, :] + grad).astype(low)

    def halves(j):
        half = pl.ds(pl.multiple_of(c * hidden, hidden), hidden)
        src, dst = (
            (mine.at[0], g_qkv.at[:, half]),
            (mine.at[1], g_up.at[:, half]),
            (down_t, g_down.at[half]),
            (out_t, g_out),
        )[j]
        return (
            pltpu.make_async_copy(src, dst, clocal.at[j]),
            pltpu.make_async_remote_copy(
                src, dst, csend.at[j], crecv.at[j], device_id={"context": 1 - c}
            ),
        )

    def deliver(j):
        for copy in halves(j):
            copy.start()

    up_piece(0).wait()
    for r in range(1, 4):
        up_piece(r).wait_recv()
    mine[1] = sum(rw[r, 0].astype(full) for r in range(4))
    down_t[...] = sum(rw[r, 1].astype(full) for r in range(4)).T
    deliver(1)
    deliver(2)

    @pl.when(mine_out)
    def _():
        out_piece(0).wait()
        for r in range(1, n):
            out_piece(r).wait_recv()
        out_t[...] = sum(ro[r].astype(full) for r in range(n)).T
        deliver(3)

    def take(core):
        qkv_piece(0, core).wait()
        for r in range(1, n):
            qkv_piece(r, core).wait_recv()
        if core:
            mine[0, :, narrow] = sum(rg[r, :, narrow].astype(full) for r in range(n))
            mine[0, :, 256:] = jnp.zeros((shard, hidden - 256), full)
        else:
            mine[0] = sum(rg[r].astype(full) for r in range(n))

    each_core(take)
    deliver(0)
    lane = lax.broadcasted_iota(jnp.int32, (shard, 128), 1)
    first = jnp.sum(w_mine[...].astype(full) * mine[0], axis=1, keepdims=True)
    second = jnp.sum(up_mine[...].astype(full) * mine[1], axis=1, keepdims=True)
    sums[0] = jnp.where(lane == 0, first, jnp.where(lane == 1, second, 0.0))

    def gain_piece(i):
        dc, r = PEERS[i]
        return pltpu.make_async_remote_copy(
            sums.at[0], sums.at[i], ssend.at[i - 1], srecv.at[i - 1], device_id=at_peer(c, t, dc, r)
        )

    for i in range(1, len(PEERS)):
        gain_piece(i).start()
    for i in range(1, len(PEERS)):
        gain_piece(i).wait()
    total = sum(sums[i] for i in range(len(PEERS)))
    g_gain[...] = total / jnp.where(lane < 2, gain_mine[...].astype(full), 1.0)

    for j in range(3):
        for copy in halves(j):
            copy.wait()

    @pl.when(mine_out)
    def _():
        local, away = halves(3)
        local.wait()
        away.wait_send()

    @pl.when(jnp.logical_not(mine_out))
    def _():
        halves(3)[1].wait_recv()

    for r in range(1, 4):
        up_piece(r).wait_send()

    def sent(core):
        for r in range(1, n):
            qkv_piece(r, core).wait_send()

    each_core(sent)
    for r in range(1, n):

        @pl.when(others[r - 1] // cut == c)
        def _():
            out_piece(r).wait_send()


def last(n, dqkv, w_all, tokens, middle, gains, w_mine, up_mine, gain_mine, gw_sum, zsum, osum):
    rows, width = tokens.shape
    _, _, shard, hidden = zsum.shape
    local = osum.shape[1]
    vmem = pl.BlockSpec(memory_space=pltpu.VMEM)
    return pl.pallas_call(
        functools.partial(last_kernel, n),
        in_specs=[vmem] * 8 + [ANY] * 3,
        out_specs=[vmem] + [ANY] * 4 + [vmem],
        out_shape=[
            shape((rows, width), low),
            shape((shard, 2 * hidden), full),
            shape((shard, 2 * hidden), full),
            shape((2 * hidden, shard), full),
            shape((local, shard), full),
            shape((shard, 128), full),
        ],
        scratch_shapes=[
            pltpu.VMEM((n, shard, hidden), low),
            pltpu.VMEM((4, 2, shard, hidden), low),
            pltpu.VMEM((n, shard, local), low),
            pltpu.VMEM((hidden, shard), full),
            pltpu.VMEM((local, shard), full),
            pltpu.VMEM((2, shard, hidden), full),
            pltpu.VMEM((8, shard, 128), full),
            dma((n - 1,)), dma((n - 1,)), dma((3,)), dma((3,)), dma((n - 1,)), dma((n - 1,)), dma((3,)),
            dma((4,)), dma((4,)), dma((7,)), dma((7,)), dma((4,)),
        ],
        compiler_params=pltpu.CompilerParams(
            vmem_limit_bytes=50 << 20, collective_id=4, has_side_effects=True
        ),
        name="last",
    )(dqkv, w_all, tokens, middle, gains, w_mine, up_mine, gain_mine, gw_sum, zsum, osum)


def gelu_and_slope(v):
    k0 = math.sqrt(2.0 / math.pi)
    square = v * v
    th = jnp.tanh(v * (k0 + (k0 * 0.044715) * square))
    half = 0.5 + 0.5 * th
    slope = half + (v * half) * ((1.0 - th) * (k0 + (3.0 * 0.044715 * k0) * square))
    return v * half, slope


def feed_kernel(
    xm, xt, gm, gt, up_ref, down_ref, om, ot, bm, bt, dup, ddown,
    x, g, x_t, g_t, up, down, act, gh, out, back, pre, ga,
):
    rows, width = xm.shape
    n = up_ref.shape[2]
    blocks = 2 * rows // QB

    @pl.when(pl.program_id(0) == 0)
    def _():
        for i, (a, b) in enumerate(((xm, gm), (xt, gt))):
            part = slice(i * rows, (i + 1) * rows)
            x[part, :] = a[...]
            g[part, :] = b[...]
            x_t[:, part] = a[...].T
            g_t[:, part] = b[...].T
        out[...] = jnp.zeros_like(out)
        back[...] = jnp.zeros_like(back)

    for i in range(2):
        up[:, i * n : (i + 1) * n] = up_ref[i]
        down[:, i * n : (i + 1) * n] = down_ref[i]

    def first(i):
        part = slice(i * QB, (i + 1) * QB)
        pre[i % 2] = nn(x[part, :], up[...])
        ga[i % 2] = nn(g[part, :], down[...])

    def second(i):
        part = slice(i * QB, (i + 1) * QB)
        a, slope = gelu_and_slope(pre[i % 2])
        act[part, :] = a.astype(low)
        gh[part, :] = (ga[i % 2] * slope).astype(low)

    def third(i):
        part = slice(i * QB, (i + 1) * QB)
        out[part, :] += nt(act[part, :], down[...])
        back[part, :] += nt(gh[part, :], up[...])

    first(0)
    for i in range(blocks):
        if i + 1 < blocks:
            first(i + 1)
        second(i)
        if i > 0:
            third(i - 1)
    third(blocks - 1)
    for m in range(0, width, QB):
        part = slice(m, m + QB)
        u = nn(x_t[part, :], gh[...]).astype(low)
        v = nn(g_t[part, :], act[...]).astype(low)
        for i in range(2):
            dup[i, part, :] = u[:, i * n : (i + 1) * n]
            ddown[i, part, :] = v[:, i * n : (i + 1) * n]

    @pl.when(pl.program_id(0) == pl.num_programs(0) - 1)
    def _():
        om[...] = out[:rows, :]
        ot[...] = out[rows:, :].astype(low)
        bm[...] = back[:rows, :]
        bt[...] = back[rows:, :].astype(low)


def feed(xm, xt, gm, gt, up, down):
    rows, width = xm.shape
    pieces, _, n = up.shape
    whole = pl.BlockSpec((rows, width), lambda j: (0, 0))
    weight = pl.BlockSpec((2, width, n), lambda j: (j, 0, 0))
    shape = jax.ShapeDtypeStruct
    return pl.pallas_call(
        feed_kernel,
        grid=(pieces // 2,),
        in_specs=[whole] * 4 + [weight] * 2,
        out_specs=[whole] * 4 + [weight] * 2,
        out_shape=[shape((rows, width), kind) for kind in (full, low, full, low)]
        + [shape(up.shape, low)] * 2,
        scratch_shapes=[pltpu.VMEM((2 * rows, width), low)] * 2
        + [pltpu.VMEM((width, 2 * rows), low)] * 2
        + [pltpu.VMEM((width, 2 * n), low)] * 2
        + [pltpu.VMEM((2 * rows, 2 * n), low)] * 2
        + [pltpu.VMEM((2 * rows, width), full)] * 2
        + [pltpu.VMEM((2, QB, 2 * n), full)] * 2,
        compiler_params=pltpu.CompilerParams(vmem_limit_bytes=60 << 20),
        cost_estimate=pl.CostEstimate(
            flops=6 * 2 * 2 * rows * width * pieces * n, bytes_accessed=20 << 20, transcendentals=0
        ),
        name="feed",
    )(xm, xt, gm, gt, up, down)


def per_device(tokens, segments, w_qkv, w_out, w_in, w_back, gain_attn, gain_mlp, cotangent):
    sequences, own, width = tokens.shape
    assert lax.axis_size("tensor") == 4 and lax.axis_size("context") == 2 and sequences == 3
    c, t, d = lax.axis_index("context"), lax.axis_index("tensor"), lax.axis_index("dp")
    span = 4 * own
    length = segments.shape[1]
    shard = w_qkv.shape[0]
    local = w_qkv.shape[2]
    heads = local // HD
    hidden = w_in.shape[1] // 2
    rows = sequences * own

    up_own = lax.dynamic_slice_in_dim(w_in, c * hidden, hidden, 1)
    down_own = lax.dynamic_slice_in_dim(w_back, c * hidden, hidden, 0).T
    pad = jnp.zeros((shard, 126), low)
    packed = [w_qkv.reshape(shard, 3 * local), w_out.T, gain_attn[:, None], gain_mlp[:, None], pad]
    packed = jnp.concatenate(packed, axis=1)
    n = lax.axis_size("dp")
    qkv, normed_units, every, up_part, gains = project(n, tokens, packed, up_own)
    gain_first, gain_second = gains[0], gains[1]
    cot_theirs = across(cotangent, "context", 1)

    lo = jnp.zeros((sequences, length), jnp.int32)
    for value in range(8):
        before = jnp.sum((segments < value).astype(jnp.int32), axis=1, keepdims=True)
        lo = jnp.where(segments == value, before, lo)
    lo = jnp.maximum(lo, jnp.arange(length, dtype=jnp.int32)[None] - (WIN - 1))
    lo = jnp.stack([jnp.where(c == 0, lo[0], lo[2]), lo[1]])[:, None]

    def inverse(v):
        return lax.rsqrt(jnp.mean(v * v, axis=-1, keepdims=True) + epsilon)

    attended, log_totals, out_full, w_up, w_down, w_proj = attend(
        n, qkv, lo, every, up_part, down_own
    )
    w_attn_all = jnp.stack(gather_tensor(every[:, : 3 * local].T, 0)).reshape(4, 3, local, width)
    w_attn_all = [lax.dynamic_index_in_dim(w_attn_all, t ^ p, 0, False) for p in range(4)]
    w_attn_all = jnp.stack(w_attn_all, axis=1).reshape(12 * local, width)
    proj_rows = w_proj[:, :, 256 - local :].transpose(0, 2, 1).reshape(4 * local, width)
    inputs = tokens.astype(full).reshape(rows, width)
    middle = inputs + tn(attended, proj_rows)
    inv_two = inverse(middle)
    normed_two = (middle * inv_two * gain_second).astype(low)

    cot = cotangent.reshape(rows, width)
    branch, branch_sent, back, back_sent, grad_up, grad_down = feed(
        normed_two, across(normed_two, "context", 1), cot, cot_theirs.reshape(rows, width), w_up, w_down
    )
    grad_norm_two = back + across(back_sent, "context", 1).astype(full)
    result = (middle + branch + across(branch_sent, "context", 1).astype(full)).astype(low)

    def norm_back(r, gain, v, inv):
        rg = r * gain
        return inv * (rg - v * (inv * inv * jnp.mean(rg * v, axis=-1, keepdims=True)))

    grad_middle = cot.astype(full) + norm_back(grad_norm_two, gain_second, middle, inv_two)
    grad_low = grad_middle.astype(low)
    grad_out = jnp.einsum(
        "plr,rw->pwl", attended.reshape(4, local, rows), grad_low, preferred_element_type=full
    ).astype(low)
    grad_att = nt(proj_rows, grad_low).astype(low).reshape(4 * heads, HD, rows)
    grad_projected, gw_sum, zsum, osum = attend_back(
        n, qkv, grad_att, lo, log_totals, out_full, normed_units, jnp.stack([grad_up, grad_down]), grad_out
    )
    two = jnp.concatenate([packed[:, : 3 * local], jnp.zeros((shard, 4 * hidden), low)], axis=1)
    w_mine = lax.dynamic_slice_in_dim(two, c * hidden, hidden, 1)
    grad_input, own_attn, own_up, own_down, own_proj, own_gains = last(
        n,
        grad_projected.reshape(12 * local, rows),
        w_attn_all,
        tokens.reshape(rows, width),
        grad_middle,
        gains,
        w_mine,
        up_own,
        packed[:, SHARED:],
        gw_sum,
        zsum,
        osum,
    )
    return (
        result.reshape(sequences, own, width),
        grad_input.reshape(sequences, own, width),
        own_attn[:, : 3 * local].reshape(shard, 3, local),
        own_proj,
        own_up,
        own_down,
        own_gains[:, 0],
        own_gains[:, 1],
    )


def solution(mesh):
    return jax.shard_map(
        per_device,
        mesh=mesh,
        in_specs=(
            P("dp", ("context", "tensor"), None),
            P("dp", None),
            P("dp", None, "tensor"),
            P("tensor", "dp"),
            P("dp", "tensor"),
            P("tensor", "dp"),
            P("dp"),
            P("dp"),
            P("dp", ("context", "tensor"), None),
        ),
        out_specs=(
            P("dp", ("context", "tensor"), None),
            P("dp", ("context", "tensor"), None),
            P("dp", None, "tensor"),
            P("tensor", "dp"),
            P("dp", "tensor"),
            P("tensor", "dp"),
            P("dp"),
            P("dp"),
        ),
        check_vma=False,
    )
```

```python
import functools
import math

import jax
import jax.numpy as jnp
from jax import lax
from jax.experimental import pallas as pl
from jax.experimental.pallas import tpu as pltpu
from jax.sharding import PartitionSpec as P

HD = 64
WIN = 1536
QB = 256
CHUNK = 128
NEG = -1e30
epsilon = 1e-06
low = jnp.bfloat16
full = jnp.float32


def dot(left, right, dims):
    return lax.dot_general(left, right, (dims, ((), ())), preferred_element_type=full)


def nn(left, right):
    return dot(left, right, ((1,), (0,)))


def nt(left, right):
    return dot(left, right, ((1,), (1,)))


def tn(left, right):
    return dot(left, right, ((0,), (0,)))


PEERS = [(dc, r) for dc in range(2) for r in range(4)]


def place():
    return lax.axis_index("context"), lax.axis_index("tensor")


def at_peer(c, t, dc, r):
    return {"context": c ^ dc, "tensor": t ^ r}


def greet(peers):
    for peer in peers:
        pl.semaphore_signal(pltpu.get_barrier_semaphore(), inc=1, device_id=peer)


def greeted(peers):
    pl.semaphore_wait(pltpu.get_barrier_semaphore(), len(peers))


def unit_place(u, c):
    return jnp.where(u < 3, u, c + u - 3), jnp.where(u < 3, 2 * c, 1)


def sends(u, c):
    return (u != 3) | (c == 0)


dma = pltpu.SemaphoreType.DMA
ANY = pl.BlockSpec(memory_space=pl.ANY)
VMEM = pl.BlockSpec(memory_space=pltpu.VMEM)
shape = jax.ShapeDtypeStruct


GAINS = 512


def project_kernel(
    n, tokens, packed, up, out_w, qkv, norm, w_t, up_all, out_all, gain_ref,
    tok, x, w, proj, tsend, trecv, tlocal, wsend, wrecv, wlocal, osend, orecv, olocal,
):
    c, t = place()
    d = lax.axis_index("dp")
    own = tokens.shape[1]
    width = tokens.shape[2]
    span = 4 * own
    shard = packed.shape[0]
    half = own // 2
    to_x, to_y, to_core = {"tensor": t ^ 1}, {"tensor": t ^ 2}, {"context": 1 - c}
    others = [{"dp": lax.rem(d + r, n)} for r in range(1, n)]
    peers = [to_x, to_y, to_core] + others
    greet(peers)

    def local(i, s):
        return pltpu.make_async_copy(tokens.at[s], tok.at[s, t], tlocal.at[i])

    def weights(j, r):
        source, target, sem = ((packed, w, 0), (out_w, out_all, 1), (up, up_all, 2))[j]
        rows = pl.ds(pl.multiple_of(d * shard, shard), shard)
        if r == 0:
            return pltpu.make_async_copy(source, target.at[rows], wlocal.at[sem])
        return pltpu.make_async_remote_copy(
            source, target.at[rows], wsend.at[sem, r - 1], wrecv.at[sem, r - 1], device_id=others[r - 1]
        )

    order = (2 * (1 - c), 1, 2 * c)
    for i, s in enumerate(order):
        local(i, s).start()
    for j in range(3):
        weights(j, 0).start()
    greeted(peers)
    for j in range(3):
        for r in range(1, n):
            weights(j, r).start()

    def hop(k, i):
        s = order[i]
        origin, rows, peer = (
            (t, slice(0, half), to_x),
            (t, slice(half, own), to_y),
            (t, slice(0, half), to_y),
            (t, slice(half, own), to_x),
            (t ^ 1, slice(0, half), to_y),
            (t ^ 2, slice(half, own), to_x),
        )[k]
        there = tok.at[s, origin, rows]
        here = tokens.at[s, rows] if k < 4 else there
        return pltpu.make_async_remote_copy(
            here, there, tsend.at[k, i], trecv.at[k, i], device_id=peer
        )

    def straight(i):
        for k in range(4):
            hop(k, i).start()

    def forward(i):
        for k in range(2):
            hop(k, i).wait_recv()
            hop(k + 4, i).start()

    units = proj.shape[1]

    def leave(i):
        out = []
        lanes = pl.ds(pl.multiple_of(c * span, span), span)
        if i != 0:
            out.append((x.at[i], norm.at[2 - i, lanes], False))
        if i != 2:
            out.append((x.at[i], norm.at[i, lanes], True))
        if i == 0:
            out.append((proj.at[0], qkv.at[pl.ds(0, units), :, lanes], True))
        if i == 2:
            out.append((proj.at[2], qkv.at[pl.ds(0, units), :, lanes], False))
        if i == 1:
            for away in (True, False):
                core = 1 - c if away else c
                for p in range(3):
                    src = proj.at[1, pl.ds(p * 3 + core, 2)]
                    out.append((src, qkv.at[pl.ds(units + 2 * p, 2), :, lanes], away))
        copies = []
        for j, (src, dst, away) in enumerate(out):
            if away:
                copies.append(
                    (away, pltpu.make_async_remote_copy(src, dst, osend.at[i, j], orecv.at[i, j], device_id=to_core))
                )
            else:
                copies.append((away, pltpu.make_async_copy(src, dst, olocal.at[i, j])))
        return copies

    def work(i):
        s = order[i]
        local(i, s).wait()
        for k in range(2, 6):
            hop(k, i).wait_recv()
        for p in range(4):
            v = tok[s, p].astype(full)
            inv = lax.rsqrt(jnp.mean(v * v, axis=-1, keepdims=True) + epsilon)
            x[i, p * own : (p + 1) * own, :] = (v * inv * gain_ref[0:1, :]).astype(low)
        for p in range(4):
            rows = slice(p * own, (p + 1) * own)
            part = nt(w_t[...], x[i, rows, :]).astype(low)
            proj[i, :, :, rows] = part.reshape(units, HD, own)
        for _, copy in leave(i):
            copy.start()

    straight(0)
    straight(1)
    forward(0)
    straight(2)
    weights(0, 0).wait()
    for r in range(1, n):
        weights(0, r).wait_recv()
    w_t[...] = w[:, : units * HD].T
    gain_ref[...] = w[:, GAINS : GAINS + 128].astype(full).T[64:72]
    forward(1)
    work(0)
    forward(2)
    work(1)
    work(2)
    for j in range(3):
        if j:
            weights(j, 0).wait()
        for r in range(1, n):
            weights(j, r).wait_send()
            if j:
                weights(j, r).wait_recv()
    for i in range(3):
        for k in range(6):
            hop(k, i).wait_send()
        for away, copy in leave(i):
            copy.wait()


def project(n, tokens, packed, up, out_w):
    sequences, own, width = tokens.shape
    shard, columns = packed.shape
    span = 4 * own
    return pl.pallas_call(
        functools.partial(project_kernel, n),
        in_specs=[ANY] * 4,
        out_specs=[ANY] * 2 + [VMEM] + [ANY] * 2 + [VMEM],
        out_shape=[
            shape((15, HD, 2 * span), low),
            shape((2, 2 * span, width), low),
            shape((9 * HD, n * shard), low),
            shape((n * shard, up.shape[1]), low),
            shape((n * shard, out_w.shape[1]), low),
            shape((8, n * shard), full),
        ],
        scratch_shapes=[
            pltpu.VMEM((sequences, 4, own, width), low),
            pltpu.VMEM((sequences, span, width), low),
            pltpu.VMEM((n * shard, columns), low),
            pltpu.VMEM((sequences, 9, HD, span), low),
            dma((6, 3)), dma((6, 3)), dma((3,)),
            dma((3, n - 1)), dma((3, n - 1)), dma((3,)),
            dma((3, 8)), dma((3, 8)), dma((3, 8)),
        ],
        compiler_params=pltpu.CompilerParams(
            vmem_limit_bytes=40 << 20, collective_id=3, has_side_effects=True
        ),
        name="project",
    )(tokens, packed, up, out_w)


UNITS = 5
def unit_block(part):
    return lambda u: (jnp.where(u < 3, part * 3 + u, 9 + part * 2 + (u - 3)), 0, 0)


def attend_kernel(
    n, q_ref, k_ref, v_ref, lo_ref, out_part, up_part, down_own, att, lse_ref, of_ref, up, down, out_w,
    qs, ks, ss, obuf, ssem, rsem, lsem, wsend, wrecv, wlocal, zsend, zrecv, fsend, frecv,
):
    u = pl.program_id(0)
    c, t = place()
    d = lax.axis_index("dp")
    shard = down_own.shape[0]
    peers = [at_peer(c, t, dc, r) for dc, r in PEERS[1:]]

    part = out_part.shape[0] // 2
    mine = pl.ds(pl.multiple_of(c * part, part), part)

    def weight(j, r):
        rows = pl.ds(pl.multiple_of(d * shard, shard), shard)
        src, dst = (
            (down_own, down.at[t, rows]),
            (up_part, up.at[t]),
            (out_part.at[mine], out_w.at[t, mine]),
        )[j]
        if r == 0:
            return pltpu.make_async_copy(src, dst, wlocal.at[j])
        return pltpu.make_async_remote_copy(
            src, dst, wsend.at[j, r - 1], wrecv.at[j, r - 1], device_id={"tensor": t ^ r}
        )

    def onward(k):
        if k == 2:
            ref, peer = out_w.at[:, mine], {"context": 1 - c}
        else:
            rows = pl.ds(k * part, part)
            ref, peer = up.at[t ^ (1 + k), rows], {"tensor": t ^ (2 - k)}
        return pltpu.make_async_remote_copy(
            ref, ref, fsend.at[k], frecv.at[k], device_id=peer
        )

    def shards(step, up_line):
        src = d - step if up_line else d + step
        rows = pl.ds(pl.multiple_of(jnp.clip(src, 0, n - 1) * shard, shard), shard)
        to = jnp.clip(d + 1 if up_line else d - 1, 0, n - 1)
        k = 0 if up_line else 1
        return pltpu.make_async_remote_copy(
            down.at[:, rows], down.at[:, rows], zsend.at[k, step], zrecv.at[k, step], device_id={"dp": to}
        )

    def line(step, what):
        for up_line in (True, False):
            inside = (d < n - 1) if up_line else (d > 0)
            has = (d >= step) if up_line else (d <= n - 1 - step)
            comes = (d >= step + 1) if up_line else (d <= n - 2 - step)
            if what == "recv":

                @pl.when(comes)
                def _():
                    shards(step, up_line).wait_recv()
            else:

                @pl.when(inside & has)
                def _():
                    if what == "start":
                        shards(step, up_line).start()
                    else:
                        shards(step, up_line).wait_send()
    length = lo_ref.shape[2]
    half = length // 2
    own = half // 4

    @pl.when(u == 0)
    def _():
        barrier = pltpu.get_barrier_semaphore()
        greet(peers)

        @pl.when(d > 0)
        def _():
            pl.semaphore_signal(barrier, inc=1, device_id={"dp": jnp.maximum(d - 1, 0)})

        @pl.when(d < n - 1)
        def _():
            pl.semaphore_signal(barrier, inc=1, device_id={"dp": jnp.minimum(d + 1, n - 1)})

        for j in range(3):
            weight(j, 0).start()
        ends = jnp.where(d > 0, 1, 0) + jnp.where(d < n - 1, 1, 0)
        pl.semaphore_wait(barrier, len(peers) + ends)
        for j in (0, 2, 1):
            for r in range(1, 3 if j == 1 else 4):
                weight(j, r).start()

    qs[...] = q_ref[0] * low(0.125)
    ks[...] = k_ref[0].T
    for start in range(0, length, QB):
        stop = start + QB
        q = qs[:, start:stop]
        lo = lo_ref[0, :, start:stop]
        first = max(0, start - WIN)
        most = jnp.full((8, QB), NEG, full)
        for at in range(first, stop, CHUNK):
            s = nn(ks[at : at + CHUNK, :], q)
            key_pos = at + lax.broadcasted_iota(jnp.int32, (CHUNK, QB), 0)
            allowed = key_pos >= lo
            if at + CHUNK - 1 > start:
                allowed &= key_pos <= start + lax.broadcasted_iota(jnp.int32, (CHUNK, QB), 1)
            s = jnp.where(allowed, s, NEG)
            ss[at - first : at - first + CHUNK, :] = s
            most = jnp.maximum(most, jnp.max(s.reshape(CHUNK // 8, 8, QB), axis=0))
        most = jnp.max(most, axis=0, keepdims=True)
        total = jnp.zeros((8, QB), full)
        acc = jnp.zeros((HD, QB), full)
        for at in range(first, stop, CHUNK):
            p = jnp.exp(ss[at - first : at - first + CHUNK, :] - most)
            total += jnp.sum(p.reshape(CHUNK // 8, 8, QB), axis=0)
            acc += nn(v_ref[0, :, at : at + CHUNK], p.astype(low))
        total = jnp.sum(total, axis=0, keepdims=True)
        lse_ref[0, :, start:stop] = most + jnp.log(total)
        o = acc * (1.0 / total)
        of_ref[0, :, start:stop] = o
        obuf[u, :, start:stop] = o.astype(low)

    @pl.when(u == 0)
    def _():
        weight(0, 0).wait()
        for r in range(1, 4):
            weight(0, r).wait_recv()
        line(0, "start")

    @pl.when(u == 3)
    def _():
        if n > 2:
            line(0, "recv")
            line(1, "start")
        for k in range(2):
            weight(1, 1 + k).wait_recv()
            onward(k).start()
        weight(2, 0).wait()
        for r in range(1, 4):
            weight(2, r).wait_recv()
        onward(2).start()

    def move(unit, i, source_core):
        dc, r = PEERS[i]
        h, seq = unit_place(unit, source_core)
        dest = pl.multiple_of(((c ^ dc) * 4 + (t ^ r)) * own, own)
        src = obuf.at[unit, :, pl.ds(dest, own)]
        dst = att.at[
            pl.ds(pl.multiple_of((t * 3 + h) * HD, HD), HD), pl.ds(pl.multiple_of(seq * own, own), own)
        ]
        if i == 0:
            return pltpu.make_async_copy(src, dst, lsem.at[unit])
        return pltpu.make_async_remote_copy(
            src, dst, ssem.at[i - 1, unit], rsem.at[i - 1, unit], device_id=at_peer(c, t, dc, r)
        )

    @pl.when(sends(u, c))
    def _():
        for i in range(1, len(PEERS)):
            move(u, i, c).start()
        move(u, 0, c).start()

    @pl.when(u == pl.num_programs(0) - 1)
    def _():
        for step in range(2, n - 1):
            line(step - 1, "recv")
            line(step, "start")
        line(n - 2, "recv")
        for step in range(n - 1):
            line(step, "sent")
        weight(1, 0).wait()
        for j in range(3):
            for r in range(1, 3 if j == 1 else 4):
                weight(j, r).wait_send()
        for k in range(3):
            onward(k).wait()
        for unit in range(UNITS):
            for i, (dc, r) in enumerate(PEERS):

                @pl.when(sends(unit, c))
                def _():
                    if i:
                        move(unit, i, c).wait_send()
                    else:
                        move(unit, i, c).wait()

                if i:

                    @pl.when(sends(unit, c ^ dc))
                    def _():
                        move(unit, i, c ^ dc).wait_recv()


def attend(n, qkv, lo, out_part, up_part, down_own):
    length = lo.shape[2]
    half = length // 2
    own = half // 4
    width, hidden = up_part.shape
    part = lambda p: pl.BlockSpec((1, HD, length), unit_block(p))
    unit = lambda rows, n: pl.BlockSpec((1, rows, n), lambda u: (u, 0, 0))
    heads = 4 * 3 * HD
    return pl.pallas_call(
        functools.partial(attend_kernel, n),
        grid=(UNITS,),
        in_specs=[part(0), part(1), part(2)]
        + [pl.BlockSpec((1, 1, length), lambda u: (u // 3, 0, 0))]
        + [ANY] * 3,
        out_specs=[ANY, unit(1, length), unit(HD, length)] + [ANY] * 3,
        scratch_shapes=[
            pltpu.VMEM((HD, length), low),
            pltpu.VMEM((length, HD), low),
            pltpu.VMEM((WIN + QB, QB), full),
            pltpu.VMEM((UNITS, HD, length), low),
            dma((7, UNITS)),
            dma((7, UNITS)),
            dma((UNITS,)),
            dma((3, 3)),
            dma((3, 3)),
            dma((3,)),
            dma((2, n - 1)),
            dma((2, n - 1)),
            dma((3,)),
            dma((3,)),
        ],
        out_shape=[
            jax.ShapeDtypeStruct((heads, 3 * own), low),
            jax.ShapeDtypeStruct((UNITS, 1, length), full),
            jax.ShapeDtypeStruct((UNITS, HD, length), full),
            shape((4, width, hidden), low),
            shape((4, width, hidden), low),
            shape((4,) + out_part.shape, low),
        ],
        compiler_params=pltpu.CompilerParams(
            vmem_limit_bytes=40 << 20, collective_id=1, has_side_effects=True
        ),
        cost_estimate=pl.CostEstimate(
            flops=UNITS * 18 * 2 * 256 * 1024 * 128, bytes_accessed=20 << 20, transcendentals=0
        ),
        name="attend",
    )(qkv, qkv, qkv, lo, out_part, up_part, down_own)


def attend_back_kernel(
    n, q_ref, k_ref, v_ref, lo_ref, lse_ref, of_ref, norm_ref, gud, gatt, gout, dall, gw_sum, zsum, osum,
    qs, ks, vs, gs, grow, qrow, delta, dqs, dbuf, gw, gwx, gwr, zr, obuf, gsem, grsem, glsem, ssem, rsem, lsem,
    zsend, zrecv, xsend, xrecv, osend, orecv, olocal,
):
    u = pl.program_id(0)
    c, t = place()
    d = lax.axis_index("dp")
    shard = gud.shape[2] // n
    peers = [at_peer(c, t, dc, r) for dc, r in PEERS[1:]]

    def rows_of(j):
        return pl.ds(pl.multiple_of(jnp.clip(j, 0, n - 1) * shard, shard), shard)

    def along(k):
        m = d if k == 0 else n - 1 - d
        to = {"dp": jnp.clip(d + 1 if k == 0 else d - 1, 0, n - 1)}
        return m, to, lambda step: (n - step + m if k == 0 else step - 1 - m)

    def pass_on(k, step, first):
        m, to, target = along(k)
        src = gud.at[:, :, rows_of(target(step))] if first else zr.at[k, max(step - 2, 0)]
        return pltpu.make_async_remote_copy(
            src, zr.at[k, step - 1], zsend.at[k, step - 1], zrecv.at[k, step - 1], device_id=to
        )

    def start_step(step):
        for k in range(2):
            m, _, target = along(k)
            if step == 1:

                @pl.when(m == 0)
                def _():
                    pass_on(k, step, True).start()

                continue

            @pl.when((m >= 1) & (step - 1 >= m))
            def _():
                pass_on(k, step - 1, False).wait_recv()

            @pl.when((m >= 1) & (m < n - 1) & (step >= m + 1))
            def _():
                rows = rows_of(target(step))
                for a in range(2):
                    for p in range(4):
                        total = zr[k, step - 2, a, p].astype(full) + gud[a, p, rows].astype(full)
                        zr[k, step - 2, a, p] = total.astype(low)
                pass_on(k, step, False).start()

            @pl.when(m == 0)
            def _():
                pass_on(k, step, True).start()

    def finish_line():
        for k in range(2):
            m, _, _ = along(k)

            @pl.when(m >= 1)
            def _():
                pass_on(k, n - 1, False).wait_recv()

            for step in range(1, n):

                @pl.when((m < n - 1) & (step >= m + 1))
                def _():
                    pass_on(k, step, False).wait_send()

        for a in range(2):
            for p in range(4):
                total = gud[a, p, rows_of(d)].astype(full)
                left, right = zr[0, n - 2, a, p].astype(full), zr[1, n - 2, a, p].astype(full)
                total += jnp.where(d > 0, left, 0.0) + jnp.where(d < n - 1, right, 0.0)
                zsum[a, p] = total.astype(low)

    part_rows = gout.shape[1] // 2

    def out_piece(i):
        dc, r = PEERS[i]
        src = gout.at[t ^ r, pl.ds(pl.multiple_of((c ^ dc) * part_rows, part_rows), part_rows)]
        if i == 0:
            return pltpu.make_async_copy(src, obuf.at[0], olocal)
        return pltpu.make_async_remote_copy(
            src, obuf.at[i], osend.at[i - 1], orecv.at[i - 1], device_id=at_peer(c, t, dc, r)
        )

    def other_core():
        return pltpu.make_async_remote_copy(
            gwx.at[1 - c], gwr, xsend, xrecv, device_id={"context": 1 - c}
        )
    length = lo_ref.shape[2]
    half = length // 2
    own = half // 4
    groups = ((0, 3), (3, 2))

    def fetch(group, i, receiving):
        dc, r = PEERS[i]
        first, count = groups[group]
        to_c, to_t = (c ^ dc, t ^ r)
        seq = 2 * to_c if group == 0 else 1
        head = to_t * 3 + (0 if group == 0 else to_c)
        src = gatt.at[pl.ds(head, count), :, pl.ds(pl.multiple_of(seq * own, own), own)]
        dst = gs.at[pl.ds(first, count), :, pl.ds(pl.multiple_of((c * 4 + t) * own, own), own)]
        if i == 0:
            return pltpu.make_async_copy(src, dst, glsem.at[group])
        return pltpu.make_async_remote_copy(
            src, dst, gsem.at[i - 1, group], grsem.at[i - 1, group], device_id=at_peer(c, t, dc, r)
        )

    @pl.when(u == 0)
    def _():
        barrier = pltpu.get_barrier_semaphore()
        greet(peers)

        @pl.when(d > 0)
        def _():
            pl.semaphore_signal(barrier, inc=1, device_id={"dp": jnp.maximum(d - 1, 0)})

        @pl.when(d < n - 1)
        def _():
            pl.semaphore_signal(barrier, inc=1, device_id={"dp": jnp.minimum(d + 1, n - 1)})

        gw[...] = jnp.zeros_like(gw)
        ends = jnp.where(d > 0, 1, 0) + jnp.where(d < n - 1, 1, 0)
        pl.semaphore_wait(barrier, len(peers) + ends)
        for group in range(2):
            for i in range(1, len(PEERS)):
                fetch(group, i, False).start()
            fetch(group, 0, False).start()
        start_step(1)
        for i in range(1, len(PEERS)):
            out_piece(i).start()
        out_piece(0).start()

    @pl.when(u == 3)
    def _():
        if n > 2:
            start_step(2)

    for group in range(2):

        @pl.when(u == groups[group][0])
        def _():
            fetch(group, 0, True).wait()
            for i in range(1, len(PEERS)):
                fetch(group, i, True).wait_recv()

    qs[...] = q_ref[0] * low(0.125)
    ks[...] = k_ref[0].T
    vs[...] = v_ref[0].T
    grow[...] = gs[u].T
    qrow[...] = qs[...].T
    delta[...] = jnp.sum(gs[u].astype(full) * of_ref[0], axis=0, keepdims=True)
    dqs[...] = jnp.zeros_like(dqs)
    for key_start in range(0, length, QB):
        rows = slice(key_start, key_start + QB)
        k, v, key_t = ks[rows, :], vs[rows, :], k_ref[0, :, rows]
        dk = jnp.zeros((QB, HD), full)
        dv = jnp.zeros((QB, HD), full)
        key_pos = key_start + lax.broadcasted_iota(jnp.int32, (QB, QB), 0)
        for start in range(key_start, min(key_start + WIN + QB, length), QB):
            cols = slice(start, start + QB)
            s = nn(k, qs[:, cols]) - lse_ref[0, :, cols]
            allowed = key_pos >= lo_ref[0, :, cols]
            if start == key_start:
                allowed &= key_pos <= start + lax.broadcasted_iota(jnp.int32, (QB, QB), 1)
            p = jnp.exp(jnp.where(allowed, s, NEG))
            dp = nn(v, gs[u, :, cols])
            ds = (p * (dp - delta[:, cols])).astype(low)
            dv += nn(p.astype(low), grow[cols, :])
            dk += nn(ds, qrow[cols, :])
            dqs[:, cols] += nn(key_t, ds)
        dbuf[u, 1, :, rows] = dk.T.astype(low)
        dbuf[u, 2, :, rows] = dv.T.astype(low)
    dbuf[u, 0] = (dqs[...] * 0.125).astype(low)

    def move(unit, i, source_core):
        dc, r = PEERS[i]
        h, seq = unit_place(unit, source_core)
        dest = pl.multiple_of(((c ^ dc) * 4 + (t ^ r)) * own, own)
        src = dbuf.at[unit, :, :, pl.ds(dest, own)]
        dst = dall.at[t, :, h, :, pl.ds(pl.multiple_of(seq * own, own), own)]
        if i == 0:
            return pltpu.make_async_copy(src, dst, lsem.at[unit])
        return pltpu.make_async_remote_copy(
            src, dst, ssem.at[i - 1, unit], rsem.at[i - 1, unit], device_id=at_peer(c, t, dc, r)
        )

    @pl.when(sends(u, c))
    def _():
        for i in range(1, len(PEERS)):
            move(u, i, c).start()
        move(u, 0, c).start()
        h, _ = unit_place(u, c)
        gw[h] += nn(dbuf[u].reshape(3 * HD, length), norm_ref[0])

    @pl.when(u == pl.num_programs(0) - 1)
    def _():
        wide_rows = [gw[h, p * HD : (p + 1) * HD, :] for p in range(3) for h in range(3)]
        gwx[0] = jnp.concatenate(wide_rows[:6], axis=0).T.astype(low)
        empty = jnp.zeros((3 * HD, gw.shape[2]), full)
        gwx[1] = jnp.concatenate(wide_rows[6:] + [empty], axis=0).T.astype(low)
        other_core().start()
        for step in range(3, n):
            start_step(step)
        out_piece(0).wait()
        for i in range(1, len(PEERS)):
            out_piece(i).wait()
        total = obuf[0].astype(full)
        for i in range(1, len(PEERS)):
            total += obuf[i].astype(full)
        osum[...] = total.astype(low)
        other_core().wait()
        gw_sum[...] = (gwx[c].astype(full) + gwr[...].astype(full)).astype(low)
        finish_line()
        for group in range(2):
            for i in range(1, len(PEERS)):
                fetch(group, i, False).wait_send()
        for unit in range(UNITS):
            for i, (dc, r) in enumerate(PEERS):

                @pl.when(sends(unit, c))
                def _():
                    if i:
                        move(unit, i, c).wait_send()
                    else:
                        move(unit, i, c).wait()

                if i:

                    @pl.when(sends(unit, c ^ dc))
                    def _():
                        move(unit, i, c ^ dc).wait_recv()


def attend_back(n, qkv, grad_attended, lo, lse, attended, normed, grad_up_down, grad_out):
    length = lo.shape[2]
    own = length // 8
    width = normed.shape[2]
    shard, hidden = grad_up_down.shape[2] // n, grad_up_down.shape[3]
    out_rows, local = grad_out.shape[1] // 2, grad_out.shape[2]
    part = lambda p: pl.BlockSpec((1, HD, length), unit_block(p))
    unit = lambda rows, m: pl.BlockSpec((1, rows, m), lambda u: (u, 0, 0))
    once = lambda dims: pl.BlockSpec(dims, lambda u: (0,) * len(dims), pipeline_mode=pl.Buffered(1))
    wide, tall = pltpu.VMEM((HD, length), low), pltpu.VMEM((length, HD), low)
    results = [(width, 2 * 3 * HD), (2, 4, shard, hidden), (out_rows, local)]
    return pl.pallas_call(
        functools.partial(attend_back_kernel, n),
        grid=(UNITS,),
        in_specs=[part(0), part(1), part(2)]
        + [
            pl.BlockSpec((1, 1, length), lambda u: (u // 3, 0, 0)),
            unit(1, length),
            unit(HD, length),
            pl.BlockSpec((1, length, width), lambda u: (u // 3, 0, 0)),
            once(grad_up_down.shape),
            ANY,
            ANY,
        ],
        out_specs=[ANY] + [once(r) for r in results],
        scratch_shapes=[
            wide, tall, tall, pltpu.VMEM((UNITS, HD, length), low), tall, tall,
            pltpu.VMEM((1, length), full), pltpu.VMEM((HD, length), full),
            pltpu.VMEM((UNITS, 3, HD, length), low), pltpu.VMEM((3, 3 * HD, width), full),
            pltpu.VMEM((2, width, 6 * HD), low), pltpu.VMEM((width, 6 * HD), low),
            pltpu.VMEM((2, n - 1, 2, 4, shard, hidden), low), pltpu.VMEM((8, out_rows, local), low),
            dma((7, 2)), dma((7, 2)), dma((2,)), dma((7, UNITS)), dma((7, UNITS)), dma((UNITS,)),
            dma((2, n - 1)), dma((2, n - 1)), dma, dma, dma((7,)), dma((7,)), dma,
        ],
        out_shape=[shape((4, 3, 3, HD, 3 * own), low)] + [shape(r, low) for r in results],
        compiler_params=pltpu.CompilerParams(
            vmem_limit_bytes=62 << 20, collective_id=2, has_side_effects=True
        ),
        cost_estimate=pl.CostEstimate(
            flops=UNITS * 18 * 5 * 256 * 1024 * 128, bytes_accessed=30 << 20, transcendentals=0
        ),
        name="attend_back",
    )(qkv, qkv, qkv, lo, lse, attended, normed, grad_up_down, grad_attended, grad_out)


def last_kernel(
    n, dqkv, w_all, tokens, middle, gains, w_mine, up_mine, gain_mine, gw_sum, zsum, osum,
    grad_in, g_qkv, g_up, g_down, g_out, g_gain,
    rg, rw, ro, down_t, out_t, mine, sums,
    gsend, grecv, wsend, wrecv, osend, orecv, lsem, csend, crecv, ssend, srecv, clocal,
):
    c, t = place()
    d = lax.axis_index("dp")
    shard, hidden = rw.shape[2], rw.shape[3]
    cut = n // 2
    group = [at_peer(c, t, dc, r) for dc, r in PEERS[1:]]
    others = [lax.rem(d + r, n) for r in range(1, n)]
    peers = group + [{"dp": o} for o in others]
    greet(peers)

    def rows_of(j):
        return pl.ds(pl.multiple_of(j * shard, shard), shard)

    narrow = slice(0, 256)

    def qkv_piece(r, core):
        src, dst = gw_sum.at[rows_of(d if r == 0 else others[r - 1])], rg.at[r]
        if core:
            src, dst = src.at[:, narrow], dst.at[:, narrow]
        if r == 0:
            return pltpu.make_async_copy(src, dst, lsem.at[0])
        return pltpu.make_async_remote_copy(
            src, dst, gsend.at[r - 1], grecv.at[r - 1], device_id={"dp": others[r - 1]}
        )

    def each_core(what):
        for core in range(2):

            @pl.when(c == core)
            def _():
                what(core)

    def up_piece(r):
        src, dst = zsum.at[:, t ^ r], rw.at[r]
        if r == 0:
            return pltpu.make_async_copy(src, dst, lsem.at[1])
        return pltpu.make_async_remote_copy(
            src, dst, wsend.at[r - 1], wrecv.at[r - 1], device_id={"tensor": t ^ r}
        )

    mine_out = d // cut == c

    def out_piece(r):
        to = d if r == 0 else others[r - 1]
        src, dst = osum.at[rows_of(lax.rem(to, cut))], ro.at[r]
        if r == 0:
            return pltpu.make_async_copy(src, dst, lsem.at[2])
        return pltpu.make_async_remote_copy(
            src, dst, osend.at[r - 1], orecv.at[r - 1], device_id={"dp": to}
        )

    def start_all(core):
        for r in range(1, n):
            qkv_piece(r, core).start()
        qkv_piece(0, core).start()

    greeted(peers)
    each_core(start_all)
    for r in range(1, 4):
        up_piece(r).start()
    up_piece(0).start()
    for r in range(1, n):

        @pl.when(others[r - 1] // cut == c)
        def _():
            out_piece(r).start()

    @pl.when(mine_out)
    def _():
        out_piece(0).start()

    for m in range(0, tokens.shape[0], QB):
        rows = slice(m, m + QB)
        r = tn(dqkv[:, rows], w_all[...])
        v = tokens[rows, :].astype(full)
        inv = lax.rsqrt(jnp.mean(v * v, axis=-1, keepdims=True) + epsilon)
        rg_ = r * gains[0:1, :]
        grad = inv * (rg_ - v * (inv * inv * jnp.mean(rg_ * v, axis=-1, keepdims=True)))
        grad_in[rows, :] = (middle[rows, :] + grad).astype(low)

    def halves(j):
        half = pl.ds(pl.multiple_of(c * hidden, hidden), hidden)
        src, dst = (
            (mine.at[0], g_qkv.at[:, half]),
            (mine.at[1], g_up.at[:, half]),
            (down_t, g_down.at[half]),
            (out_t, g_out),
        )[j]
        return (
            pltpu.make_async_copy(src, dst, clocal.at[j]),
            pltpu.make_async_remote_copy(
                src, dst, csend.at[j], crecv.at[j], device_id={"context": 1 - c}
            ),
        )

    def deliver(j):
        for copy in halves(j):
            copy.start()

    up_piece(0).wait()
    for r in range(1, 4):
        up_piece(r).wait_recv()
    mine[1] = sum(rw[r, 0].astype(full) for r in range(4))
    down_t[...] = sum(rw[r, 1].astype(full) for r in range(4)).T
    deliver(1)
    deliver(2)

    @pl.when(mine_out)
    def _():
        out_piece(0).wait()
        for r in range(1, n):
            out_piece(r).wait_recv()
        out_t[...] = sum(ro[r].astype(full) for r in range(n)).T
        deliver(3)

    def take(core):
        qkv_piece(0, core).wait()
        for r in range(1, n):
            qkv_piece(r, core).wait_recv()
        if core:
            mine[0, :, narrow] = sum(rg[r, :, narrow].astype(full) for r in range(n))
            mine[0, :, 256:] = jnp.zeros((shard, hidden - 256), full)
        else:
            mine[0] = sum(rg[r].astype(full) for r in range(n))

    each_core(take)
    deliver(0)
    lane = lax.broadcasted_iota(jnp.int32, (shard, 128), 1)
    first = jnp.sum(w_mine[...].astype(full) * mine[0], axis=1, keepdims=True)
    second = jnp.sum(up_mine[...].astype(full) * mine[1], axis=1, keepdims=True)
    sums[0] = jnp.where(lane == 0, first, jnp.where(lane == 1, second, 0.0))

    def gain_piece(i):
        dc, r = PEERS[i]
        return pltpu.make_async_remote_copy(
            sums.at[0], sums.at[i], ssend.at[i - 1], srecv.at[i - 1], device_id=at_peer(c, t, dc, r)
        )

    for i in range(1, len(PEERS)):
        gain_piece(i).start()
    for i in range(1, len(PEERS)):
        gain_piece(i).wait()
    total = sum(sums[i] for i in range(len(PEERS)))
    g_gain[...] = total / jnp.where(lane < 2, gain_mine[...].astype(full), 1.0)

    for j in range(3):
        for copy in halves(j):
            copy.wait()

    @pl.when(mine_out)
    def _():
        local, away = halves(3)
        local.wait()
        away.wait_send()

    @pl.when(jnp.logical_not(mine_out))
    def _():
        halves(3)[1].wait_recv()

    for r in range(1, 4):
        up_piece(r).wait_send()

    def sent(core):
        for r in range(1, n):
            qkv_piece(r, core).wait_send()

    each_core(sent)
    for r in range(1, n):

        @pl.when(others[r - 1] // cut == c)
        def _():
            out_piece(r).wait_send()


def last(n, dqkv, w_all, tokens, middle, gains, w_mine, up_mine, gain_mine, gw_sum, zsum, osum):
    rows, width = tokens.shape
    _, _, shard, hidden = zsum.shape
    local = osum.shape[1]
    return pl.pallas_call(
        functools.partial(last_kernel, n),
        in_specs=[VMEM] * 8 + [ANY] * 3,
        out_specs=[VMEM] + [ANY] * 4 + [VMEM],
        out_shape=[
            shape((rows, width), low),
            shape((shard, 2 * hidden), full),
            shape((shard, 2 * hidden), full),
            shape((2 * hidden, shard), full),
            shape((local, shard), full),
            shape((shard, 128), full),
        ],
        scratch_shapes=[
            pltpu.VMEM((n, shard, hidden), low),
            pltpu.VMEM((4, 2, shard, hidden), low),
            pltpu.VMEM((n, shard, local), low),
            pltpu.VMEM((hidden, shard), full),
            pltpu.VMEM((local, shard), full),
            pltpu.VMEM((2, shard, hidden), full),
            pltpu.VMEM((8, shard, 128), full),
            dma((n - 1,)), dma((n - 1,)), dma((3,)), dma((3,)), dma((n - 1,)), dma((n - 1,)), dma((3,)),
            dma((4,)), dma((4,)), dma((7,)), dma((7,)), dma((4,)),
        ],
        compiler_params=pltpu.CompilerParams(
            vmem_limit_bytes=50 << 20, collective_id=4, has_side_effects=True
        ),
        name="last",
    )(dqkv, w_all, tokens, middle, gains, w_mine, up_mine, gain_mine, gw_sum, zsum, osum)


def gelu_and_slope(v):
    k0 = math.sqrt(2.0 / math.pi)
    square = v * v
    th = jnp.tanh(v * (k0 + (k0 * 0.044715) * square))
    half = 0.5 + 0.5 * th
    slope = half + (v * half) * ((1.0 - th) * (k0 + (3.0 * 0.044715 * k0) * square))
    return v * half, slope


def feed_kernel(
    att, proj, tokens, cot, gains, w_t, up_ref, down_ref, result, middle, gud, gout, gatt, w_all,
    x, g, x_t, g_t, up, down, act, gh, out, back, pre, ga, proj_w, sent, got,
    xsend, xrecv, wsend, wrecv, wlocal,
):
    j = pl.program_id(0)
    c, t = place()
    rows, width = tokens.shape
    n = up_ref.shape[2]
    local = proj.shape[2]
    blocks = 2 * rows // QB
    other = {"context": 1 - c}
    peers = [other] + [{"tensor": t ^ r} for r in range(1, 4)]
    mine, theirs = slice(0, rows), slice(rows, 2 * rows)

    def cross(k):
        src, dst = (
            (cot, g.at[theirs]),
            (x.at[mine], x.at[theirs]),
            (sent.at[0], got.at[0]),
            (sent.at[1], got.at[1]),
        )[k]
        return pltpu.make_async_remote_copy(src, dst, xsend.at[k], xrecv.at[k], device_id=other)

    def over_tensor(r):
        if r == 0:
            return pltpu.make_async_copy(w_t, w_all.at[t], wlocal)
        return pltpu.make_async_remote_copy(
            w_t, w_all.at[t], wsend.at[r - 1], wrecv.at[r - 1], device_id={"tensor": t ^ r}
        )

    @pl.when(j == 0)
    def _():
        greet(peers)
        for p in range(4):
            proj_w[:, p * local : (p + 1) * local] = proj[p]
        greeted(peers)
        cross(0).start()
        for r in range(1, 4):
            over_tensor(r).start()
        over_tensor(0).start()
        g[mine, :] = cot[...]
        g_t[:, mine] = cot[...].T
        for m in range(0, rows, QB):
            part = slice(m, m + QB)
            v = tokens[part, :].astype(full) + nn(proj_w[...], att[:, part]).T
            middle[part, :] = v
            inv = lax.rsqrt(jnp.mean(v * v, axis=-1, keepdims=True) + epsilon)
            x[part, :] = (v * inv * gains[1:2, :]).astype(low)
        cross(1).start()
        x_t[:, mine] = x[mine, :].T
        out[...] = jnp.zeros_like(out)
        back[...] = jnp.zeros_like(back)

    for i in range(2):
        up[:, i * n : (i + 1) * n] = up_ref[i]
        down[:, i * n : (i + 1) * n] = down_ref[i]

    def first(i):
        part = slice(i * QB, (i + 1) * QB)
        pre[i % 2] = nn(x[part, :], up[...])
        ga[i % 2] = nn(g[part, :], down[...])

    def second(i):
        part = slice(i * QB, (i + 1) * QB)
        a, slope = gelu_and_slope(pre[i % 2])
        act[part, :] = a.astype(low)
        gh[part, :] = (ga[i % 2] * slope).astype(low)

    def third(i):
        part = slice(i * QB, (i + 1) * QB)
        out[part, :] += nt(act[part, :], down[...])
        back[part, :] += nt(gh[part, :], up[...])

    first(0)
    for i in range(blocks):
        if i + 1 == blocks // 2:

            @pl.when(j == 0)
            def _():
                cross(0).wait_recv()
                cross(1).wait_recv()
                x_t[:, theirs] = x[theirs, :].T
                g_t[:, theirs] = g[theirs, :].T

        if i + 1 < blocks:
            first(i + 1)
        second(i)
        if i > 0:
            third(i - 1)
    third(blocks - 1)

    @pl.when(j == pl.num_programs(0) - 1)
    def _():
        sent[0] = back[theirs, :].astype(low)
        cross(2).start()
        sent[1] = out[theirs, :].astype(low)
        cross(3).start()

    for m in range(0, width, QB):
        part = slice(m, m + QB)
        du = nn(x_t[part, :], gh[...]).astype(low)
        dd = nn(g_t[part, :], act[...]).astype(low)
        for i in range(2):
            gud[0, i, part, :] = du[:, i * n : (i + 1) * n]
            gud[1, i, part, :] = dd[:, i * n : (i + 1) * n]

    @pl.when(j == pl.num_programs(0) - 1)
    def _():
        low_t = x_t.at[:, mine]
        cross(2).wait_recv()
        gain = gains[1:2, :]
        for m in range(0, rows, QB):
            part = slice(m, m + QB)
            r = (back[part, :] + got[0, part, :].astype(full)) * gain
            v = middle[part, :]
            inv = lax.rsqrt(jnp.mean(v * v, axis=-1, keepdims=True) + epsilon)
            grad = inv * (r - v * (inv * inv * jnp.mean(r * v, axis=-1, keepdims=True)))
            back[part, :] = cot[part, :].astype(full) + grad
            low_t[:, part] = back[part, :].astype(low).T
        for m in range(0, width, QB):
            part = slice(m, m + QB)
            big = nt(low_t[part, :], att[...]).astype(low)
            for p in range(4):
                gout[p, part, :] = big[:, p * local : (p + 1) * local]
        for m in range(0, rows, QB):
            part = slice(m, m + QB)
            gatt[:, part] = tn(proj_w[...], low_t[:, part]).astype(low)
        cross(3).wait_recv()
        result[...] = (middle[...] + out[mine, :] + got[1].astype(full)).astype(low)
        middle[...] = back[mine, :]
        for k in range(4):
            cross(k).wait_send()
        over_tensor(0).wait()
        for r in range(1, 4):
            over_tensor(r).wait()


def feed(att, proj, tokens, cot, gains, w_t, up, down):
    rows, width = tokens.shape
    pieces, _, n = up.shape
    whole = lambda dims: pl.BlockSpec(dims, lambda j: (0,) * len(dims), pipeline_mode=pl.Buffered(1))
    weight = pl.BlockSpec((2, width, n), lambda j: (j, 0, 0))
    results = [shape((rows, width), low), shape((rows, width), full)]
    results += [shape((2,) + up.shape, low), shape(proj.shape, low), shape(att.shape, low)]
    return pl.pallas_call(
        feed_kernel,
        grid=(pieces // 2,),
        in_specs=[whole(a.shape) for a in (att, proj, tokens, cot, gains)] + [ANY] + [weight] * 2,
        out_specs=[whole((rows, width))] * 2
        + [pl.BlockSpec((2, 2, width, n), lambda j: (0, j, 0, 0))]
        + [whole(proj.shape), whole(att.shape), ANY],
        out_shape=results + [shape((4,) + w_t.shape, low)],
        scratch_shapes=[pltpu.VMEM((2 * rows, width), low)] * 2
        + [pltpu.VMEM((width, 2 * rows), low)] * 2
        + [pltpu.VMEM((width, 2 * n), low)] * 2
        + [pltpu.VMEM((2 * rows, 2 * n), low)] * 2
        + [pltpu.VMEM((2 * rows, width), full)] * 2
        + [pltpu.VMEM((2, QB, 2 * n), full)] * 2
        + [pltpu.VMEM((width, width), low)]
        + [pltpu.VMEM((2, rows, width), low)] * 2
        + [dma((4,)), dma((4,)), dma((3,)), dma((3,)), dma],
        compiler_params=pltpu.CompilerParams(
            vmem_limit_bytes=63 << 20, collective_id=5, has_side_effects=True
        ),
        name="feed",
    )(att, proj, tokens, cot, gains, w_t, up, down)


def per_device(tokens, segments, w_qkv, w_out, w_in, w_back, gain_attn, gain_mlp, cotangent):
    sequences, own, width = tokens.shape
    assert lax.axis_size("tensor") == 4 and lax.axis_size("context") == 2 and sequences == 3
    c, t, d = lax.axis_index("context"), lax.axis_index("tensor"), lax.axis_index("dp")
    span = 4 * own
    length = segments.shape[1]
    shard = w_qkv.shape[0]
    local = w_qkv.shape[2]
    heads = local // HD
    hidden = w_in.shape[1] // 2
    rows = sequences * own

    up_own = lax.dynamic_slice_in_dim(w_in, c * hidden, hidden, 1)
    down_own = lax.dynamic_slice_in_dim(w_back, c * hidden, hidden, 0).T
    pad = jnp.zeros((shard, 62), low)
    packed = [w_qkv.reshape(shard, 3 * local), gain_attn[:, None], gain_mlp[:, None], pad]
    packed = jnp.concatenate(packed, axis=1)
    n = lax.axis_size("dp")
    qkv, normed_units, w_t, up_part, out_part, gains = project(n, tokens, packed, up_own, w_out.T)

    lo = jnp.zeros((sequences, length), jnp.int32)
    for value in range(8):
        before = jnp.sum((segments < value).astype(jnp.int32), axis=1, keepdims=True)
        lo = jnp.where(segments == value, before, lo)
    lo = jnp.maximum(lo, jnp.arange(length, dtype=jnp.int32)[None] - (WIN - 1))
    lo = jnp.stack([jnp.where(c == 0, lo[0], lo[2]), lo[1]])[:, None]

    attended, log_totals, out_full, w_up, w_down, w_proj = attend(
        n, qkv, lo, out_part, up_part, down_own
    )
    flat = tokens.reshape(rows, width)
    result, grad_middle, grad_up_down, grad_out, grad_att, w_all = feed(
        attended, w_proj, flat, cotangent.reshape(rows, width), gains, w_t, w_up, w_down
    )
    grad_projected, gw_sum, zsum, osum = attend_back(
        n, qkv, grad_att.reshape(4 * heads, HD, rows), lo, log_totals, out_full, normed_units, grad_up_down, grad_out
    )
    two = jnp.concatenate([packed[:, : 3 * local], jnp.zeros((shard, 4 * hidden), low)], axis=1)
    w_mine = lax.dynamic_slice_in_dim(two, c * hidden, hidden, 1)
    grad_input, own_attn, own_up, own_down, own_proj, own_gains = last(
        n,
        grad_projected.reshape(12 * local, rows),
        w_all.reshape(12 * local, width),
        flat,
        grad_middle,
        gains,
        w_mine,
        up_own,
        jnp.pad(packed[:, 3 * local : 3 * local + 2], ((0, 0), (0, 126))),
        gw_sum,
        zsum,
        osum,
    )
    return (
        result.reshape(sequences, own, width),
        grad_input.reshape(sequences, own, width),
        own_attn[:, : 3 * local].reshape(shard, 3, local),
        own_proj,
        own_up,
        own_down,
        own_gains[:, 0],
        own_gains[:, 1],
    )


def solution(mesh):
    return jax.shard_map(
        per_device,
        mesh=mesh,
        in_specs=(
            P("dp", ("context", "tensor"), None),
            P("dp", None),
            P("dp", None, "tensor"),
            P("tensor", "dp"),
            P("dp", "tensor"),
            P("tensor", "dp"),
            P("dp"),
            P("dp"),
            P("dp", ("context", "tensor"), None),
        ),
        out_specs=(
            P("dp", ("context", "tensor"), None),
            P("dp", ("context", "tensor"), None),
            P("dp", None, "tensor"),
            P("tensor", "dp"),
            P("dp", "tensor"),
            P("tensor", "dp"),
            P("dp"),
            P("dp"),
        ),
        check_vma=False,
    )
```

```python
import functools
import math

import jax
import jax.numpy as jnp
from jax import lax
from jax.experimental import pallas as pl
from jax.experimental.pallas import tpu as pltpu
from jax.sharding import PartitionSpec as P

HD = 64
WIN = 1536
QB = 256
CHUNK = 128
NEG = -1e30
epsilon = 1e-06
low = jnp.bfloat16
full = jnp.float32


def dot(left, right, dims):
    return lax.dot_general(left, right, (dims, ((), ())), preferred_element_type=full)


def nn(left, right):
    return dot(left, right, ((1,), (0,)))


def nt(left, right):
    return dot(left, right, ((1,), (1,)))


def tn(left, right):
    return dot(left, right, ((0,), (0,)))


PEERS = [(dc, r) for dc in range(2) for r in range(4)]


def place():
    return lax.axis_index("context"), lax.axis_index("tensor")


def at_peer(c, t, dc, r):
    return {"context": c ^ dc, "tensor": t ^ r}


def greet(peers):
    for peer in peers:
        pl.semaphore_signal(pltpu.get_barrier_semaphore(), inc=1, device_id=peer)


def greeted(peers):
    pl.semaphore_wait(pltpu.get_barrier_semaphore(), len(peers))


def unit_place(u, c):
    return jnp.where(u < 3, u, c + u - 3), jnp.where(u < 3, 2 * c, 1)


def sends(u, c):
    return (u != 3) | (c == 0)


dma = pltpu.SemaphoreType.DMA
ANY = pl.BlockSpec(memory_space=pl.ANY)
VMEM = pl.BlockSpec(memory_space=pltpu.VMEM)
HBM = pl.BlockSpec(memory_space=pltpu.HBM)
shape = jax.ShapeDtypeStruct

class Line:
    def __init__(self, n, own, slot, send, recv):
        self.n, self.own, self.slot, self.sems = n, own, slot, (send, recv)
        self.d = lax.axis_index("dp")

    def along(self, k):
        m = self.d if k == 0 else self.n - 1 - self.d
        to = {"dp": jnp.clip(self.d + 1 if k == 0 else self.d - 1, 0, self.n - 1)}
        return m, to

    def target(self, k, step):
        m, _ = self.along(k)
        return jnp.clip(self.n - step + m if k == 0 else step - 1 - m, 0, self.n - 1)

    def copy(self, k, step, src):
        send, recv = self.sems
        _, to = self.along(k)
        return pltpu.make_async_remote_copy(
            src, self.slot(k, step), send.at[k, step - 1], recv.at[k, step - 1], device_id=to
        )

    def arrive(self, k, step):
        self.copy(k, step, self.slot(k, step)).wait_recv()

    def start(self, step, add):
        for k in range(2):
            m, _ = self.along(k)
            if step > 1:

                @pl.when((m >= 1) & (m < self.n - 1) & (step >= m + 1))
                def _():
                    add(k, self.target(k, step))
                    self.copy(k, step, self.slot(k, step - 1)).start()

            @pl.when(m == 0)
            def _():
                self.copy(k, step, self.own(self.target(k, step))).start()

    def received(self, step):
        for k in range(2):
            m, _ = self.along(k)

            @pl.when((m >= 1) & (step >= m))
            def _():
                self.arrive(k, step)

    def sent(self, step):
        for k in range(2):
            m, _ = self.along(k)

            @pl.when((m < self.n - 1) & (step >= m + 1))
            def _():
                self.copy(k, step, self.slot(k, step)).wait_send()


def greet_line(n, d):
    barrier = pltpu.get_barrier_semaphore()

    @pl.when(d > 0)
    def _():
        pl.semaphore_signal(barrier, inc=1, device_id={"dp": jnp.maximum(d - 1, 0)})

    @pl.when(d < n - 1)
    def _():
        pl.semaphore_signal(barrier, inc=1, device_id={"dp": jnp.minimum(d + 1, n - 1)})


def greeted_line(n, d, peers):
    ends = jnp.where(d > 0, 1, 0) + jnp.where(d < n - 1, 1, 0)
    pl.semaphore_wait(pltpu.get_barrier_semaphore(), len(peers) + ends)


GAINS = 512


def project_kernel(
    n, tokens, packed, up, out_w, qkv, norm, w_t, up_all, out_all, gain_ref,
    tok, x, w, proj, tsend, trecv, tlocal, wsend, wrecv, wlocal, osend, orecv, olocal,
):
    c, t = place()
    d = lax.axis_index("dp")
    own = tokens.shape[1]
    width = tokens.shape[2]
    span = 4 * own
    shard = packed.shape[0]
    half = own // 2
    to_x, to_y, to_core = {"tensor": t ^ 1}, {"tensor": t ^ 2}, {"context": 1 - c}
    others = [{"dp": lax.rem(d + r, n)} for r in range(1, n)]
    peers = [to_x, to_y, to_core] + others
    greet(peers)

    def local(i, s):
        return pltpu.make_async_copy(tokens.at[s], tok.at[s, t], tlocal.at[i])

    def weights(j, r):
        source, target, sem = ((packed, w, 0), (out_w, out_all, 1), (up, up_all, 2))[j]
        rows = pl.ds(pl.multiple_of(d * shard, shard), shard)
        if r == 0:
            return pltpu.make_async_copy(source, target.at[rows], wlocal.at[sem])
        return pltpu.make_async_remote_copy(
            source, target.at[rows], wsend.at[sem, r - 1], wrecv.at[sem, r - 1], device_id=others[r - 1]
        )

    order = (2 * (1 - c), 1, 2 * c)
    for i, s in enumerate(order):
        local(i, s).start()
    for j in range(3):
        weights(j, 0).start()
    greeted(peers)
    for j in range(3):
        for r in range(1, n):
            weights(j, r).start()

    def hop(k, i):
        s = order[i]
        origin, rows, peer = (
            (t, slice(0, half), to_x),
            (t, slice(half, own), to_y),
            (t, slice(0, half), to_y),
            (t, slice(half, own), to_x),
            (t ^ 1, slice(0, half), to_y),
            (t ^ 2, slice(half, own), to_x),
        )[k]
        there = tok.at[s, origin, rows]
        here = tokens.at[s, rows] if k < 4 else there
        return pltpu.make_async_remote_copy(
            here, there, tsend.at[k, i], trecv.at[k, i], device_id=peer
        )

    def straight(i):
        for k in range(4):
            hop(k, i).start()

    def forward(i):
        for k in range(2):
            hop(k, i).wait_recv()
            hop(k + 4, i).start()

    units = proj.shape[1]

    def leave(i):
        out = []
        lanes = pl.ds(pl.multiple_of(c * span, span), span)
        if i != 0:
            out.append((x.at[i], norm.at[2 - i, lanes], False))
        if i != 2:
            out.append((x.at[i], norm.at[i, lanes], True))
        if i == 0:
            out.append((proj.at[0], qkv.at[pl.ds(0, units), :, lanes], True))
        if i == 2:
            out.append((proj.at[2], qkv.at[pl.ds(0, units), :, lanes], False))
        if i == 1:
            for away in (True, False):
                core = 1 - c if away else c
                for p in range(3):
                    src = proj.at[1, pl.ds(p * 3 + core, 2)]
                    out.append((src, qkv.at[pl.ds(units + 2 * p, 2), :, lanes], away))
        copies = []
        for j, (src, dst, away) in enumerate(out):
            if away:
                copies.append(
                    (away, pltpu.make_async_remote_copy(src, dst, osend.at[i, j], orecv.at[i, j], device_id=to_core))
                )
            else:
                copies.append((away, pltpu.make_async_copy(src, dst, olocal.at[i, j])))
        return copies

    def work(i):
        s = order[i]
        local(i, s).wait()
        for k in range(2, 6):
            hop(k, i).wait_recv()
        for p in range(4):
            v = tok[s, p].astype(full)
            inv = lax.rsqrt(jnp.mean(v * v, axis=-1, keepdims=True) + epsilon)
            x[i, p * own : (p + 1) * own, :] = (v * inv * gain_ref[0:1, :]).astype(low)
        for p in range(4):
            rows = slice(p * own, (p + 1) * own)
            part = nt(w_t[...], x[i, rows, :]).astype(low)
            proj[i, :, :, rows] = part.reshape(units, HD, own)
        for _, copy in leave(i):
            copy.start()

    straight(0)
    straight(1)
    forward(0)
    straight(2)
    weights(0, 0).wait()
    for r in range(1, n):
        weights(0, r).wait_recv()
    w_t[...] = w[:, : units * HD].T
    gain_ref[...] = w[:, GAINS : GAINS + 128].astype(full).T[64:72]
    forward(1)
    work(0)
    forward(2)
    work(1)
    work(2)
    for j in range(3):
        if j:
            weights(j, 0).wait()
        for r in range(1, n):
            weights(j, r).wait_send()
            if j:
                weights(j, r).wait_recv()
    for i in range(3):
        for k in range(6):
            hop(k, i).wait_send()
        for away, copy in leave(i):
            copy.wait()


def project(n, tokens, packed, up, out_w):
    sequences, own, width = tokens.shape
    shard, columns = packed.shape
    span = 4 * own
    return pl.pallas_call(
        functools.partial(project_kernel, n),
        in_specs=[ANY] * 4,
        out_specs=[HBM] * 2 + [VMEM] + [HBM] * 2 + [VMEM],
        out_shape=[
            shape((15, HD, 2 * span), low),
            shape((2, 2 * span, width), low),
            shape((9 * HD, n * shard), low),
            shape((n * shard, up.shape[1]), low),
            shape((n * shard, out_w.shape[1]), low),
            shape((8, n * shard), full),
        ],
        scratch_shapes=[
            pltpu.VMEM((sequences, 4, own, width), low),
            pltpu.VMEM((sequences, span, width), low),
            pltpu.VMEM((n * shard, columns), low),
            pltpu.VMEM((sequences, 9, HD, span), low),
            dma((6, 3)), dma((6, 3)), dma((3,)),
            dma((3, n - 1)), dma((3, n - 1)), dma((3,)),
            dma((3, 8)), dma((3, 8)), dma((3, 8)),
        ],
        compiler_params=pltpu.CompilerParams(
            vmem_limit_bytes=40 << 20, collective_id=3, has_side_effects=True
        ),
        name="project",
    )(tokens, packed, up, out_w)


UNITS = 5
def unit_block(part):
    return lambda u: (jnp.where(u < 3, part * 3 + u, 9 + part * 2 + (u - 3)), 0, 0)


def attend_kernel(
    n, q_ref, k_ref, v_ref, lo_ref, out_part, up_part, down_own, att, lse_ref, of_ref, up, down, out_w,
    qs, ks, ss, obuf, ssem, rsem, lsem, wsend, wrecv, wlocal, zsend, zrecv, fsend, frecv,
):
    u = pl.program_id(0)
    c, t = place()
    d = lax.axis_index("dp")
    shard = down_own.shape[0]
    peers = [at_peer(c, t, dc, r) for dc, r in PEERS[1:]]

    part = out_part.shape[0] // 2
    mine = pl.ds(pl.multiple_of(c * part, part), part)

    def weight(j, r):
        rows = pl.ds(pl.multiple_of(d * shard, shard), shard)
        src, dst = (
            (down_own, down.at[t, rows]),
            (up_part, up.at[t]),
            (out_part.at[mine], out_w.at[t, mine]),
        )[j]
        if r == 0:
            return pltpu.make_async_copy(src, dst, wlocal.at[j])
        return pltpu.make_async_remote_copy(
            src, dst, wsend.at[j, r - 1], wrecv.at[j, r - 1], device_id={"tensor": t ^ r}
        )

    def onward(k):
        if k == 2:
            ref, peer = out_w.at[:, mine], {"context": 1 - c}
        else:
            rows = pl.ds(k * part, part)
            ref, peer = up.at[t ^ (1 + k), rows], {"tensor": t ^ (2 - k)}
        return pltpu.make_async_remote_copy(
            ref, ref, fsend.at[k], frecv.at[k], device_id=peer
        )

    def shards(step, up_line):
        src = d - step if up_line else d + step
        rows = pl.ds(pl.multiple_of(jnp.clip(src, 0, n - 1) * shard, shard), shard)
        to = jnp.clip(d + 1 if up_line else d - 1, 0, n - 1)
        k = 0 if up_line else 1
        return pltpu.make_async_remote_copy(
            down.at[:, rows], down.at[:, rows], zsend.at[k, step], zrecv.at[k, step], device_id={"dp": to}
        )

    def line(step, what):
        for up_line in (True, False):
            inside = (d < n - 1) if up_line else (d > 0)
            has = (d >= step) if up_line else (d <= n - 1 - step)
            comes = (d >= step + 1) if up_line else (d <= n - 2 - step)
            if what == "recv":

                @pl.when(comes)
                def _():
                    shards(step, up_line).wait_recv()
            else:

                @pl.when(inside & has)
                def _():
                    if what == "start":
                        shards(step, up_line).start()
                    else:
                        shards(step, up_line).wait_send()
    length = lo_ref.shape[2]
    half = length // 2
    own = half // 4

    @pl.when(u == 0)
    def _():
        greet(peers)
        greet_line(n, d)
        for j in range(3):
            weight(j, 0).start()
        greeted_line(n, d, peers)
        for r in range(1, 4):
            weight(0, r).start()

    qs[...] = q_ref[0] * low(0.125)
    ks[...] = k_ref[0].T
    for start in range(0, length, QB):
        stop = start + QB
        q = qs[:, start:stop]
        lo = lo_ref[0, :, start:stop]
        first = max(0, start - WIN)
        most = jnp.full((8, QB), NEG, full)
        for at in range(first, stop, CHUNK):
            s = nn(ks[at : at + CHUNK, :], q)
            key_pos = at + lax.broadcasted_iota(jnp.int32, (CHUNK, QB), 0)
            allowed = key_pos >= lo
            if at + CHUNK - 1 > start:
                allowed &= key_pos <= start + lax.broadcasted_iota(jnp.int32, (CHUNK, QB), 1)
            s = jnp.where(allowed, s, NEG)
            ss[at - first : at - first + CHUNK, :] = s
            most = jnp.maximum(most, jnp.max(s.reshape(CHUNK // 8, 8, QB), axis=0))
        most = jnp.max(most, axis=0, keepdims=True)
        total = jnp.zeros((8, QB), full)
        acc = jnp.zeros((HD, QB), full)
        for at in range(first, stop, CHUNK):
            p = jnp.exp(ss[at - first : at - first + CHUNK, :] - most)
            total += jnp.sum(p.reshape(CHUNK // 8, 8, QB), axis=0)
            acc += nn(v_ref[0, :, at : at + CHUNK], p.astype(low))
        total = jnp.sum(total, axis=0, keepdims=True)
        lse_ref[0, :, start:stop] = most + jnp.log(total)
        o = acc * (1.0 / total)
        of_ref[0, :, start:stop] = o
        obuf[u, :, start:stop] = o.astype(low)

    @pl.when(u == 0)
    def _():
        weight(0, 0).wait()
        for r in range(1, 4):
            weight(0, r).wait_recv()
        line(0, "start")
        for j, count in ((1, 3), (2, 4)):
            for r in range(1, count):
                weight(j, r).start()

    @pl.when(u == 3)
    def _():
        if n > 2:
            line(0, "recv")
            line(1, "start")
        for k in range(2):
            weight(1, 1 + k).wait_recv()
            onward(k).start()
        weight(2, 0).wait()
        for r in range(1, 4):
            weight(2, r).wait_recv()
        onward(2).start()

    def move(unit, i, source_core):
        dc, r = PEERS[i]
        h, seq = unit_place(unit, source_core)
        dest = pl.multiple_of(((c ^ dc) * 4 + (t ^ r)) * own, own)
        src = obuf.at[unit, :, pl.ds(dest, own)]
        dst = att.at[
            pl.ds(pl.multiple_of((t * 3 + h) * HD, HD), HD), pl.ds(pl.multiple_of(seq * own, own), own)
        ]
        if i == 0:
            return pltpu.make_async_copy(src, dst, lsem.at[unit])
        return pltpu.make_async_remote_copy(
            src, dst, ssem.at[i - 1, unit], rsem.at[i - 1, unit], device_id=at_peer(c, t, dc, r)
        )

    @pl.when(sends(u, c))
    def _():
        for i in range(1, len(PEERS)):
            move(u, i, c).start()
        move(u, 0, c).start()

    @pl.when(u == pl.num_programs(0) - 1)
    def _():
        for step in range(2, n - 1):
            line(step - 1, "recv")
            line(step, "start")
        line(n - 2, "recv")
        for step in range(n - 1):
            line(step, "sent")
        weight(1, 0).wait()
        for j in range(3):
            for r in range(1, 3 if j == 1 else 4):
                weight(j, r).wait_send()
        for k in range(3):
            onward(k).wait()
        for unit in range(UNITS):
            for i, (dc, r) in enumerate(PEERS):

                @pl.when(sends(unit, c))
                def _():
                    if i:
                        move(unit, i, c).wait_send()
                    else:
                        move(unit, i, c).wait()

                if i:

                    @pl.when(sends(unit, c ^ dc))
                    def _():
                        move(unit, i, c ^ dc).wait_recv()


def attend(n, qkv, lo, out_part, up_part, down_own):
    length = lo.shape[2]
    half = length // 2
    own = half // 4
    width, hidden = up_part.shape
    part = lambda p: pl.BlockSpec((1, HD, length), unit_block(p))
    unit = lambda rows, n: pl.BlockSpec((1, rows, n), lambda u: (u, 0, 0))
    heads = 4 * 3 * HD
    return pl.pallas_call(
        functools.partial(attend_kernel, n),
        grid=(UNITS,),
        in_specs=[part(0), part(1), part(2)]
        + [pl.BlockSpec((1, 1, length), lambda u: (u // 3, 0, 0))]
        + [ANY] * 3,
        out_specs=[HBM, unit(1, length), unit(HD, length)] + [HBM] * 3,
        scratch_shapes=[
            pltpu.VMEM((HD, length), low),
            pltpu.VMEM((length, HD), low),
            pltpu.VMEM((WIN + QB, QB), full),
            pltpu.VMEM((UNITS, HD, length), low),
            dma((7, UNITS)),
            dma((7, UNITS)),
            dma((UNITS,)),
            dma((3, 3)),
            dma((3, 3)),
            dma((3,)),
            dma((2, n - 1)),
            dma((2, n - 1)),
            dma((3,)),
            dma((3,)),
        ],
        out_shape=[
            jax.ShapeDtypeStruct((heads, 3 * own), low),
            jax.ShapeDtypeStruct((UNITS, 1, length), full),
            jax.ShapeDtypeStruct((UNITS, HD, length), full),
            shape((4, width, hidden), low),
            shape((4, width, hidden), low),
            shape((4,) + out_part.shape, low),
        ],
        compiler_params=pltpu.CompilerParams(
            vmem_limit_bytes=40 << 20, collective_id=1, has_side_effects=True
        ),
        cost_estimate=pl.CostEstimate(
            flops=UNITS * 18 * 2 * 256 * 1024 * 128, bytes_accessed=20 << 20, transcendentals=0
        ),
        name="attend",
    )(qkv, qkv, qkv, lo, out_part, up_part, down_own)


def add_to(ref, terms):
    for a in range(ref.shape[0]):
        for p in range(ref.shape[1]):
            ref[a, p] = (ref[a, p].astype(full) + terms(a, p).astype(full)).astype(low)


def attend_back_kernel(
    n, q_ref, k_ref, v_ref, lo_ref, lse_ref, of_ref, norm_ref, g_ref, gud, part_sum, gout,
    dall, gw_sum, zsum, osum,
    qs, ks, vs, grow, qrow, delta, dqs, dbuf, gw, gwx, gwr, zr, gud_v, obuf, ssem, rsem, lsem,
    zsend, zrecv, xsend, xrecv, osend, orecv, olocal, vlocal,
):
    u = pl.program_id(0)
    c, t = place()
    d = lax.axis_index("dp")
    shard = gud.shape[2] // n
    length = lo_ref.shape[2]
    own = length // 8
    peers = [at_peer(c, t, dc, r) for dc, r in PEERS[1:]]

    def rows_of(j):
        return pl.ds(pl.multiple_of(j * shard, shard), shard)

    def line_of(h):
        pair = pl.ds(2 * h, 2)
        return Line(
            n,
            lambda j: gud.at[:, pair, rows_of(j)],
            lambda k, step: zr.at[h, k, step - 1],
            zsend.at[h],
            zrecv.at[h],
        )

    lines = [line_of(0), line_of(1)]

    def step_of(h, step, arrived=True):
        if arrived and step > 1:
            lines[h].received(step - 1)

        def add(k, j):
            rows = rows_of(j)
            add_to(zr.at[h, k, step - 2], lambda a, p: gud_v[a, 2 * h + p, rows])

        lines[h].start(step, add)

    def finish(h):
        lines[h].received(n - 1)
        for step in range(3 if h == 0 else 1, n):
            lines[h].sent(step)
        for a in range(2):
            for p in range(2):
                total = gud_v[a, 2 * h + p, rows_of(d)].astype(full)
                up, down = (zr[h, k, n - 2, a, p].astype(full) for k in range(2))
                total += jnp.where(d > 0, up, 0.0) + jnp.where(d < n - 1, down, 0.0)
                zsum[a, 2 * h + p] = total.astype(low)

    part_rows = gout.shape[1] // 2

    def out_piece(i):
        dc, r = PEERS[i]
        src = gout.at[t ^ r, pl.ds(pl.multiple_of((c ^ dc) * part_rows, part_rows), part_rows)]
        if i == 0:
            return pltpu.make_async_copy(src, obuf.at[0], olocal)
        return pltpu.make_async_remote_copy(
            src, obuf.at[i], osend.at[i - 1], orecv.at[i - 1], device_id=at_peer(c, t, dc, r)
        )

    def other_core():
        return pltpu.make_async_remote_copy(
            gwx.at[1 - c], gwr, xsend, xrecv, device_id={"context": 1 - c}
        )

    def load(i):
        if i == 2:
            return pltpu.make_async_copy(gud, gud_v, vlocal.at[2])
        return pltpu.make_async_copy(part_sum.at[i], zr.at[0, i, 1], vlocal.at[i])

    @pl.when(u == 0)
    def _():
        greet(peers)
        greet_line(n, d)
        for i in range(3):
            load(i).start()
        gw[...] = jnp.zeros_like(gw)
        greeted_line(n, d, peers)
        for i in range(3):
            load(i).wait()
        step_of(0, 3, False)
        step_of(1, 1)
        for i in range(1, len(PEERS)):
            out_piece(i).start()
        out_piece(0).start()

    @pl.when(u == 3)
    def _():
        step_of(1, 2)

    @pl.when(u == 4)
    def _():
        step_of(1, 3)

    qs[...] = q_ref[0] * low(0.125)
    ks[...] = k_ref[0].T
    vs[...] = v_ref[0].T
    grow[...] = g_ref[0].T
    qrow[...] = qs[...].T
    delta[...] = jnp.sum(g_ref[0].astype(full) * of_ref[0], axis=0, keepdims=True)
    dqs[...] = jnp.zeros_like(dqs)
    for key_start in range(0, length, QB):
        rows = slice(key_start, key_start + QB)
        k, v, key_t = ks[rows, :], vs[rows, :], k_ref[0, :, rows]
        dk = jnp.zeros((QB, HD), full)
        dv = jnp.zeros((QB, HD), full)
        key_pos = key_start + lax.broadcasted_iota(jnp.int32, (QB, QB), 0)
        for start in range(key_start, min(key_start + WIN + QB, length), QB):
            cols = slice(start, start + QB)
            s = nn(k, qs[:, cols]) - lse_ref[0, :, cols]
            allowed = key_pos >= lo_ref[0, :, cols]
            if start == key_start:
                allowed &= key_pos <= start + lax.broadcasted_iota(jnp.int32, (QB, QB), 1)
            p = jnp.exp(jnp.where(allowed, s, NEG))
            dp = nn(v, g_ref[0, :, cols])
            ds = (p * (dp - delta[:, cols])).astype(low)
            dv += nn(p.astype(low), grow[cols, :])
            dk += nn(ds, qrow[cols, :])
            dqs[:, cols] += nn(key_t, ds)
        dbuf[u, 1, :, rows] = dk.T.astype(low)
        dbuf[u, 2, :, rows] = dv.T.astype(low)
    dbuf[u, 0] = (dqs[...] * 0.125).astype(low)

    def move(unit, i, source_core):
        dc, r = PEERS[i]
        h, seq = unit_place(unit, source_core)
        dest = pl.multiple_of(((c ^ dc) * 4 + (t ^ r)) * own, own)
        src = dbuf.at[unit, :, :, pl.ds(dest, own)]
        dst = dall.at[t, :, h, :, pl.ds(pl.multiple_of(seq * own, own), own)]
        if i == 0:
            return pltpu.make_async_copy(src, dst, lsem.at[unit])
        return pltpu.make_async_remote_copy(
            src, dst, ssem.at[i - 1, unit], rsem.at[i - 1, unit], device_id=at_peer(c, t, dc, r)
        )

    @pl.when(sends(u, c))
    def _():
        for i in range(1, len(PEERS)):
            move(u, i, c).start()
        move(u, 0, c).start()
        h, _ = unit_place(u, c)
        gw[h] += nn(dbuf[u].reshape(3 * HD, length), norm_ref[0])

    @pl.when(u == pl.num_programs(0) - 1)
    def _():
        wide_rows = [gw[h, p * HD : (p + 1) * HD, :] for p in range(3) for h in range(3)]
        gwx[0] = jnp.concatenate(wide_rows[:6], axis=0).T.astype(low)
        empty = jnp.zeros((3 * HD, gw.shape[2]), full)
        gwx[1] = jnp.concatenate(wide_rows[6:] + [empty], axis=0).T.astype(low)
        other_core().start()
        out_piece(0).wait()
        for i in range(1, len(PEERS)):
            out_piece(i).wait()
        total = obuf[0].astype(full)
        for i in range(1, len(PEERS)):
            total += obuf[i].astype(full)
        osum[...] = total.astype(low)
        other_core().wait()
        gw_sum[...] = (gwx[c].astype(full) + gwr[...].astype(full)).astype(low)
        for step in range(4, n):
            step_of(0, step)
            step_of(1, step)
        finish(0)
        finish(1)
        for unit in range(UNITS):
            for i, (dc, r) in enumerate(PEERS):

                @pl.when(sends(unit, c))
                def _():
                    if i:
                        move(unit, i, c).wait_send()
                    else:
                        move(unit, i, c).wait()

                if i:

                    @pl.when(sends(unit, c ^ dc))
                    def _():
                        move(unit, i, c ^ dc).wait_recv()


def attend_back(n, qkv, grad_units, lo, lse, attended, normed, grad_up_down, part_sum, grad_out):
    length = lo.shape[2]
    own = length // 8
    width = normed.shape[2]
    shard, hidden = grad_up_down.shape[2] // n, grad_up_down.shape[3]
    out_rows, local = grad_out.shape[1] // 2, grad_out.shape[2]
    part = lambda p: pl.BlockSpec((1, HD, length), unit_block(p))
    unit = lambda rows, m: pl.BlockSpec((1, rows, m), lambda u: (u, 0, 0))
    once = lambda dims: pl.BlockSpec(dims, lambda u: (0,) * len(dims), pipeline_mode=pl.Buffered(1))
    wide, tall = pltpu.VMEM((HD, length), low), pltpu.VMEM((length, HD), low)
    results = [(width, 2 * 3 * HD), (2, 4, shard, hidden), (out_rows, local)]
    return pl.pallas_call(
        functools.partial(attend_back_kernel, n),
        grid=(UNITS,),
        in_specs=[part(0), part(1), part(2)]
        + [
            pl.BlockSpec((1, 1, length), lambda u: (u // 3, 0, 0)),
            unit(1, length),
            unit(HD, length),
            pl.BlockSpec((1, length, width), lambda u: (u // 3, 0, 0)),
            unit(HD, length),
        ]
        + [HBM] * 3,
        out_specs=[HBM] + [once(r) for r in results],
        scratch_shapes=[
            wide, tall, tall, tall, tall,
            pltpu.VMEM((1, length), full), pltpu.VMEM((HD, length), full),
            pltpu.VMEM((UNITS, 3, HD, length), low), pltpu.VMEM((3, 3 * HD, width), full),
            pltpu.VMEM((2, width, 6 * HD), low), pltpu.VMEM((width, 6 * HD), low),
            pltpu.VMEM((2, 2, n - 1, 2, 2, shard, hidden), low), pltpu.VMEM(grad_up_down.shape, low),
            pltpu.VMEM((8, out_rows, local), low),
            dma((7, UNITS)), dma((7, UNITS)), dma((UNITS,)),
            dma((2, 2, n - 1)), dma((2, 2, n - 1)), dma, dma, dma((7,)), dma((7,)), dma, dma((3,)),
        ],
        out_shape=[shape((4, 3, 3, HD, 3 * own), low)] + [shape(r, low) for r in results],
        compiler_params=pltpu.CompilerParams(
            vmem_limit_bytes=62 << 20, collective_id=2, has_side_effects=True
        ),
        name="attend_back",
    )(qkv, qkv, qkv, lo, lse, attended, normed, grad_units, grad_up_down, part_sum, grad_out)


def last_kernel(
    n, dqkv_ref, w_ref, tokens_ref, middle_ref, gains, w_mine, up_mine, gain_mine, gw_sum, zsum, osum,
    grad_in, g_qkv, g_up, g_down, g_out, g_gain,
    rg, rw, ro, down_n, out_t, mine, sums, dqkv, w_all, tokens, middle,
    gsend, grecv, wsend, wrecv, osend, orecv, lsem, csend, crecv, ssend, srecv, clocal, fetch,
):
    c, t = place()
    d = lax.axis_index("dp")
    shard, hidden = rw.shape[2], rw.shape[3]
    cut = n // 2
    group = [at_peer(c, t, dc, r) for dc, r in PEERS[1:]]
    others = [lax.rem(d + r, n) for r in range(1, n)]
    peers = group + [{"dp": o} for o in others]
    greet(peers)
    loads = [
        pltpu.make_async_copy(src, dst, fetch.at[i])
        for i, (src, dst) in enumerate(
            ((tokens_ref, tokens), (w_ref, w_all), (dqkv_ref, dqkv), (middle_ref, middle))
        )
    ]
    for copy in loads:
        copy.start()

    def rows_of(j):
        return pl.ds(pl.multiple_of(j * shard, shard), shard)

    narrow = slice(0, 256)

    def qkv_piece(r, core):
        src, dst = gw_sum.at[rows_of(d if r == 0 else others[r - 1])], rg.at[r]
        if core:
            src, dst = src.at[:, narrow], dst.at[:, narrow]
        if r == 0:
            return pltpu.make_async_copy(src, dst, lsem.at[0])
        return pltpu.make_async_remote_copy(
            src, dst, gsend.at[r - 1], grecv.at[r - 1], device_id={"dp": others[r - 1]}
        )

    def each_core(what):
        for core in range(2):

            @pl.when(c == core)
            def _():
                what(core)

    def up_piece(r):
        src, dst = zsum.at[:, t ^ r], rw.at[r]
        if r == 0:
            return pltpu.make_async_copy(src, dst, lsem.at[1])
        return pltpu.make_async_remote_copy(
            src, dst, wsend.at[r - 1], wrecv.at[r - 1], device_id={"tensor": t ^ r}
        )

    mine_out = d // cut == c

    def out_piece(r):
        to = d if r == 0 else others[r - 1]
        src, dst = osum.at[rows_of(lax.rem(to, cut))], ro.at[r]
        if r == 0:
            return pltpu.make_async_copy(src, dst, lsem.at[2])
        return pltpu.make_async_remote_copy(
            src, dst, osend.at[r - 1], orecv.at[r - 1], device_id={"dp": to}
        )

    def start_all(core):
        for r in range(1, n):
            qkv_piece(r, core).start()
        qkv_piece(0, core).start()

    greeted(peers)
    each_core(start_all)
    for r in range(1, 4):
        up_piece(r).start()
    up_piece(0).start()
    for r in range(1, n):

        @pl.when(others[r - 1] // cut == c)
        def _():
            out_piece(r).start()

    @pl.when(mine_out)
    def _():
        out_piece(0).start()

    for copy in loads:
        copy.wait()
    for m in range(0, tokens.shape[0], QB):
        rows = slice(m, m + QB)
        r = tn(dqkv[:, rows], w_all[...])
        v = tokens[rows, :].astype(full)
        inv = lax.rsqrt(jnp.mean(v * v, axis=-1, keepdims=True) + epsilon)
        rg_ = r * gains[0:1, :]
        grad = inv * (rg_ - v * (inv * inv * jnp.mean(rg_ * v, axis=-1, keepdims=True)))
        grad_in[rows, :] = (middle[rows, :] + grad).astype(low)

    def halves(j):
        half = pl.ds(pl.multiple_of(c * hidden, hidden), hidden)
        src, dst = (
            (mine.at[0], g_qkv.at[:, half]),
            (mine.at[1], g_up.at[:, half]),
            (down_n, g_down.at[:, half]),
            (out_t, g_out),
        )[j]
        return (
            pltpu.make_async_copy(src, dst, clocal.at[j]),
            pltpu.make_async_remote_copy(
                src, dst, csend.at[j], crecv.at[j], device_id={"context": 1 - c}
            ),
        )

    def deliver(j):
        for copy in halves(j):
            copy.start()

    up_piece(0).wait()
    for r in range(1, 4):
        up_piece(r).wait_recv()
    mine[1] = sum(rw[r, 0].astype(full) for r in range(4))
    down_n[...] = sum(rw[r, 1].astype(full) for r in range(4))
    deliver(1)
    deliver(2)

    @pl.when(mine_out)
    def _():
        out_piece(0).wait()
        for r in range(1, n):
            out_piece(r).wait_recv()
        out_t[...] = sum(ro[r].astype(full) for r in range(n)).T
        deliver(3)

    def take(core):
        qkv_piece(0, core).wait()
        for r in range(1, n):
            qkv_piece(r, core).wait_recv()
        if core:
            mine[0, :, narrow] = sum(rg[r, :, narrow].astype(full) for r in range(n))
            mine[0, :, 256:] = jnp.zeros((shard, hidden - 256), full)
        else:
            mine[0] = sum(rg[r].astype(full) for r in range(n))

    each_core(take)
    deliver(0)
    lane = lax.broadcasted_iota(jnp.int32, (shard, 128), 1)
    first = jnp.sum(w_mine[...].astype(full) * mine[0], axis=1, keepdims=True)
    second = jnp.sum(up_mine[...].astype(full) * mine[1], axis=1, keepdims=True)
    sums[0] = jnp.where(lane == 0, first, jnp.where(lane == 1, second, 0.0))

    def gain_piece(i):
        dc, r = PEERS[i]
        return pltpu.make_async_remote_copy(
            sums.at[0], sums.at[i], ssend.at[i - 1], srecv.at[i - 1], device_id=at_peer(c, t, dc, r)
        )

    for i in range(1, len(PEERS)):
        gain_piece(i).start()
    for i in range(1, len(PEERS)):
        gain_piece(i).wait()
    total = sum(sums[i] for i in range(len(PEERS)))
    g_gain[...] = total / jnp.where(lane < 2, gain_mine[...].astype(full), 1.0)

    for j in range(3):
        for copy in halves(j):
            copy.wait()

    @pl.when(mine_out)
    def _():
        local, away = halves(3)
        local.wait()
        away.wait_send()

    @pl.when(jnp.logical_not(mine_out))
    def _():
        halves(3)[1].wait_recv()

    for r in range(1, 4):
        up_piece(r).wait_send()

    def sent(core):
        for r in range(1, n):
            qkv_piece(r, core).wait_send()

    each_core(sent)
    for r in range(1, n):

        @pl.when(others[r - 1] // cut == c)
        def _():
            out_piece(r).wait_send()


def last(n, dqkv, w_all, tokens, middle, gains, w_mine, up_mine, gain_mine, gw_sum, zsum, osum):
    rows, width = tokens.shape
    _, _, shard, hidden = zsum.shape
    local = osum.shape[1]
    return pl.pallas_call(
        functools.partial(last_kernel, n),
        in_specs=[HBM] * 4 + [VMEM] * 4 + [ANY] * 3,
        out_specs=[VMEM] + [ANY] * 4 + [VMEM],
        out_shape=[
            shape((rows, width), low),
            shape((shard, 2 * hidden), full),
            shape((shard, 2 * hidden), full),
            shape((shard, 2 * hidden), full),
            shape((local, shard), full),
            shape((shard, 128), full),
        ],
        scratch_shapes=[
            pltpu.VMEM((n, shard, hidden), low),
            pltpu.VMEM((4, 2, shard, hidden), low),
            pltpu.VMEM((n, shard, local), low),
            pltpu.VMEM((shard, hidden), full),
            pltpu.VMEM((local, shard), full),
            pltpu.VMEM((2, shard, hidden), full),
            pltpu.VMEM((8, shard, 128), full),
            pltpu.VMEM(dqkv.shape, low), pltpu.VMEM(w_all.shape, low),
            pltpu.VMEM((rows, width), low), pltpu.VMEM((rows, width), full),
            dma((n - 1,)), dma((n - 1,)), dma((3,)), dma((3,)), dma((n - 1,)), dma((n - 1,)), dma((3,)),
            dma((4,)), dma((4,)), dma((7,)), dma((7,)), dma((4,)), dma((4,)),
        ],
        compiler_params=pltpu.CompilerParams(
            vmem_limit_bytes=50 << 20, collective_id=4, has_side_effects=True
        ),
        name="last",
    )(dqkv, w_all, tokens, middle, gains, w_mine, up_mine, gain_mine, gw_sum, zsum, osum)


def close_kernel(*refs):
    count = (len(refs) - 1) // 2
    sems = refs[-1]
    copies = []
    for i, (src, dst) in enumerate(zip(refs[:count], refs[count : 2 * count])):
        copies.append(pltpu.make_async_copy(src, dst, sems.at[i]))
    for copy in copies:
        copy.start()
    for copy in copies:
        copy.wait()


def close(*arrays):
    return pl.pallas_call(
        close_kernel,
        in_specs=[ANY] * len(arrays),
        out_specs=[HBM] * len(arrays),
        out_shape=[shape(a.shape, a.dtype) for a in arrays],
        scratch_shapes=[dma((len(arrays),))],
        name="close",
    )(*arrays)


def gelu_and_slope(v):
    k0 = math.sqrt(2.0 / math.pi)
    square = v * v
    th = jnp.tanh(v * (k0 + (k0 * 0.044715) * square))
    half = 0.5 + 0.5 * th
    slope = half + (v * half) * ((1.0 - th) * (k0 + (3.0 * 0.044715 * k0) * square))
    return v * half, slope


def feed_kernel(
    dp, att, proj, tokens, cot, gains, w_t, up_ref, down_ref,
    result, middle, gout, gud, part_sum, units, w_all,
    x, g, x_t, g_t, up, down, act, gh, out, back, pre, ga, proj_w, sent, got, gbuf, zr, gatt,
    xsend, xrecv, wsend, wrecv, wlocal, zsend, zrecv, glocal, usend, urecv, ulocal,
):
    j = pl.program_id(0)
    c, t = place()
    d = lax.axis_index("dp")
    own = tokens.shape[0] // 3
    shard = tokens.shape[1] // dp
    rows, width = tokens.shape
    n = up_ref.shape[2]
    local = proj.shape[2]
    blocks = 2 * rows // QB
    other = {"context": 1 - c}
    peers = [at_peer(c, t, dc, r) for dc, r in PEERS[1:]]
    mine, theirs = slice(0, rows), slice(rows, 2 * rows)

    def cross(k):
        src, dst = (
            (cot, g.at[theirs]),
            (x.at[mine], x.at[theirs]),
            (sent.at[0], got.at[0]),
            (sent.at[1], got.at[1]),
        )[k]
        return pltpu.make_async_remote_copy(src, dst, xsend.at[k], xrecv.at[k], device_id=other)

    def over_tensor(r):
        if r == 0:
            return pltpu.make_async_copy(w_t, w_all.at[t], wlocal)
        return pltpu.make_async_remote_copy(
            w_t, w_all.at[t], wsend.at[r - 1], wrecv.at[r - 1], device_id={"tensor": t ^ r}
        )

    def rows_of(i):
        return pl.ds(pl.multiple_of(i * shard, shard), shard)

    line = Line(
        dp,
        lambda i: gbuf.at[0, :, :, rows_of(i)],
        lambda k, step: zr.at[k] if step == 1 else part_sum.at[k],
        zsend,
        zrecv,
    )

    def keep(half):
        return pltpu.make_async_copy(
            gbuf.at[half], gud.at[:, pl.ds(2 * half, 2)], glocal.at[half]
        )

    def leave(whole, i):
        dc, r = PEERS[i]
        to_c, to_t = c ^ dc, t ^ r
        head = to_t * 3 + (0 if whole else to_c)
        count, first = (3, 0) if whole else (2, 3)
        seq = 2 * to_c if whole else 1
        src = gatt.at[pl.ds(head, count), :, pl.ds(pl.multiple_of(seq * own, own), own)]
        dst = units.at[pl.ds(first, count), :, pl.ds(pl.multiple_of((c * 4 + t) * own, own), own)]
        k = 0 if whole else 1
        if i == 0:
            return pltpu.make_async_copy(src, dst, ulocal.at[k])
        return pltpu.make_async_remote_copy(
            src, dst, usend.at[k, i - 1], urecv.at[k, i - 1], device_id=at_peer(c, t, dc, r)
        )

    @pl.when(j == 0)
    def _():
        greet(peers)
        greet_line(dp, d)
        for p in range(4):
            proj_w[:, p * local : (p + 1) * local] = proj[p]
        greeted_line(dp, d, peers)
        cross(0).start()
        for r in range(1, 4):
            over_tensor(r).start()
        over_tensor(0).start()
        g[mine, :] = cot[...]
        g_t[:, mine] = cot[...].T
        for m in range(0, rows, QB):
            part = slice(m, m + QB)
            v = tokens[part, :].astype(full) + nn(proj_w[...], att[:, part]).T
            middle[part, :] = v
            inv = lax.rsqrt(jnp.mean(v * v, axis=-1, keepdims=True) + epsilon)
            x[part, :] = (v * inv * gains[1:2, :]).astype(low)
        cross(1).start()
        x_t[:, mine] = x[mine, :].T
        out[...] = jnp.zeros_like(out)
        back[...] = jnp.zeros_like(back)

    @pl.when(j == 1)
    def _():
        line.start(1, None)

    for i in range(2):
        up[:, i * n : (i + 1) * n] = up_ref[i]
        down[:, i * n : (i + 1) * n] = down_ref[i]

    def first(i):
        part = slice(i * QB, (i + 1) * QB)
        pre[i % 2] = nn(x[part, :], up[...])
        ga[i % 2] = nn(g[part, :], down[...])

    def second(i):
        part = slice(i * QB, (i + 1) * QB)
        a, slope = gelu_and_slope(pre[i % 2])
        act[part, :] = a.astype(low)
        gh[part, :] = (ga[i % 2] * slope).astype(low)

    def third(i):
        part = slice(i * QB, (i + 1) * QB)
        out[part, :] += nt(act[part, :], down[...])
        back[part, :] += nt(gh[part, :], up[...])

    first(0)
    for i in range(blocks):
        if i + 1 == blocks // 2:

            @pl.when(j == 0)
            def _():
                cross(0).wait_recv()
                cross(1).wait_recv()
                x_t[:, theirs] = x[theirs, :].T
                g_t[:, theirs] = g[theirs, :].T

        if i + 1 < blocks:
            first(i + 1)
        second(i)
        if i > 0:
            third(i - 1)
    third(blocks - 1)

    @pl.when(j == pl.num_programs(0) - 1)
    def _():
        sent[0] = back[theirs, :].astype(low)
        cross(2).start()
        sent[1] = out[theirs, :].astype(low)
        cross(3).start()

    def weight_grad(a, left_t, right):
        for m in range(0, width, QB):
            part = slice(m, m + QB)
            grad = nn(left_t[part, :], right[...]).astype(low)
            for i in range(2):
                gbuf[j, a, i, part, :] = grad[:, i * n : (i + 1) * n]

    weight_grad(1, g_t, act)

    @pl.when(j == 0)
    def _():
        weight_grad(0, x_t, gh)
        keep(0).start()

    @pl.when(j == 1)
    def _():
        line.received(1)
        line.start(2, lambda k, i: add_to(zr.at[k], lambda a, p: gbuf[0, a, p, rows_of(i)]))
        cross(2).wait_recv()
        gain = gains[1:2, :]
        for m in range(0, rows, QB):
            part = slice(m, m + QB)
            r = (back[part, :] + got[0, part, :].astype(full)) * gain
            v = middle[part, :]
            inv = lax.rsqrt(jnp.mean(v * v, axis=-1, keepdims=True) + epsilon)
            grad = inv * (r - v * (inv * inv * jnp.mean(r * v, axis=-1, keepdims=True)))
            back[part, :] = cot[part, :].astype(full) + grad
            g_t[:, part] = back[part, :].astype(low).T
        for m in range(0, rows, QB):
            part = slice(m, m + QB)
            grad = tn(proj_w[...], g_t[:, part]).astype(low)
            gatt[:, :, part] = grad.reshape(gatt.shape[0], HD, QB)
        for whole in (True, False):
            for i in range(1, len(PEERS)):
                leave(whole, i).start()
            leave(whole, 0).start()
        weight_grad(0, x_t, gh)
        keep(1).start()
        for m in range(0, width, QB):
            part = slice(m, m + QB)
            big = nt(g_t[part, mine], att[...]).astype(low)
            for p in range(4):
                gout[p, part, :] = big[:, p * local : (p + 1) * local]
        cross(3).wait_recv()
        result[...] = (middle[...] + out[mine, :] + got[1].astype(full)).astype(low)
        middle[...] = back[mine, :]
        for k in range(4):
            cross(k).wait_send()
        over_tensor(0).wait()
        for r in range(1, 4):
            over_tensor(r).wait()
        line.received(2)
        line.sent(1)
        line.sent(2)
        for half in range(2):
            keep(half).wait()
        for whole in (True, False):
            for i in range(len(PEERS)):
                leave(whole, i).wait()


def feed(dp, att, proj, tokens, cot, gains, w_t, up, down):
    rows, width = tokens.shape
    pieces, _, n = up.shape
    own = rows // 3
    assert pieces == 4 and dp > 2
    whole = lambda dims: pl.BlockSpec(dims, lambda j: (0,) * len(dims), pipeline_mode=pl.Buffered(1))
    weight = pl.BlockSpec((2, width, n), lambda j: (j, 0, 0))
    return pl.pallas_call(
        functools.partial(feed_kernel, dp),
        grid=(2,),
        in_specs=[whole(a.shape) for a in (att, proj, tokens, cot, gains)] + [HBM] + [weight] * 2,
        out_specs=[whole((rows, width))] * 2 + [whole(proj.shape)] + [HBM] * 4,
        out_shape=[
            shape((rows, width), low),
            shape((rows, width), full),
            shape(proj.shape, low),
            shape((2,) + up.shape, low),
            shape((2, 2, 2, width // dp, n), low),
            shape((UNITS, HD, 8 * own), low),
            shape((4,) + w_t.shape, low),
        ],
        scratch_shapes=[pltpu.VMEM((2 * rows, width), low)] * 2
        + [pltpu.VMEM((width, 2 * rows), low)] * 2
        + [pltpu.VMEM((width, 2 * n), low)] * 2
        + [pltpu.VMEM((2 * rows, 2 * n), low)] * 2
        + [pltpu.VMEM((2 * rows, width), full)] * 2
        + [pltpu.VMEM((2, QB, 2 * n), full)] * 2
        + [pltpu.VMEM((width, width), low)]
        + [pltpu.VMEM((2, rows, width), low)] * 2
        + [pltpu.VMEM((2, 2, 2, width, n), low), pltpu.VMEM((2, 2, 2, width // dp, n), low)]
        + [pltpu.VMEM((12, HD, rows), low)]
        + [dma((4,)), dma((4,)), dma((3,)), dma((3,)), dma]
        + [dma((2, 2)), dma((2, 2)), dma((2,)), dma((2, 7)), dma((2, 7)), dma((2,))],
        compiler_params=pltpu.CompilerParams(
            vmem_limit_bytes=63 << 20, collective_id=5, has_side_effects=True
        ),
        name="feed",
    )(att, proj, tokens, cot, gains, w_t, up, down)


def per_device(tokens, segments, w_qkv, w_out, w_in, w_back, gain_attn, gain_mlp, cotangent):
    sequences, own, width = tokens.shape
    assert lax.axis_size("tensor") == 4 and lax.axis_size("context") == 2 and sequences == 3
    c, t, d = lax.axis_index("context"), lax.axis_index("tensor"), lax.axis_index("dp")
    span = 4 * own
    length = segments.shape[1]
    shard = w_qkv.shape[0]
    local = w_qkv.shape[2]
    heads = local // HD
    hidden = w_in.shape[1] // 2
    rows = sequences * own

    up_own = lax.dynamic_slice_in_dim(w_in, c * hidden, hidden, 1)
    down_own = lax.dynamic_slice_in_dim(w_back, c * hidden, hidden, 0).T
    pad = jnp.zeros((shard, 62), low)
    packed = [w_qkv.reshape(shard, 3 * local), gain_attn[:, None], gain_mlp[:, None], pad]
    packed = jnp.concatenate(packed, axis=1)
    n = lax.axis_size("dp")
    qkv, normed_units, w_t, up_part, out_part, gains = project(n, tokens, packed, up_own, w_out.T)

    lo = jnp.zeros((sequences, length), jnp.int32)
    for value in range(8):
        before = jnp.sum((segments < value).astype(jnp.int32), axis=1, keepdims=True)
        lo = jnp.where(segments == value, before, lo)
    lo = jnp.maximum(lo, jnp.arange(length, dtype=jnp.int32)[None] - (WIN - 1))
    lo = jnp.stack([jnp.where(c == 0, lo[0], lo[2]), lo[1]])[:, None]

    attended, log_totals, out_full, w_up, w_down, w_proj = attend(
        n, qkv, lo, out_part, up_part, down_own
    )
    flat = tokens.reshape(rows, width)
    result, grad_middle, grad_out, grad_up_down, part_sum, grad_units, w_all = feed(
        n, attended, w_proj, flat, cotangent.reshape(rows, width), gains, w_t, w_up, w_down
    )
    grad_projected, gw_sum, zsum, osum = attend_back(
        n, qkv, grad_units, lo, log_totals, out_full, normed_units, grad_up_down, part_sum, grad_out
    )
    two = jnp.concatenate([packed[:, : 3 * local], jnp.zeros((shard, 4 * hidden), low)], axis=1)
    w_mine = lax.dynamic_slice_in_dim(two, c * hidden, hidden, 1)
    grad_input, own_attn, own_up, own_down, own_proj, own_gains = last(
        n,
        grad_projected.reshape(12 * local, rows),
        w_all.reshape(12 * local, width),
        flat,
        grad_middle,
        gains,
        w_mine,
        up_own,
        jnp.pad(packed[:, 3 * local : 3 * local + 2], ((0, 0), (0, 126))),
        gw_sum,
        zsum,
        osum,
    )
    own_attn = own_attn[:, : 3 * local].reshape(shard, 3, local).transpose(1, 0, 2)
    result, grad_input, own_attn, own_proj, own_up, own_down = close(
        result, grad_input, own_attn, own_proj, own_up, own_down
    )
    return (
        result.reshape(sequences, own, width),
        grad_input.reshape(sequences, own, width),
        own_attn.transpose(1, 0, 2),
        own_proj,
        own_up,
        own_down.T,
        own_gains[:, 0],
        own_gains[:, 1],
    )


def solution(mesh):
    return jax.shard_map(
        per_device,
        mesh=mesh,
        in_specs=(
            P("dp", ("context", "tensor"), None),
            P("dp", None),
            P("dp", None, "tensor"),
            P("tensor", "dp"),
            P("dp", "tensor"),
            P("tensor", "dp"),
            P("dp"),
            P("dp"),
            P("dp", ("context", "tensor"), None),
        ),
        out_specs=(
            P("dp", ("context", "tensor"), None),
            P("dp", ("context", "tensor"), None),
            P("dp", None, "tensor"),
            P("tensor", "dp"),
            P("dp", "tensor"),
            P("tensor", "dp"),
            P("dp"),
            P("dp"),
        ),
        check_vma=False,
    )
```

```python
import functools
import math

import jax
import jax.numpy as jnp
from jax import lax
from jax.experimental import pallas as pl
from jax.experimental.pallas import tpu as pltpu
from jax.sharding import PartitionSpec as P

HD = 64
WIN = 1536
QB = 256
CHUNK = 128
NEG = -1e30
epsilon = 1e-06
low = jnp.bfloat16
full = jnp.float32


def dot(left, right, dims):
    return lax.dot_general(left, right, (dims, ((), ())), preferred_element_type=full)


def nn(left, right):
    return dot(left, right, ((1,), (0,)))


def nt(left, right):
    return dot(left, right, ((1,), (1,)))


def tn(left, right):
    return dot(left, right, ((0,), (0,)))


PEERS = [(dc, r) for dc in range(2) for r in range(4)]


def place():
    return lax.axis_index("context"), lax.axis_index("tensor")


def at_peer(c, t, dc, r):
    return {"context": c ^ dc, "tensor": t ^ r}


def greet(peers):
    for peer in peers:
        pl.semaphore_signal(pltpu.get_barrier_semaphore(), inc=1, device_id=peer)


def greeted(peers):
    pl.semaphore_wait(pltpu.get_barrier_semaphore(), len(peers))


def unit_place(u, c):
    return jnp.where(u < 3, u, c + u - 3), jnp.where(u < 3, 2 * c, 1)


def sends(u, c):
    return (u != 3) | (c == 0)


dma = pltpu.SemaphoreType.DMA
ANY = pl.BlockSpec(memory_space=pl.ANY)
VMEM = pl.BlockSpec(memory_space=pltpu.VMEM)
HBM = pl.BlockSpec(memory_space=pltpu.HBM)
shape = jax.ShapeDtypeStruct

class Line:
    def __init__(self, n, own, slot, send, recv):
        self.n, self.own, self.slot, self.sems = n, own, slot, (send, recv)
        self.d = lax.axis_index("dp")

    def along(self, k):
        m = self.d if k == 0 else self.n - 1 - self.d
        to = {"dp": jnp.clip(self.d + 1 if k == 0 else self.d - 1, 0, self.n - 1)}
        return m, to

    def target(self, k, step):
        m, _ = self.along(k)
        return jnp.clip(self.n - step + m if k == 0 else step - 1 - m, 0, self.n - 1)

    def copy(self, k, step, src):
        send, recv = self.sems
        _, to = self.along(k)
        return pltpu.make_async_remote_copy(
            src, self.slot(k, step), send.at[k, step - 1], recv.at[k, step - 1], device_id=to
        )

    def arrive(self, k, step):
        self.copy(k, step, self.slot(k, step)).wait_recv()

    def start(self, step, add):
        for k in range(2):
            m, _ = self.along(k)
            if step > 1:

                @pl.when((m >= 1) & (m < self.n - 1) & (step >= m + 1))
                def _():
                    add(k, self.target(k, step))
                    self.copy(k, step, self.slot(k, step - 1)).start()

            @pl.when(m == 0)
            def _():
                self.copy(k, step, self.own(self.target(k, step))).start()

    def received(self, step):
        for k in range(2):
            m, _ = self.along(k)

            @pl.when((m >= 1) & (step >= m))
            def _():
                self.arrive(k, step)

    def sent(self, step):
        for k in range(2):
            m, _ = self.along(k)

            @pl.when((m < self.n - 1) & (step >= m + 1))
            def _():
                self.copy(k, step, self.slot(k, step)).wait_send()


def greet_line(n, d):
    barrier = pltpu.get_barrier_semaphore()

    @pl.when(d > 0)
    def _():
        pl.semaphore_signal(barrier, inc=1, device_id={"dp": jnp.maximum(d - 1, 0)})

    @pl.when(d < n - 1)
    def _():
        pl.semaphore_signal(barrier, inc=1, device_id={"dp": jnp.minimum(d + 1, n - 1)})


def greeted_line(n, d, peers):
    ends = jnp.where(d > 0, 1, 0) + jnp.where(d < n - 1, 1, 0)
    pl.semaphore_wait(pltpu.get_barrier_semaphore(), len(peers) + ends)


def project_kernel(
    n, tokens, segments, w_qkv, up, out_own, gain_own, qkv, norm, w_t, up_all, out_all, gain_ref, lo_ref,
    tok, x, w, proj, out_w, gain, tsend, trecv, tlocal, wsend, wrecv, wlocal, osend, orecv, olocal, xsend, xrecv,
):
    c, t = place()
    d = lax.axis_index("dp")
    own = tokens.shape[1]
    width = tokens.shape[2]
    span = 4 * own
    shard = up.shape[0]
    half = own // 2
    hidden = up_all.shape[1]
    cut = n // 2
    to_x, to_y, to_core = {"tensor": t ^ 1}, {"tensor": t ^ 2}, {"context": 1 - c}
    others = [{"dp": lax.rem(d + r, n)} for r in range(1, n)]
    peers = [to_x, to_y, to_core] + others
    greet(peers)

    def local(i, s):
        return pltpu.make_async_copy(tokens.at[s], tok.at[s, t], tlocal.at[i])

    def weights(j, r):
        rows = pl.ds(pl.multiple_of(d * shard, shard), shard)
        source, target = (
            (w_qkv, w.at[:, rows]),
            (out_w, out_all.at[rows]),
            (up.at[:, pl.ds(pl.multiple_of(c * hidden, hidden), hidden)], up_all.at[rows]),
            (gain_own, gain.at[d]),
        )[j]
        if r == 0:
            return pltpu.make_async_copy(source, target, wlocal.at[j])
        return pltpu.make_async_remote_copy(
            source, target, wsend.at[j, r - 1], wrecv.at[j, r - 1], device_id=others[r - 1]
        )

    def gives(j, r):
        return lax.rem(d + n - r, n) // cut == c if j < 2 else True

    def weights_do(j, r, what, source=False):
        @pl.when(gives(j, 0 if source else r))
        def _():
            getattr(weights(j, r), what)()

    def to_other(j):
        rows = pl.ds(pl.multiple_of(c * cut * shard, shard), cut * shard)
        ref = w.at[:, rows]
        return pltpu.make_async_remote_copy(ref, ref, xsend, xrecv, device_id=to_core)

    order = (2 * (1 - c), 1, 2 * c)
    for i, s in enumerate(order):
        local(i, s).start()
    out_w[...] = out_own[...].T
    for j in range(4):
        weights_do(j, 0, "start")
    greeted(peers)
    for j in (0, 3, 1, 2):
        for r in range(1, n):
            weights_do(j, r, "start", True)

    def hop(k, i):
        s = order[i]
        origin, rows, peer = (
            (t, slice(0, half), to_x),
            (t, slice(half, own), to_y),
            (t, slice(0, half), to_y),
            (t, slice(half, own), to_x),
            (t ^ 1, slice(0, half), to_y),
            (t ^ 2, slice(half, own), to_x),
        )[k]
        there = tok.at[s, origin, rows]
        here = tokens.at[s, rows] if k < 4 else there
        return pltpu.make_async_remote_copy(
            here, there, tsend.at[k, i], trecv.at[k, i], device_id=peer
        )

    def straight(i):
        for k in range(4):
            hop(k, i).start()

    def forward(i):
        for k in range(2):
            hop(k, i).wait_recv()
            hop(k + 4, i).start()

    units = proj.shape[1]

    def leave(i):
        out = []
        lanes = pl.ds(pl.multiple_of(c * span, span), span)
        if i != 0:
            out.append((x.at[i], norm.at[2 - i, lanes], False))
        if i != 2:
            out.append((x.at[i], norm.at[i, lanes], True))
        if i == 0:
            out.append((proj.at[0], qkv.at[pl.ds(0, units), :, lanes], True))
        if i == 2:
            out.append((proj.at[2], qkv.at[pl.ds(0, units), :, lanes], False))
        if i == 1:
            for away in (True, False):
                core = 1 - c if away else c
                for p in range(3):
                    src = proj.at[1, pl.ds(p * 3 + core, 2)]
                    out.append((src, qkv.at[pl.ds(units + 2 * p, 2), :, lanes], away))
        copies = []
        for j, (src, dst, away) in enumerate(out):
            if away:
                copies.append(
                    (away, pltpu.make_async_remote_copy(src, dst, osend.at[i, j], orecv.at[i, j], device_id=to_core))
                )
            else:
                copies.append((away, pltpu.make_async_copy(src, dst, olocal.at[i, j])))
        return copies

    def work(i):
        s = order[i]
        local(i, s).wait()
        for k in range(2, 6):
            hop(k, i).wait_recv()
        for p in range(4):
            v = tok[s, p].astype(full)
            inv = lax.rsqrt(jnp.mean(v * v, axis=-1, keepdims=True) + epsilon)
            x[i, p * own : (p + 1) * own, :] = (v * inv * gain_ref[0:1, :]).astype(low)
        for p in range(4):
            rows = slice(p * own, (p + 1) * own)
            part = nt(w_t[...], x[i, rows, :]).astype(low)
            proj[i, :, :, rows] = part.reshape(units, HD, own)
        for _, copy in leave(i):
            copy.start()

    straight(0)
    straight(1)
    forward(0)
    straight(2)
    seg = segments[...]
    first = jnp.zeros(seg.shape, jnp.int32)
    for value in range(8):
        before = jnp.sum((seg < value).astype(jnp.int32), axis=1, keepdims=True)
        first = jnp.where(seg == value, before, first)
    first = jnp.maximum(first, lax.broadcasted_iota(jnp.int32, seg.shape, 1) - (WIN - 1))
    lo_ref[0] = jnp.where(c == 0, first[0:1], first[2:3])
    lo_ref[1] = first[1:2]
    weights_do(0, 0, "wait")
    for r in range(1, n):
        weights_do(0, r, "wait_recv")
    to_other(0).start()
    weights(3, 0).wait()
    for r in range(1, n):
        weights(3, r).wait_recv()
    gain_ref[...] = jnp.concatenate([gain[i].astype(full) for i in range(n)], axis=1)[:8]
    to_other(0).wait_recv()
    for p in range(3):
        w_t[p * 3 * HD : (p + 1) * 3 * HD, :] = w[p].T
    forward(1)
    work(0)
    forward(2)
    work(1)
    work(2)
    to_other(0).wait_send()
    for j in range(4):
        if j in (1, 2):
            weights_do(j, 0, "wait")
        for r in range(1, n):
            weights_do(j, r, "wait_send", True)
            if j in (1, 2):
                weights_do(j, r, "wait_recv")
    for i in range(3):
        for k in range(6):
            hop(k, i).wait_send()
        for away, copy in leave(i):
            copy.wait()


def project(n, tokens, segments, w_qkv, up, out_own, gain_own):
    sequences, own, width = tokens.shape
    shard, hidden = up.shape[0], up.shape[1] // 2
    local = out_own.shape[0]
    span = 4 * own
    return pl.pallas_call(
        functools.partial(project_kernel, n),
        in_specs=[HBM, VMEM, HBM, HBM, VMEM, VMEM],
        out_specs=[HBM] * 2 + [VMEM] + [HBM] * 2 + [VMEM] * 2,
        out_shape=[
            shape((15, HD, 2 * span), low),
            shape((2, 2 * span, width), low),
            shape((9 * HD, n * shard), low),
            shape((n * shard, hidden), low),
            shape((n * shard, local), low),
            shape((8, n * shard), full),
            shape((2, 1, segments.shape[1]), jnp.int32),
        ],
        scratch_shapes=[
            pltpu.VMEM((sequences, 4, own, width), low),
            pltpu.VMEM((sequences, span, width), low),
            pltpu.VMEM((3, n * shard, local), low),
            pltpu.VMEM((sequences, 9, HD, span), low),
            pltpu.VMEM((shard, local), low),
            pltpu.VMEM((n,) + gain_own.shape, low),
            dma((6, 3)), dma((6, 3)), dma((3,)),
            dma((4, n - 1)), dma((4, n - 1)), dma((4,)),
            dma((3, 8)), dma((3, 8)), dma((3, 8)), dma, dma,
        ],
        compiler_params=pltpu.CompilerParams(
            vmem_limit_bytes=63 << 20, collective_id=3, has_side_effects=True
        ),
        name="project",
    )(tokens, segments, w_qkv, up, out_own, gain_own)


UNITS = 5
def unit_block(part):
    return lambda u: (jnp.where(u < 3, part * 3 + u, 9 + part * 2 + (u - 3)), 0, 0)


def attend_kernel(
    n, q_ref, k_ref, v_ref, lo_ref, out_part, up_part, down_own, att, lse_ref, of_ref, up, down, out_w,
    qs, ks, ss, obuf, ssem, rsem, lsem, wsend, wrecv, wlocal, zsend, zrecv, fsend, frecv,
):
    u = pl.program_id(0)
    c, t = place()
    d = lax.axis_index("dp")
    shard = down_own.shape[0]
    hidden = down.shape[2]
    peers = [at_peer(c, t, dc, r) for dc, r in PEERS[1:]]

    part = out_part.shape[0] // 2
    mine = pl.ds(pl.multiple_of(c * part, part), part)

    def weight(j, r):
        rows = pl.ds(pl.multiple_of(d * shard, shard), shard)
        src, dst = (
            (down_own.at[:, pl.ds(pl.multiple_of(c * hidden, hidden), hidden)], down.at[t, rows]),
            (up_part, up.at[t]),
            (out_part.at[mine], out_w.at[t, mine]),
        )[j]
        if r == 0:
            return pltpu.make_async_copy(src, dst, wlocal.at[j])
        return pltpu.make_async_remote_copy(
            src, dst, wsend.at[j, r - 1], wrecv.at[j, r - 1], device_id={"tensor": t ^ r}
        )

    def onward(k):
        if k == 2:
            ref, peer = out_w.at[:, mine], {"context": 1 - c}
        else:
            rows = pl.ds(k * part, part)
            ref, peer = up.at[t ^ (1 + k), rows], {"tensor": t ^ (2 - k)}
        return pltpu.make_async_remote_copy(
            ref, ref, fsend.at[k], frecv.at[k], device_id=peer
        )

    def shards(step, up_line):
        src = d - step if up_line else d + step
        rows = pl.ds(pl.multiple_of(jnp.clip(src, 0, n - 1) * shard, shard), shard)
        to = jnp.clip(d + 1 if up_line else d - 1, 0, n - 1)
        k = 0 if up_line else 1
        return pltpu.make_async_remote_copy(
            down.at[:, rows], down.at[:, rows], zsend.at[k, step], zrecv.at[k, step], device_id={"dp": to}
        )

    def line(step, what):
        for up_line in (True, False):
            inside = (d < n - 1) if up_line else (d > 0)
            has = (d >= step) if up_line else (d <= n - 1 - step)
            comes = (d >= step + 1) if up_line else (d <= n - 2 - step)
            if what == "recv":

                @pl.when(comes)
                def _():
                    shards(step, up_line).wait_recv()
            else:

                @pl.when(inside & has)
                def _():
                    if what == "start":
                        shards(step, up_line).start()
                    else:
                        shards(step, up_line).wait_send()
    length = lo_ref.shape[2]
    half = length // 2
    own = half // 4

    @pl.when(u == 0)
    def _():
        greet(peers)
        greet_line(n, d)
        for j in range(3):
            weight(j, 0).start()
        greeted_line(n, d, peers)
        for r in range(1, 4):
            weight(0, r).start()

    qs[...] = q_ref[0] * low(0.125)
    ks[...] = k_ref[0].T
    for start in range(0, length, QB):
        stop = start + QB
        q = qs[:, start:stop]
        lo = lo_ref[0, :, start:stop]
        first = max(0, start - WIN)
        most = jnp.full((8, QB), NEG, full)
        for at in range(first, stop, CHUNK):
            s = nn(ks[at : at + CHUNK, :], q)
            key_pos = at + lax.broadcasted_iota(jnp.int32, (CHUNK, QB), 0)
            allowed = key_pos >= lo
            if at + CHUNK - 1 > start:
                allowed &= key_pos <= start + lax.broadcasted_iota(jnp.int32, (CHUNK, QB), 1)
            s = jnp.where(allowed, s, NEG)
            ss[at - first : at - first + CHUNK, :] = s
            most = jnp.maximum(most, jnp.max(s.reshape(CHUNK // 8, 8, QB), axis=0))
        most = jnp.max(most, axis=0, keepdims=True)
        total = jnp.zeros((8, QB), full)
        acc = jnp.zeros((HD, QB), full)
        for at in range(first, stop, CHUNK):
            p = jnp.exp(ss[at - first : at - first + CHUNK, :] - most)
            total += jnp.sum(p.reshape(CHUNK // 8, 8, QB), axis=0)
            acc += nn(v_ref[0, :, at : at + CHUNK], p.astype(low))
        total = jnp.sum(total, axis=0, keepdims=True)
        lse_ref[0, :, start:stop] = most + jnp.log(total)
        o = acc * (1.0 / total)
        of_ref[0, :, start:stop] = o
        obuf[u, :, start:stop] = o.astype(low)

    @pl.when(u == 0)
    def _():
        weight(0, 0).wait()
        for r in range(1, 4):
            weight(0, r).wait_recv()
        line(0, "start")
        for j, count in ((1, 3), (2, 4)):
            for r in range(1, count):
                weight(j, r).start()

    @pl.when(u == 3)
    def _():
        if n > 2:
            line(0, "recv")
            line(1, "start")
        for k in range(2):
            weight(1, 1 + k).wait_recv()
            onward(k).start()
        weight(2, 0).wait()
        for r in range(1, 4):
            weight(2, r).wait_recv()
        onward(2).start()

    def move(unit, i, source_core):
        dc, r = PEERS[i]
        h, seq = unit_place(unit, source_core)
        dest = pl.multiple_of(((c ^ dc) * 4 + (t ^ r)) * own, own)
        src = obuf.at[unit, :, pl.ds(dest, own)]
        dst = att.at[
            pl.ds(pl.multiple_of((t * 3 + h) * HD, HD), HD), pl.ds(pl.multiple_of(seq * own, own), own)
        ]
        if i == 0:
            return pltpu.make_async_copy(src, dst, lsem.at[unit])
        return pltpu.make_async_remote_copy(
            src, dst, ssem.at[i - 1, unit], rsem.at[i - 1, unit], device_id=at_peer(c, t, dc, r)
        )

    @pl.when(sends(u, c))
    def _():
        for i in range(1, len(PEERS)):
            move(u, i, c).start()
        move(u, 0, c).start()

    @pl.when(u == pl.num_programs(0) - 1)
    def _():
        for step in range(2, n - 1):
            line(step - 1, "recv")
            line(step, "start")
        line(n - 2, "recv")
        for step in range(n - 1):
            line(step, "sent")
        weight(1, 0).wait()
        for j in range(3):
            for r in range(1, 3 if j == 1 else 4):
                weight(j, r).wait_send()
        for k in range(3):
            onward(k).wait()
        for unit in range(UNITS):
            for i, (dc, r) in enumerate(PEERS):

                @pl.when(sends(unit, c))
                def _():
                    if i:
                        move(unit, i, c).wait_send()
                    else:
                        move(unit, i, c).wait()

                if i:

                    @pl.when(sends(unit, c ^ dc))
                    def _():
                        move(unit, i, c ^ dc).wait_recv()


def attend(n, qkv, lo, out_part, up_part, down_own):
    length = lo.shape[2]
    half = length // 2
    own = half // 4
    width, hidden = up_part.shape
    part = lambda p: pl.BlockSpec((1, HD, length), unit_block(p))
    unit = lambda rows, n: pl.BlockSpec((1, rows, n), lambda u: (u, 0, 0))
    heads = 4 * 3 * HD
    return pl.pallas_call(
        functools.partial(attend_kernel, n),
        grid=(UNITS,),
        in_specs=[part(0), part(1), part(2)]
        + [pl.BlockSpec((1, 1, length), lambda u: (u // 3, 0, 0))]
        + [
            pl.BlockSpec(a.shape, lambda u: (0, 0), pipeline_mode=pl.Buffered(1))
            for a in (out_part, up_part, down_own)
        ],
        out_specs=[HBM, unit(1, length), unit(HD, length)] + [HBM] * 3,
        scratch_shapes=[
            pltpu.VMEM((HD, length), low),
            pltpu.VMEM((length, HD), low),
            pltpu.VMEM((WIN + QB, QB), full),
            pltpu.VMEM((UNITS, HD, length), low),
            dma((7, UNITS)),
            dma((7, UNITS)),
            dma((UNITS,)),
            dma((3, 3)),
            dma((3, 3)),
            dma((3,)),
            dma((2, n - 1)),
            dma((2, n - 1)),
            dma((3,)),
            dma((3,)),
        ],
        out_shape=[
            jax.ShapeDtypeStruct((heads, 3 * own), low),
            jax.ShapeDtypeStruct((UNITS, 1, length), full),
            jax.ShapeDtypeStruct((UNITS, HD, length), full),
            shape((4, width, hidden), low),
            shape((4, width, hidden), low),
            shape((4,) + out_part.shape, low),
        ],
        compiler_params=pltpu.CompilerParams(
            vmem_limit_bytes=63 << 20, collective_id=1, has_side_effects=True
        ),
        cost_estimate=pl.CostEstimate(
            flops=UNITS * 18 * 2 * 256 * 1024 * 128, bytes_accessed=20 << 20, transcendentals=0
        ),
        name="attend",
    )(qkv, qkv, qkv, lo, out_part, up_part, down_own)


def add_to(ref, terms):
    for a in range(ref.shape[0]):
        for p in range(ref.shape[1]):
            ref[a, p] = (ref[a, p].astype(full) + terms(a, p).astype(full)).astype(low)


def attend_back_kernel(
    n, q_ref, k_ref, v_ref, lo_ref, lse_ref, of_ref, norm_ref, g_ref, gud, part_sum, gout,
    dall, gw_sum, zsum, osum,
    qs, ks, vs, grow, qrow, delta, dqs, dbuf, gw, gwx, gwr, zr, gud_v, obuf, ssem, rsem, lsem,
    zsend, zrecv, xsend, xrecv, osend, orecv, olocal, vlocal,
):
    u = pl.program_id(0)
    c, t = place()
    d = lax.axis_index("dp")
    shard = gud.shape[2] // n
    length = lo_ref.shape[2]
    own = length // 8
    peers = [at_peer(c, t, dc, r) for dc, r in PEERS[1:]]

    def rows_of(j):
        return pl.ds(pl.multiple_of(j * shard, shard), shard)

    def line_of(h):
        pair = pl.ds(2 * h, 2)
        return Line(
            n,
            lambda j: gud.at[:, pair, rows_of(j)],
            lambda k, step: zr.at[h, k, step - 1],
            zsend.at[h],
            zrecv.at[h],
        )

    lines = [line_of(0), line_of(1)]

    def step_of(h, step, arrived=True):
        if arrived and step > 1:
            lines[h].received(step - 1)

        def add(k, j):
            rows = rows_of(j)
            add_to(zr.at[h, k, step - 2], lambda a, p: gud_v[a, 2 * h + p, rows])

        lines[h].start(step, add)

    def finish(h):
        lines[h].received(n - 1)
        for step in range(3 if h == 0 else 1, n):
            lines[h].sent(step)
        for a in range(2):
            for p in range(2):
                total = gud_v[a, 2 * h + p, rows_of(d)].astype(full)
                up, down = (zr[h, k, n - 2, a, p].astype(full) for k in range(2))
                total += jnp.where(d > 0, up, 0.0) + jnp.where(d < n - 1, down, 0.0)
                zsum[a, 2 * h + p] = total.astype(low)

    part_rows = gout.shape[1] // 2

    def out_piece(i):
        dc, r = PEERS[i]
        src = gout.at[t ^ r, pl.ds(pl.multiple_of((c ^ dc) * part_rows, part_rows), part_rows)]
        if i == 0:
            return pltpu.make_async_copy(src, obuf.at[0], olocal)
        return pltpu.make_async_remote_copy(
            src, obuf.at[i], osend.at[i - 1], orecv.at[i - 1], device_id=at_peer(c, t, dc, r)
        )

    def other_core():
        return pltpu.make_async_remote_copy(
            gwx.at[1 - c], gwr, xsend, xrecv, device_id={"context": 1 - c}
        )

    def load(i):
        if i == 2:
            return pltpu.make_async_copy(gud, gud_v, vlocal.at[2])
        return pltpu.make_async_copy(part_sum.at[i], zr.at[0, i, 1], vlocal.at[i])

    @pl.when(u == 0)
    def _():
        greet(peers)
        greet_line(n, d)
        for i in range(3):
            load(i).start()
        gw[...] = jnp.zeros_like(gw)
        greeted_line(n, d, peers)
        for i in range(3):
            load(i).wait()
        step_of(0, 3, False)
        step_of(1, 1)
        for i in range(1, len(PEERS)):
            out_piece(i).start()
        out_piece(0).start()

    @pl.when(u == 3)
    def _():
        step_of(1, 2)

    @pl.when(u == 4)
    def _():
        step_of(1, 3)

    qs[...] = q_ref[0] * low(0.125)
    ks[...] = k_ref[0].T
    vs[...] = v_ref[0].T
    grow[...] = g_ref[0].T
    qrow[...] = qs[...].T
    delta[...] = jnp.sum(g_ref[0].astype(full) * of_ref[0], axis=0, keepdims=True)
    dqs[...] = jnp.zeros_like(dqs)
    for key_start in range(0, length, QB):
        rows = slice(key_start, key_start + QB)
        k, v, key_t = ks[rows, :], vs[rows, :], k_ref[0, :, rows]
        dk = jnp.zeros((QB, HD), full)
        dv = jnp.zeros((QB, HD), full)
        key_pos = key_start + lax.broadcasted_iota(jnp.int32, (QB, QB), 0)
        for start in range(key_start, min(key_start + WIN + QB, length), QB):
            cols = slice(start, start + QB)
            s = nn(k, qs[:, cols]) - lse_ref[0, :, cols]
            allowed = key_pos >= lo_ref[0, :, cols]
            if start == key_start:
                allowed &= key_pos <= start + lax.broadcasted_iota(jnp.int32, (QB, QB), 1)
            p = jnp.exp(jnp.where(allowed, s, NEG))
            dp = nn(v, g_ref[0, :, cols])
            ds = (p * (dp - delta[:, cols])).astype(low)
            dv += nn(p.astype(low), grow[cols, :])
            dk += nn(ds, qrow[cols, :])
            dqs[:, cols] += nn(key_t, ds)
        dbuf[u, 1, :, rows] = dk.T.astype(low)
        dbuf[u, 2, :, rows] = dv.T.astype(low)
    dbuf[u, 0] = (dqs[...] * 0.125).astype(low)

    def move(unit, i, source_core):
        dc, r = PEERS[i]
        h, seq = unit_place(unit, source_core)
        dest = pl.multiple_of(((c ^ dc) * 4 + (t ^ r)) * own, own)
        src = dbuf.at[unit, :, :, pl.ds(dest, own)]
        dst = dall.at[t, :, h, :, pl.ds(pl.multiple_of(seq * own, own), own)]
        if i == 0:
            return pltpu.make_async_copy(src, dst, lsem.at[unit])
        return pltpu.make_async_remote_copy(
            src, dst, ssem.at[i - 1, unit], rsem.at[i - 1, unit], device_id=at_peer(c, t, dc, r)
        )

    @pl.when(sends(u, c))
    def _():
        for i in range(1, len(PEERS)):
            move(u, i, c).start()
        move(u, 0, c).start()
        h, _ = unit_place(u, c)
        gw[h] += nn(dbuf[u].reshape(3 * HD, length), norm_ref[0])

    @pl.when(u == pl.num_programs(0) - 1)
    def _():
        wide_rows = [gw[h, p * HD : (p + 1) * HD, :] for p in range(3) for h in range(3)]
        gwx[0] = jnp.concatenate(wide_rows[:6], axis=0).T.astype(low)
        empty = jnp.zeros((3 * HD, gw.shape[2]), full)
        gwx[1] = jnp.concatenate(wide_rows[6:] + [empty], axis=0).T.astype(low)
        other_core().start()
        out_piece(0).wait()
        for i in range(1, len(PEERS)):
            out_piece(i).wait()
        total = obuf[0].astype(full)
        for i in range(1, len(PEERS)):
            total += obuf[i].astype(full)
        osum[...] = total.astype(low)
        other_core().wait()
        gw_sum[...] = (gwx[c].astype(full) + gwr[...].astype(full)).astype(low)
        for step in range(4, n):
            step_of(0, step)
            step_of(1, step)
        finish(0)
        finish(1)
        for unit in range(UNITS):
            for i, (dc, r) in enumerate(PEERS):

                @pl.when(sends(unit, c))
                def _():
                    if i:
                        move(unit, i, c).wait_send()
                    else:
                        move(unit, i, c).wait()

                if i:

                    @pl.when(sends(unit, c ^ dc))
                    def _():
                        move(unit, i, c ^ dc).wait_recv()


def attend_back(n, qkv, grad_units, lo, lse, attended, normed, grad_up_down, part_sum, grad_out):
    length = lo.shape[2]
    own = length // 8
    width = normed.shape[2]
    shard, hidden = grad_up_down.shape[2] // n, grad_up_down.shape[3]
    out_rows, local = grad_out.shape[1] // 2, grad_out.shape[2]
    part = lambda p: pl.BlockSpec((1, HD, length), unit_block(p))
    unit = lambda rows, m: pl.BlockSpec((1, rows, m), lambda u: (u, 0, 0))
    once = lambda dims: pl.BlockSpec(dims, lambda u: (0,) * len(dims), pipeline_mode=pl.Buffered(1))
    wide, tall = pltpu.VMEM((HD, length), low), pltpu.VMEM((length, HD), low)
    results = [(width, 2 * 3 * HD), (2, 4, shard, hidden), (out_rows, local)]
    return pl.pallas_call(
        functools.partial(attend_back_kernel, n),
        grid=(UNITS,),
        in_specs=[part(0), part(1), part(2)]
        + [
            pl.BlockSpec((1, 1, length), lambda u: (u // 3, 0, 0)),
            unit(1, length),
            unit(HD, length),
            pl.BlockSpec((1, length, width), lambda u: (u // 3, 0, 0)),
            unit(HD, length),
        ]
        + [HBM] * 3,
        out_specs=[HBM] + [once(r) for r in results],
        scratch_shapes=[
            wide, tall, tall, tall, tall,
            pltpu.VMEM((1, length), full), pltpu.VMEM((HD, length), full),
            pltpu.VMEM((UNITS, 3, HD, length), low), pltpu.VMEM((3, 3 * HD, width), full),
            pltpu.VMEM((2, width, 6 * HD), low), pltpu.VMEM((width, 6 * HD), low),
            pltpu.VMEM((2, 2, n - 1, 2, 2, shard, hidden), low), pltpu.VMEM(grad_up_down.shape, low),
            pltpu.VMEM((8, out_rows, local), low),
            dma((7, UNITS)), dma((7, UNITS)), dma((UNITS,)),
            dma((2, 2, n - 1)), dma((2, 2, n - 1)), dma, dma, dma((7,)), dma((7,)), dma, dma((3,)),
        ],
        out_shape=[shape((4, 3, 3, HD, 3 * own), low)] + [shape(r, low) for r in results],
        compiler_params=pltpu.CompilerParams(
            vmem_limit_bytes=63 << 20, collective_id=2, has_side_effects=True
        ),
        name="attend_back",
    )(qkv, qkv, qkv, lo, lse, attended, normed, grad_units, grad_up_down, part_sum, grad_out)


def last_kernel(
    n, dqkv_ref, w_ref, tokens_ref, middle_ref, gains, w_own, up_own, gain_mine, gw_sum, zsum, osum,
    grad_in, g_qkv, g_up, g_down, g_out, g_gain,
    rg, rw, ro, down_n, out_t, mine, sums, dqkv, w_all, tokens, middle,
    gsend, grecv, wsend, wrecv, osend, orecv, lsem, csend, crecv, ssend, srecv, clocal, fetch,
):
    c, t = place()
    d = lax.axis_index("dp")
    shard, hidden = rw.shape[2], rw.shape[3]
    cut = n // 2
    group = [at_peer(c, t, dc, r) for dc, r in PEERS[1:]]
    others = [lax.rem(d + r, n) for r in range(1, n)]
    peers = group + [{"dp": o} for o in others]
    greet(peers)
    loads = [
        pltpu.make_async_copy(src, dst, fetch.at[i])
        for i, (src, dst) in enumerate(
            ((tokens_ref, tokens), (w_ref, w_all), (dqkv_ref, dqkv), (middle_ref, middle))
        )
    ]
    for copy in loads:
        copy.start()

    def rows_of(j):
        return pl.ds(pl.multiple_of(j * shard, shard), shard)

    narrow = slice(0, 256)

    def qkv_piece(r, core):
        src, dst = gw_sum.at[rows_of(d if r == 0 else others[r - 1])], rg.at[r]
        if core:
            src, dst = src.at[:, narrow], dst.at[:, narrow]
        if r == 0:
            return pltpu.make_async_copy(src, dst, lsem.at[0])
        return pltpu.make_async_remote_copy(
            src, dst, gsend.at[r - 1], grecv.at[r - 1], device_id={"dp": others[r - 1]}
        )

    def each_core(what):
        for core in range(2):

            @pl.when(c == core)
            def _():
                what(core)

    def up_piece(r):
        src, dst = zsum.at[:, t ^ r], rw.at[r]
        if r == 0:
            return pltpu.make_async_copy(src, dst, lsem.at[1])
        return pltpu.make_async_remote_copy(
            src, dst, wsend.at[r - 1], wrecv.at[r - 1], device_id={"tensor": t ^ r}
        )

    mine_out = d // cut == c

    def out_piece(r):
        to = d if r == 0 else others[r - 1]
        src, dst = osum.at[rows_of(lax.rem(to, cut))], ro.at[r]
        if r == 0:
            return pltpu.make_async_copy(src, dst, lsem.at[2])
        return pltpu.make_async_remote_copy(
            src, dst, osend.at[r - 1], orecv.at[r - 1], device_id={"dp": to}
        )

    def start_all(core):
        for r in range(1, n):
            qkv_piece(r, core).start()
        qkv_piece(0, core).start()

    greeted(peers)
    each_core(start_all)
    for r in range(1, 4):
        up_piece(r).start()
    up_piece(0).start()
    for r in range(1, n):

        @pl.when(others[r - 1] // cut == c)
        def _():
            out_piece(r).start()

    @pl.when(mine_out)
    def _():
        out_piece(0).start()

    for copy in loads:
        copy.wait()
    for m in range(0, tokens.shape[0], QB):
        rows = slice(m, m + QB)
        r = tn(dqkv[:, rows], w_all[...])
        v = tokens[rows, :].astype(full)
        inv = lax.rsqrt(jnp.mean(v * v, axis=-1, keepdims=True) + epsilon)
        rg_ = r * gains[0:1, :]
        grad = inv * (rg_ - v * (inv * inv * jnp.mean(rg_ * v, axis=-1, keepdims=True)))
        grad_in[rows, :] = (middle[rows, :] + grad).astype(low)

    def halves(j):
        half = pl.ds(pl.multiple_of(c * hidden, hidden), hidden)
        src, dst = (
            (mine.at[0], g_qkv.at[:, half]),
            (mine.at[1], g_up.at[:, half]),
            (down_n, g_down.at[:, half]),
            (out_t, g_out),
        )[j]
        return (
            pltpu.make_async_copy(src, dst, clocal.at[j]),
            pltpu.make_async_remote_copy(
                src, dst, csend.at[j], crecv.at[j], device_id={"context": 1 - c}
            ),
        )

    def deliver(j):
        for copy in halves(j):
            copy.start()

    up_piece(0).wait()
    for r in range(1, 4):
        up_piece(r).wait_recv()
    mine[1] = sum(rw[r, 0].astype(full) for r in range(4))
    down_n[...] = sum(rw[r, 1].astype(full) for r in range(4))
    deliver(1)
    deliver(2)

    @pl.when(mine_out)
    def _():
        out_piece(0).wait()
        for r in range(1, n):
            out_piece(r).wait_recv()
        out_t[...] = sum(ro[r].astype(full) for r in range(n)).T
        deliver(3)

    def take(core):
        qkv_piece(0, core).wait()
        for r in range(1, n):
            qkv_piece(r, core).wait_recv()
        if core:
            mine[0, :, narrow] = sum(rg[r, :, narrow].astype(full) for r in range(n))
            mine[0, :, 256:] = jnp.zeros((shard, hidden - 256), full)
        else:
            mine[0] = sum(rg[r].astype(full) for r in range(n))

    each_core(take)
    deliver(0)
    lane = lax.broadcasted_iota(jnp.int32, (shard, 128), 1)
    halves_of = [jnp.concatenate([w_own[0], w_own[1]], axis=1), jnp.pad(w_own[2], ((0, 0), (0, osum.shape[1])))]
    w_mine = jnp.where(c == 0, halves_of[0].astype(full), halves_of[1].astype(full))
    up_mine = up_own[:, pl.ds(pl.multiple_of(c * hidden, hidden), hidden)].astype(full)
    first = jnp.sum(w_mine * mine[0], axis=1, keepdims=True)
    second = jnp.sum(up_mine * mine[1], axis=1, keepdims=True)
    sums[0] = jnp.where(lane == 0, first, jnp.where(lane == 1, second, 0.0))

    def gain_piece(i):
        dc, r = PEERS[i]
        return pltpu.make_async_remote_copy(
            sums.at[0], sums.at[i], ssend.at[i - 1], srecv.at[i - 1], device_id=at_peer(c, t, dc, r)
        )

    for i in range(1, len(PEERS)):
        gain_piece(i).start()
    for i in range(1, len(PEERS)):
        gain_piece(i).wait()
    total = sum(sums[i] for i in range(len(PEERS)))
    g_gain[...] = total / jnp.where(lane < 2, gain_mine[...].astype(full), 1.0)

    for j in range(3):
        for copy in halves(j):
            copy.wait()

    @pl.when(mine_out)
    def _():
        local, away = halves(3)
        local.wait()
        away.wait_send()

    @pl.when(jnp.logical_not(mine_out))
    def _():
        halves(3)[1].wait_recv()

    for r in range(1, 4):
        up_piece(r).wait_send()

    def sent(core):
        for r in range(1, n):
            qkv_piece(r, core).wait_send()

    each_core(sent)
    for r in range(1, n):

        @pl.when(others[r - 1] // cut == c)
        def _():
            out_piece(r).wait_send()


def last(n, dqkv, w_all, tokens, middle, gains, w_own, up_own, gain_mine, gw_sum, zsum, osum):
    rows, width = tokens.shape
    _, _, shard, hidden = zsum.shape
    local = osum.shape[1]
    return pl.pallas_call(
        functools.partial(last_kernel, n),
        in_specs=[HBM] * 4 + [VMEM] * 4 + [ANY] * 3,
        out_specs=[VMEM] + [ANY] * 4 + [VMEM],
        out_shape=[
            shape((rows, width), low),
            shape((shard, 2 * hidden), full),
            shape((shard, 2 * hidden), full),
            shape((shard, 2 * hidden), full),
            shape((local, shard), full),
            shape((shard, 128), full),
        ],
        scratch_shapes=[
            pltpu.VMEM((n, shard, hidden), low),
            pltpu.VMEM((4, 2, shard, hidden), low),
            pltpu.VMEM((n, shard, local), low),
            pltpu.VMEM((shard, hidden), full),
            pltpu.VMEM((local, shard), full),
            pltpu.VMEM((2, shard, hidden), full),
            pltpu.VMEM((8, shard, 128), full),
            pltpu.VMEM(dqkv.shape, low), pltpu.VMEM(w_all.shape, low),
            pltpu.VMEM((rows, width), low), pltpu.VMEM((rows, width), full),
            dma((n - 1,)), dma((n - 1,)), dma((3,)), dma((3,)), dma((n - 1,)), dma((n - 1,)), dma((3,)),
            dma((4,)), dma((4,)), dma((7,)), dma((7,)), dma((4,)), dma((4,)),
        ],
        compiler_params=pltpu.CompilerParams(
            vmem_limit_bytes=63 << 20, collective_id=4, has_side_effects=True
        ),
        name="last",
    )(dqkv, w_all, tokens, middle, gains, w_own, up_own, gain_mine, gw_sum, zsum, osum)


def close_kernel(*refs):
    count = len(refs) // 2
    for i, (src, dst) in enumerate(zip(refs[:count], refs[count:])):
        if i == 2:
            local = dst.shape[2]
            for p in range(3):
                dst[p] = src[:, p * local : (p + 1) * local]
        else:
            dst[...] = src[...]


def close(result, grad_input, own_attn, *others):
    arrays = (result, grad_input, own_attn, *others)
    rows = lambda a: pl.BlockSpec((a.shape[0] // 2, a.shape[1]), lambda i: (i, 0))
    shard, local = own_attn.shape[0], others[0].shape[0]
    parts = pl.BlockSpec((3, shard // 2, local), lambda i: (0, i, 0))
    outs = [shape(a.shape, a.dtype) for a in arrays]
    outs[2] = shape((3, shard, local), full)
    return pl.pallas_call(
        close_kernel,
        grid=(2,),
        in_specs=[rows(a) for a in arrays],
        out_specs=[parts if i == 2 else rows(a) for i, a in enumerate(arrays)],
        out_shape=outs,
        compiler_params=pltpu.CompilerParams(vmem_limit_bytes=63 << 20),
        name="close",
    )(*arrays)


def gelu_and_slope(v):
    k0 = math.sqrt(2.0 / math.pi)
    square = v * v
    th = jnp.tanh(v * (k0 + (k0 * 0.044715) * square))
    half = 0.5 + 0.5 * th
    slope = half + (v * half) * ((1.0 - th) * (k0 + (3.0 * 0.044715 * k0) * square))
    return v * half, slope


def feed_kernel(
    dp, att, proj, tokens, cot, gains, w_t, up_ref, down_ref,
    result, middle, gout, gud, part_sum, units, w_all,
    x, g, x_t, g_t, up, down, act, gh, out, back, pre, ga, proj_w, sent, got, gbuf, zr, gatt,
    xsend, xrecv, wsend, wrecv, wlocal, zsend, zrecv, glocal, usend, urecv, ulocal,
):
    j = pl.program_id(0)
    c, t = place()
    d = lax.axis_index("dp")
    own = tokens.shape[0] // 3
    shard = tokens.shape[1] // dp
    rows, width = tokens.shape
    n = up_ref.shape[2]
    local = proj.shape[2]
    blocks = 2 * rows // QB
    other = {"context": 1 - c}
    peers = [at_peer(c, t, dc, r) for dc, r in PEERS[1:]]
    mine, theirs = slice(0, rows), slice(rows, 2 * rows)

    def cross(k):
        src, dst = (
            (cot, g.at[theirs]),
            (x.at[mine], x.at[theirs]),
            (sent.at[0], got.at[0]),
            (sent.at[1], got.at[1]),
        )[k]
        return pltpu.make_async_remote_copy(src, dst, xsend.at[k], xrecv.at[k], device_id=other)

    def over_tensor(r):
        if r == 0:
            return pltpu.make_async_copy(w_t, w_all.at[t], wlocal)
        return pltpu.make_async_remote_copy(
            w_t, w_all.at[t], wsend.at[r - 1], wrecv.at[r - 1], device_id={"tensor": t ^ r}
        )

    def rows_of(i):
        return pl.ds(pl.multiple_of(i * shard, shard), shard)

    line = Line(
        dp,
        lambda i: gbuf.at[0, :, :, rows_of(i)],
        lambda k, step: zr.at[k] if step == 1 else part_sum.at[k],
        zsend,
        zrecv,
    )

    def keep(half):
        return pltpu.make_async_copy(
            gbuf.at[half], gud.at[:, pl.ds(2 * half, 2)], glocal.at[half]
        )

    def leave(whole, i):
        dc, r = PEERS[i]
        to_c, to_t = c ^ dc, t ^ r
        head = to_t * 3 + (0 if whole else to_c)
        count, first = (3, 0) if whole else (2, 3)
        seq = 2 * to_c if whole else 1
        src = gatt.at[pl.ds(head, count), :, pl.ds(pl.multiple_of(seq * own, own), own)]
        dst = units.at[pl.ds(first, count), :, pl.ds(pl.multiple_of((c * 4 + t) * own, own), own)]
        k = 0 if whole else 1
        if i == 0:
            return pltpu.make_async_copy(src, dst, ulocal.at[k])
        return pltpu.make_async_remote_copy(
            src, dst, usend.at[k, i - 1], urecv.at[k, i - 1], device_id=at_peer(c, t, dc, r)
        )

    @pl.when(j == 0)
    def _():
        greet(peers)
        greet_line(dp, d)
        for p in range(4):
            proj_w[:, p * local : (p + 1) * local] = proj[p]
        greeted_line(dp, d, peers)
        cross(0).start()
        for r in range(1, 4):
            over_tensor(r).start()
        over_tensor(0).start()
        g[mine, :] = cot[...]
        g_t[:, mine] = cot[...].T
        for m in range(0, rows, QB):
            part = slice(m, m + QB)
            v = tokens[part, :].astype(full) + nn(proj_w[...], att[:, part]).T
            middle[part, :] = v
            inv = lax.rsqrt(jnp.mean(v * v, axis=-1, keepdims=True) + epsilon)
            x[part, :] = (v * inv * gains[1:2, :]).astype(low)
        cross(1).start()
        x_t[:, mine] = x[mine, :].T
        out[...] = jnp.zeros_like(out)
        back[...] = jnp.zeros_like(back)

    @pl.when(j == 1)
    def _():
        line.start(1, None)

    for i in range(2):
        up[:, i * n : (i + 1) * n] = up_ref[i]
        down[:, i * n : (i + 1) * n] = down_ref[i]

    def first(i):
        part = slice(i * QB, (i + 1) * QB)
        pre[i % 2] = nn(x[part, :], up[...])
        ga[i % 2] = nn(g[part, :], down[...])

    def second(i):
        part = slice(i * QB, (i + 1) * QB)
        a, slope = gelu_and_slope(pre[i % 2])
        act[part, :] = a.astype(low)
        gh[part, :] = (ga[i % 2] * slope).astype(low)

    def third(i):
        part = slice(i * QB, (i + 1) * QB)
        out[part, :] += nt(act[part, :], down[...])
        back[part, :] += nt(gh[part, :], up[...])

    first(0)
    for i in range(blocks):
        if i + 1 == blocks // 2:

            @pl.when(j == 0)
            def _():
                cross(0).wait_recv()
                cross(1).wait_recv()
                x_t[:, theirs] = x[theirs, :].T
                g_t[:, theirs] = g[theirs, :].T

        if i + 1 < blocks:
            first(i + 1)
        second(i)
        if i > 0:
            third(i - 1)
    third(blocks - 1)

    @pl.when(j == pl.num_programs(0) - 1)
    def _():
        sent[0] = back[theirs, :].astype(low)
        cross(2).start()
        sent[1] = out[theirs, :].astype(low)
        cross(3).start()

    def weight_grad(a, left_t, right):
        for m in range(0, width, QB):
            part = slice(m, m + QB)
            grad = nn(left_t[part, :], right[...]).astype(low)
            for i in range(2):
                gbuf[j, a, i, part, :] = grad[:, i * n : (i + 1) * n]

    weight_grad(1, g_t, act)

    @pl.when(j == 0)
    def _():
        weight_grad(0, x_t, gh)
        keep(0).start()

    @pl.when(j == 1)
    def _():
        line.received(1)
        line.start(2, lambda k, i: add_to(zr.at[k], lambda a, p: gbuf[0, a, p, rows_of(i)]))
        cross(2).wait_recv()
        gain = gains[1:2, :]
        for m in range(0, rows, QB):
            part = slice(m, m + QB)
            r = (back[part, :] + got[0, part, :].astype(full)) * gain
            v = middle[part, :]
            inv = lax.rsqrt(jnp.mean(v * v, axis=-1, keepdims=True) + epsilon)
            grad = inv * (r - v * (inv * inv * jnp.mean(r * v, axis=-1, keepdims=True)))
            back[part, :] = cot[part, :].astype(full) + grad
            g_t[:, part] = back[part, :].astype(low).T
        for m in range(0, rows, QB):
            part = slice(m, m + QB)
            grad = tn(proj_w[...], g_t[:, part]).astype(low)
            gatt[:, :, part] = grad.reshape(gatt.shape[0], HD, QB)
        for whole in (True, False):
            for i in range(1, len(PEERS)):
                leave(whole, i).start()
            leave(whole, 0).start()
        weight_grad(0, x_t, gh)
        keep(1).start()
        for m in range(0, width, QB):
            part = slice(m, m + QB)
            big = nt(g_t[part, mine], att[...]).astype(low)
            for p in range(4):
                gout[p, part, :] = big[:, p * local : (p + 1) * local]
        cross(3).wait_recv()
        result[...] = (middle[...] + out[mine, :] + got[1].astype(full)).astype(low)
        middle[...] = back[mine, :]
        for k in range(4):
            cross(k).wait_send()
        over_tensor(0).wait()
        for r in range(1, 4):
            over_tensor(r).wait()
        line.received(2)
        line.sent(1)
        line.sent(2)
        for half in range(2):
            keep(half).wait()
        for whole in (True, False):
            for i in range(len(PEERS)):
                leave(whole, i).wait()


def feed(dp, att, proj, tokens, cot, gains, w_t, up, down):
    rows, width = tokens.shape
    pieces, _, n = up.shape
    own = rows // 3
    assert pieces == 4 and dp > 2
    whole = lambda dims: pl.BlockSpec(dims, lambda j: (0,) * len(dims), pipeline_mode=pl.Buffered(1))
    weight = pl.BlockSpec((2, width, n), lambda j: (j, 0, 0))
    return pl.pallas_call(
        functools.partial(feed_kernel, dp),
        grid=(2,),
        in_specs=[whole(a.shape) for a in (att, proj, tokens, cot, gains, w_t)] + [weight] * 2,
        out_specs=[whole((rows, width))] * 2 + [whole(proj.shape)] + [HBM] * 4,
        out_shape=[
            shape((rows, width), low),
            shape((rows, width), full),
            shape(proj.shape, low),
            shape((2,) + up.shape, low),
            shape((2, 2, 2, width // dp, n), low),
            shape((UNITS, HD, 8 * own), low),
            shape((4,) + w_t.shape, low),
        ],
        scratch_shapes=[pltpu.VMEM((2 * rows, width), low)] * 2
        + [pltpu.VMEM((width, 2 * rows), low)] * 2
        + [pltpu.VMEM((width, 2 * n), low)] * 2
        + [pltpu.VMEM((2 * rows, 2 * n), low)] * 2
        + [pltpu.VMEM((2 * rows, width), full)] * 2
        + [pltpu.VMEM((2, QB, 2 * n), full)] * 2
        + [pltpu.VMEM((width, width), low)]
        + [pltpu.VMEM((2, rows, width), low)] * 2
        + [pltpu.VMEM((2, 2, 2, width, n), low), pltpu.VMEM((2, 2, 2, width // dp, n), low)]
        + [pltpu.VMEM((12, HD, rows), low)]
        + [dma((4,)), dma((4,)), dma((3,)), dma((3,)), dma]
        + [dma((2, 2)), dma((2, 2)), dma((2,)), dma((2, 7)), dma((2, 7)), dma((2,))],
        compiler_params=pltpu.CompilerParams(
            vmem_limit_bytes=63 << 20, collective_id=5, has_side_effects=True
        ),
        name="feed",
    )(att, proj, tokens, cot, gains, w_t, up, down)


def per_device(tokens, segments, w_qkv, w_out, w_in, w_back, gain_attn, gain_mlp, cotangent):
    sequences, own, width = tokens.shape
    assert lax.axis_size("tensor") == 4 and lax.axis_size("context") == 2 and sequences == 3
    n = lax.axis_size("dp")
    length = segments.shape[1]
    shard = w_qkv.shape[0]
    local = w_qkv.shape[2]
    rows = sequences * own
    parts = w_qkv.transpose(1, 0, 2)
    gain_own = jnp.pad(jnp.stack([gain_attn, gain_mlp]), ((0, 14), (0, 0)))
    qkv, normed_units, w_t, up_part, out_part, gains, lo = project(
        n, tokens, segments, parts, w_in, w_out, gain_own
    )
    attended, log_totals, out_full, w_up, w_down, w_proj = attend(
        n, qkv, lo, out_part, up_part, w_back.T
    )
    flat = tokens.reshape(rows, width)
    result, grad_middle, grad_out, grad_up_down, part_sum, grad_units, w_all = feed(
        n, attended, w_proj, flat, cotangent.reshape(rows, width), gains, w_t, w_up, w_down
    )
    grad_projected, gw_sum, zsum, osum = attend_back(
        n, qkv, grad_units, lo, log_totals, out_full, normed_units, grad_up_down, part_sum, grad_out
    )
    grad_input, own_attn, own_up, own_down, own_proj, own_gains = last(
        n,
        grad_projected.reshape(12 * local, rows),
        w_all.reshape(12 * local, width),
        flat,
        grad_middle,
        gains,
        parts,
        w_in,
        jnp.pad(jnp.stack([gain_attn, gain_mlp], axis=1), ((0, 0), (0, 126))),
        gw_sum,
        zsum,
        osum,
    )
    result, grad_input, own_attn, own_proj, own_up, own_down = close(
        result, grad_input, own_attn, own_proj, own_up, own_down
    )
    return (
        result.reshape(sequences, own, width),
        grad_input.reshape(sequences, own, width),
        own_attn.transpose(1, 0, 2),
        own_proj,
        own_up,
        own_down.T,
        own_gains[:, 0],
        own_gains[:, 1],
    )


def solution(mesh):
    return jax.shard_map(
        per_device,
        mesh=mesh,
        in_specs=(
            P("dp", ("context", "tensor"), None),
            P("dp", None),
            P("dp", None, "tensor"),
            P("tensor", "dp"),
            P("dp", "tensor"),
            P("tensor", "dp"),
            P("dp"),
            P("dp"),
            P("dp", ("context", "tensor"), None),
        ),
        out_specs=(
            P("dp", ("context", "tensor"), None),
            P("dp", ("context", "tensor"), None),
            P("dp", None, "tensor"),
            P("tensor", "dp"),
            P("dp", "tensor"),
            P("tensor", "dp"),
            P("dp"),
            P("dp"),
        ),
        check_vma=False,
    )
```

```python
import functools
import math

import jax
import jax.numpy as jnp
from jax import lax
from jax.experimental import pallas as pl
from jax.experimental.pallas import tpu as pltpu
from jax.sharding import PartitionSpec as P

HD = 64
WIN = 1536
QB = 256
CHUNK = 128
NEG = -1e30
epsilon = 1e-06
low = jnp.bfloat16
full = jnp.float32


def dot(left, right, dims):
    return lax.dot_general(left, right, (dims, ((), ())), preferred_element_type=full)


def nn(left, right):
    return dot(left, right, ((1,), (0,)))


def nt(left, right):
    return dot(left, right, ((1,), (1,)))


def tn(left, right):
    return dot(left, right, ((0,), (0,)))


PEERS = [(dc, r) for dc in range(2) for r in range(4)]


def place():
    return lax.axis_index("context"), lax.axis_index("tensor")


def at_peer(c, t, dc, r):
    return {"context": c ^ dc, "tensor": t ^ r}


def greet(peers):
    for peer in peers:
        pl.semaphore_signal(pltpu.get_barrier_semaphore(), inc=1, device_id=peer)


def greeted(peers):
    pl.semaphore_wait(pltpu.get_barrier_semaphore(), len(peers))


def unit_place(u, c):
    return jnp.where(u < 3, u, c + u - 3), jnp.where(u < 3, 2 * c, 1)


def sends(u, c):
    return (u != 3) | (c == 0)


dma = pltpu.SemaphoreType.DMA
ANY = pl.BlockSpec(memory_space=pl.ANY)
VMEM = pl.BlockSpec(memory_space=pltpu.VMEM)
HBM = pl.BlockSpec(memory_space=pltpu.HBM)
shape = jax.ShapeDtypeStruct

class Line:
    def __init__(self, n, own, slot, send, recv):
        self.n, self.own, self.slot, self.sems = n, own, slot, (send, recv)
        self.d = lax.axis_index("dp")

    def along(self, k):
        m = self.d if k == 0 else self.n - 1 - self.d
        to = {"dp": jnp.clip(self.d + 1 if k == 0 else self.d - 1, 0, self.n - 1)}
        return m, to

    def target(self, k, step):
        m, _ = self.along(k)
        return jnp.clip(self.n - step + m if k == 0 else step - 1 - m, 0, self.n - 1)

    def copy(self, k, step, src):
        send, recv = self.sems
        _, to = self.along(k)
        return pltpu.make_async_remote_copy(
            src, self.slot(k, step), send.at[k, step - 1], recv.at[k, step - 1], device_id=to
        )

    def arrive(self, k, step):
        self.copy(k, step, self.slot(k, step)).wait_recv()

    def start(self, step, add):
        for k in range(2):
            m, _ = self.along(k)
            if step > 1:

                @pl.when((m >= 1) & (m < self.n - 1) & (step >= m + 1))
                def _():
                    add(k, self.target(k, step))
                    self.copy(k, step, self.slot(k, step - 1)).start()

            @pl.when(m == 0)
            def _():
                self.copy(k, step, self.own(self.target(k, step))).start()

    def received(self, step):
        for k in range(2):
            m, _ = self.along(k)

            @pl.when((m >= 1) & (step >= m))
            def _():
                self.arrive(k, step)

    def sent(self, step):
        for k in range(2):
            m, _ = self.along(k)

            @pl.when((m < self.n - 1) & (step >= m + 1))
            def _():
                self.copy(k, step, self.slot(k, step)).wait_send()


def greet_line(n, d):
    barrier = pltpu.get_barrier_semaphore()

    @pl.when(d > 0)
    def _():
        pl.semaphore_signal(barrier, inc=1, device_id={"dp": jnp.maximum(d - 1, 0)})

    @pl.when(d < n - 1)
    def _():
        pl.semaphore_signal(barrier, inc=1, device_id={"dp": jnp.minimum(d + 1, n - 1)})


def greeted_line(n, d, peers):
    ends = jnp.where(d > 0, 1, 0) + jnp.where(d < n - 1, 1, 0)
    pl.semaphore_wait(pltpu.get_barrier_semaphore(), len(peers) + ends)


def project_kernel(
    n, tokens, segments, w_qkv, up, out_own, gain_own, qkv, norm, w_t, up_all, out_all, gain_ref, lo_ref,
    tok, x, w, proj, out_w, gain, tsend, trecv, tlocal, wsend, wrecv, wlocal, osend, orecv, olocal, xsend, xrecv,
):
    c, t = place()
    d = lax.axis_index("dp")
    own = tokens.shape[1]
    width = tokens.shape[2]
    span = 4 * own
    shard = up.shape[0]
    half = own // 2
    hidden = up_all.shape[1]
    cut = n // 2
    to_x, to_y, to_core = {"tensor": t ^ 1}, {"tensor": t ^ 2}, {"context": 1 - c}
    others = [{"dp": lax.rem(d + r, n)} for r in range(1, n)]
    peers = [to_x, to_y, to_core] + others
    greet(peers)

    def local(i, s):
        return pltpu.make_async_copy(tokens.at[s], tok.at[s, t], tlocal.at[i])

    def weights(j, r):
        rows = pl.ds(pl.multiple_of(d * shard, shard), shard)
        source, target = (
            (w_qkv, w.at[:, rows]),
            (out_w, out_all.at[rows]),
            (up.at[:, pl.ds(pl.multiple_of(c * hidden, hidden), hidden)], up_all.at[rows]),
            (gain_own, gain.at[d]),
        )[j]
        if r == 0:
            return pltpu.make_async_copy(source, target, wlocal.at[j])
        return pltpu.make_async_remote_copy(
            source, target, wsend.at[j, r - 1], wrecv.at[j, r - 1], device_id=others[r - 1]
        )

    def gives(j, r):
        return lax.rem(d + n - r, n) // cut == c if j < 2 else True

    def weights_do(j, r, what, source=False):
        @pl.when(gives(j, 0 if source else r))
        def _():
            getattr(weights(j, r), what)()

    def to_other(j):
        rows = pl.ds(pl.multiple_of(c * cut * shard, shard), cut * shard)
        ref = w.at[:, rows]
        return pltpu.make_async_remote_copy(ref, ref, xsend, xrecv, device_id=to_core)

    order = (2 * (1 - c), 1, 2 * c)
    for i, s in enumerate(order):
        local(i, s).start()
    out_w[...] = out_own[...].T
    for j in range(4):
        weights_do(j, 0, "start")
    greeted(peers)
    for j in (0, 3, 1, 2):
        for r in range(1, n):
            weights_do(j, r, "start", True)

    def hop(k, i):
        s = order[i]
        origin, rows, peer = (
            (t, slice(0, half), to_x),
            (t, slice(half, own), to_y),
            (t, slice(0, half), to_y),
            (t, slice(half, own), to_x),
            (t ^ 1, slice(0, half), to_y),
            (t ^ 2, slice(half, own), to_x),
        )[k]
        there = tok.at[s, origin, rows]
        here = tokens.at[s, rows] if k < 4 else there
        return pltpu.make_async_remote_copy(
            here, there, tsend.at[k, i], trecv.at[k, i], device_id=peer
        )

    def straight(i):
        for k in range(4):
            hop(k, i).start()

    def forward(i):
        for k in range(2):
            hop(k, i).wait_recv()
            hop(k + 4, i).start()

    units = proj.shape[1]

    def leave(i):
        out = []
        lanes = pl.ds(pl.multiple_of(c * span, span), span)
        if i != 0:
            out.append((x.at[i], norm.at[2 - i, lanes], False))
        if i != 2:
            out.append((x.at[i], norm.at[i, lanes], True))
        if i == 0:
            out.append((proj.at[0], qkv.at[pl.ds(0, units), :, lanes], True))
        if i == 2:
            out.append((proj.at[2], qkv.at[pl.ds(0, units), :, lanes], False))
        if i == 1:
            for away in (True, False):
                core = 1 - c if away else c
                for p in range(3):
                    src = proj.at[1, pl.ds(p * 3 + core, 2)]
                    out.append((src, qkv.at[pl.ds(units + 2 * p, 2), :, lanes], away))
        copies = []
        for j, (src, dst, away) in enumerate(out):
            if away:
                copies.append(
                    (away, pltpu.make_async_remote_copy(src, dst, osend.at[i, j], orecv.at[i, j], device_id=to_core))
                )
            else:
                copies.append((away, pltpu.make_async_copy(src, dst, olocal.at[i, j])))
        return copies

    def work(i):
        s = order[i]
        local(i, s).wait()
        for k in range(2, 6):
            hop(k, i).wait_recv()
        for p in range(4):
            v = tok[s, p].astype(full)
            inv = lax.rsqrt(jnp.mean(v * v, axis=-1, keepdims=True) + epsilon)
            x[i, p * own : (p + 1) * own, :] = (v * inv * gain_ref[0:1, :]).astype(low)
        for p in range(4):
            rows = slice(p * own, (p + 1) * own)
            part = nt(w_t[...], x[i, rows, :]).astype(low)
            proj[i, :, :, rows] = part.reshape(units, HD, own)
        for _, copy in leave(i):
            copy.start()

    straight(0)
    straight(1)
    forward(0)
    straight(2)
    seg = segments[...]
    first = jnp.zeros(seg.shape, jnp.int32)
    for value in range(8):
        before = jnp.sum((seg < value).astype(jnp.int32), axis=1, keepdims=True)
        first = jnp.where(seg == value, before, first)
    first = jnp.maximum(first, lax.broadcasted_iota(jnp.int32, seg.shape, 1) - (WIN - 1))
    lo_ref[0] = jnp.where(c == 0, first[0:1], first[2:3])
    lo_ref[1] = first[1:2]
    weights_do(0, 0, "wait")
    for r in range(1, n):
        weights_do(0, r, "wait_recv")
    to_other(0).start()
    weights(3, 0).wait()
    for r in range(1, n):
        weights(3, r).wait_recv()
    gain_ref[...] = jnp.concatenate([gain[i].astype(full) for i in range(n)], axis=1)[:8]
    to_other(0).wait_recv()
    for p in range(3):
        w_t[p * 3 * HD : (p + 1) * 3 * HD, :] = w[p].T
    forward(1)
    work(0)
    forward(2)
    work(1)
    work(2)
    to_other(0).wait_send()
    for j in range(4):
        if j in (1, 2):
            weights_do(j, 0, "wait")
        for r in range(1, n):
            weights_do(j, r, "wait_send", True)
            if j in (1, 2):
                weights_do(j, r, "wait_recv")
    for i in range(3):
        for k in range(6):
            hop(k, i).wait_send()
        for away, copy in leave(i):
            copy.wait()


def project(n, tokens, segments, w_qkv, up, out_own, gain_own):
    sequences, own, width = tokens.shape
    shard, hidden = up.shape[0], up.shape[1] // 2
    local = out_own.shape[0]
    span = 4 * own
    return pl.pallas_call(
        functools.partial(project_kernel, n),
        in_specs=[HBM, VMEM, HBM, HBM, VMEM, VMEM],
        out_specs=[HBM] * 2 + [VMEM] + [HBM] * 2 + [VMEM] * 2,
        out_shape=[
            shape((15, HD, 2 * span), low),
            shape((2, 2 * span, width), low),
            shape((9 * HD, n * shard), low),
            shape((n * shard, hidden), low),
            shape((n * shard, local), low),
            shape((8, n * shard), full),
            shape((2, 1, segments.shape[1]), jnp.int32),
        ],
        scratch_shapes=[
            pltpu.VMEM((sequences, 4, own, width), low),
            pltpu.VMEM((sequences, span, width), low),
            pltpu.VMEM((3, n * shard, local), low),
            pltpu.VMEM((sequences, 9, HD, span), low),
            pltpu.VMEM((shard, local), low),
            pltpu.VMEM((n,) + gain_own.shape, low),
            dma((6, 3)), dma((6, 3)), dma((3,)),
            dma((4, n - 1)), dma((4, n - 1)), dma((4,)),
            dma((3, 8)), dma((3, 8)), dma((3, 8)), dma, dma,
        ],
        compiler_params=pltpu.CompilerParams(
            vmem_limit_bytes=63 << 20, collective_id=3, has_side_effects=True
        ),
        name="project",
    )(tokens, segments, w_qkv, up, out_own, gain_own)


UNITS = 5
def unit_block(part):
    return lambda u: (jnp.where(u < 3, part * 3 + u, 9 + part * 2 + (u - 3)), 0, 0)


def attend_kernel(
    n, q_ref, k_ref, v_ref, lo_ref, out_part, up_part, down_own, att, lse_ref, of_ref, up, down, out_w,
    qs, ks, ss, obuf, ssem, rsem, lsem, wsend, wrecv, wlocal, zsend, zrecv, fsend, frecv,
):
    u = pl.program_id(0)
    c, t = place()
    d = lax.axis_index("dp")
    shard = down_own.shape[0]
    hidden = down.shape[2]
    peers = [at_peer(c, t, dc, r) for dc, r in PEERS[1:]]

    part = out_part.shape[0] // 2
    mine = pl.ds(pl.multiple_of(c * part, part), part)

    def weight(j, r):
        rows = pl.ds(pl.multiple_of(d * shard, shard), shard)
        src, dst = (
            (down_own.at[:, pl.ds(pl.multiple_of(c * hidden, hidden), hidden)], down.at[t, rows]),
            (up_part, up.at[t]),
            (out_part.at[mine], out_w.at[t, mine]),
        )[j]
        if r == 0:
            return pltpu.make_async_copy(src, dst, wlocal.at[j])
        return pltpu.make_async_remote_copy(
            src, dst, wsend.at[j, r - 1], wrecv.at[j, r - 1], device_id={"tensor": t ^ r}
        )

    def onward(k):
        if k == 2:
            ref, peer = out_w.at[:, mine], {"context": 1 - c}
        else:
            rows = pl.ds(k * part, part)
            ref, peer = up.at[t ^ (1 + k), rows], {"tensor": t ^ (2 - k)}
        return pltpu.make_async_remote_copy(
            ref, ref, fsend.at[k], frecv.at[k], device_id=peer
        )

    def shards(step, up_line):
        src = d - step if up_line else d + step
        rows = pl.ds(pl.multiple_of(jnp.clip(src, 0, n - 1) * shard, shard), shard)
        to = jnp.clip(d + 1 if up_line else d - 1, 0, n - 1)
        k = 0 if up_line else 1
        return pltpu.make_async_remote_copy(
            down.at[:, rows], down.at[:, rows], zsend.at[k, step], zrecv.at[k, step], device_id={"dp": to}
        )

    def line(step, what):
        for up_line in (True, False):
            inside = (d < n - 1) if up_line else (d > 0)
            has = (d >= step) if up_line else (d <= n - 1 - step)
            comes = (d >= step + 1) if up_line else (d <= n - 2 - step)
            if what == "recv":

                @pl.when(comes)
                def _():
                    shards(step, up_line).wait_recv()
            else:

                @pl.when(inside & has)
                def _():
                    if what == "start":
                        shards(step, up_line).start()
                    else:
                        shards(step, up_line).wait_send()
    length = lo_ref.shape[2]
    half = length // 2
    own = half // 4

    @pl.when(u == 0)
    def _():
        greet(peers)
        greet_line(n, d)
        for j in range(3):
            weight(j, 0).start()
        greeted_line(n, d, peers)
        for r in range(1, 4):
            weight(0, r).start()

    qs[...] = q_ref[0] * low(0.125)
    ks[...] = k_ref[0].T
    for start in range(0, length, QB):
        stop = start + QB
        q = qs[:, start:stop]
        lo = lo_ref[0, :, start:stop]
        first = max(0, start - WIN)
        most = jnp.full((8, QB), NEG, full)
        for at in range(first, stop, CHUNK):
            s = nn(ks[at : at + CHUNK, :], q)
            key_pos = at + lax.broadcasted_iota(jnp.int32, (CHUNK, QB), 0)
            allowed = key_pos >= lo
            if at + CHUNK - 1 > start:
                allowed &= key_pos <= start + lax.broadcasted_iota(jnp.int32, (CHUNK, QB), 1)
            s = jnp.where(allowed, s, NEG)
            ss[at - first : at - first + CHUNK, :] = s
            most = jnp.maximum(most, jnp.max(s.reshape(CHUNK // 8, 8, QB), axis=0))
        most = jnp.max(most, axis=0, keepdims=True)
        total = jnp.zeros((8, QB), full)
        acc = jnp.zeros((HD, QB), full)
        for at in range(first, stop, CHUNK):
            p = jnp.exp(ss[at - first : at - first + CHUNK, :] - most)
            total += jnp.sum(p.reshape(CHUNK // 8, 8, QB), axis=0)
            acc += nn(v_ref[0, :, at : at + CHUNK], p.astype(low))
        total = jnp.sum(total, axis=0, keepdims=True)
        lse_ref[0, :, start:stop] = most + jnp.log(total)
        o = acc * (1.0 / total)
        of_ref[0, :, start:stop] = o
        obuf[u, :, start:stop] = o.astype(low)

    @pl.when(u == 0)
    def _():
        weight(0, 0).wait()
        for r in range(1, 4):
            weight(0, r).wait_recv()
        line(0, "start")
        for j, count in ((1, 3), (2, 4)):
            for r in range(1, count):
                weight(j, r).start()

    @pl.when(u == 3)
    def _():
        if n > 2:
            line(0, "recv")
            line(1, "start")
        for k in range(2):
            weight(1, 1 + k).wait_recv()
            onward(k).start()
        weight(2, 0).wait()
        for r in range(1, 4):
            weight(2, r).wait_recv()
        onward(2).start()

    def move(unit, i, source_core):
        dc, r = PEERS[i]
        h, seq = unit_place(unit, source_core)
        dest = pl.multiple_of(((c ^ dc) * 4 + (t ^ r)) * own, own)
        src = obuf.at[unit, :, pl.ds(dest, own)]
        dst = att.at[
            pl.ds(pl.multiple_of((t * 3 + h) * HD, HD), HD), pl.ds(pl.multiple_of(seq * own, own), own)
        ]
        if i == 0:
            return pltpu.make_async_copy(src, dst, lsem.at[unit])
        return pltpu.make_async_remote_copy(
            src, dst, ssem.at[i - 1, unit], rsem.at[i - 1, unit], device_id=at_peer(c, t, dc, r)
        )

    @pl.when(sends(u, c))
    def _():
        for i in range(1, len(PEERS)):
            move(u, i, c).start()
        move(u, 0, c).start()

    @pl.when(u == pl.num_programs(0) - 1)
    def _():
        for step in range(2, n - 1):
            line(step - 1, "recv")
            line(step, "start")
        line(n - 2, "recv")
        for step in range(n - 1):
            line(step, "sent")
        weight(1, 0).wait()
        for j in range(3):
            for r in range(1, 3 if j == 1 else 4):
                weight(j, r).wait_send()
        for k in range(3):
            onward(k).wait()
        for unit in range(UNITS):
            for i, (dc, r) in enumerate(PEERS):

                @pl.when(sends(unit, c))
                def _():
                    if i:
                        move(unit, i, c).wait_send()
                    else:
                        move(unit, i, c).wait()

                if i:

                    @pl.when(sends(unit, c ^ dc))
                    def _():
                        move(unit, i, c ^ dc).wait_recv()


def attend(n, qkv, lo, out_part, up_part, down_own):
    length = lo.shape[2]
    half = length // 2
    own = half // 4
    width, hidden = up_part.shape
    part = lambda p: pl.BlockSpec((1, HD, length), unit_block(p))
    unit = lambda rows, n: pl.BlockSpec((1, rows, n), lambda u: (u, 0, 0))
    heads = 4 * 3 * HD
    return pl.pallas_call(
        functools.partial(attend_kernel, n),
        grid=(UNITS,),
        in_specs=[part(0), part(1), part(2)]
        + [pl.BlockSpec((1, 1, length), lambda u: (u // 3, 0, 0))]
        + [
            pl.BlockSpec(a.shape, lambda u: (0, 0), pipeline_mode=pl.Buffered(1))
            for a in (out_part, up_part, down_own)
        ],
        out_specs=[HBM, unit(1, length), unit(HD, length)] + [HBM] * 3,
        scratch_shapes=[
            pltpu.VMEM((HD, length), low),
            pltpu.VMEM((length, HD), low),
            pltpu.VMEM((WIN + QB, QB), full),
            pltpu.VMEM((UNITS, HD, length), low),
            dma((7, UNITS)),
            dma((7, UNITS)),
            dma((UNITS,)),
            dma((3, 3)),
            dma((3, 3)),
            dma((3,)),
            dma((2, n - 1)),
            dma((2, n - 1)),
            dma((3,)),
            dma((3,)),
        ],
        out_shape=[
            jax.ShapeDtypeStruct((heads, 3 * own), low),
            jax.ShapeDtypeStruct((UNITS, 1, length), full),
            jax.ShapeDtypeStruct((UNITS, HD, length), full),
            shape((4, width, hidden), low),
            shape((4, width, hidden), low),
            shape((4,) + out_part.shape, low),
        ],
        compiler_params=pltpu.CompilerParams(
            vmem_limit_bytes=63 << 20, collective_id=1, has_side_effects=True
        ),
        cost_estimate=pl.CostEstimate(
            flops=UNITS * 18 * 2 * 256 * 1024 * 128, bytes_accessed=20 << 20, transcendentals=0
        ),
        name="attend",
    )(qkv, qkv, qkv, lo, out_part, up_part, down_own)


def add_to(ref, terms):
    for a in range(ref.shape[0]):
        for p in range(ref.shape[1]):
            ref[a, p] = (ref[a, p].astype(full) + terms(a, p).astype(full)).astype(low)


def attend_back_kernel(
    n, q_ref, k_ref, v_ref, lo_ref, lse_ref, of_ref, norm_ref, g_ref, gud, part_sum, gout,
    dall, gw_sum, zsum, osum,
    qs, ks, vs, grow, qrow, delta, dqs, dbuf, gw, gwx, gwr, zr, gud_v, obuf, ssem, rsem, lsem,
    zsend, zrecv, xsend, xrecv, osend, orecv, olocal, vlocal,
):
    u = pl.program_id(0)
    c, t = place()
    d = lax.axis_index("dp")
    shard = gud.shape[2] // n
    length = lo_ref.shape[2]
    own = length // 8
    peers = [at_peer(c, t, dc, r) for dc, r in PEERS[1:]]

    def rows_of(j):
        return pl.ds(pl.multiple_of(j * shard, shard), shard)

    def line_of(h):
        pair = pl.ds(2 * h, 2)
        return Line(
            n,
            lambda j: gud.at[:, pair, rows_of(j)],
            lambda k, step: zr.at[h, k, step - 1],
            zsend.at[h],
            zrecv.at[h],
        )

    lines = [line_of(0), line_of(1)]

    def step_of(h, step, arrived=True):
        if arrived and step > 1:
            lines[h].received(step - 1)

        def add(k, j):
            rows = rows_of(j)
            add_to(zr.at[h, k, step - 2], lambda a, p: gud_v[a, 2 * h + p, rows])

        lines[h].start(step, add)

    def finish(h):
        lines[h].received(n - 1)
        for step in range(2 if h == 0 else 1, n):
            lines[h].sent(step)
        for a in range(2):
            for p in range(2):
                total = gud_v[a, 2 * h + p, rows_of(d)].astype(full)
                up, down = (zr[h, k, n - 2, a, p].astype(full) for k in range(2))
                total += jnp.where(d > 0, up, 0.0) + jnp.where(d < n - 1, down, 0.0)
                zsum[a, 2 * h + p] = total.astype(low)

    part_rows = gout.shape[1] // 2

    def out_piece(i):
        dc, r = PEERS[i]
        src = gout.at[t ^ r, pl.ds(pl.multiple_of((c ^ dc) * part_rows, part_rows), part_rows)]
        if i == 0:
            return pltpu.make_async_copy(src, obuf.at[0], olocal)
        return pltpu.make_async_remote_copy(
            src, obuf.at[i], osend.at[i - 1], orecv.at[i - 1], device_id=at_peer(c, t, dc, r)
        )

    def other_core():
        return pltpu.make_async_remote_copy(
            gwx.at[1 - c], gwr, xsend, xrecv, device_id={"context": 1 - c}
        )

    def load(i):
        if i == 2:
            return pltpu.make_async_copy(gud, gud_v, vlocal.at[2])
        return pltpu.make_async_copy(part_sum.at[i], zr.at[0, i, 0], vlocal.at[i])

    @pl.when(u == 0)
    def _():
        greet(peers)
        greet_line(n, d)
        for i in range(3):
            load(i).start()
        gw[...] = jnp.zeros_like(gw)
        greeted_line(n, d, peers)
        for i in range(3):
            load(i).wait()
        step_of(0, 2, False)
        step_of(1, 1)
        for i in range(1, len(PEERS)):
            out_piece(i).start()
        out_piece(0).start()

    @pl.when(u == 2)
    def _():
        step_of(0, 3)

    @pl.when(u == 3)
    def _():
        step_of(1, 2)

    qs[...] = q_ref[0] * low(0.125)
    ks[...] = k_ref[0].T
    vs[...] = v_ref[0].T
    grow[...] = g_ref[0].T
    qrow[...] = qs[...].T
    delta[...] = jnp.sum(g_ref[0].astype(full) * of_ref[0], axis=0, keepdims=True)
    dqs[...] = jnp.zeros_like(dqs)
    for key_start in range(0, length, QB):
        rows = slice(key_start, key_start + QB)
        k, v, key_t = ks[rows, :], vs[rows, :], k_ref[0, :, rows]
        dk = jnp.zeros((QB, HD), full)
        dv = jnp.zeros((QB, HD), full)
        key_pos = key_start + lax.broadcasted_iota(jnp.int32, (QB, QB), 0)
        for start in range(key_start, min(key_start + WIN + QB, length), QB):
            cols = slice(start, start + QB)
            s = nn(k, qs[:, cols]) - lse_ref[0, :, cols]
            allowed = key_pos >= lo_ref[0, :, cols]
            if start == key_start:
                allowed &= key_pos <= start + lax.broadcasted_iota(jnp.int32, (QB, QB), 1)
            p = jnp.exp(jnp.where(allowed, s, NEG))
            dp = nn(v, g_ref[0, :, cols])
            ds = (p * (dp - delta[:, cols])).astype(low)
            dv += nn(p.astype(low), grow[cols, :])
            dk += nn(ds, qrow[cols, :])
            dqs[:, cols] += nn(key_t, ds)
        dbuf[u, 1, :, rows] = dk.T.astype(low)
        dbuf[u, 2, :, rows] = dv.T.astype(low)
    dbuf[u, 0] = (dqs[...] * 0.125).astype(low)

    def move(unit, i, source_core):
        dc, r = PEERS[i]
        h, seq = unit_place(unit, source_core)
        dest = pl.multiple_of(((c ^ dc) * 4 + (t ^ r)) * own, own)
        src = dbuf.at[unit, :, :, pl.ds(dest, own)]
        dst = dall.at[t, :, h, :, pl.ds(pl.multiple_of(seq * own, own), own)]
        if i == 0:
            return pltpu.make_async_copy(src, dst, lsem.at[unit])
        return pltpu.make_async_remote_copy(
            src, dst, ssem.at[i - 1, unit], rsem.at[i - 1, unit], device_id=at_peer(c, t, dc, r)
        )

    @pl.when(sends(u, c))
    def _():
        for i in range(1, len(PEERS)):
            move(u, i, c).start()
        move(u, 0, c).start()
        h, _ = unit_place(u, c)
        gw[h] += nn(dbuf[u].reshape(3 * HD, length), norm_ref[0])

    @pl.when(u == pl.num_programs(0) - 1)
    def _():
        wide_rows = [gw[h, p * HD : (p + 1) * HD, :] for p in range(3) for h in range(3)]
        gwx[0] = jnp.concatenate(wide_rows[:6], axis=0).T.astype(low)
        empty = jnp.zeros((3 * HD, gw.shape[2]), full)
        gwx[1] = jnp.concatenate(wide_rows[6:] + [empty], axis=0).T.astype(low)
        other_core().start()
        step_of(1, 3)
        out_piece(0).wait()
        for i in range(1, len(PEERS)):
            out_piece(i).wait()
        total = obuf[0].astype(full)
        for i in range(1, len(PEERS)):
            total += obuf[i].astype(full)
        osum[...] = total.astype(low)
        other_core().wait()
        gw_sum[...] = (gwx[c].astype(full) + gwr[...].astype(full)).astype(low)
        for step in range(4, n):
            step_of(0, step)
            step_of(1, step)
        finish(0)
        finish(1)
        for unit in range(UNITS):
            for i, (dc, r) in enumerate(PEERS):

                @pl.when(sends(unit, c))
                def _():
                    if i:
                        move(unit, i, c).wait_send()
                    else:
                        move(unit, i, c).wait()

                if i:

                    @pl.when(sends(unit, c ^ dc))
                    def _():
                        move(unit, i, c ^ dc).wait_recv()


def attend_back(n, qkv, grad_units, lo, lse, attended, normed, grad_up_down, part_sum, grad_out):
    length = lo.shape[2]
    own = length // 8
    width = normed.shape[2]
    shard, hidden = grad_up_down.shape[2] // n, grad_up_down.shape[3]
    out_rows, local = grad_out.shape[1] // 2, grad_out.shape[2]
    part = lambda p: pl.BlockSpec((1, HD, length), unit_block(p))
    unit = lambda rows, m: pl.BlockSpec((1, rows, m), lambda u: (u, 0, 0))
    once = lambda dims: pl.BlockSpec(dims, lambda u: (0,) * len(dims), pipeline_mode=pl.Buffered(1))
    wide, tall = pltpu.VMEM((HD, length), low), pltpu.VMEM((length, HD), low)
    results = [(width, 2 * 3 * HD), (2, 4, shard, hidden), (out_rows, local)]
    return pl.pallas_call(
        functools.partial(attend_back_kernel, n),
        grid=(UNITS,),
        in_specs=[part(0), part(1), part(2)]
        + [
            pl.BlockSpec((1, 1, length), lambda u: (u // 3, 0, 0)),
            unit(1, length),
            unit(HD, length),
            pl.BlockSpec((1, length, width), lambda u: (u // 3, 0, 0)),
            unit(HD, length),
        ]
        + [HBM] * 3,
        out_specs=[HBM] + [once(r) for r in results],
        scratch_shapes=[
            wide, tall, tall, tall, tall,
            pltpu.VMEM((1, length), full), pltpu.VMEM((HD, length), full),
            pltpu.VMEM((UNITS, 3, HD, length), low), pltpu.VMEM((3, 3 * HD, width), full),
            pltpu.VMEM((2, width, 6 * HD), low), pltpu.VMEM((width, 6 * HD), low),
            pltpu.VMEM((2, 2, n - 1, 2, 2, shard, hidden), low), pltpu.VMEM(grad_up_down.shape, low),
            pltpu.VMEM((8, out_rows, local), low),
            dma((7, UNITS)), dma((7, UNITS)), dma((UNITS,)),
            dma((2, 2, n - 1)), dma((2, 2, n - 1)), dma, dma, dma((7,)), dma((7,)), dma, dma((3,)),
        ],
        out_shape=[shape((4, 3, 3, HD, 3 * own), low)] + [shape(r, low) for r in results],
        compiler_params=pltpu.CompilerParams(
            vmem_limit_bytes=63 << 20, collective_id=2, has_side_effects=True
        ),
        name="attend_back",
    )(qkv, qkv, qkv, lo, lse, attended, normed, grad_units, grad_up_down, part_sum, grad_out)


def last_kernel(
    n, dqkv_ref, w_ref, tokens_ref, middle_ref, gains, w_own, up_own, gain_mine, gw_sum, zsum, osum,
    grad_in, g_qkv, g_up, g_down, g_out, g_gain,
    rg, rw, ro, down_n, out_t, mine, sums, dqkv, w_all, tokens, middle,
    gsend, grecv, wsend, wrecv, osend, orecv, lsem, csend, crecv, ssend, srecv, clocal, fetch,
):
    c, t = place()
    d = lax.axis_index("dp")
    shard, hidden = rw.shape[2], rw.shape[3]
    cut = n // 2
    group = [at_peer(c, t, dc, r) for dc, r in PEERS[1:]]
    others = [lax.rem(d + r, n) for r in range(1, n)]
    peers = group + [{"dp": o} for o in others]
    greet(peers)
    loads = [
        pltpu.make_async_copy(src, dst, fetch.at[i])
        for i, (src, dst) in enumerate(
            ((tokens_ref, tokens), (w_ref, w_all), (dqkv_ref, dqkv), (middle_ref, middle))
        )
    ]
    for copy in loads:
        copy.start()

    def rows_of(j):
        return pl.ds(pl.multiple_of(j * shard, shard), shard)

    narrow = slice(0, 256)

    def qkv_piece(r, core):
        src, dst = gw_sum.at[rows_of(d if r == 0 else others[r - 1])], rg.at[r]
        if core:
            src, dst = src.at[:, narrow], dst.at[:, narrow]
        if r == 0:
            return pltpu.make_async_copy(src, dst, lsem.at[0])
        return pltpu.make_async_remote_copy(
            src, dst, gsend.at[r - 1], grecv.at[r - 1], device_id={"dp": others[r - 1]}
        )

    def each_core(what):
        for core in range(2):

            @pl.when(c == core)
            def _():
                what(core)

    def up_piece(r):
        src, dst = zsum.at[:, t ^ r], rw.at[r]
        if r == 0:
            return pltpu.make_async_copy(src, dst, lsem.at[1])
        return pltpu.make_async_remote_copy(
            src, dst, wsend.at[r - 1], wrecv.at[r - 1], device_id={"tensor": t ^ r}
        )

    mine_out = d // cut == c

    def out_piece(r):
        to = d if r == 0 else others[r - 1]
        src, dst = osum.at[rows_of(lax.rem(to, cut))], ro.at[r]
        if r == 0:
            return pltpu.make_async_copy(src, dst, lsem.at[2])
        return pltpu.make_async_remote_copy(
            src, dst, osend.at[r - 1], orecv.at[r - 1], device_id={"dp": to}
        )

    def start_all(core):
        for r in range(1, n):
            qkv_piece(r, core).start()
        qkv_piece(0, core).start()

    greeted(peers)
    each_core(start_all)
    for r in range(1, 4):
        up_piece(r).start()
    up_piece(0).start()
    for r in range(1, n):

        @pl.when(others[r - 1] // cut == c)
        def _():
            out_piece(r).start()

    @pl.when(mine_out)
    def _():
        out_piece(0).start()

    for copy in loads:
        copy.wait()
    for m in range(0, tokens.shape[0], QB):
        rows = slice(m, m + QB)
        r = tn(dqkv[:, rows], w_all[...])
        v = tokens[rows, :].astype(full)
        inv = lax.rsqrt(jnp.mean(v * v, axis=-1, keepdims=True) + epsilon)
        rg_ = r * gains[0:1, :]
        grad = inv * (rg_ - v * (inv * inv * jnp.mean(rg_ * v, axis=-1, keepdims=True)))
        grad_in[rows, :] = (middle[rows, :] + grad).astype(low)

    def halves(j):
        half = pl.ds(pl.multiple_of(c * hidden, hidden), hidden)
        src, dst = (
            (mine.at[0], g_qkv.at[:, half]),
            (mine.at[1], g_up.at[:, half]),
            (down_n, g_down.at[:, half]),
            (out_t, g_out),
        )[j]
        return (
            pltpu.make_async_copy(src, dst, clocal.at[j]),
            pltpu.make_async_remote_copy(
                src, dst, csend.at[j], crecv.at[j], device_id={"context": 1 - c}
            ),
        )

    def deliver(j):
        for copy in halves(j):
            copy.start()

    up_piece(0).wait()
    for r in range(1, 4):
        up_piece(r).wait_recv()
    mine[1] = sum(rw[r, 0].astype(full) for r in range(4))
    down_n[...] = sum(rw[r, 1].astype(full) for r in range(4))
    deliver(1)
    deliver(2)

    @pl.when(mine_out)
    def _():
        out_piece(0).wait()
        for r in range(1, n):
            out_piece(r).wait_recv()
        out_t[...] = sum(ro[r].astype(full) for r in range(n)).T
        deliver(3)

    def take(core):
        qkv_piece(0, core).wait()
        for r in range(1, n):
            qkv_piece(r, core).wait_recv()
        if core:
            mine[0, :, narrow] = sum(rg[r, :, narrow].astype(full) for r in range(n))
            mine[0, :, 256:] = jnp.zeros((shard, hidden - 256), full)
        else:
            mine[0] = sum(rg[r].astype(full) for r in range(n))

    each_core(take)
    deliver(0)
    lane = lax.broadcasted_iota(jnp.int32, (shard, 128), 1)
    halves_of = [jnp.concatenate([w_own[0], w_own[1]], axis=1), jnp.pad(w_own[2], ((0, 0), (0, osum.shape[1])))]
    w_mine = jnp.where(c == 0, halves_of[0].astype(full), halves_of[1].astype(full))
    up_mine = up_own[:, pl.ds(pl.multiple_of(c * hidden, hidden), hidden)].astype(full)
    first = jnp.sum(w_mine * mine[0], axis=1, keepdims=True)
    second = jnp.sum(up_mine * mine[1], axis=1, keepdims=True)
    sums[0] = jnp.where(lane == 0, first, jnp.where(lane == 1, second, 0.0))

    def gain_piece(i):
        dc, r = PEERS[i]
        return pltpu.make_async_remote_copy(
            sums.at[0], sums.at[i], ssend.at[i - 1], srecv.at[i - 1], device_id=at_peer(c, t, dc, r)
        )

    for i in range(1, len(PEERS)):
        gain_piece(i).start()
    for i in range(1, len(PEERS)):
        gain_piece(i).wait()
    total = sum(sums[i] for i in range(len(PEERS)))
    g_gain[...] = total / jnp.where(lane < 2, gain_mine[...].astype(full), 1.0)

    for j in range(3):
        for copy in halves(j):
            copy.wait()

    @pl.when(mine_out)
    def _():
        local, away = halves(3)
        local.wait()
        away.wait_send()

    @pl.when(jnp.logical_not(mine_out))
    def _():
        halves(3)[1].wait_recv()

    for r in range(1, 4):
        up_piece(r).wait_send()

    def sent(core):
        for r in range(1, n):
            qkv_piece(r, core).wait_send()

    each_core(sent)
    for r in range(1, n):

        @pl.when(others[r - 1] // cut == c)
        def _():
            out_piece(r).wait_send()


def last(n, dqkv, w_all, tokens, middle, gains, w_own, up_own, gain_mine, gw_sum, zsum, osum):
    rows, width = tokens.shape
    _, _, shard, hidden = zsum.shape
    local = osum.shape[1]
    return pl.pallas_call(
        functools.partial(last_kernel, n),
        in_specs=[HBM] * 4 + [VMEM] * 4 + [ANY] * 3,
        out_specs=[VMEM] + [ANY] * 4 + [VMEM],
        out_shape=[
            shape((rows, width), low),
            shape((shard, 2 * hidden), full),
            shape((shard, 2 * hidden), full),
            shape((shard, 2 * hidden), full),
            shape((local, shard), full),
            shape((shard, 128), full),
        ],
        scratch_shapes=[
            pltpu.VMEM((n, shard, hidden), low),
            pltpu.VMEM((4, 2, shard, hidden), low),
            pltpu.VMEM((n, shard, local), low),
            pltpu.VMEM((shard, hidden), full),
            pltpu.VMEM((local, shard), full),
            pltpu.VMEM((2, shard, hidden), full),
            pltpu.VMEM((8, shard, 128), full),
            pltpu.VMEM(dqkv.shape, low), pltpu.VMEM(w_all.shape, low),
            pltpu.VMEM((rows, width), low), pltpu.VMEM((rows, width), full),
            dma((n - 1,)), dma((n - 1,)), dma((3,)), dma((3,)), dma((n - 1,)), dma((n - 1,)), dma((3,)),
            dma((4,)), dma((4,)), dma((7,)), dma((7,)), dma((4,)), dma((4,)),
        ],
        compiler_params=pltpu.CompilerParams(
            vmem_limit_bytes=63 << 20, collective_id=4, has_side_effects=True
        ),
        name="last",
    )(dqkv, w_all, tokens, middle, gains, w_own, up_own, gain_mine, gw_sum, zsum, osum)


def close_kernel(*refs):
    count = len(refs) // 2
    for i, (src, dst) in enumerate(zip(refs[:count], refs[count:])):
        if i == 2:
            local = dst.shape[2]
            for p in range(3):
                dst[p] = src[:, p * local : (p + 1) * local]
        else:
            dst[...] = src[...]


def close(result, grad_input, own_attn, *others):
    arrays = (result, grad_input, own_attn, *others)
    rows = lambda a: pl.BlockSpec((a.shape[0] // 2, a.shape[1]), lambda i: (i, 0))
    shard, local = own_attn.shape[0], others[0].shape[0]
    parts = pl.BlockSpec((3, shard // 2, local), lambda i: (0, i, 0))
    outs = [shape(a.shape, a.dtype) for a in arrays]
    outs[2] = shape((3, shard, local), full)
    return pl.pallas_call(
        close_kernel,
        grid=(2,),
        in_specs=[rows(a) for a in arrays],
        out_specs=[parts if i == 2 else rows(a) for i, a in enumerate(arrays)],
        out_shape=outs,
        compiler_params=pltpu.CompilerParams(vmem_limit_bytes=63 << 20),
        name="close",
    )(*arrays)


def gelu_and_slope(v):
    k0 = math.sqrt(2.0 / math.pi)
    square = v * v
    th = jnp.tanh(v * (k0 + (k0 * 0.044715) * square))
    half = 0.5 + 0.5 * th
    slope = half + (v * half) * ((1.0 - th) * (k0 + (3.0 * 0.044715 * k0) * square))
    return v * half, slope


def feed_kernel(
    dp, att, proj, tokens, cot, gains, w_t, up_ref, down_ref,
    result, middle, gout, gud, part_sum, units, w_all,
    x, g, x_t, g_t, up, down, act, gh, out, back, proj_w, sent, got, gbuf, gatt,
    xsend, xrecv, wsend, wrecv, wlocal, zsend, zrecv, glocal, usend, urecv, ulocal, load,
):
    c, t = place()
    d = lax.axis_index("dp")
    rows, width = tokens.shape
    own = rows // 3
    shard = width // dp
    n = up_ref.shape[2]
    local = proj.shape[2]
    other = {"context": 1 - c}
    peers = [at_peer(c, t, dc, r) for dc, r in PEERS[1:]]
    mine, theirs = slice(0, rows), slice(rows, 2 * rows)
    block = rows // 3

    def cross(k):
        src, dst = (
            (cot, g.at[theirs]),
            (x.at[mine], x.at[theirs]),
            (sent.at[0], got.at[0]),
            (sent.at[1], got.at[1]),
        )[k]
        return pltpu.make_async_remote_copy(src, dst, xsend.at[k], xrecv.at[k], device_id=other)

    half = pl.ds(pl.multiple_of(c * (w_t.shape[0] // 2), 8), w_t.shape[0] // 2)

    def over_tensor(r):
        if r == 4:
            ref = w_all.at[:, half]
            return pltpu.make_async_remote_copy(ref, ref, wsend.at[3], wrecv.at[3], device_id=other)
        src, dst = w_t.at[half], w_all.at[t, half]
        if r == 0:
            return pltpu.make_async_copy(src, dst, wlocal)
        return pltpu.make_async_remote_copy(
            src, dst, wsend.at[r - 1], wrecv.at[r - 1], device_id={"tensor": t ^ r}
        )

    def rows_of(i):
        return pl.ds(pl.multiple_of(i * shard, shard), shard)

    line = Line(
        dp,
        lambda i: gbuf.at[0, :, :, rows_of(i)],
        lambda k, step: part_sum.at[k],
        zsend,
        zrecv,
    )

    def keep(j):
        return pltpu.make_async_copy(gbuf.at[j], gud.at[:, pl.ds(2 * j, 2)], glocal.at[j])

    def leave(whole, i):
        dc, r = PEERS[i]
        to_c, to_t = c ^ dc, t ^ r
        head = to_t * 3 + (0 if whole else to_c)
        count, first = (3, 0) if whole else (2, 3)
        seq = 2 * to_c if whole else 1
        src = gatt.at[pl.ds(head, count), :, pl.ds(pl.multiple_of(seq * own, own), own)]
        dst = units.at[pl.ds(first, count), :, pl.ds(pl.multiple_of((c * 4 + t) * own, own), own)]
        k = 0 if whole else 1
        if i == 0:
            return pltpu.make_async_copy(src, dst, ulocal.at[k])
        return pltpu.make_async_remote_copy(
            src, dst, usend.at[k, i - 1], urecv.at[k, i - 1], device_id=at_peer(c, t, dc, r)
        )

    loads = [
        pltpu.make_async_copy(ref.at[p], dst.at[p // 2, :, pl.ds((p % 2) * n, n)], load.at[i, p])
        for i, (ref, dst) in enumerate(((up_ref, up), (down_ref, down)))
        for p in range(4)
    ]
    greet(peers)
    greet_line(dp, d)
    for copy in loads:
        copy.start()
    for p in range(4):
        proj_w[:, p * local : (p + 1) * local] = proj[p]
    greeted_line(dp, d, peers)
    cross(0).start()
    for r in range(1, 4):
        over_tensor(r).start()
    over_tensor(0).start()
    for m in range(0, rows, block):
        part = slice(m, m + block)
        v = tokens[part, :].astype(full) + nn(proj_w[...], att[:, part]).T
        middle[part, :] = v
        inv = lax.rsqrt(jnp.mean(v * v, axis=-1, keepdims=True) + epsilon)
        x[part, :] = (v * inv * gains[1:2, :]).astype(low)
    cross(1).start()
    g[mine, :] = cot[...]
    g_t[:, mine] = cot[...].T
    x_t[:, mine] = x[mine, :].T
    for copy in loads:
        copy.wait()

    def hidden(side):
        @pl.loop(0, 6)
        def _(i):
            j = i // 3
            part = pl.ds(pl.multiple_of((side * 3 + i % 3) * block, block), block)
            pre = nn(x[part, :], up[j])
            ga = nn(g[part, :], down[j])
            a, slope = gelu_and_slope(pre)
            act[j, part, :] = a.astype(low)
            gh[j, part, :] = (ga * slope).astype(low)

    def branch(left, right, part):
        return nt(left[0, part, :], right[0]) + nt(left[1, part, :], right[1])

    hidden(0)
    cross(0).wait_recv()
    cross(1).wait_recv()
    hidden(1)

    def cut(side, left, right, put):
        @pl.loop(0, 3)
        def _(i):
            here = pl.ds(pl.multiple_of(i * block, block), block)
            part = pl.ds(pl.multiple_of(side * rows + i * block, block), block)
            put(here, branch(left, right, part))

    def put_sent(k):
        def put(here, value):
            sent[k, here, :] = value.astype(low)

        return put

    def put_own(ref):
        def put(here, value):
            ref[here, :] = value

        return put

    cut(1, gh, up, put_sent(0))
    cross(2).start()
    cut(0, gh, up, put_own(back))
    over_tensor(0).wait()
    for r in range(1, 4):
        over_tensor(r).wait_recv()
    over_tensor(4).start()
    x_t[:, theirs] = x[theirs, :].T
    g_t[:, theirs] = g[theirs, :].T
    cross(2).wait_recv()
    gain = gains[1:2, :]
    low_t = x
    for m in range(0, rows, block):
        part = slice(m, m + block)
        r = (back[part, :] + got[0, part, :].astype(full)) * gain
        v = middle[part, :]
        inv = lax.rsqrt(jnp.mean(v * v, axis=-1, keepdims=True) + epsilon)
        grad = inv * (r - v * (inv * inv * jnp.mean(r * v, axis=-1, keepdims=True)))
        back[part, :] = cot[part, :].astype(full) + grad
        low_t[rows : rows + width, part] = back[part, :].astype(low).T
        grad = tn(proj_w[...], low_t[rows : rows + width, part]).astype(low)
        gatt[:, :, part] = grad.reshape(gatt.shape[0], HD, block)
    for whole in (True, False):
        for i in range(1, len(PEERS)):
            leave(whole, i).start()
        leave(whole, 0).start()

    def weight_grad(j, a, left_t, right):
        @pl.loop(0, 3)
        def _(i):
            part = pl.ds(pl.multiple_of(i * (width // 3), width // 3), width // 3)
            grad = nn(left_t[part, :], right[j]).astype(low)
            for p in range(2):
                gbuf[j, a, p, part, :] = grad[:, p * n : (p + 1) * n]

    weight_grad(0, 0, x_t, gh)
    weight_grad(0, 1, g_t, act)
    line.start(1, None)
    keep(0).start()
    cut(1, act, down, put_sent(1))
    cross(3).start()
    weight_grad(1, 0, x_t, gh)
    weight_grad(1, 1, g_t, act)
    keep(1).start()
    cut(0, act, down, put_own(out))
    for m in range(0, width, block):
        part = slice(m, m + block)
        big = nt(low_t[rows + m : rows + m + block, :], att[...]).astype(low)
        for p in range(4):
            gout[p, part, :] = big[:, p * local : (p + 1) * local]
    cross(3).wait_recv()
    result[...] = (middle[...] + out[...] + got[1].astype(full)).astype(low)
    middle[...] = back[...]
    for k in range(4):
        cross(k).wait_send()
    for r in range(1, 4):
        over_tensor(r).wait_send()
    over_tensor(4).wait()
    line.received(1)
    line.sent(1)
    for j in range(2):
        keep(j).wait()
    for whole in (True, False):
        for i in range(len(PEERS)):
            leave(whole, i).wait()


def feed(dp, att, proj, tokens, cot, gains, w_t, up, down):
    rows, width = tokens.shape
    pieces, _, n = up.shape
    own = rows // 3
    assert pieces == 4 and dp > 2 and rows == width
    return pl.pallas_call(
        functools.partial(feed_kernel, dp),
        in_specs=[VMEM] * 6 + [HBM] * 2,
        out_specs=[VMEM] * 3 + [HBM] * 4,
        out_shape=[
            shape((rows, width), low),
            shape((rows, width), full),
            shape(proj.shape, low),
            shape((2,) + up.shape, low),
            shape((2, 2, 2, width // dp, n), low),
            shape((UNITS, HD, 8 * own), low),
            shape((4,) + w_t.shape, low),
        ],
        scratch_shapes=[pltpu.VMEM((2 * rows, width), low)] * 2
        + [pltpu.VMEM((width, 2 * rows), low)] * 2
        + [pltpu.VMEM((2, width, 2 * n), low)] * 2
        + [pltpu.VMEM((2, 2 * rows, 2 * n), low)] * 2
        + [pltpu.VMEM((rows, width), full)] * 2
        + [pltpu.VMEM((width, width), low)]
        + [pltpu.VMEM((2, rows, width), low)] * 2
        + [pltpu.VMEM((2, 2, 2, width, n), low)]
        + [pltpu.VMEM((12, HD, rows), low)]
        + [dma((4,)), dma((4,)), dma((4,)), dma((4,)), dma]
        + [dma((2, 1)), dma((2, 1)), dma((2,)), dma((2, 7)), dma((2, 7)), dma((2,)), dma((2, 4))],
        compiler_params=pltpu.CompilerParams(
            vmem_limit_bytes=63 << 20, collective_id=5, has_side_effects=True
        ),
        name="feed",
    )(att, proj, tokens, cot, gains, w_t, up, down)


def per_device(tokens, segments, w_qkv, w_out, w_in, w_back, gain_attn, gain_mlp, cotangent):
    sequences, own, width = tokens.shape
    assert lax.axis_size("tensor") == 4 and lax.axis_size("context") == 2 and sequences == 3
    n = lax.axis_size("dp")
    length = segments.shape[1]
    shard = w_qkv.shape[0]
    local = w_qkv.shape[2]
    rows = sequences * own
    parts = w_qkv.transpose(1, 0, 2)
    gain_own = jnp.pad(jnp.stack([gain_attn, gain_mlp]), ((0, 14), (0, 0)))
    qkv, normed_units, w_t, up_part, out_part, gains, lo = project(
        n, tokens, segments, parts, w_in, w_out, gain_own
    )
    attended, log_totals, out_full, w_up, w_down, w_proj = attend(
        n, qkv, lo, out_part, up_part, w_back.T
    )
    flat = tokens.reshape(rows, width)
    result, grad_middle, grad_out, grad_up_down, part_sum, grad_units, w_all = feed(
        n, attended, w_proj, flat, cotangent.reshape(rows, width), gains, w_t, w_up, w_down
    )
    grad_projected, gw_sum, zsum, osum = attend_back(
        n, qkv, grad_units, lo, log_totals, out_full, normed_units, grad_up_down, part_sum, grad_out
    )
    grad_input, own_attn, own_up, own_down, own_proj, own_gains = last(
        n,
        grad_projected.reshape(12 * local, rows),
        w_all.reshape(12 * local, width),
        flat,
        grad_middle,
        gains,
        parts,
        w_in,
        jnp.pad(jnp.stack([gain_attn, gain_mlp], axis=1), ((0, 0), (0, 126))),
        gw_sum,
        zsum,
        osum,
    )
    result, grad_input, own_attn, own_proj, own_up, own_down = close(
        result, grad_input, own_attn, own_proj, own_up, own_down
    )
    return (
        result.reshape(sequences, own, width),
        grad_input.reshape(sequences, own, width),
        own_attn.transpose(1, 0, 2),
        own_proj,
        own_up,
        own_down.T,
        own_gains[:, 0],
        own_gains[:, 1],
    )


def solution(mesh):
    return jax.shard_map(
        per_device,
        mesh=mesh,
        in_specs=(
            P("dp", ("context", "tensor"), None),
            P("dp", None),
            P("dp", None, "tensor"),
            P("tensor", "dp"),
            P("dp", "tensor"),
            P("tensor", "dp"),
            P("dp"),
            P("dp"),
            P("dp", ("context", "tensor"), None),
        ),
        out_specs=(
            P("dp", ("context", "tensor"), None),
            P("dp", ("context", "tensor"), None),
            P("dp", None, "tensor"),
            P("tensor", "dp"),
            P("dp", "tensor"),
            P("tensor", "dp"),
            P("dp"),
            P("dp"),
        ),
        check_vma=False,
    )
```

```python
import functools
import math

import jax
import jax.numpy as jnp
from jax import lax
from jax.experimental import pallas as pl
from jax.experimental.pallas import tpu as pltpu
from jax.sharding import PartitionSpec as P

HD = 64
WIN = 1536
QB = 256
CHUNK = 128
NEG = -1e30
epsilon = 1e-06
low = jnp.bfloat16
full = jnp.float32


def dot(left, right, dims):
    return lax.dot_general(left, right, (dims, ((), ())), preferred_element_type=full)


def nn(left, right):
    return dot(left, right, ((1,), (0,)))


def nt(left, right):
    return dot(left, right, ((1,), (1,)))


def tn(left, right):
    return dot(left, right, ((0,), (0,)))


PEERS = [(dc, r) for dc in range(2) for r in range(4)]


def place():
    return lax.axis_index("context"), lax.axis_index("tensor")


def at_peer(c, t, dc, r):
    return {"context": c ^ dc, "tensor": t ^ r}


def greet(peers):
    for peer in peers:
        pl.semaphore_signal(pltpu.get_barrier_semaphore(), inc=1, device_id=peer)


def greeted(peers):
    pl.semaphore_wait(pltpu.get_barrier_semaphore(), len(peers))


def unit_place(u, c):
    return jnp.where(u < 3, u, c + u - 3), jnp.where(u < 3, 2 * c, 1)


def sends(u, c):
    return (u != 3) | (c == 0)


dma = pltpu.SemaphoreType.DMA
ANY = pl.BlockSpec(memory_space=pl.ANY)
VMEM = pl.BlockSpec(memory_space=pltpu.VMEM)
HBM = pl.BlockSpec(memory_space=pltpu.HBM)
shape = jax.ShapeDtypeStruct

class Line:
    def __init__(self, n, own, slot, send, recv):
        self.n, self.own, self.slot, self.sems = n, own, slot, (send, recv)
        self.d = lax.axis_index("dp")

    def along(self, k):
        m = self.d if k == 0 else self.n - 1 - self.d
        to = {"dp": jnp.clip(self.d + 1 if k == 0 else self.d - 1, 0, self.n - 1)}
        return m, to

    def target(self, k, step):
        m, _ = self.along(k)
        return jnp.clip(self.n - step + m if k == 0 else step - 1 - m, 0, self.n - 1)

    def copy(self, k, step, src):
        send, recv = self.sems
        _, to = self.along(k)
        return pltpu.make_async_remote_copy(
            src, self.slot(k, step), send.at[k, step - 1], recv.at[k, step - 1], device_id=to
        )

    def arrive(self, k, step):
        self.copy(k, step, self.slot(k, step)).wait_recv()

    def start(self, step, add):
        for k in range(2):
            m, _ = self.along(k)
            if step > 1:

                @pl.when((m >= 1) & (m < self.n - 1) & (step >= m + 1))
                def _():
                    add(k, self.target(k, step))
                    self.copy(k, step, self.slot(k, step - 1)).start()

            @pl.when(m == 0)
            def _():
                self.copy(k, step, self.own(self.target(k, step))).start()

    def received(self, step):
        for k in range(2):
            m, _ = self.along(k)

            @pl.when((m >= 1) & (step >= m))
            def _():
                self.arrive(k, step)

    def sent(self, step):
        for k in range(2):
            m, _ = self.along(k)

            @pl.when((m < self.n - 1) & (step >= m + 1))
            def _():
                self.copy(k, step, self.slot(k, step)).wait_send()


def greet_line(n, d):
    barrier = pltpu.get_barrier_semaphore()

    @pl.when(d > 0)
    def _():
        pl.semaphore_signal(barrier, inc=1, device_id={"dp": jnp.maximum(d - 1, 0)})

    @pl.when(d < n - 1)
    def _():
        pl.semaphore_signal(barrier, inc=1, device_id={"dp": jnp.minimum(d + 1, n - 1)})


def greeted_line(n, d, peers):
    ends = jnp.where(d > 0, 1, 0) + jnp.where(d < n - 1, 1, 0)
    pl.semaphore_wait(pltpu.get_barrier_semaphore(), len(peers) + ends)


def project_kernel(
    n, tokens, segments, w_qkv, up, out_own, gain_one, gain_two, qkv, norm, w_t, up_all, out_all, gain_ref, lo_ref,
    tok, x, w, proj, out_w, gain, own_gain, tsend, trecv, tlocal, wsend, wrecv, wlocal, osend, orecv, olocal, xsend, xrecv,
):
    c, t = place()
    d = lax.axis_index("dp")
    own = tokens.shape[1]
    width = tokens.shape[2]
    span = 4 * own
    shard = up.shape[0]
    half = own // 2
    hidden = up_all.shape[1]
    cut = n // 2
    to_x, to_y, to_core = {"tensor": t ^ 1}, {"tensor": t ^ 2}, {"context": 1 - c}
    others = [{"dp": lax.rem(d + r, n)} for r in range(1, n)]
    peers = [to_x, to_y, to_core] + others
    greet(peers)

    def local(i, s):
        return pltpu.make_async_copy(tokens.at[s], tok.at[s, t], tlocal.at[i])

    def weights(j, r):
        rows = pl.ds(pl.multiple_of(d * shard, shard), shard)
        source, target = (
            (w_qkv, w.at[:, rows]),
            (out_w, out_all.at[rows]),
            (up.at[:, pl.ds(pl.multiple_of(c * hidden, hidden), hidden)], up_all.at[rows]),
            (own_gain, gain.at[d]),
        )[j]
        if r == 0:
            return pltpu.make_async_copy(source, target, wlocal.at[j])
        return pltpu.make_async_remote_copy(
            source, target, wsend.at[j, r - 1], wrecv.at[j, r - 1], device_id=others[r - 1]
        )

    def gives(j, r):
        return lax.rem(d + n - r, n) // cut == c if j < 2 else True

    def weights_do(j, r, what, source=False):
        @pl.when(gives(j, 0 if source else r))
        def _():
            getattr(weights(j, r), what)()

    def to_other(j):
        rows = pl.ds(pl.multiple_of(c * cut * shard, shard), cut * shard)
        ref = w.at[:, rows]
        return pltpu.make_async_remote_copy(ref, ref, xsend, xrecv, device_id=to_core)

    order = (2 * (1 - c), 1, 2 * c)
    for i, s in enumerate(order):
        local(i, s).start()
    out_w[...] = out_own[...].T
    own_gain[...] = jnp.zeros_like(own_gain)
    own_gain[0:1, :] = gain_one[...]
    own_gain[1:2, :] = gain_two[...]
    for j in range(4):
        weights_do(j, 0, "start")
    greeted(peers)
    for j in (0, 3, 1, 2):
        for r in range(1, n):
            weights_do(j, r, "start", True)

    def hop(k, i):
        s = order[i]
        origin, rows, peer = (
            (t, slice(0, half), to_x),
            (t, slice(half, own), to_y),
            (t, slice(0, half), to_y),
            (t, slice(half, own), to_x),
            (t ^ 1, slice(0, half), to_y),
            (t ^ 2, slice(half, own), to_x),
        )[k]
        there = tok.at[s, origin, rows]
        here = tokens.at[s, rows] if k < 4 else there
        return pltpu.make_async_remote_copy(
            here, there, tsend.at[k, i], trecv.at[k, i], device_id=peer
        )

    def straight(i):
        for k in range(4):
            hop(k, i).start()

    def forward(i):
        for k in range(2):
            hop(k, i).wait_recv()
            hop(k + 4, i).start()

    units = proj.shape[1]

    def leave(i):
        out = []
        lanes = pl.ds(pl.multiple_of(c * span, span), span)
        if i != 0:
            out.append((x.at[i], norm.at[2 - i, lanes], False))
        if i != 2:
            out.append((x.at[i], norm.at[i, lanes], True))
        if i == 0:
            out.append((proj.at[0], qkv.at[pl.ds(0, units), :, lanes], True))
        if i == 2:
            out.append((proj.at[2], qkv.at[pl.ds(0, units), :, lanes], False))
        if i == 1:
            for away in (True, False):
                core = 1 - c if away else c
                for p in range(3):
                    src = proj.at[1, pl.ds(p * 3 + core, 2)]
                    out.append((src, qkv.at[pl.ds(units + 2 * p, 2), :, lanes], away))
        copies = []
        for j, (src, dst, away) in enumerate(out):
            if away:
                copies.append(
                    (away, pltpu.make_async_remote_copy(src, dst, osend.at[i, j], orecv.at[i, j], device_id=to_core))
                )
            else:
                copies.append((away, pltpu.make_async_copy(src, dst, olocal.at[i, j])))
        return copies

    def work(i):
        s = order[i]
        local(i, s).wait()
        for k in range(2, 6):
            hop(k, i).wait_recv()
        for p in range(4):
            v = tok[s, p].astype(full)
            inv = lax.rsqrt(jnp.mean(v * v, axis=-1, keepdims=True) + epsilon)
            x[i, p * own : (p + 1) * own, :] = (v * inv * gain_ref[0:1, :]).astype(low)
        for p in range(4):
            rows = slice(p * own, (p + 1) * own)
            part = nt(w_t[...], x[i, rows, :]).astype(low)
            proj[i, :, :, rows] = part.reshape(units, HD, own)
        for _, copy in leave(i):
            copy.start()

    straight(0)
    straight(1)
    forward(0)
    straight(2)
    seg = segments[...]
    first = jnp.zeros(seg.shape, jnp.int32)
    for value in range(8):
        before = jnp.sum((seg < value).astype(jnp.int32), axis=1, keepdims=True)
        first = jnp.where(seg == value, before, first)
    first = jnp.maximum(first, lax.broadcasted_iota(jnp.int32, seg.shape, 1) - (WIN - 1))
    lo_ref[0] = jnp.where(c == 0, first[0:1], first[2:3])
    lo_ref[1] = first[1:2]
    weights_do(0, 0, "wait")
    for r in range(1, n):
        weights_do(0, r, "wait_recv")
    to_other(0).start()
    weights(3, 0).wait()
    for r in range(1, n):
        weights(3, r).wait_recv()
    gain_ref[...] = jnp.concatenate([gain[i].astype(full) for i in range(n)], axis=1)[:8]
    to_other(0).wait_recv()
    for p in range(3):
        w_t[p * 3 * HD : (p + 1) * 3 * HD, :] = w[p].T
    forward(1)
    work(0)
    forward(2)
    work(1)
    work(2)
    to_other(0).wait_send()
    for j in range(4):
        if j in (1, 2):
            weights_do(j, 0, "wait")
        for r in range(1, n):
            weights_do(j, r, "wait_send", True)
            if j in (1, 2):
                weights_do(j, r, "wait_recv")
    for i in range(3):
        for k in range(6):
            hop(k, i).wait_send()
        for away, copy in leave(i):
            copy.wait()


def project(n, tokens, segments, w_qkv, up, out_own, gain_one, gain_two):
    sequences, own, width = tokens.shape
    shard, hidden = up.shape[0], up.shape[1] // 2
    local = out_own.shape[0]
    span = 4 * own
    return pl.pallas_call(
        functools.partial(project_kernel, n),
        in_specs=[HBM, VMEM, HBM, HBM, VMEM, VMEM, VMEM],
        out_specs=[HBM] * 2 + [VMEM] + [HBM] * 2 + [VMEM] * 2,
        out_shape=[
            shape((15, HD, 2 * span), low),
            shape((2, 2 * span, width), low),
            shape((9 * HD, n * shard), low),
            shape((n * shard, hidden), low),
            shape((n * shard, local), low),
            shape((8, n * shard), full),
            shape((2, 1, segments.shape[1]), jnp.int32),
        ],
        scratch_shapes=[
            pltpu.VMEM((sequences, 4, own, width), low),
            pltpu.VMEM((sequences, span, width), low),
            pltpu.VMEM((3, n * shard, local), low),
            pltpu.VMEM((sequences, 9, HD, span), low),
            pltpu.VMEM((shard, local), low),
            pltpu.VMEM((n, 16, shard), low),
            pltpu.VMEM((16, shard), low),
            dma((6, 3)), dma((6, 3)), dma((3,)),
            dma((4, n - 1)), dma((4, n - 1)), dma((4,)),
            dma((3, 8)), dma((3, 8)), dma((3, 8)), dma, dma,
        ],
        compiler_params=pltpu.CompilerParams(
            vmem_limit_bytes=63 << 20, collective_id=3, has_side_effects=True
        ),
        name="project",
    )(tokens, segments, w_qkv, up, out_own, gain_one, gain_two)


UNITS = 5
def unit_block(part):
    return lambda u: (jnp.where(u < 3, part * 3 + u, 9 + part * 2 + (u - 3)), 0, 0)


def attend_kernel(
    n, q_ref, k_ref, v_ref, lo_ref, out_part, up_part, down_own, att, lse_ref, of_ref, up, down, out_w,
    qs, ks, ss, obuf, ssem, rsem, lsem, wsend, wrecv, wlocal, zsend, zrecv, fsend, frecv,
):
    u = pl.program_id(0)
    c, t = place()
    d = lax.axis_index("dp")
    shard = down_own.shape[0]
    hidden = down.shape[2]
    peers = [at_peer(c, t, dc, r) for dc, r in PEERS[1:]]

    part = out_part.shape[0] // 2
    mine = pl.ds(pl.multiple_of(c * part, part), part)

    def weight(j, r):
        rows = pl.ds(pl.multiple_of(d * shard, shard), shard)
        src, dst = (
            (down_own.at[:, pl.ds(pl.multiple_of(c * hidden, hidden), hidden)], down.at[t, rows]),
            (up_part, up.at[t]),
            (out_part.at[mine], out_w.at[t, mine]),
        )[j]
        if r == 0:
            return pltpu.make_async_copy(src, dst, wlocal.at[j])
        return pltpu.make_async_remote_copy(
            src, dst, wsend.at[j, r - 1], wrecv.at[j, r - 1], device_id={"tensor": t ^ r}
        )

    def onward(k):
        if k == 2:
            ref, peer = out_w.at[:, mine], {"context": 1 - c}
        else:
            rows = pl.ds(k * part, part)
            ref, peer = up.at[t ^ (1 + k), rows], {"tensor": t ^ (2 - k)}
        return pltpu.make_async_remote_copy(
            ref, ref, fsend.at[k], frecv.at[k], device_id=peer
        )

    def shards(step, up_line):
        src = d - step if up_line else d + step
        rows = pl.ds(pl.multiple_of(jnp.clip(src, 0, n - 1) * shard, shard), shard)
        to = jnp.clip(d + 1 if up_line else d - 1, 0, n - 1)
        k = 0 if up_line else 1
        return pltpu.make_async_remote_copy(
            down.at[:, rows], down.at[:, rows], zsend.at[k, step], zrecv.at[k, step], device_id={"dp": to}
        )

    def line(step, what):
        for up_line in (True, False):
            inside = (d < n - 1) if up_line else (d > 0)
            has = (d >= step) if up_line else (d <= n - 1 - step)
            comes = (d >= step + 1) if up_line else (d <= n - 2 - step)
            if what == "recv":

                @pl.when(comes)
                def _():
                    shards(step, up_line).wait_recv()
            else:

                @pl.when(inside & has)
                def _():
                    if what == "start":
                        shards(step, up_line).start()
                    else:
                        shards(step, up_line).wait_send()
    length = lo_ref.shape[2]
    half = length // 2
    own = half // 4

    @pl.when(u == 0)
    def _():
        greet(peers)
        greet_line(n, d)
        for j in range(3):
            weight(j, 0).start()
        greeted_line(n, d, peers)
        for r in range(1, 4):
            weight(0, r).start()

    qs[...] = q_ref[0] * low(0.125)
    ks[...] = k_ref[0].T
    for start in range(0, length, QB):
        stop = start + QB
        q = qs[:, start:stop]
        lo = lo_ref[0, :, start:stop]
        first = max(0, start - WIN)
        most = jnp.full((8, QB), NEG, full)
        for at in range(first, stop, CHUNK):
            s = nn(ks[at : at + CHUNK, :], q)
            key_pos = at + lax.broadcasted_iota(jnp.int32, (CHUNK, QB), 0)
            allowed = key_pos >= lo
            if at + CHUNK - 1 > start:
                allowed &= key_pos <= start + lax.broadcasted_iota(jnp.int32, (CHUNK, QB), 1)
            s = jnp.where(allowed, s, NEG)
            ss[at - first : at - first + CHUNK, :] = s
            most = jnp.maximum(most, jnp.max(s.reshape(CHUNK // 8, 8, QB), axis=0))
        most = jnp.max(most, axis=0, keepdims=True)
        total = jnp.zeros((8, QB), full)
        acc = jnp.zeros((HD, QB), full)
        for at in range(first, stop, CHUNK):
            p = jnp.exp(ss[at - first : at - first + CHUNK, :] - most)
            total += jnp.sum(p.reshape(CHUNK // 8, 8, QB), axis=0)
            acc += nn(v_ref[0, :, at : at + CHUNK], p.astype(low))
        total = jnp.sum(total, axis=0, keepdims=True)
        lse_ref[0, :, start:stop] = most + jnp.log(total)
        o = acc * (1.0 / total)
        of_ref[0, :, start:stop] = o
        obuf[u, :, start:stop] = o.astype(low)

    @pl.when(u == 0)
    def _():
        weight(0, 0).wait()
        for r in range(1, 4):
            weight(0, r).wait_recv()
        line(0, "start")
        for j, count in ((1, 3), (2, 4)):
            for r in range(1, count):
                weight(j, r).start()

    @pl.when(u == 3)
    def _():
        if n > 2:
            line(0, "recv")
            line(1, "start")
        for k in range(2):
            weight(1, 1 + k).wait_recv()
            onward(k).start()
        weight(2, 0).wait()
        for r in range(1, 4):
            weight(2, r).wait_recv()
        onward(2).start()

    def move(unit, i, source_core):
        dc, r = PEERS[i]
        h, seq = unit_place(unit, source_core)
        dest = pl.multiple_of(((c ^ dc) * 4 + (t ^ r)) * own, own)
        src = obuf.at[unit, :, pl.ds(dest, own)]
        dst = att.at[
            pl.ds(pl.multiple_of((t * 3 + h) * HD, HD), HD), pl.ds(pl.multiple_of(seq * own, own), own)
        ]
        if i == 0:
            return pltpu.make_async_copy(src, dst, lsem.at[unit])
        return pltpu.make_async_remote_copy(
            src, dst, ssem.at[i - 1, unit], rsem.at[i - 1, unit], device_id=at_peer(c, t, dc, r)
        )

    @pl.when(sends(u, c))
    def _():
        for i in range(1, len(PEERS)):
            move(u, i, c).start()
        move(u, 0, c).start()

    @pl.when(u == pl.num_programs(0) - 1)
    def _():
        for step in range(2, n - 1):
            line(step - 1, "recv")
            line(step, "start")
        line(n - 2, "recv")
        for step in range(n - 1):
            line(step, "sent")
        weight(1, 0).wait()
        for j in range(3):
            for r in range(1, 3 if j == 1 else 4):
                weight(j, r).wait_send()
        for k in range(3):
            onward(k).wait()
        for unit in range(UNITS):
            for i, (dc, r) in enumerate(PEERS):

                @pl.when(sends(unit, c))
                def _():
                    if i:
                        move(unit, i, c).wait_send()
                    else:
                        move(unit, i, c).wait()

                if i:

                    @pl.when(sends(unit, c ^ dc))
                    def _():
                        move(unit, i, c ^ dc).wait_recv()


def attend(n, qkv, lo, out_part, up_part, down_own):
    length = lo.shape[2]
    half = length // 2
    own = half // 4
    width, hidden = up_part.shape
    part = lambda p: pl.BlockSpec((1, HD, length), unit_block(p))
    unit = lambda rows, n: pl.BlockSpec((1, rows, n), lambda u: (u, 0, 0))
    heads = 4 * 3 * HD
    return pl.pallas_call(
        functools.partial(attend_kernel, n),
        grid=(UNITS,),
        in_specs=[part(0), part(1), part(2)]
        + [pl.BlockSpec((1, 1, length), lambda u: (u // 3, 0, 0))]
        + [
            pl.BlockSpec(a.shape, lambda u: (0, 0), pipeline_mode=pl.Buffered(1))
            for a in (out_part, up_part, down_own)
        ],
        out_specs=[HBM, unit(1, length), unit(HD, length)] + [HBM] * 3,
        scratch_shapes=[
            pltpu.VMEM((HD, length), low),
            pltpu.VMEM((length, HD), low),
            pltpu.VMEM((WIN + QB, QB), full),
            pltpu.VMEM((UNITS, HD, length), low),
            dma((7, UNITS)),
            dma((7, UNITS)),
            dma((UNITS,)),
            dma((3, 3)),
            dma((3, 3)),
            dma((3,)),
            dma((2, n - 1)),
            dma((2, n - 1)),
            dma((3,)),
            dma((3,)),
        ],
        out_shape=[
            jax.ShapeDtypeStruct((heads, 3 * own), low),
            jax.ShapeDtypeStruct((UNITS, 1, length), full),
            jax.ShapeDtypeStruct((UNITS, HD, length), full),
            shape((4, width, hidden), low),
            shape((4, width, hidden), low),
            shape((4,) + out_part.shape, low),
        ],
        compiler_params=pltpu.CompilerParams(
            vmem_limit_bytes=63 << 20, collective_id=1, has_side_effects=True
        ),
        cost_estimate=pl.CostEstimate(
            flops=UNITS * 18 * 2 * 256 * 1024 * 128, bytes_accessed=20 << 20, transcendentals=0
        ),
        name="attend",
    )(qkv, qkv, qkv, lo, out_part, up_part, down_own)


def add_to(ref, terms):
    for a in range(ref.shape[0]):
        for p in range(ref.shape[1]):
            ref[a, p] = (ref[a, p].astype(full) + terms(a, p).astype(full)).astype(low)


def attend_back_kernel(
    n, q_ref, k_ref, v_ref, lo_ref, lse_ref, of_ref, norm_ref, g_ref, gud, part_sum, gout,
    dall, gw_sum, zsum, osum,
    qs, ks, vs, grow, qrow, delta, dqs, dbuf, gw, gwx, gwr, zr, gud_v, obuf, ssem, rsem, lsem,
    zsend, zrecv, xsend, xrecv, osend, orecv, olocal, vlocal,
):
    u = pl.program_id(0)
    c, t = place()
    d = lax.axis_index("dp")
    shard = gud.shape[2] // n
    length = lo_ref.shape[2]
    own = length // 8
    peers = [at_peer(c, t, dc, r) for dc, r in PEERS[1:]]

    def rows_of(j):
        return pl.ds(pl.multiple_of(j * shard, shard), shard)

    def line_of(h):
        pair = pl.ds(2 * h, 2)
        return Line(
            n,
            lambda j: gud.at[:, pair, rows_of(j)],
            lambda k, step: zr.at[h, k, step - 1],
            zsend.at[h],
            zrecv.at[h],
        )

    lines = [line_of(0), line_of(1)]

    def step_of(h, step, arrived=True):
        if arrived and step > 1:
            lines[h].received(step - 1)

        def add(k, j):
            rows = rows_of(j)
            add_to(zr.at[h, k, step - 2], lambda a, p: gud_v[a, 2 * h + p, rows])

        lines[h].start(step, add)

    def finish(h):
        lines[h].received(n - 1)
        for step in range(2 if h == 0 else 1, n):
            lines[h].sent(step)
        for a in range(2):
            for p in range(2):
                total = gud_v[a, 2 * h + p, rows_of(d)].astype(full)
                up, down = (zr[h, k, n - 2, a, p].astype(full) for k in range(2))
                total += jnp.where(d > 0, up, 0.0) + jnp.where(d < n - 1, down, 0.0)
                zsum[a, 2 * h + p] = total.astype(low)

    part_rows = gout.shape[1] // 2

    def out_piece(i):
        dc, r = PEERS[i]
        src = gout.at[t ^ r, pl.ds(pl.multiple_of((c ^ dc) * part_rows, part_rows), part_rows)]
        if i == 0:
            return pltpu.make_async_copy(src, obuf.at[0], olocal)
        return pltpu.make_async_remote_copy(
            src, obuf.at[i], osend.at[i - 1], orecv.at[i - 1], device_id=at_peer(c, t, dc, r)
        )

    def other_core():
        return pltpu.make_async_remote_copy(
            gwx.at[1 - c], gwr, xsend, xrecv, device_id={"context": 1 - c}
        )

    def load(i):
        if i == 2:
            return pltpu.make_async_copy(gud, gud_v, vlocal.at[2])
        return pltpu.make_async_copy(part_sum.at[i], zr.at[0, i, 0], vlocal.at[i])

    @pl.when(u == 0)
    def _():
        greet(peers)
        greet_line(n, d)
        for i in range(3):
            load(i).start()
        gw[...] = jnp.zeros_like(gw)
        greeted_line(n, d, peers)
        for i in range(3):
            load(i).wait()
        step_of(0, 2, False)
        step_of(1, 1)
        for i in range(1, len(PEERS)):
            out_piece(i).start()
        out_piece(0).start()

    @pl.when(u == 2)
    def _():
        step_of(0, 3)

    @pl.when(u == 3)
    def _():
        step_of(1, 2)

    qs[...] = q_ref[0] * low(0.125)
    ks[...] = k_ref[0].T
    vs[...] = v_ref[0].T
    grow[...] = g_ref[0].T
    qrow[...] = qs[...].T
    delta[...] = jnp.sum(g_ref[0].astype(full) * of_ref[0], axis=0, keepdims=True)
    dqs[...] = jnp.zeros_like(dqs)
    for key_start in range(0, length, QB):
        rows = slice(key_start, key_start + QB)
        k, v, key_t = ks[rows, :], vs[rows, :], k_ref[0, :, rows]
        dk = jnp.zeros((QB, HD), full)
        dv = jnp.zeros((QB, HD), full)
        key_pos = key_start + lax.broadcasted_iota(jnp.int32, (QB, QB), 0)
        for start in range(key_start, min(key_start + WIN + QB, length), QB):
            cols = slice(start, start + QB)
            s = nn(k, qs[:, cols]) - lse_ref[0, :, cols]
            allowed = key_pos >= lo_ref[0, :, cols]
            if start == key_start:
                allowed &= key_pos <= start + lax.broadcasted_iota(jnp.int32, (QB, QB), 1)
            p = jnp.exp(jnp.where(allowed, s, NEG))
            dp = nn(v, g_ref[0, :, cols])
            ds = (p * (dp - delta[:, cols])).astype(low)
            dv += nn(p.astype(low), grow[cols, :])
            dk += nn(ds, qrow[cols, :])
            dqs[:, cols] += nn(key_t, ds)
        dbuf[u, 1, :, rows] = dk.T.astype(low)
        dbuf[u, 2, :, rows] = dv.T.astype(low)
    dbuf[u, 0] = (dqs[...] * 0.125).astype(low)

    def move(unit, i, source_core):
        dc, r = PEERS[i]
        h, seq = unit_place(unit, source_core)
        dest = pl.multiple_of(((c ^ dc) * 4 + (t ^ r)) * own, own)
        src = dbuf.at[unit, :, :, pl.ds(dest, own)]
        dst = dall.at[t, :, h, :, pl.ds(pl.multiple_of(seq * own, own), own)]
        if i == 0:
            return pltpu.make_async_copy(src, dst, lsem.at[unit])
        return pltpu.make_async_remote_copy(
            src, dst, ssem.at[i - 1, unit], rsem.at[i - 1, unit], device_id=at_peer(c, t, dc, r)
        )

    @pl.when(sends(u, c))
    def _():
        for i in range(1, len(PEERS)):
            move(u, i, c).start()
        move(u, 0, c).start()
        h, _ = unit_place(u, c)
        gw[h] += nn(dbuf[u].reshape(3 * HD, length), norm_ref[0])

    @pl.when(u == pl.num_programs(0) - 1)
    def _():
        wide_rows = [gw[h, p * HD : (p + 1) * HD, :] for p in range(3) for h in range(3)]
        gwx[0] = jnp.concatenate(wide_rows[:6], axis=0).T.astype(low)
        empty = jnp.zeros((3 * HD, gw.shape[2]), full)
        gwx[1] = jnp.concatenate(wide_rows[6:] + [empty], axis=0).T.astype(low)
        other_core().start()
        step_of(1, 3)
        out_piece(0).wait()
        for i in range(1, len(PEERS)):
            out_piece(i).wait()
        total = obuf[0].astype(full)
        for i in range(1, len(PEERS)):
            total += obuf[i].astype(full)
        osum[...] = total.astype(low)
        other_core().wait()
        gw_sum[...] = (gwx[c].astype(full) + gwr[...].astype(full)).astype(low)
        for step in range(4, n):
            step_of(0, step)
            step_of(1, step)
        finish(0)
        finish(1)
        for unit in range(UNITS):
            for i, (dc, r) in enumerate(PEERS):

                @pl.when(sends(unit, c))
                def _():
                    if i:
                        move(unit, i, c).wait_send()
                    else:
                        move(unit, i, c).wait()

                if i:

                    @pl.when(sends(unit, c ^ dc))
                    def _():
                        move(unit, i, c ^ dc).wait_recv()


def attend_back(n, qkv, grad_units, lo, lse, attended, normed, grad_up_down, part_sum, grad_out):
    length = lo.shape[2]
    own = length // 8
    width = normed.shape[2]
    shard, hidden = grad_up_down.shape[2] // n, grad_up_down.shape[3]
    out_rows, local = grad_out.shape[1] // 2, grad_out.shape[2]
    part = lambda p: pl.BlockSpec((1, HD, length), unit_block(p))
    unit = lambda rows, m: pl.BlockSpec((1, rows, m), lambda u: (u, 0, 0))
    once = lambda dims: pl.BlockSpec(dims, lambda u: (0,) * len(dims), pipeline_mode=pl.Buffered(1))
    wide, tall = pltpu.VMEM((HD, length), low), pltpu.VMEM((length, HD), low)
    results = [(width, 2 * 3 * HD), (2, 4, shard, hidden), (out_rows, local)]
    return pl.pallas_call(
        functools.partial(attend_back_kernel, n),
        grid=(UNITS,),
        in_specs=[part(0), part(1), part(2)]
        + [
            pl.BlockSpec((1, 1, length), lambda u: (u // 3, 0, 0)),
            unit(1, length),
            unit(HD, length),
            pl.BlockSpec((1, length, width), lambda u: (u // 3, 0, 0)),
            unit(HD, length),
        ]
        + [HBM] * 3,
        out_specs=[HBM] + [once(r) for r in results],
        scratch_shapes=[
            wide, tall, tall, tall, tall,
            pltpu.VMEM((1, length), full), pltpu.VMEM((HD, length), full),
            pltpu.VMEM((UNITS, 3, HD, length), low), pltpu.VMEM((3, 3 * HD, width), full),
            pltpu.VMEM((2, width, 6 * HD), low), pltpu.VMEM((width, 6 * HD), low),
            pltpu.VMEM((2, 2, n - 1, 2, 2, shard, hidden), low), pltpu.VMEM(grad_up_down.shape, low),
            pltpu.VMEM((8, out_rows, local), low),
            dma((7, UNITS)), dma((7, UNITS)), dma((UNITS,)),
            dma((2, 2, n - 1)), dma((2, 2, n - 1)), dma, dma, dma((7,)), dma((7,)), dma, dma((3,)),
        ],
        out_shape=[shape((4, 3, 3, HD, 3 * own), low)] + [shape(r, low) for r in results],
        compiler_params=pltpu.CompilerParams(
            vmem_limit_bytes=63 << 20, collective_id=2, has_side_effects=True
        ),
        name="attend_back",
    )(qkv, qkv, qkv, lo, lse, attended, normed, grad_units, grad_up_down, part_sum, grad_out)


def last_kernel(
    n, dqkv_ref, w_ref, tokens_ref, middle_ref, gains, w_own, up_own, gain_one, gain_two, gw_sum, zsum, osum,
    grad_in, g_qkv, g_up, g_down, g_out, g_one, g_two,
    rg, rw, ro, down_n, out_t, mine, sums, dqkv, w_all, tokens, middle,
    gsend, grecv, wsend, wrecv, osend, orecv, lsem, csend, crecv, ssend, srecv, clocal, fetch,
):
    c, t = place()
    d = lax.axis_index("dp")
    shard, hidden = rw.shape[2], rw.shape[3]
    cut = n // 2
    group = [at_peer(c, t, dc, r) for dc, r in PEERS[1:]]
    others = [lax.rem(d + r, n) for r in range(1, n)]
    peers = group + [{"dp": o} for o in others]
    greet(peers)
    loads = [
        pltpu.make_async_copy(src, dst, fetch.at[i])
        for i, (src, dst) in enumerate(
            ((tokens_ref, tokens), (w_ref, w_all), (dqkv_ref, dqkv), (middle_ref, middle))
        )
    ]
    for copy in loads:
        copy.start()

    def rows_of(j):
        return pl.ds(pl.multiple_of(j * shard, shard), shard)

    narrow = slice(0, 256)

    def qkv_piece(r, core):
        src, dst = gw_sum.at[rows_of(d if r == 0 else others[r - 1])], rg.at[r]
        if core:
            src, dst = src.at[:, narrow], dst.at[:, narrow]
        if r == 0:
            return pltpu.make_async_copy(src, dst, lsem.at[0])
        return pltpu.make_async_remote_copy(
            src, dst, gsend.at[r - 1], grecv.at[r - 1], device_id={"dp": others[r - 1]}
        )

    def each_core(what):
        for core in range(2):

            @pl.when(c == core)
            def _():
                what(core)

    def up_piece(r):
        src, dst = zsum.at[:, t ^ r], rw.at[r]
        if r == 0:
            return pltpu.make_async_copy(src, dst, lsem.at[1])
        return pltpu.make_async_remote_copy(
            src, dst, wsend.at[r - 1], wrecv.at[r - 1], device_id={"tensor": t ^ r}
        )

    mine_out = d // cut == c

    def out_piece(r):
        to = d if r == 0 else others[r - 1]
        src, dst = osum.at[rows_of(lax.rem(to, cut))], ro.at[r]
        if r == 0:
            return pltpu.make_async_copy(src, dst, lsem.at[2])
        return pltpu.make_async_remote_copy(
            src, dst, osend.at[r - 1], orecv.at[r - 1], device_id={"dp": to}
        )

    def start_all(core):
        for r in range(1, n):
            qkv_piece(r, core).start()
        qkv_piece(0, core).start()

    greeted(peers)
    each_core(start_all)
    for r in range(1, 4):
        up_piece(r).start()
    up_piece(0).start()
    for r in range(1, n):

        @pl.when(others[r - 1] // cut == c)
        def _():
            out_piece(r).start()

    @pl.when(mine_out)
    def _():
        out_piece(0).start()

    for copy in loads:
        copy.wait()
    for m in range(0, tokens.shape[0], QB):
        rows = slice(m, m + QB)
        r = tn(dqkv[:, rows], w_all[...])
        v = tokens[rows, :].astype(full)
        inv = lax.rsqrt(jnp.mean(v * v, axis=-1, keepdims=True) + epsilon)
        rg_ = r * gains[0:1, :]
        grad = inv * (rg_ - v * (inv * inv * jnp.mean(rg_ * v, axis=-1, keepdims=True)))
        grad_in[rows, :] = (middle[rows, :] + grad).astype(low)

    def halves(j):
        half = pl.ds(pl.multiple_of(c * hidden, hidden), hidden)
        src, dst = (
            (mine.at[0], g_qkv.at[:, half]),
            (mine.at[1], g_up.at[:, half]),
            (down_n, g_down.at[:, half]),
            (out_t, g_out),
        )[j]
        return (
            pltpu.make_async_copy(src, dst, clocal.at[j]),
            pltpu.make_async_remote_copy(
                src, dst, csend.at[j], crecv.at[j], device_id={"context": 1 - c}
            ),
        )

    def deliver(j):
        for copy in halves(j):
            copy.start()

    up_piece(0).wait()
    for r in range(1, 4):
        up_piece(r).wait_recv()
    mine[1] = sum(rw[r, 0].astype(full) for r in range(4))
    down_n[...] = sum(rw[r, 1].astype(full) for r in range(4))
    deliver(1)
    deliver(2)

    @pl.when(mine_out)
    def _():
        out_piece(0).wait()
        for r in range(1, n):
            out_piece(r).wait_recv()
        out_t[...] = sum(ro[r].astype(full) for r in range(n)).T
        deliver(3)

    def take(core):
        qkv_piece(0, core).wait()
        for r in range(1, n):
            qkv_piece(r, core).wait_recv()
        if core:
            mine[0, :, narrow] = sum(rg[r, :, narrow].astype(full) for r in range(n))
            mine[0, :, 256:] = jnp.zeros((shard, hidden - 256), full)
        else:
            mine[0] = sum(rg[r].astype(full) for r in range(n))

    each_core(take)
    deliver(0)
    lane = lax.broadcasted_iota(jnp.int32, (shard, 128), 1)
    halves_of = [jnp.concatenate([w_own[0], w_own[1]], axis=1), jnp.pad(w_own[2], ((0, 0), (0, osum.shape[1])))]
    w_mine = jnp.where(c == 0, halves_of[0].astype(full), halves_of[1].astype(full))
    up_mine = up_own[:, pl.ds(pl.multiple_of(c * hidden, hidden), hidden)].astype(full)
    first = jnp.sum(w_mine * mine[0], axis=1, keepdims=True)
    second = jnp.sum(up_mine * mine[1], axis=1, keepdims=True)
    sums[0] = jnp.where(lane == 0, first, jnp.where(lane == 1, second, 0.0)).T[:8]

    def gain_piece(i):
        dc, r = PEERS[i]
        return pltpu.make_async_remote_copy(
            sums.at[0], sums.at[i], ssend.at[i - 1], srecv.at[i - 1], device_id=at_peer(c, t, dc, r)
        )

    for i in range(1, len(PEERS)):
        gain_piece(i).start()
    for i in range(1, len(PEERS)):
        gain_piece(i).wait()
    total = sum(sums[i] for i in range(len(PEERS)))
    g_one[...] = total[0:1, :] / gain_one[...].astype(full)
    g_two[...] = total[1:2, :] / gain_two[...].astype(full)

    for j in range(3):
        for copy in halves(j):
            copy.wait()

    @pl.when(mine_out)
    def _():
        local, away = halves(3)
        local.wait()
        away.wait_send()

    @pl.when(jnp.logical_not(mine_out))
    def _():
        halves(3)[1].wait_recv()

    for r in range(1, 4):
        up_piece(r).wait_send()

    def sent(core):
        for r in range(1, n):
            qkv_piece(r, core).wait_send()

    each_core(sent)
    for r in range(1, n):

        @pl.when(others[r - 1] // cut == c)
        def _():
            out_piece(r).wait_send()


def last(n, dqkv, w_all, tokens, middle, gains, w_own, up_own, gain_one, gain_two, gw_sum, zsum, osum):
    rows, width = tokens.shape
    _, _, shard, hidden = zsum.shape
    local = osum.shape[1]
    return pl.pallas_call(
        functools.partial(last_kernel, n),
        in_specs=[HBM] * 4 + [VMEM] * 5 + [ANY] * 3,
        out_specs=[VMEM] + [ANY] * 4 + [VMEM] * 2,
        out_shape=[
            shape((rows, width), low),
            shape((shard, 2 * hidden), full),
            shape((shard, 2 * hidden), full),
            shape((shard, 2 * hidden), full),
            shape((local, shard), full),
            shape((1, shard), full),
            shape((1, shard), full),
        ],
        scratch_shapes=[
            pltpu.VMEM((n, shard, hidden), low),
            pltpu.VMEM((4, 2, shard, hidden), low),
            pltpu.VMEM((n, shard, local), low),
            pltpu.VMEM((shard, hidden), full),
            pltpu.VMEM((local, shard), full),
            pltpu.VMEM((2, shard, hidden), full),
            pltpu.VMEM((8, 8, shard), full),
            pltpu.VMEM(dqkv.shape, low), pltpu.VMEM(w_all.shape, low),
            pltpu.VMEM((rows, width), low), pltpu.VMEM((rows, width), full),
            dma((n - 1,)), dma((n - 1,)), dma((3,)), dma((3,)), dma((n - 1,)), dma((n - 1,)), dma((3,)),
            dma((4,)), dma((4,)), dma((7,)), dma((7,)), dma((4,)), dma((4,)),
        ],
        compiler_params=pltpu.CompilerParams(
            vmem_limit_bytes=63 << 20, collective_id=4, has_side_effects=True
        ),
        name="last",
    )(dqkv, w_all, tokens, middle, gains, w_own, up_own, gain_one, gain_two, gw_sum, zsum, osum)


def close_kernel(*refs):
    count = len(refs) // 2
    for i, (src, dst) in enumerate(zip(refs[:count], refs[count:])):
        if i == 2:
            local = dst.shape[2]
            for p in range(3):
                dst[p] = src[:, p * local : (p + 1) * local]
        else:
            dst[...] = src[...]


def close(result, grad_input, own_attn, *others):
    arrays = (result, grad_input, own_attn, *others)
    rows = lambda a: pl.BlockSpec((a.shape[0] // 2, a.shape[1]), lambda i: (i, 0))
    shard, local = own_attn.shape[0], others[0].shape[0]
    parts = pl.BlockSpec((3, shard // 2, local), lambda i: (0, i, 0))
    outs = [shape(a.shape, a.dtype) for a in arrays]
    outs[2] = shape((3, shard, local), full)
    return pl.pallas_call(
        close_kernel,
        grid=(2,),
        in_specs=[rows(a) for a in arrays],
        out_specs=[parts if i == 2 else rows(a) for i, a in enumerate(arrays)],
        out_shape=outs,
        compiler_params=pltpu.CompilerParams(vmem_limit_bytes=63 << 20),
        name="close",
    )(*arrays)


def gelu_and_slope(v):
    k0 = math.sqrt(2.0 / math.pi)
    square = v * v
    th = jnp.tanh(v * (k0 + (k0 * 0.044715) * square))
    half = 0.5 + 0.5 * th
    slope = half + (v * half) * ((1.0 - th) * (k0 + (3.0 * 0.044715 * k0) * square))
    return v * half, slope


def feed_kernel(
    dp, att, proj, tokens, cot, gains, w_t, up_ref, down_ref,
    result, middle, gout, gud, part_sum, units, w_all,
    x, g, x_t, g_t, up, down, act, gh, out, back, proj_w, sent, got, gbuf, gatt,
    xsend, xrecv, wsend, wrecv, wlocal, zsend, zrecv, glocal, usend, urecv, ulocal, load,
):
    c, t = place()
    d = lax.axis_index("dp")
    rows, width = tokens.shape
    own = rows // 3
    shard = width // dp
    n = up_ref.shape[2]
    local = proj.shape[2]
    other = {"context": 1 - c}
    peers = [at_peer(c, t, dc, r) for dc, r in PEERS[1:]]
    mine, theirs = slice(0, rows), slice(rows, 2 * rows)
    block = rows // 3

    def cross(k):
        src, dst = (
            (cot, g.at[theirs]),
            (x.at[mine], x.at[theirs]),
            (sent.at[0], got.at[0]),
            (sent.at[1], got.at[1]),
        )[k]
        return pltpu.make_async_remote_copy(src, dst, xsend.at[k], xrecv.at[k], device_id=other)

    half = pl.ds(pl.multiple_of(c * (w_t.shape[0] // 2), 8), w_t.shape[0] // 2)

    def over_tensor(r):
        if r == 4:
            ref = w_all.at[:, half]
            return pltpu.make_async_remote_copy(ref, ref, wsend.at[3], wrecv.at[3], device_id=other)
        src, dst = w_t.at[half], w_all.at[t, half]
        if r == 0:
            return pltpu.make_async_copy(src, dst, wlocal)
        return pltpu.make_async_remote_copy(
            src, dst, wsend.at[r - 1], wrecv.at[r - 1], device_id={"tensor": t ^ r}
        )

    def rows_of(i):
        return pl.ds(pl.multiple_of(i * shard, shard), shard)

    line = Line(
        dp,
        lambda i: gbuf.at[0, :, :, rows_of(i)],
        lambda k, step: part_sum.at[k],
        zsend,
        zrecv,
    )

    def keep(j):
        return pltpu.make_async_copy(gbuf.at[j], gud.at[:, pl.ds(2 * j, 2)], glocal.at[j])

    def leave(whole, i):
        dc, r = PEERS[i]
        to_c, to_t = c ^ dc, t ^ r
        head = to_t * 3 + (0 if whole else to_c)
        count, first = (3, 0) if whole else (2, 3)
        seq = 2 * to_c if whole else 1
        src = gatt.at[pl.ds(head, count), :, pl.ds(pl.multiple_of(seq * own, own), own)]
        dst = units.at[pl.ds(first, count), :, pl.ds(pl.multiple_of((c * 4 + t) * own, own), own)]
        k = 0 if whole else 1
        if i == 0:
            return pltpu.make_async_copy(src, dst, ulocal.at[k])
        return pltpu.make_async_remote_copy(
            src, dst, usend.at[k, i - 1], urecv.at[k, i - 1], device_id=at_peer(c, t, dc, r)
        )

    loads = [
        pltpu.make_async_copy(ref.at[p], dst.at[p // 2, :, pl.ds((p % 2) * n, n)], load.at[i, p])
        for i, (ref, dst) in enumerate(((up_ref, up), (down_ref, down)))
        for p in range(4)
    ]
    greet(peers)
    greet_line(dp, d)
    for copy in loads:
        copy.start()
    for p in range(4):
        proj_w[:, p * local : (p + 1) * local] = proj[p]
    greeted_line(dp, d, peers)
    cross(0).start()
    for r in range(1, 4):
        over_tensor(r).start()
    over_tensor(0).start()
    for m in range(0, rows, block):
        part = slice(m, m + block)
        v = tokens[part, :].astype(full) + nn(proj_w[...], att[:, part]).T
        middle[part, :] = v
        inv = lax.rsqrt(jnp.mean(v * v, axis=-1, keepdims=True) + epsilon)
        x[part, :] = (v * inv * gains[1:2, :]).astype(low)
    cross(1).start()
    g[mine, :] = cot[...]
    g_t[:, mine] = cot[...].T
    x_t[:, mine] = x[mine, :].T
    for copy in loads:
        copy.wait()

    def hidden(side):
        @pl.loop(0, 6)
        def _(i):
            j = i // 3
            part = pl.ds(pl.multiple_of((side * 3 + i % 3) * block, block), block)
            pre = nn(x[part, :], up[j])
            ga = nn(g[part, :], down[j])
            a, slope = gelu_and_slope(pre)
            act[j, part, :] = a.astype(low)
            gh[j, part, :] = (ga * slope).astype(low)

    def branch(left, right, part):
        return nt(left[0, part, :], right[0]) + nt(left[1, part, :], right[1])

    hidden(0)
    cross(0).wait_recv()
    cross(1).wait_recv()
    hidden(1)

    def cut(side, left, right, put):
        @pl.loop(0, 3)
        def _(i):
            here = pl.ds(pl.multiple_of(i * block, block), block)
            part = pl.ds(pl.multiple_of(side * rows + i * block, block), block)
            put(here, branch(left, right, part))

    def put_sent(k):
        def put(here, value):
            sent[k, here, :] = value.astype(low)

        return put

    def put_own(ref):
        def put(here, value):
            ref[here, :] = value

        return put

    cut(1, gh, up, put_sent(0))
    cross(2).start()
    cut(0, gh, up, put_own(back))
    over_tensor(0).wait()
    for r in range(1, 4):
        over_tensor(r).wait_recv()
    over_tensor(4).start()
    x_t[:, theirs] = x[theirs, :].T
    g_t[:, theirs] = g[theirs, :].T
    cross(2).wait_recv()
    gain = gains[1:2, :]
    low_t = x
    for m in range(0, rows, block):
        part = slice(m, m + block)
        r = (back[part, :] + got[0, part, :].astype(full)) * gain
        v = middle[part, :]
        inv = lax.rsqrt(jnp.mean(v * v, axis=-1, keepdims=True) + epsilon)
        grad = inv * (r - v * (inv * inv * jnp.mean(r * v, axis=-1, keepdims=True)))
        back[part, :] = cot[part, :].astype(full) + grad
        low_t[rows : rows + width, part] = back[part, :].astype(low).T
        grad = tn(proj_w[...], low_t[rows : rows + width, part]).astype(low)
        gatt[:, :, part] = grad.reshape(gatt.shape[0], HD, block)
    for whole in (True, False):
        for i in range(1, len(PEERS)):
            leave(whole, i).start()
        leave(whole, 0).start()

    def weight_grad(j, a, left_t, right):
        @pl.loop(0, 3)
        def _(i):
            part = pl.ds(pl.multiple_of(i * (width // 3), width // 3), width // 3)
            grad = nn(left_t[part, :], right[j]).astype(low)
            for p in range(2):
                gbuf[j, a, p, part, :] = grad[:, p * n : (p + 1) * n]

    weight_grad(0, 0, x_t, gh)
    weight_grad(0, 1, g_t, act)
    line.start(1, None)
    keep(0).start()
    cut(1, act, down, put_sent(1))
    cross(3).start()
    weight_grad(1, 0, x_t, gh)
    weight_grad(1, 1, g_t, act)
    keep(1).start()
    cut(0, act, down, put_own(out))
    for m in range(0, width, block):
        part = slice(m, m + block)
        big = nt(low_t[rows + m : rows + m + block, :], att[...]).astype(low)
        for p in range(4):
            gout[p, part, :] = big[:, p * local : (p + 1) * local]
    cross(3).wait_recv()
    result[...] = (middle[...] + out[...] + got[1].astype(full)).astype(low)
    middle[...] = back[...]
    for k in range(4):
        cross(k).wait_send()
    for r in range(1, 4):
        over_tensor(r).wait_send()
    over_tensor(4).wait()
    line.received(1)
    line.sent(1)
    for j in range(2):
        keep(j).wait()
    for whole in (True, False):
        for i in range(len(PEERS)):
            leave(whole, i).wait()


def feed(dp, att, proj, tokens, cot, gains, w_t, up, down):
    rows, width = tokens.shape
    pieces, _, n = up.shape
    own = rows // 3
    assert pieces == 4 and dp > 2 and rows == width
    return pl.pallas_call(
        functools.partial(feed_kernel, dp),
        in_specs=[VMEM] * 6 + [HBM] * 2,
        out_specs=[VMEM] * 3 + [HBM] * 4,
        out_shape=[
            shape((rows, width), low),
            shape((rows, width), full),
            shape(proj.shape, low),
            shape((2,) + up.shape, low),
            shape((2, 2, 2, width // dp, n), low),
            shape((UNITS, HD, 8 * own), low),
            shape((4,) + w_t.shape, low),
        ],
        scratch_shapes=[pltpu.VMEM((2 * rows, width), low)] * 2
        + [pltpu.VMEM((width, 2 * rows), low)] * 2
        + [pltpu.VMEM((2, width, 2 * n), low)] * 2
        + [pltpu.VMEM((2, 2 * rows, 2 * n), low)] * 2
        + [pltpu.VMEM((rows, width), full)] * 2
        + [pltpu.VMEM((width, width), low)]
        + [pltpu.VMEM((2, rows, width), low)] * 2
        + [pltpu.VMEM((2, 2, 2, width, n), low)]
        + [pltpu.VMEM((12, HD, rows), low)]
        + [dma((4,)), dma((4,)), dma((4,)), dma((4,)), dma]
        + [dma((2, 1)), dma((2, 1)), dma((2,)), dma((2, 7)), dma((2, 7)), dma((2,)), dma((2, 4))],
        compiler_params=pltpu.CompilerParams(
            vmem_limit_bytes=63 << 20, collective_id=5, has_side_effects=True
        ),
        name="feed",
    )(att, proj, tokens, cot, gains, w_t, up, down)


def per_device(tokens, segments, w_qkv, w_out, w_in, w_back, gain_attn, gain_mlp, cotangent):
    sequences, own, width = tokens.shape
    assert lax.axis_size("tensor") == 4 and lax.axis_size("context") == 2 and sequences == 3
    n = lax.axis_size("dp")
    length = segments.shape[1]
    shard = w_qkv.shape[0]
    local = w_qkv.shape[2]
    rows = sequences * own
    parts = w_qkv.transpose(1, 0, 2)
    gain_one, gain_two = gain_attn.reshape(1, shard), gain_mlp.reshape(1, shard)
    qkv, normed_units, w_t, up_part, out_part, gains, lo = project(
        n, tokens, segments, parts, w_in, w_out, gain_one, gain_two
    )
    attended, log_totals, out_full, w_up, w_down, w_proj = attend(
        n, qkv, lo, out_part, up_part, w_back.T
    )
    flat = tokens.reshape(rows, width)
    result, grad_middle, grad_out, grad_up_down, part_sum, grad_units, w_all = feed(
        n, attended, w_proj, flat, cotangent.reshape(rows, width), gains, w_t, w_up, w_down
    )
    grad_projected, gw_sum, zsum, osum = attend_back(
        n, qkv, grad_units, lo, log_totals, out_full, normed_units, grad_up_down, part_sum, grad_out
    )
    grad_input, own_attn, own_up, own_down, own_proj, own_one, own_two = last(
        n,
        grad_projected.reshape(12 * local, rows),
        w_all.reshape(12 * local, width),
        flat,
        grad_middle,
        gains,
        parts,
        w_in,
        gain_one,
        gain_two,
        gw_sum,
        zsum,
        osum,
    )
    result, grad_input, own_attn, own_proj, own_up, own_down = close(
        result, grad_input, own_attn, own_proj, own_up, own_down
    )
    return (
        result.reshape(sequences, own, width),
        grad_input.reshape(sequences, own, width),
        own_attn.transpose(1, 0, 2),
        own_proj,
        own_up,
        own_down.T,
        own_one.reshape(shard),
        own_two.reshape(shard),
    )


def solution(mesh):
    return jax.shard_map(
        per_device,
        mesh=mesh,
        in_specs=(
            P("dp", ("context", "tensor"), None),
            P("dp", None),
            P("dp", None, "tensor"),
            P("tensor", "dp"),
            P("dp", "tensor"),
            P("tensor", "dp"),
            P("dp"),
            P("dp"),
            P("dp", ("context", "tensor"), None),
        ),
        out_specs=(
            P("dp", ("context", "tensor"), None),
            P("dp", ("context", "tensor"), None),
            P("dp", None, "tensor"),
            P("tensor", "dp"),
            P("dp", "tensor"),
            P("tensor", "dp"),
            P("dp"),
            P("dp"),
        ),
        check_vma=False,
    )
```

```python
import functools
import math

import jax
import jax.numpy as jnp
from jax import lax
from jax.experimental import pallas as pl
from jax.experimental.pallas import tpu as pltpu
from jax.sharding import PartitionSpec as P

HD = 64
WIN = 1536
QB = 256
CHUNK = 128
NEG = -1e30
epsilon = 1e-06
low = jnp.bfloat16
full = jnp.float32


def dot(left, right, dims):
    return lax.dot_general(left, right, (dims, ((), ())), preferred_element_type=full)


def nn(left, right):
    return dot(left, right, ((1,), (0,)))


def nt(left, right):
    return dot(left, right, ((1,), (1,)))


def tn(left, right):
    return dot(left, right, ((0,), (0,)))


PEERS = [(dc, r) for dc in range(2) for r in range(4)]


def place():
    return lax.axis_index("context"), lax.axis_index("tensor")


def at_peer(c, t, dc, r):
    return {"context": c ^ dc, "tensor": t ^ r}


def greet(peers):
    for peer in peers:
        pl.semaphore_signal(pltpu.get_barrier_semaphore(), inc=1, device_id=peer)


def greeted(peers):
    pl.semaphore_wait(pltpu.get_barrier_semaphore(), len(peers))


def unit_place(u, c):
    return jnp.where(u < 3, u, c + u - 3), jnp.where(u < 3, 2 * c, 1)


def sends(u, c):
    return (u != 3) | (c == 0)


dma = pltpu.SemaphoreType.DMA
ANY = pl.BlockSpec(memory_space=pl.ANY)
VMEM = pl.BlockSpec(memory_space=pltpu.VMEM)
HBM = pl.BlockSpec(memory_space=pltpu.HBM)
shape = jax.ShapeDtypeStruct

SIDE = 128


class Line:
    def __init__(self, n, own, slot, send, recv):
        self.n, self.own, self.slot, self.sems = n, own, slot, (send, recv)
        self.d = lax.axis_index("dp")

    def along(self, k):
        m = self.d if k == 0 else self.n - 1 - self.d
        to = {"dp": jnp.clip(self.d + 1 if k == 0 else self.d - 1, 0, self.n - 1)}
        return m, to

    def target(self, k, step):
        m, _ = self.along(k)
        return jnp.clip(self.n - step + m if k == 0 else step - 1 - m, 0, self.n - 1)

    def copy(self, k, step, src):
        send, recv = self.sems
        _, to = self.along(k)
        return pltpu.make_async_remote_copy(
            src, self.slot(k, step), send.at[k, step - 1], recv.at[k, step - 1], device_id=to
        )

    def arrive(self, k, step):
        self.copy(k, step, self.slot(k, step)).wait_recv()

    def start(self, step, add):
        for k in range(2):
            m, _ = self.along(k)
            if step > 1:

                @pl.when((m >= 1) & (m < self.n - 1) & (step >= m + 1))
                def _():
                    add(k, self.target(k, step))
                    self.copy(k, step, self.slot(k, step - 1)).start()

            @pl.when(m == 0)
            def _():
                self.copy(k, step, self.own(self.target(k, step))).start()

    def received(self, step):
        for k in range(2):
            m, _ = self.along(k)

            @pl.when((m >= 1) & (step >= m))
            def _():
                self.arrive(k, step)

    def sent(self, step):
        for k in range(2):
            m, _ = self.along(k)

            @pl.when((m < self.n - 1) & (step >= m + 1))
            def _():
                self.copy(k, step, self.slot(k, step)).wait_send()


def greet_line(n, d):
    barrier = pltpu.get_barrier_semaphore()

    @pl.when(d > 0)
    def _():
        pl.semaphore_signal(barrier, inc=1, device_id={"dp": jnp.maximum(d - 1, 0)})

    @pl.when(d < n - 1)
    def _():
        pl.semaphore_signal(barrier, inc=1, device_id={"dp": jnp.minimum(d + 1, n - 1)})


def greeted_line(n, d, peers):
    ends = jnp.where(d > 0, 1, 0) + jnp.where(d < n - 1, 1, 0)
    pl.semaphore_wait(pltpu.get_barrier_semaphore(), len(peers) + ends)


def project_kernel(
    n, tokens, segments, w_qkv, up, out_own, gain_one, gain_two, qkv, norm, w_t, up_all, out_all, gain_ref, lo_ref,
    tok, x, w, proj, out_w, gain, own_gain, tsend, trecv, tlocal, wsend, wrecv, wlocal, osend, orecv, olocal, xsend, xrecv,
):
    c, t = place()
    d = lax.axis_index("dp")
    own = tokens.shape[1]
    width = tokens.shape[2]
    span = 4 * own
    shard = up.shape[0]
    half = own // 2
    hidden = up_all.shape[1]
    cut = n // 2
    to_x, to_y, to_core = {"tensor": t ^ 1}, {"tensor": t ^ 2}, {"context": 1 - c}
    others = [{"dp": lax.rem(d + r, n)} for r in range(1, n)]
    peers = [to_x, to_y, to_core] + others
    greet(peers)

    def local(i, s):
        return pltpu.make_async_copy(tokens.at[s], tok.at[s, t], tlocal.at[i])

    def weights(j, r):
        rows = pl.ds(pl.multiple_of(d * shard, shard), shard)
        source, target = (
            (w_qkv, w.at[:, rows]),
            (out_w, out_all.at[rows]),
            (up.at[:, pl.ds(pl.multiple_of(c * hidden, hidden), hidden)], up_all.at[rows]),
            (own_gain, gain.at[d]),
        )[j]
        if r == 0:
            return pltpu.make_async_copy(source, target, wlocal.at[j])
        return pltpu.make_async_remote_copy(
            source, target, wsend.at[j, r - 1], wrecv.at[j, r - 1], device_id=others[r - 1]
        )

    def gives(j, r):
        return lax.rem(d + n - r, n) // cut == c if j < 2 else True

    def weights_do(j, r, what, source=False):
        @pl.when(gives(j, 0 if source else r))
        def _():
            getattr(weights(j, r), what)()

    def to_other(j):
        rows = pl.ds(pl.multiple_of(c * cut * shard, shard), cut * shard)
        ref = w.at[:, rows]
        return pltpu.make_async_remote_copy(ref, ref, xsend, xrecv, device_id=to_core)

    order = (2 * (1 - c), 1, 2 * c)
    for i, s in enumerate(order):
        local(i, s).start()
    out_w[...] = out_own[...].T
    own_gain[...] = jnp.zeros_like(own_gain)
    own_gain[0:1, :] = gain_one[...]
    own_gain[1:2, :] = gain_two[...]
    for j in range(4):
        weights_do(j, 0, "start")
    greeted(peers)
    for j in (0, 3, 1, 2):
        for r in range(1, n):
            weights_do(j, r, "start", True)

    def hop(k, i):
        s = order[i]
        origin, rows, peer = (
            (t, slice(0, half), to_x),
            (t, slice(half, own), to_y),
            (t, slice(0, half), to_y),
            (t, slice(half, own), to_x),
            (t ^ 1, slice(0, half), to_y),
            (t ^ 2, slice(half, own), to_x),
        )[k]
        there = tok.at[s, origin, rows]
        here = tokens.at[s, rows] if k < 4 else there
        return pltpu.make_async_remote_copy(
            here, there, tsend.at[k, i], trecv.at[k, i], device_id=peer
        )

    def straight(i):
        for k in range(4):
            hop(k, i).start()

    def forward(i):
        for k in range(2):
            hop(k, i).wait_recv()
            hop(k + 4, i).start()

    units = proj.shape[1]

    def leave(i):
        out = []
        lanes = pl.ds(pl.multiple_of(c * span, span), span)
        if i != 0:
            out.append((x.at[i], norm.at[2 - i, lanes], False))
        if i != 2:
            out.append((x.at[i], norm.at[i, lanes], True))
        if i == 0:
            out.append((proj.at[0], qkv.at[pl.ds(0, units), :, lanes], True))
        if i == 2:
            out.append((proj.at[2], qkv.at[pl.ds(0, units), :, lanes], False))
        if i == 1:
            for away in (True, False):
                core = 1 - c if away else c
                for p in range(3):
                    src = proj.at[1, pl.ds(p * 3 + core, 2)]
                    out.append((src, qkv.at[pl.ds(units + 2 * p, 2), :, lanes], away))
        copies = []
        for j, (src, dst, away) in enumerate(out):
            if away:
                copies.append(
                    (away, pltpu.make_async_remote_copy(src, dst, osend.at[i, j], orecv.at[i, j], device_id=to_core))
                )
            else:
                copies.append((away, pltpu.make_async_copy(src, dst, olocal.at[i, j])))
        return copies

    def work(i):
        s = order[i]
        local(i, s).wait()
        for k in range(2, 6):
            hop(k, i).wait_recv()
        for p in range(4):
            v = tok[s, p].astype(full)
            inv = lax.rsqrt(jnp.mean(v * v, axis=-1, keepdims=True) + epsilon)
            x[i, p * own : (p + 1) * own, :] = (v * inv * gain_ref[0:1, :]).astype(low)
        for p in range(4):
            rows = slice(p * own, (p + 1) * own)
            part = nt(w_t[...], x[i, rows, :]).astype(low)
            proj[i, :, :, rows] = part.reshape(units, HD, own)
        for _, copy in leave(i):
            copy.start()

    straight(0)
    straight(1)
    forward(0)
    straight(2)
    seg = segments[...]
    first = jnp.zeros(seg.shape, jnp.int32)
    for value in range(8):
        before = jnp.sum((seg < value).astype(jnp.int32), axis=1, keepdims=True)
        first = jnp.where(seg == value, before, first)
    first = jnp.maximum(first, lax.broadcasted_iota(jnp.int32, seg.shape, 1) - (WIN - 1))
    lo_ref[0] = jnp.where(c == 0, first[0:1], first[2:3])
    lo_ref[1] = first[1:2]
    weights_do(0, 0, "wait")
    for r in range(1, n):
        weights_do(0, r, "wait_recv")
    to_other(0).start()
    weights(3, 0).wait()
    for r in range(1, n):
        weights(3, r).wait_recv()
    gain_ref[...] = jnp.concatenate([gain[i].astype(full) for i in range(n)], axis=1)[:8]
    to_other(0).wait_recv()
    for p in range(3):
        w_t[p * 3 * HD : (p + 1) * 3 * HD, :] = w[p].T
    forward(1)
    work(0)
    forward(2)
    work(1)
    work(2)
    to_other(0).wait_send()
    for j in range(4):
        if j in (1, 2):
            weights_do(j, 0, "wait")
        for r in range(1, n):
            weights_do(j, r, "wait_send", True)
            if j in (1, 2):
                weights_do(j, r, "wait_recv")
    for i in range(3):
        for k in range(6):
            hop(k, i).wait_send()
        for away, copy in leave(i):
            copy.wait()


def project(n, tokens, segments, w_qkv, up, out_own, gain_one, gain_two):
    sequences, own, width = tokens.shape
    shard, hidden = up.shape[0], up.shape[1] // 2
    local = out_own.shape[0]
    span = 4 * own
    return pl.pallas_call(
        functools.partial(project_kernel, n),
        in_specs=[HBM, VMEM, HBM, HBM, VMEM, VMEM, VMEM],
        out_specs=[HBM] * 2 + [VMEM] + [HBM] * 2 + [VMEM] * 2,
        out_shape=[
            shape((15, HD, 2 * span), low),
            shape((2, 2 * span, width), low),
            shape((9 * HD, n * shard), low),
            shape((n * shard, hidden), low),
            shape((n * shard, local), low),
            shape((8, n * shard), full),
            shape((2, 1, segments.shape[1]), jnp.int32),
        ],
        scratch_shapes=[
            pltpu.VMEM((sequences, 4, own, width), low),
            pltpu.VMEM((sequences, span, width), low),
            pltpu.VMEM((3, n * shard, local), low),
            pltpu.VMEM((sequences, 9, HD, span), low),
            pltpu.VMEM((shard, local), low),
            pltpu.VMEM((n, 16, shard), low),
            pltpu.VMEM((16, shard), low),
            dma((6, 3)), dma((6, 3)), dma((3,)),
            dma((4, n - 1)), dma((4, n - 1)), dma((4,)),
            dma((3, 8)), dma((3, 8)), dma((3, 8)), dma, dma,
        ],
        compiler_params=pltpu.CompilerParams(
            vmem_limit_bytes=63 << 20, collective_id=3, has_side_effects=True
        ),
        name="project",
    )(tokens, segments, w_qkv, up, out_own, gain_one, gain_two)


UNITS = 5
def unit_block(part):
    return lambda u: (jnp.where(u < 3, part * 3 + u, 9 + part * 2 + (u - 3)), 0, 0)


def attend_kernel(
    n, q_ref, k_ref, v_ref, lo_ref, out_part, up_part, down_own, att, lse_ref, of_ref, up, down, out_w,
    qs, ks, ss, obuf, ssem, rsem, lsem, wsend, wrecv, wlocal, zsend, zrecv, fsend, frecv,
):
    u = pl.program_id(0)
    c, t = place()
    d = lax.axis_index("dp")
    shard = down_own.shape[0]
    hidden = down.shape[2]
    peers = [at_peer(c, t, dc, r) for dc, r in PEERS[1:]]

    part = out_part.shape[0] // 2
    mine = pl.ds(pl.multiple_of(c * part, part), part)

    def weight(j, r):
        rows = pl.ds(pl.multiple_of(d * shard, shard), shard)
        src, dst = (
            (down_own.at[:, pl.ds(pl.multiple_of(c * hidden, hidden), hidden)], down.at[t, rows]),
            (up_part, up.at[t]),
            (out_part.at[mine], out_w.at[t, mine]),
        )[j]
        if r == 0:
            return pltpu.make_async_copy(src, dst, wlocal.at[j])
        return pltpu.make_async_remote_copy(
            src, dst, wsend.at[j, r - 1], wrecv.at[j, r - 1], device_id={"tensor": t ^ r}
        )

    def onward(k):
        if k == 2:
            ref, peer = out_w.at[:, mine], {"context": 1 - c}
        else:
            rows = pl.ds(k * part, part)
            ref, peer = up.at[t ^ (1 + k), rows], {"tensor": t ^ (2 - k)}
        return pltpu.make_async_remote_copy(
            ref, ref, fsend.at[k], frecv.at[k], device_id=peer
        )

    def shards(step, up_line):
        src = d - step if up_line else d + step
        rows = pl.ds(pl.multiple_of(jnp.clip(src, 0, n - 1) * shard, shard), shard)
        to = jnp.clip(d + 1 if up_line else d - 1, 0, n - 1)
        k = 0 if up_line else 1
        return pltpu.make_async_remote_copy(
            down.at[:, rows], down.at[:, rows], zsend.at[k, step], zrecv.at[k, step], device_id={"dp": to}
        )

    def line(step, what):
        for up_line in (True, False):
            inside = (d < n - 1) if up_line else (d > 0)
            has = (d >= step) if up_line else (d <= n - 1 - step)
            comes = (d >= step + 1) if up_line else (d <= n - 2 - step)
            if what == "recv":

                @pl.when(comes)
                def _():
                    shards(step, up_line).wait_recv()
            else:

                @pl.when(inside & has)
                def _():
                    if what == "start":
                        shards(step, up_line).start()
                    else:
                        shards(step, up_line).wait_send()
    length = lo_ref.shape[2]
    half = length // 2
    own = half // 4

    @pl.when(u == 0)
    def _():
        greet(peers)
        greet_line(n, d)
        for j in range(3):
            weight(j, 0).start()
        greeted_line(n, d, peers)
        for r in range(1, 4):
            weight(0, r).start()

    qs[...] = q_ref[0] * low(0.125)
    ks[...] = k_ref[0].T
    for start in range(0, length, QB):
        stop = start + QB
        q = qs[:, start:stop]
        lo = lo_ref[0, :, start:stop]
        first = max(0, start - WIN)
        most = jnp.full((8, QB), NEG, full)
        for at in range(first, stop, CHUNK):
            s = nn(ks[at : at + CHUNK, :], q)
            key_pos = at + lax.broadcasted_iota(jnp.int32, (CHUNK, QB), 0)
            allowed = key_pos >= lo
            if at + CHUNK - 1 > start:
                allowed &= key_pos <= start + lax.broadcasted_iota(jnp.int32, (CHUNK, QB), 1)
            s = jnp.where(allowed, s, NEG)
            ss[at - first : at - first + CHUNK, :] = s
            most = jnp.maximum(most, jnp.max(s.reshape(CHUNK // 8, 8, QB), axis=0))
        most = jnp.max(most, axis=0, keepdims=True)
        total = jnp.zeros((8, QB), full)
        acc = jnp.zeros((HD, QB), full)
        for at in range(first, stop, CHUNK):
            p = jnp.exp(ss[at - first : at - first + CHUNK, :] - most)
            total += jnp.sum(p.reshape(CHUNK // 8, 8, QB), axis=0)
            acc += nn(v_ref[0, :, at : at + CHUNK], p.astype(low))
        total = jnp.sum(total, axis=0, keepdims=True)
        lse_ref[0, :, start:stop] = most + jnp.log(total)
        o = acc * (1.0 / total)
        of_ref[0, :, start:stop] = o
        obuf[u, :, start:stop] = o.astype(low)

    @pl.when(u == 0)
    def _():
        weight(0, 0).wait()
        for r in range(1, 4):
            weight(0, r).wait_recv()
        line(0, "start")
        for j, count in ((1, 3), (2, 4)):
            for r in range(1, count):
                weight(j, r).start()

    @pl.when(u == 3)
    def _():
        if n > 2:
            line(0, "recv")
            line(1, "start")
        for k in range(2):
            weight(1, 1 + k).wait_recv()
            onward(k).start()
        weight(2, 0).wait()
        for r in range(1, 4):
            weight(2, r).wait_recv()
        onward(2).start()

    def move(unit, i, source_core):
        dc, r = PEERS[i]
        h, seq = unit_place(unit, source_core)
        dest = pl.multiple_of(((c ^ dc) * 4 + (t ^ r)) * own, own)
        src = obuf.at[unit, :, pl.ds(dest, own)]
        dst = att.at[
            pl.ds(pl.multiple_of((t * 3 + h) * HD, HD), HD), pl.ds(pl.multiple_of(seq * own, own), own)
        ]
        if i == 0:
            return pltpu.make_async_copy(src, dst, lsem.at[unit])
        return pltpu.make_async_remote_copy(
            src, dst, ssem.at[i - 1, unit], rsem.at[i - 1, unit], device_id=at_peer(c, t, dc, r)
        )

    @pl.when(sends(u, c))
    def _():
        for i in range(1, len(PEERS)):
            move(u, i, c).start()
        move(u, 0, c).start()

    @pl.when(u == pl.num_programs(0) - 1)
    def _():
        for step in range(2, n - 1):
            line(step - 1, "recv")
            line(step, "start")
        line(n - 2, "recv")
        for step in range(n - 1):
            line(step, "sent")
        weight(1, 0).wait()
        for j in range(3):
            for r in range(1, 3 if j == 1 else 4):
                weight(j, r).wait_send()
        for k in range(3):
            onward(k).wait()
        for unit in range(UNITS):
            for i, (dc, r) in enumerate(PEERS):

                @pl.when(sends(unit, c))
                def _():
                    if i:
                        move(unit, i, c).wait_send()
                    else:
                        move(unit, i, c).wait()

                if i:

                    @pl.when(sends(unit, c ^ dc))
                    def _():
                        move(unit, i, c ^ dc).wait_recv()


def attend(n, qkv, lo, out_part, up_part, down_own):
    length = lo.shape[2]
    half = length // 2
    own = half // 4
    width, hidden = up_part.shape
    part = lambda p: pl.BlockSpec((1, HD, length), unit_block(p))
    unit = lambda rows, n: pl.BlockSpec((1, rows, n), lambda u: (u, 0, 0))
    heads = 4 * 3 * HD
    return pl.pallas_call(
        functools.partial(attend_kernel, n),
        grid=(UNITS,),
        in_specs=[part(0), part(1), part(2)]
        + [pl.BlockSpec((1, 1, length), lambda u: (u // 3, 0, 0))]
        + [
            pl.BlockSpec(a.shape, lambda u: (0, 0), pipeline_mode=pl.Buffered(1))
            for a in (out_part, up_part, down_own)
        ],
        out_specs=[HBM, unit(1, length), unit(HD, length)] + [HBM] * 3,
        scratch_shapes=[
            pltpu.VMEM((HD, length), low),
            pltpu.VMEM((length, HD), low),
            pltpu.VMEM((WIN + QB, QB), full),
            pltpu.VMEM((UNITS, HD, length), low),
            dma((7, UNITS)),
            dma((7, UNITS)),
            dma((UNITS,)),
            dma((3, 3)),
            dma((3, 3)),
            dma((3,)),
            dma((2, n - 1)),
            dma((2, n - 1)),
            dma((3,)),
            dma((3,)),
        ],
        out_shape=[
            jax.ShapeDtypeStruct((heads, 3 * own), low),
            jax.ShapeDtypeStruct((UNITS, 1, length), full),
            jax.ShapeDtypeStruct((UNITS, HD, length), full),
            shape((4, width, hidden), low),
            shape((4, width, hidden), low),
            shape((4,) + out_part.shape, low),
        ],
        compiler_params=pltpu.CompilerParams(
            vmem_limit_bytes=63 << 20, collective_id=1, has_side_effects=True
        ),
        cost_estimate=pl.CostEstimate(
            flops=UNITS * 18 * 2 * 256 * 1024 * 128, bytes_accessed=20 << 20, transcendentals=0
        ),
        name="attend",
    )(qkv, qkv, qkv, lo, out_part, up_part, down_own)


def add_to(ref, terms):
    for p in range(ref.shape[0]):
        ref[p] = (ref[p].astype(full) + terms(p).astype(full)).astype(low)


def attend_back_kernel(
    n, q_ref, k_ref, v_ref, lo_ref, lse_ref, of_ref, norm_ref, g_ref, gout, gud, side, part_sum,
    dall, gw_sum, zsum, osum, ssum,
    qs, ks, vs, grow, qrow, delta, dqs, soft, dscore, dbuf, gw, gwx, gwr, zr, gud_v, obuf, ogot, sgot, stot, sdp, ssem, rsem, lsem,
    zsend, zrecv, xsend, xrecv, osend, orecv, olocal, vlocal, s_send, s_recv, s_local, dsend, drecv,
):
    u = pl.program_id(0)
    c, t = place()
    d = lax.axis_index("dp")
    shard = gud.shape[1] // n
    length = lo_ref.shape[2]
    own = length // 8
    others = [lax.rem(d + r, n) for r in range(1, n)]
    peers = [at_peer(c, t, dc, r) for dc, r in PEERS[1:]] + [{"dp": o} for o in others]

    def rows_of(j):
        return pl.ds(pl.multiple_of(j * shard, shard), shard)

    def side_tensor(r):
        if r == 0:
            return pltpu.make_async_copy(side.at[t], sgot.at[0], s_local)
        return pltpu.make_async_remote_copy(
            side.at[t ^ r], sgot.at[r], s_send.at[r - 1], s_recv.at[r - 1], device_id={"tensor": t ^ r}
        )

    def side_dp(r):
        return pltpu.make_async_remote_copy(
            stot.at[rows_of(others[r - 1])],
            sdp.at[r - 1],
            dsend.at[r - 1],
            drecv.at[r - 1],
            device_id={"dp": others[r - 1]},
        )

    def line_of(h):
        pair = pl.ds(2 * h, 2)
        return Line(
            n,
            lambda j: gud.at[pair, rows_of(j)],
            lambda k, step: zr.at[h, k, step - 1],
            zsend.at[h],
            zrecv.at[h],
        )

    lines = [line_of(0), line_of(1)]

    def step_of(h, step, arrived=True):
        if arrived and step > 1:
            lines[h].received(step - 1)

        def add(k, j):
            rows = rows_of(j)
            add_to(zr.at[h, k, step - 2], lambda p: gud_v[2 * h + p, rows])

        lines[h].start(step, add)

    def finish(h):
        lines[h].received(n - 1)
        for step in range(2 if h == 0 else 1, n):
            lines[h].sent(step)
        for p in range(2):
            total = gud_v[2 * h + p, rows_of(d)].astype(full)
            up, down = (zr[h, k, n - 2, p].astype(full) for k in range(2))
            total += jnp.where(d > 0, up, 0.0) + jnp.where(d < n - 1, down, 0.0)
            zsum[2 * h + p] = total.astype(low)

    part_rows = gout.shape[1] // 2
    own_half = pl.ds(pl.multiple_of(c * part_rows, part_rows), part_rows)
    other_half = pl.ds(pl.multiple_of((1 - c) * part_rows, part_rows), part_rows)

    def out_grad(r):
        if r == 4:
            return pltpu.make_async_remote_copy(
                gout.at[:, other_half], ogot, osend.at[3], orecv.at[3], device_id={"context": 1 - c}
            )
        src, dst = ogot.at[t ^ r], obuf.at[r]
        if r == 0:
            return pltpu.make_async_copy(src, dst, olocal)
        return pltpu.make_async_remote_copy(
            src, dst, osend.at[r - 1], orecv.at[r - 1], device_id={"tensor": t ^ r}
        )

    def other_core():
        return pltpu.make_async_remote_copy(
            gwx.at[1 - c], gwr, xsend, xrecv, device_id={"context": 1 - c}
        )

    def load(i):
        if i == 2:
            return pltpu.make_async_copy(gud, gud_v, vlocal.at[2])
        return pltpu.make_async_copy(part_sum.at[i], zr.at[0, i, 0], vlocal.at[i])

    @pl.when(u == 0)
    def _():
        greet(peers)
        for i in range(3):
            load(i).start()
        gw[...] = jnp.zeros_like(gw)
        greeted(peers)
        out_grad(4).start()
        for r in range(1, 4):
            side_tensor(r).start()
        side_tensor(0).start()
        for i in range(3):
            load(i).wait()
        step_of(0, 2, False)
        step_of(1, 1)

    @pl.when(u == 1)
    def _():
        step_of(0, 3)
        out_grad(4).wait()
        for p in range(4):
            ogot[p] = (ogot[p].astype(full) + gout[p, own_half, :].astype(full)).astype(low)
        for r in range(1, 4):
            out_grad(r).start()
        out_grad(0).start()

    @pl.when(u == 2)
    def _():
        step_of(1, 2)

    @pl.when(u == 3)
    def _():
        side_tensor(0).wait()
        for r in range(1, 4):
            side_tensor(r).wait_recv()
        stot[...] = sum(sgot[r].astype(full) for r in range(4)).astype(low)
        for r in range(1, n):
            side_dp(r).start()

    @pl.when(u == 4)
    def _():
        step_of(1, 3)

    qs[...] = q_ref[0] * low(0.125)
    ks[...] = k_ref[0].T
    vs[...] = v_ref[0].T
    grow[...] = g_ref[0].T
    qrow[...] = qs[...].T
    delta[...] = jnp.sum(g_ref[0].astype(full) * of_ref[0], axis=0, keepdims=True)
    dqs[...] = jnp.zeros_like(dqs)
    for key_start in range(0, length, QB):
        rows = slice(key_start, key_start + QB)
        k, v, key_t = ks[rows, :], vs[rows, :], k_ref[0, :, rows]
        stop = min(key_start + WIN + QB, length)
        key_pos = key_start + lax.broadcasted_iota(jnp.int32, (QB, QB), 0)
        for start in range(key_start, stop, QB):
            cols = slice(start, start + QB)
            held = slice(start - key_start, start - key_start + QB)
            s = nn(k, qs[:, cols]) - lse_ref[0, :, cols]
            allowed = key_pos >= lo_ref[0, :, cols]
            if start == key_start:
                allowed &= key_pos <= start + lax.broadcasted_iota(jnp.int32, (QB, QB), 1)
            p = jnp.exp(jnp.where(allowed, s, NEG))
            dp = nn(v, g_ref[0, :, cols])
            soft[:, held] = p.astype(low)
            dscore[:, held] = (p * (dp - delta[:, cols])).astype(low)
        cols, held = slice(key_start, stop), slice(0, stop - key_start)
        dv = nn(soft[:, held], grow[cols, :])
        dk = nn(dscore[:, held], qrow[cols, :])
        dqs[:, cols] += nn(key_t, dscore[:, held])
        dbuf[u, 1, :, rows] = dk.T.astype(low)
        dbuf[u, 2, :, rows] = dv.T.astype(low)
    dbuf[u, 0] = (dqs[...] * 0.125).astype(low)

    def move(unit, i, source_core):
        dc, r = PEERS[i]
        h, seq = unit_place(unit, source_core)
        dest = pl.multiple_of(((c ^ dc) * 4 + (t ^ r)) * own, own)
        src = dbuf.at[unit, :, :, pl.ds(dest, own)]
        dst = dall.at[t, :, h, :, pl.ds(pl.multiple_of(seq * own, own), own)]
        if i == 0:
            return pltpu.make_async_copy(src, dst, lsem.at[unit])
        return pltpu.make_async_remote_copy(
            src, dst, ssem.at[i - 1, unit], rsem.at[i - 1, unit], device_id=at_peer(c, t, dc, r)
        )

    @pl.when(sends(u, c))
    def _():
        for i in range(1, len(PEERS)):
            move(u, i, c).start()
        move(u, 0, c).start()
        h, _ = unit_place(u, c)
        gw[h] += nn(dbuf[u].reshape(3 * HD, length), norm_ref[0])

    @pl.when(u == pl.num_programs(0) - 1)
    def _():
        wide_rows = [gw[h, p * HD : (p + 1) * HD, :] for p in range(3) for h in range(3)]
        gwx[0] = jnp.concatenate(wide_rows[:6], axis=0).T.astype(low)
        empty = jnp.zeros((3 * HD, gw.shape[2]), full)
        gwx[1] = jnp.concatenate(wide_rows[6:] + [empty], axis=0).T.astype(low)
        other_core().start()
        out_grad(0).wait()
        for r in range(1, 4):
            out_grad(r).wait()
        total = sum(obuf[r].astype(full) for r in range(4))
        osum[...] = total.astype(low)
        other_core().wait()
        gw_sum[...] = (gwx[c].astype(full) + gwr[...].astype(full)).astype(low)
        for step in range(4, n):
            step_of(0, step)
            step_of(1, step)
        finish(0)
        finish(1)
        total = stot[rows_of(d)].astype(full)
        for r in range(1, n):
            side_tensor(r).wait_send() if r < 4 else None
            side_dp(r).wait()
            total += sdp[r - 1].astype(full)
        ssum[...] = total
        for unit in range(UNITS):
            for i, (dc, r) in enumerate(PEERS):

                @pl.when(sends(unit, c))
                def _():
                    if i:
                        move(unit, i, c).wait_send()
                    else:
                        move(unit, i, c).wait()

                if i:

                    @pl.when(sends(unit, c ^ dc))
                    def _():
                        move(unit, i, c ^ dc).wait_recv()


def attend_back(n, qkv, grad_units, lo, lse, attended, normed, grad_out, grad_up_down, side, part_sum):
    length = lo.shape[2]
    own = length // 8
    width = normed.shape[2]
    shard, columns = grad_up_down.shape[1] // n, grad_up_down.shape[2]
    out_rows, local = grad_out.shape[1] // 2, grad_out.shape[2]
    part = lambda p: pl.BlockSpec((1, HD, length), unit_block(p))
    unit = lambda rows, m: pl.BlockSpec((1, rows, m), lambda u: (u, 0, 0))
    once = lambda dims: pl.BlockSpec(dims, lambda u: (0,) * len(dims), pipeline_mode=pl.Buffered(1))
    wide, tall = pltpu.VMEM((HD, length), low), pltpu.VMEM((length, HD), low)
    results = [(width, 2 * 3 * HD), (4, shard, columns), (out_rows, local)]
    return pl.pallas_call(
        functools.partial(attend_back_kernel, n),
        grid=(UNITS,),
        in_specs=[part(0), part(1), part(2)]
        + [
            pl.BlockSpec((1, 1, length), lambda u: (u // 3, 0, 0)),
            unit(1, length),
            unit(HD, length),
            pl.BlockSpec((1, length, width), lambda u: (u // 3, 0, 0)),
            unit(HD, length),
            once(grad_out.shape),
        ]
        + [HBM] * 3,
        out_specs=[HBM] + [once(r) for r in results] + [once((shard, SIDE))],
        scratch_shapes=[
            wide, tall, tall, tall, tall,
            pltpu.VMEM((1, length), full), pltpu.VMEM((HD, length), full),
            pltpu.VMEM((QB, WIN + QB), low), pltpu.VMEM((QB, WIN + QB), low),
            pltpu.VMEM((UNITS, 3, HD, length), low), pltpu.VMEM((3, 3 * HD, width), full),
            pltpu.VMEM((2, width, 6 * HD), low), pltpu.VMEM((width, 6 * HD), low),
            pltpu.VMEM((2, 2, n - 1, 2, shard, columns), low), pltpu.VMEM(grad_up_down.shape, low),
            pltpu.VMEM((4, out_rows, local), low), pltpu.VMEM((4, out_rows, local), low),
            pltpu.VMEM((4, width, SIDE), low), pltpu.VMEM((width, SIDE), low), pltpu.VMEM((n - 1, shard, SIDE), low),
            dma((7, UNITS)), dma((7, UNITS)), dma((UNITS,)),
            dma((2, 2, n - 1)), dma((2, 2, n - 1)), dma, dma, dma((4,)), dma((4,)), dma, dma((3,)),
            dma((3,)), dma((3,)), dma, dma((n - 1,)), dma((n - 1,)),
        ],
        out_shape=[shape((4, 3, 3, HD, 3 * own), low)]
        + [shape(r, low) for r in results]
        + [shape((shard, SIDE), full)],
        compiler_params=pltpu.CompilerParams(
            vmem_limit_bytes=63 << 20, collective_id=2, has_side_effects=True
        ),
        name="attend_back",
    )(qkv, qkv, qkv, lo, lse, attended, normed, grad_units, grad_out, grad_up_down, side, part_sum)


def last_kernel(
    n, dqkv_ref, w_ref, tokens_ref, middle_ref, gains, w_own, up_own, gain_one, gain_two, ssum, gw_sum, zsum, osum,
    grad_in, g_qkv, g_up, g_down, g_out, g_one, g_two,
    rg, rw, ro, down_n, out_t, mine, sums, dqkv, w_all, tokens, middle,
    gsend, grecv, wsend, wrecv, osend, orecv, lsem, csend, crecv, ssend, srecv, clocal, fetch,
):
    c, t = place()
    d = lax.axis_index("dp")
    shard, hidden = rg.shape[1], rg.shape[2]
    cut = n // 2
    group = [at_peer(c, t, dc, r) for dc, r in PEERS[1:]]
    others = [lax.rem(d + r, n) for r in range(1, n)]
    peers = group + [{"dp": o} for o in others]
    greet(peers)
    loads = [
        pltpu.make_async_copy(src, dst, fetch.at[i])
        for i, (src, dst) in enumerate(
            ((tokens_ref, tokens), (w_ref, w_all), (dqkv_ref, dqkv), (middle_ref, middle))
        )
    ]
    for copy in loads:
        copy.start()

    def rows_of(j):
        return pl.ds(pl.multiple_of(j * shard, shard), shard)

    narrow = slice(0, 256)

    def qkv_piece(r, core):
        src, dst = gw_sum.at[rows_of(d if r == 0 else others[r - 1])], rg.at[r]
        if core:
            src, dst = src.at[:, narrow], dst.at[:, narrow]
        if r == 0:
            return pltpu.make_async_copy(src, dst, lsem.at[0])
        return pltpu.make_async_remote_copy(
            src, dst, gsend.at[r - 1], grecv.at[r - 1], device_id={"dp": others[r - 1]}
        )

    def each_core(what):
        for core in range(2):

            @pl.when(c == core)
            def _():
                what(core)

    def up_piece(r):
        src, dst = zsum.at[t ^ r], rw.at[r]
        if r == 0:
            return pltpu.make_async_copy(src, dst, lsem.at[1])
        return pltpu.make_async_remote_copy(
            src, dst, wsend.at[r - 1], wrecv.at[r - 1], device_id={"tensor": t ^ r}
        )

    mine_out = d // cut == c

    def out_piece(r):
        to = d if r == 0 else others[r - 1]
        src, dst = osum.at[rows_of(lax.rem(to, cut))], ro.at[r]
        if r == 0:
            return pltpu.make_async_copy(src, dst, lsem.at[2])
        return pltpu.make_async_remote_copy(
            src, dst, osend.at[r - 1], orecv.at[r - 1], device_id={"dp": to}
        )

    def start_all(core):
        for r in range(1, n):
            qkv_piece(r, core).start()
        qkv_piece(0, core).start()

    greeted(peers)
    each_core(start_all)
    for r in range(1, 4):
        up_piece(r).start()
    up_piece(0).start()
    for r in range(1, n):

        @pl.when(others[r - 1] // cut == c)
        def _():
            out_piece(r).start()

    @pl.when(mine_out)
    def _():
        out_piece(0).start()

    for copy in loads:
        copy.wait()
    for m in range(0, tokens.shape[0], QB):
        rows = slice(m, m + QB)
        r = tn(dqkv[:, rows], w_all[...])
        v = tokens[rows, :].astype(full)
        inv = lax.rsqrt(jnp.mean(v * v, axis=-1, keepdims=True) + epsilon)
        rg_ = r * gains[0:1, :]
        grad = inv * (rg_ - v * (inv * inv * jnp.mean(rg_ * v, axis=-1, keepdims=True)))
        grad_in[rows, :] = (middle[rows, :] + grad).astype(low)

    def halves(j):
        half = pl.ds(pl.multiple_of(c * hidden, hidden), hidden)
        src, dst = (
            (mine.at[0], g_qkv.at[:, half]),
            (mine.at[1], g_up.at[:, half]),
            (down_n, g_down.at[:, half]),
            (out_t, g_out),
        )[j]
        return (
            pltpu.make_async_copy(src, dst, clocal.at[j]),
            pltpu.make_async_remote_copy(
                src, dst, csend.at[j], crecv.at[j], device_id={"context": 1 - c}
            ),
        )

    def deliver(j):
        for copy in halves(j):
            copy.start()

    up_piece(0).wait()
    for r in range(1, 4):
        up_piece(r).wait_recv()
    main = hidden - SIDE
    mine[1, :, :main] = sum(rw[r, :, :main].astype(full) for r in range(4))
    mine[1, :, main:] = ssum[...]
    down_n[...] = sum(rw[r, :, main:].astype(full) for r in range(4))
    deliver(1)
    deliver(2)

    @pl.when(mine_out)
    def _():
        out_piece(0).wait()
        for r in range(1, n):
            out_piece(r).wait_recv()
        out_t[...] = sum(ro[r].astype(full) for r in range(n)).T
        deliver(3)

    def take(core):
        qkv_piece(0, core).wait()
        for r in range(1, n):
            qkv_piece(r, core).wait_recv()
        if core:
            mine[0, :, narrow] = sum(rg[r, :, narrow].astype(full) for r in range(n))
            mine[0, :, 256:] = jnp.zeros((shard, hidden - 256), full)
        else:
            mine[0] = sum(rg[r].astype(full) for r in range(n))

    each_core(take)
    deliver(0)
    lane = lax.broadcasted_iota(jnp.int32, (shard, 128), 1)
    halves_of = [jnp.concatenate([w_own[0], w_own[1]], axis=1), jnp.pad(w_own[2], ((0, 0), (0, osum.shape[1])))]
    w_mine = jnp.where(c == 0, halves_of[0].astype(full), halves_of[1].astype(full))
    up_mine = up_own[:, pl.ds(pl.multiple_of(c * hidden, hidden), hidden)].astype(full)
    first = jnp.sum(w_mine * mine[0], axis=1, keepdims=True)
    second = jnp.sum(up_mine * mine[1], axis=1, keepdims=True)
    sums[0] = jnp.where(lane == 0, first, jnp.where(lane == 1, second, 0.0)).T[:8]

    def gain_piece(i):
        dc, r = PEERS[i]
        return pltpu.make_async_remote_copy(
            sums.at[0], sums.at[i], ssend.at[i - 1], srecv.at[i - 1], device_id=at_peer(c, t, dc, r)
        )

    for i in range(1, len(PEERS)):
        gain_piece(i).start()
    for i in range(1, len(PEERS)):
        gain_piece(i).wait()
    total = sum(sums[i] for i in range(len(PEERS)))
    g_one[...] = total[0:1, :] / gain_one[...].astype(full)
    g_two[...] = total[1:2, :] / gain_two[...].astype(full)

    for j in range(3):
        for copy in halves(j):
            copy.wait()

    @pl.when(mine_out)
    def _():
        local, away = halves(3)
        local.wait()
        away.wait_send()

    @pl.when(jnp.logical_not(mine_out))
    def _():
        halves(3)[1].wait_recv()

    for r in range(1, 4):
        up_piece(r).wait_send()

    def sent(core):
        for r in range(1, n):
            qkv_piece(r, core).wait_send()

    each_core(sent)
    for r in range(1, n):

        @pl.when(others[r - 1] // cut == c)
        def _():
            out_piece(r).wait_send()


def last(n, dqkv, w_all, tokens, middle, gains, w_own, up_own, gain_one, gain_two, ssum, gw_sum, zsum, osum):
    rows, width = tokens.shape
    shard, hidden = zsum.shape[1], gw_sum.shape[1]
    local = osum.shape[1]
    return pl.pallas_call(
        functools.partial(last_kernel, n),
        in_specs=[HBM] * 4 + [VMEM] * 6 + [ANY] * 3,
        out_specs=[VMEM] + [ANY] * 4 + [VMEM] * 2,
        out_shape=[
            shape((rows, width), low),
            shape((shard, 2 * hidden), full),
            shape((shard, 2 * hidden), full),
            shape((shard, 2 * hidden), full),
            shape((local, shard), full),
            shape((1, shard), full),
            shape((1, shard), full),
        ],
        scratch_shapes=[
            pltpu.VMEM((n, shard, hidden), low),
            pltpu.VMEM((4, shard, 2 * hidden - SIDE), low),
            pltpu.VMEM((n, shard, local), low),
            pltpu.VMEM((shard, hidden), full),
            pltpu.VMEM((local, shard), full),
            pltpu.VMEM((2, shard, hidden), full),
            pltpu.VMEM((8, 8, shard), full),
            pltpu.VMEM(dqkv.shape, low), pltpu.VMEM(w_all.shape, low),
            pltpu.VMEM((rows, width), low), pltpu.VMEM((rows, width), full),
            dma((n - 1,)), dma((n - 1,)), dma((3,)), dma((3,)), dma((n - 1,)), dma((n - 1,)), dma((3,)),
            dma((4,)), dma((4,)), dma((7,)), dma((7,)), dma((4,)), dma((4,)),
        ],
        compiler_params=pltpu.CompilerParams(
            vmem_limit_bytes=63 << 20, collective_id=4, has_side_effects=True
        ),
        name="last",
    )(dqkv, w_all, tokens, middle, gains, w_own, up_own, gain_one, gain_two, ssum, gw_sum, zsum, osum)


def close_kernel(*refs):
    count = len(refs) // 2
    for i, (src, dst) in enumerate(zip(refs[:count], refs[count:])):
        if i == 2:
            local = dst.shape[2]
            for p in range(3):
                dst[p] = src[:, p * local : (p + 1) * local]
        else:
            dst[...] = src[...]


def close(result, grad_input, own_attn, *others):
    arrays = (result, grad_input, own_attn, *others)
    rows = lambda a: pl.BlockSpec((a.shape[0] // 2, a.shape[1]), lambda i: (i, 0))
    shard, local = own_attn.shape[0], others[0].shape[0]
    parts = pl.BlockSpec((3, shard // 2, local), lambda i: (0, i, 0))
    outs = [shape(a.shape, a.dtype) for a in arrays]
    outs[2] = shape((3, shard, local), full)
    return pl.pallas_call(
        close_kernel,
        grid=(2,),
        in_specs=[rows(a) for a in arrays],
        out_specs=[parts if i == 2 else rows(a) for i, a in enumerate(arrays)],
        out_shape=outs,
        compiler_params=pltpu.CompilerParams(vmem_limit_bytes=63 << 20),
        name="close",
    )(*arrays)


def gelu_and_slope(v):
    k0 = math.sqrt(2.0 / math.pi)
    square = v * v
    th = jnp.tanh(v * (k0 + (k0 * 0.044715) * square))
    half = 0.5 + 0.5 * th
    slope = half + (v * half) * ((1.0 - th) * (k0 + (3.0 * 0.044715 * k0) * square))
    return v * half, slope


def feed_kernel(
    dp, att, proj, tokens, cot, gains, w_t, up_ref, down_ref,
    result, middle, gout, gud, side, part_sum, units, w_all,
    x, g, x_t, g_t, up, down, act, gh, out, back, proj_w, sent, got, gbuf, sbuf, gatt,
    xsend, xrecv, wsend, wrecv, wlocal, zsend, zrecv, glocal, usend, urecv, ulocal, load,
):
    c, t = place()
    d = lax.axis_index("dp")
    rows, width = tokens.shape
    own = rows // 3
    shard = width // dp
    n = up_ref.shape[2]
    local = proj.shape[2]
    other = {"context": 1 - c}
    peers = [at_peer(c, t, dc, r) for dc, r in PEERS[1:]]
    mine, theirs = slice(0, rows), slice(rows, 2 * rows)
    block = rows // 3

    def cross(k):
        src, dst = (
            (cot, g.at[theirs]),
            (x.at[mine], x.at[theirs]),
            (sent.at[0], got.at[0]),
            (sent.at[1], got.at[1]),
        )[k]
        return pltpu.make_async_remote_copy(src, dst, xsend.at[k], xrecv.at[k], device_id=other)

    half = pl.ds(pl.multiple_of(c * (w_t.shape[0] // 2), 8), w_t.shape[0] // 2)

    def over_tensor(r):
        if r == 4:
            ref = w_all.at[:, half]
            return pltpu.make_async_remote_copy(ref, ref, wsend.at[3], wrecv.at[3], device_id=other)
        src, dst = w_t.at[half], w_all.at[t, half]
        if r == 0:
            return pltpu.make_async_copy(src, dst, wlocal)
        return pltpu.make_async_remote_copy(
            src, dst, wsend.at[r - 1], wrecv.at[r - 1], device_id={"tensor": t ^ r}
        )

    def rows_of(i):
        return pl.ds(pl.multiple_of(i * shard, shard), shard)

    line = Line(
        dp,
        lambda i: gbuf.at[0, :, rows_of(i)],
        lambda k, step: part_sum.at[k],
        zsend,
        zrecv,
    )

    def keep(j):
        if j == 2:
            return pltpu.make_async_copy(sbuf, side, glocal.at[2])
        return pltpu.make_async_copy(gbuf.at[j], gud.at[pl.ds(2 * j, 2)], glocal.at[j])

    def leave(whole, i):
        dc, r = PEERS[i]
        to_c, to_t = c ^ dc, t ^ r
        head = to_t * 3 + (0 if whole else to_c)
        count, first = (3, 0) if whole else (2, 3)
        seq = 2 * to_c if whole else 1
        src = gatt.at[pl.ds(head, count), :, pl.ds(pl.multiple_of(seq * own, own), own)]
        dst = units.at[pl.ds(first, count), :, pl.ds(pl.multiple_of((c * 4 + t) * own, own), own)]
        k = 0 if whole else 1
        if i == 0:
            return pltpu.make_async_copy(src, dst, ulocal.at[k])
        return pltpu.make_async_remote_copy(
            src, dst, usend.at[k, i - 1], urecv.at[k, i - 1], device_id=at_peer(c, t, dc, r)
        )

    loads = [
        pltpu.make_async_copy(ref.at[p], dst.at[p // 2, :, pl.ds((p % 2) * n, n)], load.at[i, p])
        for i, (ref, dst) in enumerate(((up_ref, up), (down_ref, down)))
        for p in range(4)
    ]
    greet(peers)
    greet_line(dp, d)
    for copy in loads:
        copy.start()
    for p in range(4):
        proj_w[:, p * local : (p + 1) * local] = proj[p]
    greeted_line(dp, d, peers)
    cross(0).start()
    for r in range(1, 4):
        over_tensor(r).start()
    over_tensor(0).start()
    for m in range(0, rows, block):
        part = slice(m, m + block)
        v = tokens[part, :].astype(full) + nn(proj_w[...], att[:, part]).T
        middle[part, :] = v
        inv = lax.rsqrt(jnp.mean(v * v, axis=-1, keepdims=True) + epsilon)
        x[part, :] = (v * inv * gains[1:2, :]).astype(low)
    cross(1).start()
    g[mine, :] = cot[...]
    g_t[:, mine] = cot[...].T
    x_t[:, mine] = x[mine, :].T
    for copy in loads:
        copy.wait()

    def hidden(side):
        @pl.loop(0, 6)
        def _(i):
            j = i // 3
            part = pl.ds(pl.multiple_of((side * 3 + i % 3) * block, block), block)
            pre = nn(x[part, :], up[j])
            ga = nn(g[part, :], down[j])
            a, slope = gelu_and_slope(pre)
            act[j, part, :] = a.astype(low)
            gh[j, part, :] = (ga * slope).astype(low)

    def branch(left, right, part):
        return nt(left[0, part, :], right[0]) + nt(left[1, part, :], right[1])

    hidden(0)
    cross(0).wait_recv()
    cross(1).wait_recv()
    hidden(1)

    def cut(side, left, right, put):
        @pl.loop(0, 3)
        def _(i):
            here = pl.ds(pl.multiple_of(i * block, block), block)
            part = pl.ds(pl.multiple_of(side * rows + i * block, block), block)
            put(here, branch(left, right, part))

    def put_sent(k):
        def put(here, value):
            sent[k, here, :] = value.astype(low)

        return put

    def put_own(ref):
        def put(here, value):
            ref[here, :] = value

        return put

    cut(1, gh, up, put_sent(0))
    cross(2).start()
    cut(0, gh, up, put_own(back))
    over_tensor(0).wait()
    for r in range(1, 4):
        over_tensor(r).wait_recv()
    over_tensor(4).start()
    x_t[:, theirs] = x[theirs, :].T
    g_t[:, theirs] = g[theirs, :].T
    cross(2).wait_recv()
    gain = gains[1:2, :]
    low_t = x
    for m in range(0, rows, block):
        part = slice(m, m + block)
        r = (back[part, :] + got[0, part, :].astype(full)) * gain
        v = middle[part, :]
        inv = lax.rsqrt(jnp.mean(v * v, axis=-1, keepdims=True) + epsilon)
        grad = inv * (r - v * (inv * inv * jnp.mean(r * v, axis=-1, keepdims=True)))
        back[part, :] = cot[part, :].astype(full) + grad
        low_t[rows : rows + width, part] = back[part, :].astype(low).T
        grad = tn(proj_w[...], low_t[rows : rows + width, part]).astype(low)
        gatt[:, :, part] = grad.reshape(gatt.shape[0], HD, block)
    for whole in (True, False):
        for i in range(1, len(PEERS)):
            leave(whole, i).start()
        leave(whole, 0).start()

    def weight_grad(j, a, left_t, right):
        @pl.loop(0, 3)
        def _(i):
            part = pl.ds(pl.multiple_of(i * (width // 3), width // 3), width // 3)
            grad = nn(left_t[part, :], right[j]).astype(low)
            main = n - SIDE
            for p in range(2):
                if a:
                    gbuf[j, p, part, main:] = grad[:, p * n : (p + 1) * n]
                else:
                    gbuf[j, p, part, :main] = grad[:, p * n : p * n + main]
                    sbuf[2 * j + p, part, :] = grad[:, p * n + main : (p + 1) * n]

    weight_grad(0, 0, x_t, gh)
    weight_grad(0, 1, g_t, act)
    line.start(1, None)
    keep(0).start()
    cut(1, act, down, put_sent(1))
    cross(3).start()
    weight_grad(1, 0, x_t, gh)
    weight_grad(1, 1, g_t, act)
    keep(1).start()
    keep(2).start()
    cut(0, act, down, put_own(out))
    for m in range(0, width, block):
        part = slice(m, m + block)
        big = nt(low_t[rows + m : rows + m + block, :], att[...]).astype(low)
        for p in range(4):
            gout[p, part, :] = big[:, p * local : (p + 1) * local]
    cross(3).wait_recv()
    result[...] = (middle[...] + out[...] + got[1].astype(full)).astype(low)
    middle[...] = back[...]
    for k in range(4):
        cross(k).wait_send()
    for r in range(1, 4):
        over_tensor(r).wait_send()
    over_tensor(4).wait()
    line.received(1)
    line.sent(1)
    for j in range(3):
        keep(j).wait()
    for whole in (True, False):
        for i in range(len(PEERS)):
            leave(whole, i).wait()


def feed(dp, att, proj, tokens, cot, gains, w_t, up, down):
    rows, width = tokens.shape
    pieces, _, n = up.shape
    own = rows // 3
    assert pieces == 4 and dp > 2 and rows == width
    return pl.pallas_call(
        functools.partial(feed_kernel, dp),
        in_specs=[VMEM] * 6 + [HBM] * 2,
        out_specs=[VMEM] * 3 + [HBM] * 5,
        out_shape=[
            shape((rows, width), low),
            shape((rows, width), full),
            shape(proj.shape, low),
            shape((4, width, 2 * n - SIDE), low),
            shape((4, width, SIDE), low),
            shape((2, 2, width // dp, 2 * n - SIDE), low),
            shape((UNITS, HD, 8 * own), low),
            shape((4,) + w_t.shape, low),
        ],
        scratch_shapes=[pltpu.VMEM((2 * rows, width), low)] * 2
        + [pltpu.VMEM((width, 2 * rows), low)] * 2
        + [pltpu.VMEM((2, width, 2 * n), low)] * 2
        + [pltpu.VMEM((2, 2 * rows, 2 * n), low)] * 2
        + [pltpu.VMEM((rows, width), full)] * 2
        + [pltpu.VMEM((width, width), low)]
        + [pltpu.VMEM((2, rows, width), low)] * 2
        + [pltpu.VMEM((2, 2, width, 2 * n - SIDE), low), pltpu.VMEM((4, width, SIDE), low)]
        + [pltpu.VMEM((12, HD, rows), low)]
        + [dma((4,)), dma((4,)), dma((4,)), dma((4,)), dma]
        + [dma((2, 1)), dma((2, 1)), dma((3,)), dma((2, 7)), dma((2, 7)), dma((2,)), dma((2, 4))],
        compiler_params=pltpu.CompilerParams(
            vmem_limit_bytes=63 << 20, collective_id=5, has_side_effects=True
        ),
        name="feed",
    )(att, proj, tokens, cot, gains, w_t, up, down)


def per_device(tokens, segments, w_qkv, w_out, w_in, w_back, gain_attn, gain_mlp, cotangent):
    sequences, own, width = tokens.shape
    assert lax.axis_size("tensor") == 4 and lax.axis_size("context") == 2 and sequences == 3
    n = lax.axis_size("dp")
    length = segments.shape[1]
    shard = w_qkv.shape[0]
    local = w_qkv.shape[2]
    rows = sequences * own
    parts = w_qkv.transpose(1, 0, 2)
    gain_one, gain_two = gain_attn.reshape(1, shard), gain_mlp.reshape(1, shard)
    qkv, normed_units, w_t, up_part, out_part, gains, lo = project(
        n, tokens, segments, parts, w_in, w_out, gain_one, gain_two
    )
    attended, log_totals, out_full, w_up, w_down, w_proj = attend(
        n, qkv, lo, out_part, up_part, w_back.T
    )
    flat = tokens.reshape(rows, width)
    result, grad_middle, grad_out, grad_up_down, side, part_sum, grad_units, w_all = feed(
        n, attended, w_proj, flat, cotangent.reshape(rows, width), gains, w_t, w_up, w_down
    )
    grad_projected, gw_sum, zsum, osum, ssum = attend_back(
        n, qkv, grad_units, lo, log_totals, out_full, normed_units, grad_out, grad_up_down, side, part_sum
    )
    grad_input, own_attn, own_up, own_down, own_proj, own_one, own_two = last(
        n,
        grad_projected.reshape(12 * local, rows),
        w_all.reshape(12 * local, width),
        flat,
        grad_middle,
        gains,
        parts,
        w_in,
        gain_one,
        gain_two,
        ssum,
        gw_sum,
        zsum,
        osum,
    )
    result, grad_input, own_attn, own_proj, own_up, own_down = close(
        result, grad_input, own_attn, own_proj, own_up, own_down
    )
    return (
        result.reshape(sequences, own, width),
        grad_input.reshape(sequences, own, width),
        own_attn.transpose(1, 0, 2),
        own_proj,
        own_up,
        own_down.T,
        own_one.reshape(shard),
        own_two.reshape(shard),
    )


def solution(mesh):
    return jax.shard_map(
        per_device,
        mesh=mesh,
        in_specs=(
            P("dp", ("context", "tensor"), None),
            P("dp", None),
            P("dp", None, "tensor"),
            P("tensor", "dp"),
            P("dp", "tensor"),
            P("tensor", "dp"),
            P("dp"),
            P("dp"),
            P("dp", ("context", "tensor"), None),
        ),
        out_specs=(
            P("dp", ("context", "tensor"), None),
            P("dp", ("context", "tensor"), None),
            P("dp", None, "tensor"),
            P("tensor", "dp"),
            P("dp", "tensor"),
            P("tensor", "dp"),
            P("dp"),
            P("dp"),
        ),
        check_vma=False,
    )
```

```python
import functools
import math

import jax
import jax.numpy as jnp
from jax import lax
from jax.experimental import pallas as pl
from jax.experimental.pallas import tpu as pltpu
from jax.sharding import PartitionSpec as P

HD = 64
WIN = 1536
QB = 256
CHUNK = 128
NEG = -1e30
epsilon = 1e-06
low = jnp.bfloat16
full = jnp.float32


def dot(left, right, dims):
    return lax.dot_general(left, right, (dims, ((), ())), preferred_element_type=full)


def nn(left, right):
    return dot(left, right, ((1,), (0,)))


def nt(left, right):
    return dot(left, right, ((1,), (1,)))


def tn(left, right):
    return dot(left, right, ((0,), (0,)))


PEERS = [(dc, r) for dc in range(2) for r in range(4)]


def place():
    return lax.axis_index("context"), lax.axis_index("tensor")


def at_peer(c, t, dc, r):
    return {"context": c ^ dc, "tensor": t ^ r}


def greet(peers):
    for peer in peers:
        pl.semaphore_signal(pltpu.get_barrier_semaphore(), inc=1, device_id=peer)


def greeted(peers):
    pl.semaphore_wait(pltpu.get_barrier_semaphore(), len(peers))


def unit_place(u, c):
    return jnp.where(u < 3, u, c + u - 3), jnp.where(u < 3, 2 * c, 1)


def sends(u, c):
    return (u != 3) | (c == 0)


dma = pltpu.SemaphoreType.DMA
ANY = pl.BlockSpec(memory_space=pl.ANY)
VMEM = pl.BlockSpec(memory_space=pltpu.VMEM)
HBM = pl.BlockSpec(memory_space=pltpu.HBM)
shape = jax.ShapeDtypeStruct

SIDE = 128


class Line:
    def __init__(self, n, own, slot, send, recv):
        self.n, self.own, self.slot, self.sems = n, own, slot, (send, recv)
        self.d = lax.axis_index("dp")

    def along(self, k):
        m = self.d if k == 0 else self.n - 1 - self.d
        to = {"dp": jnp.clip(self.d + 1 if k == 0 else self.d - 1, 0, self.n - 1)}
        return m, to

    def target(self, k, step):
        m, _ = self.along(k)
        return jnp.clip(self.n - step + m if k == 0 else step - 1 - m, 0, self.n - 1)

    def copy(self, k, step, src):
        send, recv = self.sems
        _, to = self.along(k)
        return pltpu.make_async_remote_copy(
            src, self.slot(k, step), send.at[k, step - 1], recv.at[k, step - 1], device_id=to
        )

    def arrive(self, k, step):
        self.copy(k, step, self.slot(k, step)).wait_recv()

    def start(self, step, add):
        for k in range(2):
            m, _ = self.along(k)
            if step > 1:

                @pl.when((m >= 1) & (m < self.n - 1) & (step >= m + 1))
                def _():
                    add(k, self.target(k, step))
                    self.copy(k, step, self.slot(k, step - 1)).start()

            @pl.when(m == 0)
            def _():
                self.copy(k, step, self.own(self.target(k, step))).start()

    def received(self, step):
        for k in range(2):
            m, _ = self.along(k)

            @pl.when((m >= 1) & (step >= m))
            def _():
                self.arrive(k, step)

    def sent(self, step):
        for k in range(2):
            m, _ = self.along(k)

            @pl.when((m < self.n - 1) & (step >= m + 1))
            def _():
                self.copy(k, step, self.slot(k, step)).wait_send()


def greet_line(n, d):
    barrier = pltpu.get_barrier_semaphore()

    @pl.when(d > 0)
    def _():
        pl.semaphore_signal(barrier, inc=1, device_id={"dp": jnp.maximum(d - 1, 0)})

    @pl.when(d < n - 1)
    def _():
        pl.semaphore_signal(barrier, inc=1, device_id={"dp": jnp.minimum(d + 1, n - 1)})


def greeted_line(n, d, peers):
    ends = jnp.where(d > 0, 1, 0) + jnp.where(d < n - 1, 1, 0)
    pl.semaphore_wait(pltpu.get_barrier_semaphore(), len(peers) + ends)


def project_kernel(
    n, tokens, segments, w_qkv, up, out_own, gain_one, gain_two, qkv, norm, w_t, up_all, out_all, gain_ref, lo_ref,
    tok, x, w, proj, out_w, gain, own_gain, tsend, trecv, tlocal, wsend, wrecv, wlocal, osend, orecv, olocal, xsend, xrecv,
):
    c, t = place()
    d = lax.axis_index("dp")
    own = tokens.shape[1]
    width = tokens.shape[2]
    span = 4 * own
    shard = up.shape[0]
    half = own // 2
    hidden = up_all.shape[1]
    cut = n // 2
    to_x, to_y, to_core = {"tensor": t ^ 1}, {"tensor": t ^ 2}, {"context": 1 - c}
    others = [{"dp": lax.rem(d + r, n)} for r in range(1, n)]
    peers = [to_x, to_y, to_core] + others
    greet(peers)

    def local(i, s):
        return pltpu.make_async_copy(tokens.at[s], tok.at[s, t], tlocal.at[i])

    def weights(j, r):
        rows = pl.ds(pl.multiple_of(d * shard, shard), shard)
        source, target = (
            (w_qkv, w.at[:, rows]),
            (out_w, out_all.at[rows]),
            (up.at[:, pl.ds(pl.multiple_of(c * hidden, hidden), hidden)], up_all.at[rows]),
            (own_gain, gain.at[d]),
        )[j]
        if r == 0:
            return pltpu.make_async_copy(source, target, wlocal.at[j])
        return pltpu.make_async_remote_copy(
            source, target, wsend.at[j, r - 1], wrecv.at[j, r - 1], device_id=others[r - 1]
        )

    def gives(j, r):
        return lax.rem(d + n - r, n) // cut == c if j < 2 else True

    def weights_do(j, r, what, source=False):
        @pl.when(gives(j, 0 if source else r))
        def _():
            getattr(weights(j, r), what)()

    def to_other(j):
        rows = pl.ds(pl.multiple_of(c * cut * shard, shard), cut * shard)
        ref = w.at[:, rows]
        return pltpu.make_async_remote_copy(ref, ref, xsend, xrecv, device_id=to_core)

    order = (2 * (1 - c), 1, 2 * c)
    for i, s in enumerate(order):
        local(i, s).start()
    out_w[...] = out_own[...].T
    own_gain[...] = jnp.zeros_like(own_gain)
    own_gain[0:1, :] = gain_one[...]
    own_gain[1:2, :] = gain_two[...]
    for j in range(4):
        weights_do(j, 0, "start")
    greeted(peers)
    for j in (0, 3, 1, 2):
        for r in range(1, n):
            weights_do(j, r, "start", True)

    def hop(k, i):
        s = order[i]
        origin, rows, peer = (
            (t, slice(0, half), to_x),
            (t, slice(half, own), to_y),
            (t, slice(0, half), to_y),
            (t, slice(half, own), to_x),
            (t ^ 1, slice(0, half), to_y),
            (t ^ 2, slice(half, own), to_x),
        )[k]
        there = tok.at[s, origin, rows]
        here = tokens.at[s, rows] if k < 4 else there
        return pltpu.make_async_remote_copy(
            here, there, tsend.at[k, i], trecv.at[k, i], device_id=peer
        )

    def straight(i):
        for k in range(4):
            hop(k, i).start()

    def forward(i):
        for k in range(2):
            hop(k, i).wait_recv()
            hop(k + 4, i).start()

    units = proj.shape[1]

    def leave(i):
        out = []
        lanes = pl.ds(pl.multiple_of(c * span, span), span)
        if i != 0:
            out.append((x.at[i], norm.at[2 - i, lanes], False))
        if i != 2:
            out.append((x.at[i], norm.at[i, lanes], True))
        if i == 0:
            out.append((proj.at[0], qkv.at[pl.ds(0, units), :, lanes], True))
        if i == 2:
            out.append((proj.at[2], qkv.at[pl.ds(0, units), :, lanes], False))
        if i == 1:
            for away in (True, False):
                core = 1 - c if away else c
                for p in range(3):
                    src = proj.at[1, pl.ds(p * 3 + core, 2)]
                    out.append((src, qkv.at[pl.ds(units + 2 * p, 2), :, lanes], away))
        copies = []
        for j, (src, dst, away) in enumerate(out):
            if away:
                copies.append(
                    (away, pltpu.make_async_remote_copy(src, dst, osend.at[i, j], orecv.at[i, j], device_id=to_core))
                )
            else:
                copies.append((away, pltpu.make_async_copy(src, dst, olocal.at[i, j])))
        return copies

    def work(i):
        s = order[i]
        local(i, s).wait()
        for k in range(2, 6):
            hop(k, i).wait_recv()

        @pl.loop(0, 4)
        def _(p):
            rows = pl.ds(pl.multiple_of(p * own, own), own)
            v = tok[s, p].astype(full)
            inv = lax.rsqrt(jnp.mean(v * v, axis=-1, keepdims=True) + epsilon)
            normed = (v * inv * gain_ref[0:1, :]).astype(low)
            x[i, rows, :] = normed
            proj[i, :, :, rows] = nt(w_t[...], normed).astype(low).reshape(units, HD, own)

        for _, copy in leave(i):
            copy.start()

    straight(0)
    straight(1)
    forward(0)
    straight(2)
    seg = segments[...]
    first = jnp.zeros(seg.shape, jnp.int32)
    for value in range(8):
        before = jnp.sum((seg < value).astype(jnp.int32), axis=1, keepdims=True)
        first = jnp.where(seg == value, before, first)
    first = jnp.maximum(first, lax.broadcasted_iota(jnp.int32, seg.shape, 1) - (WIN - 1))
    lo_ref[0] = jnp.where(c == 0, first[0:1], first[2:3])
    lo_ref[1] = first[1:2]
    weights_do(0, 0, "wait")
    for r in range(1, n):
        weights_do(0, r, "wait_recv")
    to_other(0).start()
    weights(3, 0).wait()
    for r in range(1, n):
        weights(3, r).wait_recv()
    gain_ref[...] = jnp.concatenate([gain[i].astype(full) for i in range(n)], axis=1)[:8]
    to_other(0).wait_recv()
    for p in range(3):
        w_t[p * 3 * HD : (p + 1) * 3 * HD, :] = w[p].T
    forward(1)
    work(0)
    forward(2)
    work(1)
    work(2)
    to_other(0).wait_send()
    for j in range(4):
        if j in (1, 2):
            weights_do(j, 0, "wait")
        for r in range(1, n):
            weights_do(j, r, "wait_send", True)
            if j in (1, 2):
                weights_do(j, r, "wait_recv")
    for i in range(3):
        for k in range(6):
            hop(k, i).wait_send()
        for away, copy in leave(i):
            copy.wait()


def project(n, tokens, segments, w_qkv, up, out_own, gain_one, gain_two):
    sequences, own, width = tokens.shape
    shard, hidden = up.shape[0], up.shape[1] // 2
    local = out_own.shape[0]
    span = 4 * own
    return pl.pallas_call(
        functools.partial(project_kernel, n),
        in_specs=[HBM, VMEM, HBM, HBM, VMEM, VMEM, VMEM],
        out_specs=[HBM] * 2 + [VMEM] + [HBM] * 2 + [VMEM] * 2,
        out_shape=[
            shape((15, HD, 2 * span), low),
            shape((2, 2 * span, width), low),
            shape((9 * HD, n * shard), low),
            shape((n * shard, hidden), low),
            shape((n * shard, local), low),
            shape((8, n * shard), full),
            shape((2, 1, segments.shape[1]), jnp.int32),
        ],
        scratch_shapes=[
            pltpu.VMEM((sequences, 4, own, width), low),
            pltpu.VMEM((sequences, span, width), low),
            pltpu.VMEM((3, n * shard, local), low),
            pltpu.VMEM((sequences, 9, HD, span), low),
            pltpu.VMEM((shard, local), low),
            pltpu.VMEM((n, 16, shard), low),
            pltpu.VMEM((16, shard), low),
            dma((6, 3)), dma((6, 3)), dma((3,)),
            dma((4, n - 1)), dma((4, n - 1)), dma((4,)),
            dma((3, 8)), dma((3, 8)), dma((3, 8)), dma, dma,
        ],
        compiler_params=pltpu.CompilerParams(
            vmem_limit_bytes=63 << 20, collective_id=3, has_side_effects=True
        ),
        name="project",
    )(tokens, segments, w_qkv, up, out_own, gain_one, gain_two)


UNITS = 5
def unit_block(part):
    return lambda u: (jnp.where(u < 3, part * 3 + u, 9 + part * 2 + (u - 3)), 0, 0)


def attend_kernel(
    n, q_ref, k_ref, v_ref, lo_ref, out_part, up_part, down_own, att, lse_ref, of_ref, up, down, out_w,
    qs, ks, ss, obuf, ssem, rsem, lsem, wsend, wrecv, wlocal, zsend, zrecv, fsend, frecv,
):
    u = pl.program_id(0)
    c, t = place()
    d = lax.axis_index("dp")
    shard = down_own.shape[0]
    hidden = down.shape[2]
    peers = [at_peer(c, t, dc, r) for dc, r in PEERS[1:]]

    part = out_part.shape[0] // 2
    mine = pl.ds(pl.multiple_of(c * part, part), part)

    def weight(j, r):
        rows = pl.ds(pl.multiple_of(d * shard, shard), shard)
        src, dst = (
            (down_own.at[:, pl.ds(pl.multiple_of(c * hidden, hidden), hidden)], down.at[t, rows]),
            (up_part, up.at[t]),
            (out_part.at[mine], out_w.at[t, mine]),
        )[j]
        if r == 0:
            return pltpu.make_async_copy(src, dst, wlocal.at[j])
        return pltpu.make_async_remote_copy(
            src, dst, wsend.at[j, r - 1], wrecv.at[j, r - 1], device_id={"tensor": t ^ r}
        )

    def onward(k):
        if k == 2:
            ref, peer = out_w.at[:, mine], {"context": 1 - c}
        else:
            rows = pl.ds(k * part, part)
            ref, peer = up.at[t ^ (1 + k), rows], {"tensor": t ^ (2 - k)}
        return pltpu.make_async_remote_copy(
            ref, ref, fsend.at[k], frecv.at[k], device_id=peer
        )

    def shards(step, up_line):
        src = d - step if up_line else d + step
        rows = pl.ds(pl.multiple_of(jnp.clip(src, 0, n - 1) * shard, shard), shard)
        to = jnp.clip(d + 1 if up_line else d - 1, 0, n - 1)
        k = 0 if up_line else 1
        return pltpu.make_async_remote_copy(
            down.at[:, rows], down.at[:, rows], zsend.at[k, step], zrecv.at[k, step], device_id={"dp": to}
        )

    def line(step, what):
        for up_line in (True, False):
            inside = (d < n - 1) if up_line else (d > 0)
            has = (d >= step) if up_line else (d <= n - 1 - step)
            comes = (d >= step + 1) if up_line else (d <= n - 2 - step)
            if what == "recv":

                @pl.when(comes)
                def _():
                    shards(step, up_line).wait_recv()
            else:

                @pl.when(inside & has)
                def _():
                    if what == "start":
                        shards(step, up_line).start()
                    else:
                        shards(step, up_line).wait_send()
    length = lo_ref.shape[2]
    half = length // 2
    own = half // 4

    @pl.when(u == 0)
    def _():
        greet(peers)
        greet_line(n, d)
        for j in range(3):
            weight(j, 0).start()
        greeted_line(n, d, peers)
        for r in range(1, 4):
            weight(0, r).start()

    qs[...] = q_ref[0] * low(0.125)
    ks[...] = k_ref[0].T
    for start in range(0, length, QB):
        stop = start + QB
        q = qs[:, start:stop]
        lo = lo_ref[0, :, start:stop]
        first = max(0, start - WIN)
        most = jnp.full((8, QB), NEG, full)
        for at in range(first, stop, CHUNK):
            s = nn(ks[at : at + CHUNK, :], q)
            key_pos = at + lax.broadcasted_iota(jnp.int32, (CHUNK, QB), 0)
            allowed = key_pos >= lo
            if at + CHUNK - 1 > start:
                allowed &= key_pos <= start + lax.broadcasted_iota(jnp.int32, (CHUNK, QB), 1)
            s = jnp.where(allowed, s, NEG)
            ss[at - first : at - first + CHUNK, :] = s
            most = jnp.maximum(most, jnp.max(s.reshape(CHUNK // 8, 8, QB), axis=0))
        most = jnp.max(most, axis=0, keepdims=True)
        total = jnp.zeros((8, QB), full)
        acc = jnp.zeros((HD, QB), full)
        for at in range(first, stop, CHUNK):
            p = jnp.exp(ss[at - first : at - first + CHUNK, :] - most)
            total += jnp.sum(p.reshape(CHUNK // 8, 8, QB), axis=0)
            acc += nn(v_ref[0, :, at : at + CHUNK], p.astype(low))
        total = jnp.sum(total, axis=0, keepdims=True)
        lse_ref[0, :, start:stop] = most + jnp.log(total)
        o = acc * (1.0 / total)
        of_ref[0, :, start:stop] = o
        obuf[u, :, start:stop] = o.astype(low)

    @pl.when(u == 0)
    def _():
        weight(0, 0).wait()
        for r in range(1, 4):
            weight(0, r).wait_recv()
        line(0, "start")
        for j, count in ((1, 3), (2, 4)):
            for r in range(1, count):
                weight(j, r).start()

    @pl.when(u == 3)
    def _():
        if n > 2:
            line(0, "recv")
            line(1, "start")
        for k in range(2):
            weight(1, 1 + k).wait_recv()
            onward(k).start()
        weight(2, 0).wait()
        for r in range(1, 4):
            weight(2, r).wait_recv()
        onward(2).start()

    def move(unit, i, source_core):
        dc, r = PEERS[i]
        h, seq = unit_place(unit, source_core)
        dest = pl.multiple_of(((c ^ dc) * 4 + (t ^ r)) * own, own)
        src = obuf.at[unit, :, pl.ds(dest, own)]
        dst = att.at[
            pl.ds(pl.multiple_of((t * 3 + h) * HD, HD), HD), pl.ds(pl.multiple_of(seq * own, own), own)
        ]
        if i == 0:
            return pltpu.make_async_copy(src, dst, lsem.at[unit])
        return pltpu.make_async_remote_copy(
            src, dst, ssem.at[i - 1, unit], rsem.at[i - 1, unit], device_id=at_peer(c, t, dc, r)
        )

    @pl.when(sends(u, c))
    def _():
        for i in range(1, len(PEERS)):
            move(u, i, c).start()
        move(u, 0, c).start()

    @pl.when(u == pl.num_programs(0) - 1)
    def _():
        for step in range(2, n - 1):
            line(step - 1, "recv")
            line(step, "start")
        line(n - 2, "recv")
        for step in range(n - 1):
            line(step, "sent")
        weight(1, 0).wait()
        for j in range(3):
            for r in range(1, 3 if j == 1 else 4):
                weight(j, r).wait_send()
        for k in range(3):
            onward(k).wait()
        for unit in range(UNITS):
            for i, (dc, r) in enumerate(PEERS):

                @pl.when(sends(unit, c))
                def _():
                    if i:
                        move(unit, i, c).wait_send()
                    else:
                        move(unit, i, c).wait()

                if i:

                    @pl.when(sends(unit, c ^ dc))
                    def _():
                        move(unit, i, c ^ dc).wait_recv()


def attend(n, qkv, lo, out_part, up_part, down_own):
    length = lo.shape[2]
    half = length // 2
    own = half // 4
    width, hidden = up_part.shape
    part = lambda p: pl.BlockSpec((1, HD, length), unit_block(p))
    unit = lambda rows, n: pl.BlockSpec((1, rows, n), lambda u: (u, 0, 0))
    heads = 4 * 3 * HD
    return pl.pallas_call(
        functools.partial(attend_kernel, n),
        grid=(UNITS,),
        in_specs=[part(0), part(1), part(2)]
        + [pl.BlockSpec((1, 1, length), lambda u: (u // 3, 0, 0))]
        + [
            pl.BlockSpec(a.shape, lambda u: (0, 0), pipeline_mode=pl.Buffered(1))
            for a in (out_part, up_part, down_own)
        ],
        out_specs=[HBM, unit(1, length), unit(HD, length)] + [HBM] * 3,
        scratch_shapes=[
            pltpu.VMEM((HD, length), low),
            pltpu.VMEM((length, HD), low),
            pltpu.VMEM((WIN + QB, QB), full),
            pltpu.VMEM((UNITS, HD, length), low),
            dma((7, UNITS)),
            dma((7, UNITS)),
            dma((UNITS,)),
            dma((3, 3)),
            dma((3, 3)),
            dma((3,)),
            dma((2, n - 1)),
            dma((2, n - 1)),
            dma((3,)),
            dma((3,)),
        ],
        out_shape=[
            jax.ShapeDtypeStruct((heads, 3 * own), low),
            jax.ShapeDtypeStruct((UNITS, 1, length), full),
            jax.ShapeDtypeStruct((UNITS, HD, length), full),
            shape((4, width, hidden), low),
            shape((4, width, hidden), low),
            shape((4,) + out_part.shape, low),
        ],
        compiler_params=pltpu.CompilerParams(
            vmem_limit_bytes=63 << 20, collective_id=1, has_side_effects=True
        ),
        cost_estimate=pl.CostEstimate(
            flops=UNITS * 18 * 2 * 256 * 1024 * 128, bytes_accessed=20 << 20, transcendentals=0
        ),
        name="attend",
    )(qkv, qkv, qkv, lo, out_part, up_part, down_own)


def add_to(ref, terms):
    for p in range(ref.shape[0]):
        ref[p] = (ref[p].astype(full) + terms(p).astype(full)).astype(low)


def attend_back_kernel(
    n, q_ref, k_ref, v_ref, lo_ref, lse_ref, of_ref, norm_ref, g_ref, gout, gud, side, part_sum,
    dall, gw_sum, zsum, osum, ssum,
    qs, ks, vs, grow, qrow, delta, dqs, soft, dscore, dbuf, gw, gwx, gwr, zr, gud_v, obuf, ogot, sgot, stot, sdp, ssem, rsem, lsem,
    zsend, zrecv, xsend, xrecv, osend, orecv, olocal, vlocal, s_send, s_recv, s_local, dsend, drecv,
):
    u = pl.program_id(0)
    c, t = place()
    d = lax.axis_index("dp")
    shard = gud.shape[1] // n
    length = lo_ref.shape[2]
    own = length // 8
    others = [lax.rem(d + r, n) for r in range(1, n)]
    peers = [at_peer(c, t, dc, r) for dc, r in PEERS[1:]] + [{"dp": o} for o in others]

    def rows_of(j):
        return pl.ds(pl.multiple_of(j * shard, shard), shard)

    def side_tensor(r):
        if r == 0:
            return pltpu.make_async_copy(side.at[t], sgot.at[0], s_local)
        return pltpu.make_async_remote_copy(
            side.at[t ^ r], sgot.at[r], s_send.at[r - 1], s_recv.at[r - 1], device_id={"tensor": t ^ r}
        )

    def side_dp(r):
        return pltpu.make_async_remote_copy(
            stot.at[rows_of(others[r - 1])],
            sdp.at[r - 1],
            dsend.at[r - 1],
            drecv.at[r - 1],
            device_id={"dp": others[r - 1]},
        )

    def line_of(h):
        pair = pl.ds(2 * h, 2)
        return Line(
            n,
            lambda j: gud.at[pair, rows_of(j)],
            lambda k, step: zr.at[h, k, step - 1],
            zsend.at[h],
            zrecv.at[h],
        )

    lines = [line_of(0), line_of(1)]

    def step_of(h, step, arrived=True):
        if arrived and step > 1:
            lines[h].received(step - 1)

        def add(k, j):
            rows = rows_of(j)
            add_to(zr.at[h, k, step - 2], lambda p: gud_v[2 * h + p, rows])

        lines[h].start(step, add)

    def finish(h):
        lines[h].received(n - 1)
        for step in range(2 if h == 0 else 1, n):
            lines[h].sent(step)
        for p in range(2):
            total = gud_v[2 * h + p, rows_of(d)].astype(full)
            up, down = (zr[h, k, n - 2, p].astype(full) for k in range(2))
            total += jnp.where(d > 0, up, 0.0) + jnp.where(d < n - 1, down, 0.0)
            zsum[2 * h + p] = total.astype(low)

    part_rows = gout.shape[2] // 2
    own_half = pl.ds(pl.multiple_of(c * part_rows, part_rows), part_rows)
    other_half = pl.ds(pl.multiple_of((1 - c) * part_rows, part_rows), part_rows)

    def out_grad(r):
        if r == 4:
            return pltpu.make_async_remote_copy(
                gout.at[:, :, other_half], ogot, osend.at[3], orecv.at[3], device_id={"context": 1 - c}
            )
        src, dst = ogot.at[t ^ r], obuf.at[r]
        if r == 0:
            return pltpu.make_async_copy(src, dst, olocal)
        return pltpu.make_async_remote_copy(
            src, dst, osend.at[r - 1], orecv.at[r - 1], device_id={"tensor": t ^ r}
        )

    def other_core():
        return pltpu.make_async_remote_copy(
            gwx.at[1 - c], gwr, xsend, xrecv, device_id={"context": 1 - c}
        )

    def load(i):
        if i == 2:
            return pltpu.make_async_copy(gud, gud_v, vlocal.at[2])
        return pltpu.make_async_copy(part_sum.at[i], zr.at[0, i, 0], vlocal.at[i])

    @pl.when(u == 0)
    def _():
        greet(peers)
        for i in range(3):
            load(i).start()
        gw[...] = jnp.zeros_like(gw)
        greeted(peers)
        out_grad(4).start()
        for r in range(1, 4):
            side_tensor(r).start()
        side_tensor(0).start()
        for i in range(3):
            load(i).wait()
        step_of(0, 2, False)
        step_of(1, 1)

    @pl.when(u == 1)
    def _():
        step_of(0, 3)
        out_grad(4).wait()
        for p in range(4):
            ogot[p] = (ogot[p].astype(full) + gout[p, :, own_half].astype(full)).astype(low)
        for r in range(1, 4):
            out_grad(r).start()
        out_grad(0).start()

    @pl.when(u == 2)
    def _():
        step_of(1, 2)

    @pl.when(u == 3)
    def _():
        side_tensor(0).wait()
        for r in range(1, 4):
            side_tensor(r).wait_recv()
        stot[...] = sum(sgot[r].astype(full) for r in range(4)).astype(low)
        for r in range(1, n):
            side_dp(r).start()

    @pl.when(u == 4)
    def _():
        step_of(1, 3)

    qs[...] = q_ref[0] * low(0.125)
    ks[...] = k_ref[0].T
    vs[...] = v_ref[0].T
    grow[...] = g_ref[0].T
    qrow[...] = qs[...].T
    delta[...] = jnp.sum(g_ref[0].astype(full) * of_ref[0], axis=0, keepdims=True)
    dqs[...] = jnp.zeros_like(dqs)
    for key_start in range(0, length, QB):
        rows = slice(key_start, key_start + QB)
        k, v, key_t = ks[rows, :], vs[rows, :], k_ref[0, :, rows]
        stop = min(key_start + WIN + QB, length)
        key_pos = key_start + lax.broadcasted_iota(jnp.int32, (QB, QB), 0)
        for start in range(key_start, stop, QB):
            cols = slice(start, start + QB)
            held = slice(start - key_start, start - key_start + QB)
            s = nn(k, qs[:, cols]) - lse_ref[0, :, cols]
            allowed = key_pos >= lo_ref[0, :, cols]
            if start == key_start:
                allowed &= key_pos <= start + lax.broadcasted_iota(jnp.int32, (QB, QB), 1)
            p = jnp.exp(jnp.where(allowed, s, NEG))
            dp = nn(v, g_ref[0, :, cols])
            soft[:, held] = p.astype(low)
            dscore[:, held] = (p * (dp - delta[:, cols])).astype(low)
        cols, held = slice(key_start, stop), slice(0, stop - key_start)
        dv = nn(soft[:, held], grow[cols, :])
        dk = nn(dscore[:, held], qrow[cols, :])
        dqs[:, cols] += nn(key_t, dscore[:, held])
        dbuf[u, 1, :, rows] = dk.T.astype(low)
        dbuf[u, 2, :, rows] = dv.T.astype(low)
    dbuf[u, 0] = (dqs[...] * 0.125).astype(low)

    def move(unit, i, source_core):
        dc, r = PEERS[i]
        h, seq = unit_place(unit, source_core)
        dest = pl.multiple_of(((c ^ dc) * 4 + (t ^ r)) * own, own)
        src = dbuf.at[unit, :, :, pl.ds(dest, own)]
        dst = dall.at[t, :, h, :, pl.ds(pl.multiple_of(seq * own, own), own)]
        if i == 0:
            return pltpu.make_async_copy(src, dst, lsem.at[unit])
        return pltpu.make_async_remote_copy(
            src, dst, ssem.at[i - 1, unit], rsem.at[i - 1, unit], device_id=at_peer(c, t, dc, r)
        )

    @pl.when(sends(u, c))
    def _():
        for i in range(1, len(PEERS)):
            move(u, i, c).start()
        move(u, 0, c).start()
        h, _ = unit_place(u, c)
        gw[h] += nn(dbuf[u].reshape(3 * HD, length), norm_ref[0])

    @pl.when(u == pl.num_programs(0) - 1)
    def _():
        wide_rows = [gw[h, p * HD : (p + 1) * HD, :] for p in range(3) for h in range(3)]
        gwx[0] = jnp.concatenate(wide_rows[:6], axis=0).T.astype(low)
        empty = jnp.zeros((3 * HD, gw.shape[2]), full)
        gwx[1] = jnp.concatenate(wide_rows[6:] + [empty], axis=0).T.astype(low)
        other_core().start()
        out_grad(0).wait()
        for r in range(1, 4):
            out_grad(r).wait()
        osum[...] = sum(obuf[r].astype(full) for r in range(4)).T.astype(low)
        other_core().wait()
        gw_sum[...] = (gwx[c].astype(full) + gwr[...].astype(full)).astype(low)
        for step in range(4, n):
            step_of(0, step)
            step_of(1, step)
        finish(0)
        finish(1)
        total = stot[rows_of(d)].astype(full)
        for r in range(1, n):
            side_tensor(r).wait_send() if r < 4 else None
            side_dp(r).wait()
            total += sdp[r - 1].astype(full)
        ssum[...] = total
        for unit in range(UNITS):
            for i, (dc, r) in enumerate(PEERS):

                @pl.when(sends(unit, c))
                def _():
                    if i:
                        move(unit, i, c).wait_send()
                    else:
                        move(unit, i, c).wait()

                if i:

                    @pl.when(sends(unit, c ^ dc))
                    def _():
                        move(unit, i, c ^ dc).wait_recv()


def attend_back(n, qkv, grad_units, lo, lse, attended, normed, grad_out, grad_up_down, side, part_sum):
    length = lo.shape[2]
    own = length // 8
    width = normed.shape[2]
    shard, columns = grad_up_down.shape[1] // n, grad_up_down.shape[2]
    out_rows, local = grad_out.shape[2] // 2, grad_out.shape[1]
    part = lambda p: pl.BlockSpec((1, HD, length), unit_block(p))
    unit = lambda rows, m: pl.BlockSpec((1, rows, m), lambda u: (u, 0, 0))
    once = lambda dims: pl.BlockSpec(dims, lambda u: (0,) * len(dims), pipeline_mode=pl.Buffered(1))
    wide, tall = pltpu.VMEM((HD, length), low), pltpu.VMEM((length, HD), low)
    results = [(width, 2 * 3 * HD), (4, shard, columns), (out_rows, local)]
    return pl.pallas_call(
        functools.partial(attend_back_kernel, n),
        grid=(UNITS,),
        in_specs=[part(0), part(1), part(2)]
        + [
            pl.BlockSpec((1, 1, length), lambda u: (u // 3, 0, 0)),
            unit(1, length),
            unit(HD, length),
            pl.BlockSpec((1, length, width), lambda u: (u // 3, 0, 0)),
            unit(HD, length),
            once(grad_out.shape),
        ]
        + [HBM] * 3,
        out_specs=[HBM] + [once(r) for r in results] + [once((shard, SIDE))],
        scratch_shapes=[
            wide, tall, tall, tall, tall,
            pltpu.VMEM((1, length), full), pltpu.VMEM((HD, length), full),
            pltpu.VMEM((QB, WIN + QB), low), pltpu.VMEM((QB, WIN + QB), low),
            pltpu.VMEM((UNITS, 3, HD, length), low), pltpu.VMEM((3, 3 * HD, width), full),
            pltpu.VMEM((2, width, 6 * HD), low), pltpu.VMEM((width, 6 * HD), low),
            pltpu.VMEM((2, 2, n - 1, 2, shard, columns), low), pltpu.VMEM(grad_up_down.shape, low),
            pltpu.VMEM((4, local, out_rows), low), pltpu.VMEM((4, local, out_rows), low),
            pltpu.VMEM((4, width, SIDE), low), pltpu.VMEM((width, SIDE), low), pltpu.VMEM((n - 1, shard, SIDE), low),
            dma((7, UNITS)), dma((7, UNITS)), dma((UNITS,)),
            dma((2, 2, n - 1)), dma((2, 2, n - 1)), dma, dma, dma((4,)), dma((4,)), dma, dma((3,)),
            dma((3,)), dma((3,)), dma, dma((n - 1,)), dma((n - 1,)),
        ],
        out_shape=[shape((4, 3, 3, HD, 3 * own), low)]
        + [shape(r, low) for r in results]
        + [shape((shard, SIDE), full)],
        compiler_params=pltpu.CompilerParams(
            vmem_limit_bytes=63 << 20, collective_id=2, has_side_effects=True
        ),
        name="attend_back",
    )(qkv, qkv, qkv, lo, lse, attended, normed, grad_units, grad_out, grad_up_down, side, part_sum)


def last_kernel(
    n, dqkv_ref, w_ref, tokens_ref, middle_ref, gains, w_own, up_own, gain_one, gain_two, ssum, gw_sum, zsum, osum,
    grad_in, g_qkv, g_up, g_down, g_out, g_one, g_two,
    rg, rw, ro, down_n, out_t, mine, sums, dqkv, w_all, tokens, middle,
    gsend, grecv, wsend, wrecv, osend, orecv, lsem, csend, crecv, ssend, srecv, clocal, fetch,
):
    c, t = place()
    d = lax.axis_index("dp")
    shard, hidden = rg.shape[1], rg.shape[2]
    cut = n // 2
    group = [at_peer(c, t, dc, r) for dc, r in PEERS[1:]]
    others = [lax.rem(d + r, n) for r in range(1, n)]
    peers = group + [{"dp": o} for o in others]
    greet(peers)
    loads = [
        pltpu.make_async_copy(src, dst, fetch.at[i])
        for i, (src, dst) in enumerate(
            ((tokens_ref, tokens), (w_ref, w_all), (dqkv_ref, dqkv), (middle_ref, middle))
        )
    ]
    for copy in loads:
        copy.start()

    def rows_of(j):
        return pl.ds(pl.multiple_of(j * shard, shard), shard)

    narrow = slice(0, 256)

    def qkv_piece(r, core):
        src, dst = gw_sum.at[rows_of(d if r == 0 else others[r - 1])], rg.at[r]
        if core:
            src, dst = src.at[:, narrow], dst.at[:, narrow]
        if r == 0:
            return pltpu.make_async_copy(src, dst, lsem.at[0])
        return pltpu.make_async_remote_copy(
            src, dst, gsend.at[r - 1], grecv.at[r - 1], device_id={"dp": others[r - 1]}
        )

    def each_core(what):
        for core in range(2):

            @pl.when(c == core)
            def _():
                what(core)

    def up_piece(r):
        src, dst = zsum.at[t ^ r], rw.at[r]
        if r == 0:
            return pltpu.make_async_copy(src, dst, lsem.at[1])
        return pltpu.make_async_remote_copy(
            src, dst, wsend.at[r - 1], wrecv.at[r - 1], device_id={"tensor": t ^ r}
        )

    mine_out = d // cut == c

    def out_piece(r):
        to = d if r == 0 else others[r - 1]
        src, dst = osum.at[rows_of(lax.rem(to, cut))], ro.at[r]
        if r == 0:
            return pltpu.make_async_copy(src, dst, lsem.at[2])
        return pltpu.make_async_remote_copy(
            src, dst, osend.at[r - 1], orecv.at[r - 1], device_id={"dp": to}
        )

    def start_all(core):
        for r in range(1, n):
            qkv_piece(r, core).start()
        qkv_piece(0, core).start()

    greeted(peers)
    each_core(start_all)
    for r in range(1, 4):
        up_piece(r).start()
    up_piece(0).start()
    for r in range(1, n):

        @pl.when(others[r - 1] // cut == c)
        def _():
            out_piece(r).start()

    @pl.when(mine_out)
    def _():
        out_piece(0).start()

    for copy in loads:
        copy.wait()
    @pl.loop(0, tokens.shape[0] // QB)
    def _(m):
        rows = pl.ds(pl.multiple_of(m * QB, QB), QB)
        r = tn(dqkv[:, rows], w_all[...])
        v = tokens[rows, :].astype(full)
        inv = lax.rsqrt(jnp.mean(v * v, axis=-1, keepdims=True) + epsilon)
        rg_ = r * gains[0:1, :]
        grad = inv * (rg_ - v * (inv * inv * jnp.mean(rg_ * v, axis=-1, keepdims=True)))
        grad_in[rows, :] = (middle[rows, :] + grad).astype(low)

    def halves(j):
        half = pl.ds(pl.multiple_of(c * hidden, hidden), hidden)
        src, dst = (
            (mine.at[0], g_qkv.at[:, half]),
            (mine.at[1], g_up.at[:, half]),
            (down_n, g_down.at[:, half]),
            (out_t, g_out),
        )[j]
        return (
            pltpu.make_async_copy(src, dst, clocal.at[j]),
            pltpu.make_async_remote_copy(
                src, dst, csend.at[j], crecv.at[j], device_id={"context": 1 - c}
            ),
        )

    def deliver(j):
        for copy in halves(j):
            copy.start()

    up_piece(0).wait()
    for r in range(1, 4):
        up_piece(r).wait_recv()
    main = hidden - SIDE
    mine[1, :, :main] = sum(rw[r, :, :main].astype(full) for r in range(4))
    mine[1, :, main:] = ssum[...]
    down_n[...] = sum(rw[r, :, main:].astype(full) for r in range(4))
    deliver(1)
    deliver(2)

    @pl.when(mine_out)
    def _():
        out_piece(0).wait()
        for r in range(1, n):
            out_piece(r).wait_recv()
        out_t[...] = sum(ro[r].astype(full) for r in range(n)).T
        deliver(3)

    def take(core):
        qkv_piece(0, core).wait()
        for r in range(1, n):
            qkv_piece(r, core).wait_recv()
        if core:
            mine[0, :, narrow] = sum(rg[r, :, narrow].astype(full) for r in range(n))
            mine[0, :, 256:] = jnp.zeros((shard, hidden - 256), full)
        else:
            mine[0] = sum(rg[r].astype(full) for r in range(n))

    each_core(take)
    deliver(0)
    lane = lax.broadcasted_iota(jnp.int32, (shard, 128), 1)
    halves_of = [jnp.concatenate([w_own[0], w_own[1]], axis=1), jnp.pad(w_own[2], ((0, 0), (0, osum.shape[1])))]
    w_mine = jnp.where(c == 0, halves_of[0].astype(full), halves_of[1].astype(full))
    up_mine = up_own[:, pl.ds(pl.multiple_of(c * hidden, hidden), hidden)].astype(full)
    first = jnp.sum(w_mine * mine[0], axis=1, keepdims=True)
    second = jnp.sum(up_mine * mine[1], axis=1, keepdims=True)
    sums[0] = jnp.where(lane == 0, first, jnp.where(lane == 1, second, 0.0)).T[:8]

    def gain_piece(i):
        dc, r = PEERS[i]
        return pltpu.make_async_remote_copy(
            sums.at[0], sums.at[i], ssend.at[i - 1], srecv.at[i - 1], device_id=at_peer(c, t, dc, r)
        )

    for i in range(1, len(PEERS)):
        gain_piece(i).start()
    for i in range(1, len(PEERS)):
        gain_piece(i).wait()
    total = sum(sums[i] for i in range(len(PEERS)))
    g_one[...] = total[0:1, :] / gain_one[...].astype(full)
    g_two[...] = total[1:2, :] / gain_two[...].astype(full)

    for j in range(3):
        for copy in halves(j):
            copy.wait()

    @pl.when(mine_out)
    def _():
        local, away = halves(3)
        local.wait()
        away.wait_send()

    @pl.when(jnp.logical_not(mine_out))
    def _():
        halves(3)[1].wait_recv()

    for r in range(1, 4):
        up_piece(r).wait_send()

    def sent(core):
        for r in range(1, n):
            qkv_piece(r, core).wait_send()

    each_core(sent)
    for r in range(1, n):

        @pl.when(others[r - 1] // cut == c)
        def _():
            out_piece(r).wait_send()


def last(n, dqkv, w_all, tokens, middle, gains, w_own, up_own, gain_one, gain_two, ssum, gw_sum, zsum, osum):
    rows, width = tokens.shape
    shard, hidden = zsum.shape[1], gw_sum.shape[1]
    local = osum.shape[1]
    return pl.pallas_call(
        functools.partial(last_kernel, n),
        in_specs=[HBM] * 4 + [VMEM] * 6 + [ANY] * 3,
        out_specs=[VMEM] + [ANY] * 4 + [VMEM] * 2,
        out_shape=[
            shape((rows, width), low),
            shape((shard, 2 * hidden), full),
            shape((shard, 2 * hidden), full),
            shape((shard, 2 * hidden), full),
            shape((local, shard), full),
            shape((1, shard), full),
            shape((1, shard), full),
        ],
        scratch_shapes=[
            pltpu.VMEM((n, shard, hidden), low),
            pltpu.VMEM((4, shard, 2 * hidden - SIDE), low),
            pltpu.VMEM((n, shard, local), low),
            pltpu.VMEM((shard, hidden), full),
            pltpu.VMEM((local, shard), full),
            pltpu.VMEM((2, shard, hidden), full),
            pltpu.VMEM((8, 8, shard), full),
            pltpu.VMEM(dqkv.shape, low), pltpu.VMEM(w_all.shape, low),
            pltpu.VMEM((rows, width), low), pltpu.VMEM((rows, width), full),
            dma((n - 1,)), dma((n - 1,)), dma((3,)), dma((3,)), dma((n - 1,)), dma((n - 1,)), dma((3,)),
            dma((4,)), dma((4,)), dma((7,)), dma((7,)), dma((4,)), dma((4,)),
        ],
        compiler_params=pltpu.CompilerParams(
            vmem_limit_bytes=63 << 20, collective_id=4, has_side_effects=True
        ),
        name="last",
    )(dqkv, w_all, tokens, middle, gains, w_own, up_own, gain_one, gain_two, ssum, gw_sum, zsum, osum)


def close_kernel(*refs):
    count = len(refs) // 2
    for i, (src, dst) in enumerate(zip(refs[:count], refs[count:])):
        if i == 2:
            local = dst.shape[2]
            for p in range(3):
                dst[p] = src[:, p * local : (p + 1) * local]
        else:
            dst[...] = src[...]


def close(result, grad_input, own_attn, *others):
    arrays = (result, grad_input, own_attn, *others)
    rows = lambda a: pl.BlockSpec((a.shape[0] // 2, a.shape[1]), lambda i: (i, 0))
    shard, local = own_attn.shape[0], others[0].shape[0]
    parts = pl.BlockSpec((3, shard // 2, local), lambda i: (0, i, 0))
    outs = [shape(a.shape, a.dtype) for a in arrays]
    outs[2] = shape((3, shard, local), full)
    return pl.pallas_call(
        close_kernel,
        grid=(2,),
        in_specs=[rows(a) for a in arrays],
        out_specs=[parts if i == 2 else rows(a) for i, a in enumerate(arrays)],
        out_shape=outs,
        compiler_params=pltpu.CompilerParams(vmem_limit_bytes=63 << 20),
        name="close",
    )(*arrays)


def gelu_and_slope(v):
    k0 = math.sqrt(2.0 / math.pi)
    square = v * v
    th = jnp.tanh(v * (k0 + (k0 * 0.044715) * square))
    half = 0.5 + 0.5 * th
    slope = half + (v * half) * ((1.0 - th) * (k0 + (3.0 * 0.044715 * k0) * square))
    return v * half, slope


def feed_kernel(
    dp, att, proj, tokens, cot, gains, w_t, up_ref, down_ref,
    result, middle, gout, gud, side, part_sum, units, w_all,
    x, g, x_t, g_t, up, down, act, gh, out, back, proj_w, sent, got, gbuf, sbuf, gatt,
    xsend, xrecv, wsend, wrecv, wlocal, zsend, zrecv, glocal, usend, urecv, ulocal, load,
):
    c, t = place()
    d = lax.axis_index("dp")
    rows, width = tokens.shape
    own = rows // 3
    shard = width // dp
    n = up_ref.shape[2]
    local = proj.shape[2]
    other = {"context": 1 - c}
    peers = [at_peer(c, t, dc, r) for dc, r in PEERS[1:]]
    mine, theirs = slice(0, rows), slice(rows, 2 * rows)
    block = rows // 3

    def cross(k):
        src, dst = (
            (cot, g.at[theirs]),
            (x.at[mine], x.at[theirs]),
            (sent.at[0], got.at[0]),
            (sent.at[1], got.at[1]),
        )[k]
        return pltpu.make_async_remote_copy(src, dst, xsend.at[k], xrecv.at[k], device_id=other)

    half = pl.ds(pl.multiple_of(c * (w_t.shape[0] // 2), 8), w_t.shape[0] // 2)

    def over_tensor(r):
        if r == 4:
            ref = w_all.at[:, half]
            return pltpu.make_async_remote_copy(ref, ref, wsend.at[3], wrecv.at[3], device_id=other)
        src, dst = w_t.at[half], w_all.at[t, half]
        if r == 0:
            return pltpu.make_async_copy(src, dst, wlocal)
        return pltpu.make_async_remote_copy(
            src, dst, wsend.at[r - 1], wrecv.at[r - 1], device_id={"tensor": t ^ r}
        )

    def rows_of(i):
        return pl.ds(pl.multiple_of(i * shard, shard), shard)

    line = Line(
        dp,
        lambda i: gbuf.at[0, :, rows_of(i)],
        lambda k, step: part_sum.at[k],
        zsend,
        zrecv,
    )

    def keep(j):
        if j == 2:
            return pltpu.make_async_copy(sbuf, side, glocal.at[2])
        return pltpu.make_async_copy(gbuf.at[j], gud.at[pl.ds(2 * j, 2)], glocal.at[j])

    def leave(whole, i):
        dc, r = PEERS[i]
        to_c, to_t = c ^ dc, t ^ r
        head = to_t * 3 + (0 if whole else to_c)
        count, first = (3, 0) if whole else (2, 3)
        seq = 2 * to_c if whole else 1
        src = gatt.at[pl.ds(head, count), :, pl.ds(pl.multiple_of(seq * own, own), own)]
        dst = units.at[pl.ds(first, count), :, pl.ds(pl.multiple_of((c * 4 + t) * own, own), own)]
        k = 0 if whole else 1
        if i == 0:
            return pltpu.make_async_copy(src, dst, ulocal.at[k])
        return pltpu.make_async_remote_copy(
            src, dst, usend.at[k, i - 1], urecv.at[k, i - 1], device_id=at_peer(c, t, dc, r)
        )

    loads = [
        pltpu.make_async_copy(ref.at[p], dst.at[p // 2, :, pl.ds((p % 2) * n, n)], load.at[i, p])
        for i, (ref, dst) in enumerate(((up_ref, up), (down_ref, down)))
        for p in range(4)
    ]
    greet(peers)
    greet_line(dp, d)
    for copy in loads:
        copy.start()
    for p in range(4):
        proj_w[:, p * local : (p + 1) * local] = proj[p]
    greeted_line(dp, d, peers)
    cross(0).start()
    for r in range(1, 4):
        over_tensor(r).start()
    over_tensor(0).start()
    for m in range(0, rows, block):
        part = slice(m, m + block)
        v = tokens[part, :].astype(full) + nn(proj_w[...], att[:, part]).T
        middle[part, :] = v
        inv = lax.rsqrt(jnp.mean(v * v, axis=-1, keepdims=True) + epsilon)
        x[part, :] = (v * inv * gains[1:2, :]).astype(low)
    cross(1).start()
    g[mine, :] = cot[...]
    g_t[:, mine] = cot[...].T
    x_t[:, mine] = x[mine, :].T
    for copy in loads:
        copy.wait()

    def hidden(side):
        @pl.loop(0, 6)
        def _(i):
            j = i // 3
            part = pl.ds(pl.multiple_of((side * 3 + i % 3) * block, block), block)
            pre = nn(x[part, :], up[j])
            ga = nn(g[part, :], down[j])
            a, slope = gelu_and_slope(pre)
            act[j, part, :] = a.astype(low)
            gh[j, part, :] = (ga * slope).astype(low)

    def branch(left, right, part):
        return nt(left[0, part, :], right[0]) + nt(left[1, part, :], right[1])

    hidden(0)
    cross(0).wait_recv()
    cross(1).wait_recv()
    hidden(1)

    def cut(side, left, right, put):
        @pl.loop(0, 3)
        def _(i):
            here = pl.ds(pl.multiple_of(i * block, block), block)
            part = pl.ds(pl.multiple_of(side * rows + i * block, block), block)
            put(here, branch(left, right, part))

    def put_sent(k):
        def put(here, value):
            sent[k, here, :] = value.astype(low)

        return put

    def put_own(ref):
        def put(here, value):
            ref[here, :] = value

        return put

    cut(1, gh, up, put_sent(0))
    cross(2).start()
    cut(0, gh, up, put_own(back))
    over_tensor(0).wait()
    for r in range(1, 4):
        over_tensor(r).wait_recv()
    over_tensor(4).start()
    x_t[:, theirs] = x[theirs, :].T
    g_t[:, theirs] = g[theirs, :].T
    cross(1).wait_send()
    cross(2).wait_recv()
    gain = gains[1:2, :]
    low_t = x
    for m in range(0, rows, block):
        part = slice(m, m + block)
        r = (back[part, :] + got[0, part, :].astype(full)) * gain
        v = middle[part, :]
        inv = lax.rsqrt(jnp.mean(v * v, axis=-1, keepdims=True) + epsilon)
        grad = inv * (r - v * (inv * inv * jnp.mean(r * v, axis=-1, keepdims=True)))
        back[part, :] = cot[part, :].astype(full) + grad
        x[part, :] = back[part, :].astype(low)
        low_t[rows : rows + width, part] = x[part, :].T
        grad = tn(proj_w[...], low_t[rows : rows + width, part]).astype(low)
        gatt[:, :, part] = grad.reshape(gatt.shape[0], HD, block)
    for whole in (True, False):
        for i in range(1, len(PEERS)):
            leave(whole, i).start()
        leave(whole, 0).start()

    def weight_grad(j, a, left_t, right):
        @pl.loop(0, 3)
        def _(i):
            part = pl.ds(pl.multiple_of(i * (width // 3), width // 3), width // 3)
            grad = nn(left_t[part, :], right[j]).astype(low)
            main = n - SIDE
            for p in range(2):
                if a:
                    gbuf[j, p, part, main:] = grad[:, p * n : (p + 1) * n]
                else:
                    gbuf[j, p, part, :main] = grad[:, p * n : p * n + main]
                    sbuf[2 * j + p, part, :] = grad[:, p * n + main : (p + 1) * n]

    weight_grad(0, 0, x_t, gh)
    weight_grad(0, 1, g_t, act)
    line.start(1, None)
    keep(0).start()
    cut(1, act, down, put_sent(1))
    cross(3).start()
    weight_grad(1, 0, x_t, gh)
    weight_grad(1, 1, g_t, act)
    keep(1).start()
    keep(2).start()
    cut(0, act, down, put_own(out))
    for p in range(4):
        gout[p] = nn(att[p * local : (p + 1) * local, :], x[mine, :]).astype(low)
    cross(3).wait_recv()
    result[...] = (middle[...] + out[...] + got[1].astype(full)).astype(low)
    middle[...] = back[...]
    for k in (0, 2, 3):
        cross(k).wait_send()
    for r in range(1, 4):
        over_tensor(r).wait_send()
    over_tensor(4).wait()
    line.received(1)
    line.sent(1)
    for j in range(3):
        keep(j).wait()
    for whole in (True, False):
        for i in range(len(PEERS)):
            leave(whole, i).wait()


def feed(dp, att, proj, tokens, cot, gains, w_t, up, down):
    rows, width = tokens.shape
    pieces, _, n = up.shape
    own = rows // 3
    assert pieces == 4 and dp > 2 and rows == width
    return pl.pallas_call(
        functools.partial(feed_kernel, dp),
        in_specs=[VMEM] * 6 + [HBM] * 2,
        out_specs=[VMEM] * 3 + [HBM] * 5,
        out_shape=[
            shape((rows, width), low),
            shape((rows, width), full),
            shape((4, proj.shape[2], width), low),
            shape((4, width, 2 * n - SIDE), low),
            shape((4, width, SIDE), low),
            shape((2, 2, width // dp, 2 * n - SIDE), low),
            shape((UNITS, HD, 8 * own), low),
            shape((4,) + w_t.shape, low),
        ],
        scratch_shapes=[pltpu.VMEM((2 * rows, width), low)] * 2
        + [pltpu.VMEM((width, 2 * rows), low)] * 2
        + [pltpu.VMEM((2, width, 2 * n), low)] * 2
        + [pltpu.VMEM((2, 2 * rows, 2 * n), low)] * 2
        + [pltpu.VMEM((rows, width), full)] * 2
        + [pltpu.VMEM((width, width), low)]
        + [pltpu.VMEM((2, rows, width), low)] * 2
        + [pltpu.VMEM((2, 2, width, 2 * n - SIDE), low), pltpu.VMEM((4, width, SIDE), low)]
        + [pltpu.VMEM((12, HD, rows), low)]
        + [dma((4,)), dma((4,)), dma((4,)), dma((4,)), dma]
        + [dma((2, 1)), dma((2, 1)), dma((3,)), dma((2, 7)), dma((2, 7)), dma((2,)), dma((2, 4))],
        compiler_params=pltpu.CompilerParams(
            vmem_limit_bytes=63 << 20, collective_id=5, has_side_effects=True
        ),
        name="feed",
    )(att, proj, tokens, cot, gains, w_t, up, down)


def per_device(tokens, segments, w_qkv, w_out, w_in, w_back, gain_attn, gain_mlp, cotangent):
    sequences, own, width = tokens.shape
    assert lax.axis_size("tensor") == 4 and lax.axis_size("context") == 2 and sequences == 3
    n = lax.axis_size("dp")
    length = segments.shape[1]
    shard = w_qkv.shape[0]
    local = w_qkv.shape[2]
    rows = sequences * own
    parts = w_qkv.transpose(1, 0, 2)
    gain_one, gain_two = gain_attn.reshape(1, shard), gain_mlp.reshape(1, shard)
    qkv, normed_units, w_t, up_part, out_part, gains, lo = project(
        n, tokens, segments, parts, w_in, w_out, gain_one, gain_two
    )
    attended, log_totals, out_full, w_up, w_down, w_proj = attend(
        n, qkv, lo, out_part, up_part, w_back.T
    )
    flat = tokens.reshape(rows, width)
    result, grad_middle, grad_out, grad_up_down, side, part_sum, grad_units, w_all = feed(
        n, attended, w_proj, flat, cotangent.reshape(rows, width), gains, w_t, w_up, w_down
    )
    grad_projected, gw_sum, zsum, osum, ssum = attend_back(
        n, qkv, grad_units, lo, log_totals, out_full, normed_units, grad_out, grad_up_down, side, part_sum
    )
    grad_input, own_attn, own_up, own_down, own_proj, own_one, own_two = last(
        n,
        grad_projected.reshape(12 * local, rows),
        w_all.reshape(12 * local, width),
        flat,
        grad_middle,
        gains,
        parts,
        w_in,
        gain_one,
        gain_two,
        ssum,
        gw_sum,
        zsum,
        osum,
    )
    result, grad_input, own_attn, own_proj, own_up, own_down = close(
        result, grad_input, own_attn, own_proj, own_up, own_down
    )
    return (
        result.reshape(sequences, own, width),
        grad_input.reshape(sequences, own, width),
        own_attn.transpose(1, 0, 2),
        own_proj,
        own_up,
        own_down.T,
        own_one.reshape(shard),
        own_two.reshape(shard),
    )


def solution(mesh):
    return jax.shard_map(
        per_device,
        mesh=mesh,
        in_specs=(
            P("dp", ("context", "tensor"), None),
            P("dp", None),
            P("dp", None, "tensor"),
            P("tensor", "dp"),
            P("dp", "tensor"),
            P("tensor", "dp"),
            P("dp"),
            P("dp"),
            P("dp", ("context", "tensor"), None),
        ),
        out_specs=(
            P("dp", ("context", "tensor"), None),
            P("dp", ("context", "tensor"), None),
            P("dp", None, "tensor"),
            P("tensor", "dp"),
            P("dp", "tensor"),
            P("tensor", "dp"),
            P("dp"),
            P("dp"),
        ),
        check_vma=False,
    )
```

```python
import functools
import math

import jax
import jax.numpy as jnp
from jax import lax
from jax.experimental import pallas as pl
from jax.experimental.pallas import tpu as pltpu
from jax.sharding import PartitionSpec as P

HD = 64
WIN = 1536
QB = 256
CHUNK = 128
NEG = -1e30
epsilon = 1e-06
low = jnp.bfloat16
full = jnp.float32


def dot(left, right, dims):
    return lax.dot_general(left, right, (dims, ((), ())), preferred_element_type=full)


def nn(left, right):
    return dot(left, right, ((1,), (0,)))


def nt(left, right):
    return dot(left, right, ((1,), (1,)))


def tn(left, right):
    return dot(left, right, ((0,), (0,)))


PEERS = [(dc, r) for dc in range(2) for r in range(4)]


def place():
    return lax.axis_index("context"), lax.axis_index("tensor")


def at_peer(c, t, dc, r):
    return {"context": c ^ dc, "tensor": t ^ r}


def greet(peers):
    for peer in peers:
        pl.semaphore_signal(pltpu.get_barrier_semaphore(), inc=1, device_id=peer)


def greeted(peers):
    pl.semaphore_wait(pltpu.get_barrier_semaphore(), len(peers))


def unit_place(u, c):
    return jnp.where(u < 3, u, c + u - 3), jnp.where(u < 3, 2 * c, 1)


def sends(u, c):
    return (u != 3) | (c == 0)


dma = pltpu.SemaphoreType.DMA
ANY = pl.BlockSpec(memory_space=pl.ANY)
VMEM = pl.BlockSpec(memory_space=pltpu.VMEM)
HBM = pl.BlockSpec(memory_space=pltpu.HBM)
shape = jax.ShapeDtypeStruct

SIDE = 128


class Line:
    def __init__(self, n, own, slot, send, recv):
        self.n, self.own, self.slot, self.sems = n, own, slot, (send, recv)
        self.d = lax.axis_index("dp")

    def along(self, k):
        m = self.d if k == 0 else self.n - 1 - self.d
        to = {"dp": jnp.clip(self.d + 1 if k == 0 else self.d - 1, 0, self.n - 1)}
        return m, to

    def target(self, k, step):
        m, _ = self.along(k)
        return jnp.clip(self.n - step + m if k == 0 else step - 1 - m, 0, self.n - 1)

    def copy(self, k, step, src):
        send, recv = self.sems
        _, to = self.along(k)
        return pltpu.make_async_remote_copy(
            src, self.slot(k, step), send.at[k, step - 1], recv.at[k, step - 1], device_id=to
        )

    def arrive(self, k, step):
        self.copy(k, step, self.slot(k, step)).wait_recv()

    def start(self, step, add):
        for k in range(2):
            m, _ = self.along(k)
            if step > 1:

                @pl.when((m >= 1) & (m < self.n - 1) & (step >= m + 1))
                def _():
                    add(k, self.target(k, step))
                    self.copy(k, step, self.slot(k, step - 1)).start()

            @pl.when(m == 0)
            def _():
                self.copy(k, step, self.own(self.target(k, step))).start()

    def received(self, step):
        for k in range(2):
            m, _ = self.along(k)

            @pl.when((m >= 1) & (step >= m))
            def _():
                self.arrive(k, step)

    def sent(self, step):
        for k in range(2):
            m, _ = self.along(k)

            @pl.when((m < self.n - 1) & (step >= m + 1))
            def _():
                self.copy(k, step, self.slot(k, step)).wait_send()


def greet_line(n, d):
    barrier = pltpu.get_barrier_semaphore()

    @pl.when(d > 0)
    def _():
        pl.semaphore_signal(barrier, inc=1, device_id={"dp": jnp.maximum(d - 1, 0)})

    @pl.when(d < n - 1)
    def _():
        pl.semaphore_signal(barrier, inc=1, device_id={"dp": jnp.minimum(d + 1, n - 1)})


def greeted_line(n, d, peers):
    ends = jnp.where(d > 0, 1, 0) + jnp.where(d < n - 1, 1, 0)
    pl.semaphore_wait(pltpu.get_barrier_semaphore(), len(peers) + ends)


def project_kernel(
    n, tokens, segments, w_qkv, up, out_own, gain_one, gain_two, qkv, norm, w_t, up_all, out_all, gain_ref, lo_ref,
    tok, x, w, proj, out_w, gain, own_gain, tsend, trecv, tlocal, wsend, wrecv, wlocal, osend, orecv, olocal, xsend, xrecv,
):
    c, t = place()
    d = lax.axis_index("dp")
    own = tokens.shape[1]
    width = tokens.shape[2]
    span = 4 * own
    shard = up.shape[0]
    half = own // 2
    hidden = up_all.shape[1]
    cut = n // 2
    to_x, to_y, to_core = {"tensor": t ^ 1}, {"tensor": t ^ 2}, {"context": 1 - c}
    others = [{"dp": lax.rem(d + r, n)} for r in range(1, n)]
    peers = [to_x, to_y, to_core] + others
    greet(peers)

    def local(i, s):
        return pltpu.make_async_copy(tokens.at[s], tok.at[s, t], tlocal.at[i])

    def weights(j, r):
        rows = pl.ds(pl.multiple_of(d * shard, shard), shard)
        source, target = (
            (w_qkv, w.at[:, rows]),
            (out_w, out_all.at[rows]),
            (up.at[:, pl.ds(pl.multiple_of(c * hidden, hidden), hidden)], up_all.at[rows]),
            (own_gain, gain.at[d]),
        )[j]
        if r == 0:
            return pltpu.make_async_copy(source, target, wlocal.at[j])
        return pltpu.make_async_remote_copy(
            source, target, wsend.at[j, r - 1], wrecv.at[j, r - 1], device_id=others[r - 1]
        )

    def gives(j, r):
        return lax.rem(d + n - r, n) // cut == c if j < 2 else True

    def weights_do(j, r, what, source=False):
        @pl.when(gives(j, 0 if source else r))
        def _():
            getattr(weights(j, r), what)()

    def to_other(j):
        rows = pl.ds(pl.multiple_of(c * cut * shard, shard), cut * shard)
        ref = w.at[:, rows]
        return pltpu.make_async_remote_copy(ref, ref, xsend, xrecv, device_id=to_core)

    order = (2 * (1 - c), 1, 2 * c)
    for i, s in enumerate(order):
        local(i, s).start()
    out_w[...] = out_own[...].T
    own_gain[...] = jnp.zeros_like(own_gain)
    own_gain[0:1, :] = gain_one[...]
    own_gain[1:2, :] = gain_two[...]
    for j in range(4):
        weights_do(j, 0, "start")
    greeted(peers)
    for j in (0, 3, 1, 2):
        for r in range(1, n):
            weights_do(j, r, "start", True)

    def hop(k, i):
        s = order[i]
        origin, rows, peer = (
            (t, slice(0, half), to_x),
            (t, slice(half, own), to_y),
            (t, slice(0, half), to_y),
            (t, slice(half, own), to_x),
            (t ^ 1, slice(0, half), to_y),
            (t ^ 2, slice(half, own), to_x),
        )[k]
        there = tok.at[s, origin, rows]
        here = tokens.at[s, rows] if k < 4 else there
        return pltpu.make_async_remote_copy(
            here, there, tsend.at[k, i], trecv.at[k, i], device_id=peer
        )

    def straight(i):
        for k in range(4):
            hop(k, i).start()

    def forward(i):
        for k in range(2):
            hop(k, i).wait_recv()
            hop(k + 4, i).start()

    units = proj.shape[1]

    def leave(i):
        out = []
        lanes = pl.ds(pl.multiple_of(c * span, span), span)
        if i != 0:
            out.append((x.at[i], norm.at[2 - i, lanes], False))
        if i != 2:
            out.append((x.at[i], norm.at[i, lanes], True))
        if i == 0:
            out.append((proj.at[0], qkv.at[pl.ds(0, units), :, lanes], True))
        if i == 2:
            out.append((proj.at[2], qkv.at[pl.ds(0, units), :, lanes], False))
        if i == 1:
            for away in (True, False):
                core = 1 - c if away else c
                for p in range(3):
                    src = proj.at[1, pl.ds(p * 3 + core, 2)]
                    out.append((src, qkv.at[pl.ds(units + 2 * p, 2), :, lanes], away))
        copies = []
        for j, (src, dst, away) in enumerate(out):
            if away:
                copies.append(
                    (away, pltpu.make_async_remote_copy(src, dst, osend.at[i, j], orecv.at[i, j], device_id=to_core))
                )
            else:
                copies.append((away, pltpu.make_async_copy(src, dst, olocal.at[i, j])))
        return copies

    def work(i):
        s = order[i]
        local(i, s).wait()
        for k in range(2, 6):
            hop(k, i).wait_recv()

        @pl.loop(0, 4)
        def _(p):
            rows = pl.ds(pl.multiple_of(p * own, own), own)
            v = tok[s, p].astype(full)
            inv = lax.rsqrt(jnp.mean(v * v, axis=-1, keepdims=True) + epsilon)
            normed = (v * inv * gain_ref[0:1, :]).astype(low)
            x[i, rows, :] = normed
            proj[i, :, :, rows] = nt(w_t[...], normed).astype(low).reshape(units, HD, own)

        for _, copy in leave(i):
            copy.start()

    straight(0)
    straight(1)
    forward(0)
    straight(2)
    seg = segments[...]
    first = jnp.zeros(seg.shape, jnp.int32)
    for value in range(8):
        before = jnp.sum((seg < value).astype(jnp.int32), axis=1, keepdims=True)
        first = jnp.where(seg == value, before, first)
    first = jnp.maximum(first, lax.broadcasted_iota(jnp.int32, seg.shape, 1) - (WIN - 1))
    lo_ref[0] = jnp.where(c == 0, first[0:1], first[2:3])
    lo_ref[1] = first[1:2]
    weights_do(0, 0, "wait")
    for r in range(1, n):
        weights_do(0, r, "wait_recv")
    to_other(0).start()
    weights(3, 0).wait()
    for r in range(1, n):
        weights(3, r).wait_recv()
    gain_ref[...] = jnp.concatenate([gain[i].astype(full) for i in range(n)], axis=1)[:8]
    to_other(0).wait_recv()
    for p in range(3):
        w_t[p * 3 * HD : (p + 1) * 3 * HD, :] = w[p].T
    forward(1)
    work(0)
    forward(2)
    work(1)
    work(2)
    to_other(0).wait_send()
    for j in range(4):
        if j in (1, 2):
            weights_do(j, 0, "wait")
        for r in range(1, n):
            weights_do(j, r, "wait_send", True)
            if j in (1, 2):
                weights_do(j, r, "wait_recv")
    for i in range(3):
        for k in range(6):
            hop(k, i).wait_send()
        for away, copy in leave(i):
            copy.wait()


def project(n, tokens, segments, w_qkv, up, out_own, gain_one, gain_two):
    sequences, own, width = tokens.shape
    shard, hidden = up.shape[0], up.shape[1] // 2
    local = out_own.shape[0]
    span = 4 * own
    return pl.pallas_call(
        functools.partial(project_kernel, n),
        in_specs=[HBM, VMEM, HBM, HBM, VMEM, VMEM, VMEM],
        out_specs=[HBM] * 2 + [VMEM] + [HBM] * 2 + [VMEM] * 2,
        out_shape=[
            shape((15, HD, 2 * span), low),
            shape((2, 2 * span, width), low),
            shape((9 * HD, n * shard), low),
            shape((n * shard, hidden), low),
            shape((n * shard, local), low),
            shape((8, n * shard), full),
            shape((2, 1, segments.shape[1]), jnp.int32),
        ],
        scratch_shapes=[
            pltpu.VMEM((sequences, 4, own, width), low),
            pltpu.VMEM((sequences, span, width), low),
            pltpu.VMEM((3, n * shard, local), low),
            pltpu.VMEM((sequences, 9, HD, span), low),
            pltpu.VMEM((shard, local), low),
            pltpu.VMEM((n, 16, shard), low),
            pltpu.VMEM((16, shard), low),
            dma((6, 3)), dma((6, 3)), dma((3,)),
            dma((4, n - 1)), dma((4, n - 1)), dma((4,)),
            dma((3, 8)), dma((3, 8)), dma((3, 8)), dma, dma,
        ],
        compiler_params=pltpu.CompilerParams(
            vmem_limit_bytes=63 << 20, collective_id=3, has_side_effects=True
        ),
        name="project",
    )(tokens, segments, w_qkv, up, out_own, gain_one, gain_two)


UNITS = 5
def unit_block(part):
    return lambda u: (jnp.where(u < 3, part * 3 + u, 9 + part * 2 + (u - 3)), 0, 0)


def attend_kernel(
    n, q_ref, k_ref, v_ref, lo_ref, out_part, up_part, down_own, att, lse_ref, of_ref, up, down, out_w,
    qs, ks, ss, obuf, ssem, rsem, lsem, wsend, wrecv, wlocal, zsend, zrecv, fsend, frecv,
):
    u = pl.program_id(0)
    c, t = place()
    d = lax.axis_index("dp")
    shard = down_own.shape[0]
    hidden = down.shape[2]
    peers = [at_peer(c, t, dc, r) for dc, r in PEERS[1:]]

    part = out_part.shape[0] // 2
    mine = pl.ds(pl.multiple_of(c * part, part), part)

    def weight(j, r):
        rows = pl.ds(pl.multiple_of(d * shard, shard), shard)
        src, dst = (
            (down_own.at[:, pl.ds(pl.multiple_of(c * hidden, hidden), hidden)], down.at[t, rows]),
            (up_part, up.at[t]),
            (out_part.at[mine], out_w.at[t, mine]),
        )[j]
        if r == 0:
            return pltpu.make_async_copy(src, dst, wlocal.at[j])
        return pltpu.make_async_remote_copy(
            src, dst, wsend.at[j, r - 1], wrecv.at[j, r - 1], device_id={"tensor": t ^ r}
        )

    def onward(k):
        if k == 2:
            ref, peer = out_w.at[:, mine], {"context": 1 - c}
        else:
            rows = pl.ds(k * part, part)
            ref, peer = up.at[t ^ (1 + k), rows], {"tensor": t ^ (2 - k)}
        return pltpu.make_async_remote_copy(
            ref, ref, fsend.at[k], frecv.at[k], device_id=peer
        )

    def shards(step, up_line):
        src = d - step if up_line else d + step
        rows = pl.ds(pl.multiple_of(jnp.clip(src, 0, n - 1) * shard, shard), shard)
        to = jnp.clip(d + 1 if up_line else d - 1, 0, n - 1)
        k = 0 if up_line else 1
        return pltpu.make_async_remote_copy(
            down.at[:, rows], down.at[:, rows], zsend.at[k, step], zrecv.at[k, step], device_id={"dp": to}
        )

    def line(step, what):
        for up_line in (True, False):
            inside = (d < n - 1) if up_line else (d > 0)
            has = (d >= step) if up_line else (d <= n - 1 - step)
            comes = (d >= step + 1) if up_line else (d <= n - 2 - step)
            if what == "recv":

                @pl.when(comes)
                def _():
                    shards(step, up_line).wait_recv()
            else:

                @pl.when(inside & has)
                def _():
                    if what == "start":
                        shards(step, up_line).start()
                    else:
                        shards(step, up_line).wait_send()
    length = lo_ref.shape[2]
    half = length // 2
    own = half // 4

    @pl.when(u == 0)
    def _():
        greet(peers)
        greet_line(n, d)
        for j in range(3):
            weight(j, 0).start()
        greeted_line(n, d, peers)
        for r in range(1, 4):
            weight(0, r).start()
        for r in range(1, 3):
            weight(1, r).start()

    qs[...] = q_ref[0] * low(0.125)
    ks[...] = k_ref[0].T
    for start in range(0, length, QB):
        stop = start + QB
        q = qs[:, start:stop]
        lo = lo_ref[0, :, start:stop]
        first = max(0, start - WIN)
        most = jnp.full((8, QB), NEG, full)
        for at in range(first, stop, CHUNK):
            s = nn(ks[at : at + CHUNK, :], q)
            key_pos = at + lax.broadcasted_iota(jnp.int32, (CHUNK, QB), 0)
            allowed = key_pos >= lo
            if at + CHUNK - 1 > start:
                allowed &= key_pos <= start + lax.broadcasted_iota(jnp.int32, (CHUNK, QB), 1)
            s = jnp.where(allowed, s, NEG)
            ss[at - first : at - first + CHUNK, :] = s
            most = jnp.maximum(most, jnp.max(s.reshape(CHUNK // 8, 8, QB), axis=0))
        most = jnp.max(most, axis=0, keepdims=True)
        total = jnp.zeros((8, QB), full)
        acc = jnp.zeros((HD, QB), full)
        for at in range(first, stop, CHUNK):
            p = jnp.exp(ss[at - first : at - first + CHUNK, :] - most)
            total += jnp.sum(p.reshape(CHUNK // 8, 8, QB), axis=0)
            acc += nn(v_ref[0, :, at : at + CHUNK], p.astype(low))
        total = jnp.sum(total, axis=0, keepdims=True)
        lse_ref[0, :, start:stop] = most + jnp.log(total)
        o = acc * (1.0 / total)
        of_ref[0, :, start:stop] = o
        obuf[u, :, start:stop] = o.astype(low)

    @pl.when(u == 0)
    def _():
        weight(0, 0).wait()
        for r in range(1, 4):
            weight(0, r).wait_recv()
        line(0, "start")
        for r in range(1, 4):
            weight(2, r).start()

    @pl.when(u == 3)
    def _():
        if n > 2:
            line(0, "recv")
            line(1, "start")
        for k in range(2):
            weight(1, 1 + k).wait_recv()
            onward(k).start()
        weight(2, 0).wait()
        for r in range(1, 4):
            weight(2, r).wait_recv()
        onward(2).start()

    def move(unit, i, source_core):
        dc, r = PEERS[i]
        h, seq = unit_place(unit, source_core)
        dest = pl.multiple_of(((c ^ dc) * 4 + (t ^ r)) * own, own)
        src = obuf.at[unit, :, pl.ds(dest, own)]
        dst = att.at[
            pl.ds(pl.multiple_of((t * 3 + h) * HD, HD), HD), pl.ds(pl.multiple_of(seq * own, own), own)
        ]
        if i == 0:
            return pltpu.make_async_copy(src, dst, lsem.at[unit])
        return pltpu.make_async_remote_copy(
            src, dst, ssem.at[i - 1, unit], rsem.at[i - 1, unit], device_id=at_peer(c, t, dc, r)
        )

    @pl.when(sends(u, c))
    def _():
        for i in range(1, len(PEERS)):
            move(u, i, c).start()
        move(u, 0, c).start()

    @pl.when(u == pl.num_programs(0) - 1)
    def _():
        for step in range(2, n - 1):
            line(step - 1, "recv")
            line(step, "start")
        line(n - 2, "recv")
        for step in range(n - 1):
            line(step, "sent")
        weight(1, 0).wait()
        for j in range(3):
            for r in range(1, 3 if j == 1 else 4):
                weight(j, r).wait_send()
        for k in range(3):
            onward(k).wait()
        for unit in range(UNITS):
            for i, (dc, r) in enumerate(PEERS):

                @pl.when(sends(unit, c))
                def _():
                    if i:
                        move(unit, i, c).wait_send()
                    else:
                        move(unit, i, c).wait()

                if i:

                    @pl.when(sends(unit, c ^ dc))
                    def _():
                        move(unit, i, c ^ dc).wait_recv()


def attend(n, qkv, lo, out_part, up_part, down_own):
    length = lo.shape[2]
    half = length // 2
    own = half // 4
    width, hidden = up_part.shape
    part = lambda p: pl.BlockSpec((1, HD, length), unit_block(p))
    unit = lambda rows, n: pl.BlockSpec((1, rows, n), lambda u: (u, 0, 0))
    heads = 4 * 3 * HD
    return pl.pallas_call(
        functools.partial(attend_kernel, n),
        grid=(UNITS,),
        in_specs=[part(0), part(1), part(2)]
        + [pl.BlockSpec((1, 1, length), lambda u: (u // 3, 0, 0))]
        + [
            pl.BlockSpec(a.shape, lambda u: (0, 0), pipeline_mode=pl.Buffered(1))
            for a in (out_part, up_part, down_own)
        ],
        out_specs=[HBM, unit(1, length), unit(HD, length)] + [HBM] * 3,
        scratch_shapes=[
            pltpu.VMEM((HD, length), low),
            pltpu.VMEM((length, HD), low),
            pltpu.VMEM((WIN + QB, QB), full),
            pltpu.VMEM((UNITS, HD, length), low),
            dma((7, UNITS)),
            dma((7, UNITS)),
            dma((UNITS,)),
            dma((3, 3)),
            dma((3, 3)),
            dma((3,)),
            dma((2, n - 1)),
            dma((2, n - 1)),
            dma((3,)),
            dma((3,)),
        ],
        out_shape=[
            jax.ShapeDtypeStruct((heads, 3 * own), low),
            jax.ShapeDtypeStruct((UNITS, 1, length), full),
            jax.ShapeDtypeStruct((UNITS, HD, length), full),
            shape((4, width, hidden), low),
            shape((4, width, hidden), low),
            shape((4,) + out_part.shape, low),
        ],
        compiler_params=pltpu.CompilerParams(
            vmem_limit_bytes=63 << 20, collective_id=1, has_side_effects=True
        ),
        cost_estimate=pl.CostEstimate(
            flops=UNITS * 18 * 2 * 256 * 1024 * 128, bytes_accessed=20 << 20, transcendentals=0
        ),
        name="attend",
    )(qkv, qkv, qkv, lo, out_part, up_part, down_own)


def add_to(ref, terms):
    for p in range(ref.shape[0]):
        ref[p] = (ref[p].astype(full) + terms(p).astype(full)).astype(low)


def attend_back_kernel(
    n, q_ref, k_ref, v_ref, lo_ref, lse_ref, of_ref, norm_ref, g_ref, gout, gud, side, part_sum,
    dall, gw_sum, zsum, osum, ssum,
    qs, ks, vs, grow, qrow, delta, dqs, soft, dscore, dbuf, gw, gwx, gwr, zr, gud_v, obuf, ogot, sgot, stot, sdp, ssem, rsem, lsem,
    zsend, zrecv, xsend, xrecv, osend, orecv, olocal, vlocal, s_send, s_recv, s_local, dsend, drecv,
):
    u = pl.program_id(0)
    c, t = place()
    d = lax.axis_index("dp")
    shard = gud.shape[1] // n
    length = lo_ref.shape[2]
    own = length // 8
    others = [lax.rem(d + r, n) for r in range(1, n)]
    peers = [at_peer(c, t, dc, r) for dc, r in PEERS[1:]] + [{"dp": o} for o in others]

    def rows_of(j):
        return pl.ds(pl.multiple_of(j * shard, shard), shard)

    def side_tensor(r):
        if r == 0:
            return pltpu.make_async_copy(side.at[t], sgot.at[0], s_local)
        return pltpu.make_async_remote_copy(
            side.at[t ^ r], sgot.at[r], s_send.at[r - 1], s_recv.at[r - 1], device_id={"tensor": t ^ r}
        )

    def side_dp(r):
        return pltpu.make_async_remote_copy(
            stot.at[rows_of(others[r - 1])],
            sdp.at[r - 1],
            dsend.at[r - 1],
            drecv.at[r - 1],
            device_id={"dp": others[r - 1]},
        )

    def line_of(h):
        pair = pl.ds(2 * h, 2)
        return Line(
            n,
            lambda j: gud.at[pair, rows_of(j)],
            lambda k, step: zr.at[h, k, step - 1],
            zsend.at[h],
            zrecv.at[h],
        )

    lines = [line_of(0), line_of(1)]

    def step_of(h, step, arrived=True):
        if arrived and step > 1:
            lines[h].received(step - 1)

        def add(k, j):
            rows = rows_of(j)
            add_to(zr.at[h, k, step - 2], lambda p: gud_v[2 * h + p, rows])

        lines[h].start(step, add)

    def finish(h):
        lines[h].received(n - 1)
        for step in range(2 if h == 0 else 1, n):
            lines[h].sent(step)
        for p in range(2):
            total = gud_v[2 * h + p, rows_of(d)].astype(full)
            up, down = (zr[h, k, n - 2, p].astype(full) for k in range(2))
            total += jnp.where(d > 0, up, 0.0) + jnp.where(d < n - 1, down, 0.0)
            zsum[2 * h + p] = total.astype(low)

    part_rows = gout.shape[2] // 2
    own_half = pl.ds(pl.multiple_of(c * part_rows, part_rows), part_rows)
    other_half = pl.ds(pl.multiple_of((1 - c) * part_rows, part_rows), part_rows)

    def out_grad(r):
        if r == 4:
            return pltpu.make_async_remote_copy(
                gout.at[:, :, other_half], ogot, osend.at[3], orecv.at[3], device_id={"context": 1 - c}
            )
        src, dst = ogot.at[t ^ r], obuf.at[r]
        if r == 0:
            return pltpu.make_async_copy(src, dst, olocal)
        return pltpu.make_async_remote_copy(
            src, dst, osend.at[r - 1], orecv.at[r - 1], device_id={"tensor": t ^ r}
        )

    def other_core():
        return pltpu.make_async_remote_copy(
            gwx.at[1 - c], gwr, xsend, xrecv, device_id={"context": 1 - c}
        )

    def load(i):
        if i == 2:
            return pltpu.make_async_copy(gud, gud_v, vlocal.at[2])
        return pltpu.make_async_copy(part_sum.at[i], zr.at[0, i, 0], vlocal.at[i])

    @pl.when(u == 0)
    def _():
        greet(peers)
        for i in range(3):
            load(i).start()
        gw[...] = jnp.zeros_like(gw)
        greeted(peers)
        out_grad(4).start()
        for r in range(1, 4):
            side_tensor(r).start()
        side_tensor(0).start()
        step_of(1, 1)
        for i in range(3):
            load(i).wait()
        step_of(0, 2, False)

    @pl.when(u == 1)
    def _():
        out_grad(4).wait()
        for p in range(4):
            ogot[p] = (ogot[p].astype(full) + gout[p, :, own_half].astype(full)).astype(low)
        for r in range(1, 4):
            out_grad(r).start()
        out_grad(0).start()
        step_of(1, 2)

    @pl.when(u == 2)
    def _():
        side_tensor(0).wait()
        for r in range(1, 4):
            side_tensor(r).wait_recv()
        stot[...] = sum(sgot[r].astype(full) for r in range(4)).astype(low)
        for r in range(1, n):
            side_dp(r).start()

    @pl.when(u == 3)
    def _():
        step_of(0, 3)

    @pl.when(u == 4)
    def _():
        step_of(1, 3)

    qs[...] = q_ref[0] * low(0.125)
    ks[...] = k_ref[0].T
    vs[...] = v_ref[0].T
    grow[...] = g_ref[0].T
    qrow[...] = qs[...].T
    delta[...] = jnp.sum(g_ref[0].astype(full) * of_ref[0], axis=0, keepdims=True)
    dqs[...] = jnp.zeros_like(dqs)
    for key_start in range(0, length, QB):
        rows = slice(key_start, key_start + QB)
        k, v, key_t = ks[rows, :], vs[rows, :], k_ref[0, :, rows]
        stop = min(key_start + WIN + QB, length)
        key_pos = key_start + lax.broadcasted_iota(jnp.int32, (QB, QB), 0)
        for start in range(key_start, stop, QB):
            cols = slice(start, start + QB)
            held = slice(start - key_start, start - key_start + QB)
            s = nn(k, qs[:, cols]) - lse_ref[0, :, cols]
            allowed = key_pos >= lo_ref[0, :, cols]
            if start == key_start:
                allowed &= key_pos <= start + lax.broadcasted_iota(jnp.int32, (QB, QB), 1)
            p = jnp.exp(jnp.where(allowed, s, NEG))
            dp = nn(v, g_ref[0, :, cols])
            soft[:, held] = p.astype(low)
            dscore[:, held] = (p * (dp - delta[:, cols])).astype(low)
        cols, held = slice(key_start, stop), slice(0, stop - key_start)
        dv = nn(soft[:, held], grow[cols, :])
        dk = nn(dscore[:, held], qrow[cols, :])
        dqs[:, cols] += nn(key_t, dscore[:, held])
        dbuf[u, 1, :, rows] = dk.T.astype(low)
        dbuf[u, 2, :, rows] = dv.T.astype(low)
    dbuf[u, 0] = (dqs[...] * 0.125).astype(low)

    def move(unit, i, source_core):
        dc, r = PEERS[i]
        h, seq = unit_place(unit, source_core)
        dest = pl.multiple_of(((c ^ dc) * 4 + (t ^ r)) * own, own)
        src = dbuf.at[unit, :, :, pl.ds(dest, own)]
        dst = dall.at[t, :, h, :, pl.ds(pl.multiple_of(seq * own, own), own)]
        if i == 0:
            return pltpu.make_async_copy(src, dst, lsem.at[unit])
        return pltpu.make_async_remote_copy(
            src, dst, ssem.at[i - 1, unit], rsem.at[i - 1, unit], device_id=at_peer(c, t, dc, r)
        )

    @pl.when(sends(u, c))
    def _():
        for i in range(1, len(PEERS)):
            move(u, i, c).start()
        move(u, 0, c).start()
        h, _ = unit_place(u, c)
        gw[h] += nn(dbuf[u].reshape(3 * HD, length), norm_ref[0])

    @pl.when(u == pl.num_programs(0) - 1)
    def _():
        wide_rows = [gw[h, p * HD : (p + 1) * HD, :] for p in range(3) for h in range(3)]
        gwx[0] = jnp.concatenate(wide_rows[:6], axis=0).T.astype(low)
        empty = jnp.zeros((3 * HD, gw.shape[2]), full)
        gwx[1] = jnp.concatenate(wide_rows[6:] + [empty], axis=0).T.astype(low)
        other_core().start()
        out_grad(0).wait()
        for r in range(1, 4):
            out_grad(r).wait()
        osum[...] = sum(obuf[r].astype(full) for r in range(4)).T.astype(low)
        other_core().wait()
        gw_sum[...] = (gwx[c].astype(full) + gwr[...].astype(full)).astype(low)
        for step in range(4, n):
            step_of(0, step)
            step_of(1, step)
        finish(0)
        finish(1)
        total = stot[rows_of(d)].astype(full)
        for r in range(1, n):
            side_tensor(r).wait_send() if r < 4 else None
            side_dp(r).wait()
            total += sdp[r - 1].astype(full)
        ssum[...] = total
        for unit in range(UNITS):
            for i, (dc, r) in enumerate(PEERS):

                @pl.when(sends(unit, c))
                def _():
                    if i:
                        move(unit, i, c).wait_send()
                    else:
                        move(unit, i, c).wait()

                if i:

                    @pl.when(sends(unit, c ^ dc))
                    def _():
                        move(unit, i, c ^ dc).wait_recv()


def attend_back(n, qkv, grad_units, lo, lse, attended, normed, grad_out, grad_up_down, side, part_sum):
    length = lo.shape[2]
    own = length // 8
    width = normed.shape[2]
    shard, columns = grad_up_down.shape[1] // n, grad_up_down.shape[2]
    out_rows, local = grad_out.shape[2] // 2, grad_out.shape[1]
    part = lambda p: pl.BlockSpec((1, HD, length), unit_block(p))
    unit = lambda rows, m: pl.BlockSpec((1, rows, m), lambda u: (u, 0, 0))
    once = lambda dims: pl.BlockSpec(dims, lambda u: (0,) * len(dims), pipeline_mode=pl.Buffered(1))
    wide, tall = pltpu.VMEM((HD, length), low), pltpu.VMEM((length, HD), low)
    results = [(width, 2 * 3 * HD), (4, shard, columns), (out_rows, local)]
    return pl.pallas_call(
        functools.partial(attend_back_kernel, n),
        grid=(UNITS,),
        in_specs=[part(0), part(1), part(2)]
        + [
            pl.BlockSpec((1, 1, length), lambda u: (u // 3, 0, 0)),
            unit(1, length),
            unit(HD, length),
            pl.BlockSpec((1, length, width), lambda u: (u // 3, 0, 0)),
            unit(HD, length),
            once(grad_out.shape),
        ]
        + [HBM] * 3,
        out_specs=[HBM] + [once(r) for r in results] + [once((shard, SIDE))],
        scratch_shapes=[
            wide, tall, tall, tall, tall,
            pltpu.VMEM((1, length), full), pltpu.VMEM((HD, length), full),
            pltpu.VMEM((QB, WIN + QB), low), pltpu.VMEM((QB, WIN + QB), low),
            pltpu.VMEM((UNITS, 3, HD, length), low), pltpu.VMEM((3, 3 * HD, width), full),
            pltpu.VMEM((2, width, 6 * HD), low), pltpu.VMEM((width, 6 * HD), low),
            pltpu.VMEM((2, 2, n - 1, 2, shard, columns), low), pltpu.VMEM(grad_up_down.shape, low),
            pltpu.VMEM((4, local, out_rows), low), pltpu.VMEM((4, local, out_rows), low),
            pltpu.VMEM((4, width, SIDE), low), pltpu.VMEM((width, SIDE), low), pltpu.VMEM((n - 1, shard, SIDE), low),
            dma((7, UNITS)), dma((7, UNITS)), dma((UNITS,)),
            dma((2, 2, n - 1)), dma((2, 2, n - 1)), dma, dma, dma((4,)), dma((4,)), dma, dma((3,)),
            dma((3,)), dma((3,)), dma, dma((n - 1,)), dma((n - 1,)),
        ],
        out_shape=[shape((4, 3, 3, HD, 3 * own), low)]
        + [shape(r, low) for r in results]
        + [shape((shard, SIDE), full)],
        compiler_params=pltpu.CompilerParams(
            vmem_limit_bytes=63 << 20, collective_id=2, has_side_effects=True
        ),
        name="attend_back",
    )(qkv, qkv, qkv, lo, lse, attended, normed, grad_units, grad_out, grad_up_down, side, part_sum)


def last_kernel(
    n, dqkv_ref, w_ref, tokens_ref, middle_ref, gains, w_own, up_own, gain_one, gain_two, ssum, gw_sum, zsum, osum,
    grad_in, g_qkv, g_up, g_down, g_out, g_one, g_two,
    rg, rw, ro, down_n, out_t, mine, sums, dqkv, w_all, tokens, middle,
    gsend, grecv, wsend, wrecv, osend, orecv, lsem, csend, crecv, ssend, srecv, clocal, fetch,
):
    c, t = place()
    d = lax.axis_index("dp")
    shard, hidden = rg.shape[1], rg.shape[2]
    cut = n // 2
    group = [at_peer(c, t, dc, r) for dc, r in PEERS[1:]]
    others = [lax.rem(d + r, n) for r in range(1, n)]
    peers = group + [{"dp": o} for o in others]
    greet(peers)
    loads = [
        pltpu.make_async_copy(src, dst, fetch.at[i])
        for i, (src, dst) in enumerate(
            ((tokens_ref, tokens), (w_ref, w_all), (dqkv_ref, dqkv), (middle_ref, middle))
        )
    ]
    for copy in loads:
        copy.start()

    def rows_of(j):
        return pl.ds(pl.multiple_of(j * shard, shard), shard)

    narrow = slice(0, 256)

    def qkv_piece(r, core):
        src, dst = gw_sum.at[rows_of(d if r == 0 else others[r - 1])], rg.at[r]
        if core:
            src, dst = src.at[:, narrow], dst.at[:, narrow]
        if r == 0:
            return pltpu.make_async_copy(src, dst, lsem.at[0])
        return pltpu.make_async_remote_copy(
            src, dst, gsend.at[r - 1], grecv.at[r - 1], device_id={"dp": others[r - 1]}
        )

    def each_core(what):
        for core in range(2):

            @pl.when(c == core)
            def _():
                what(core)

    def up_piece(r):
        src, dst = zsum.at[t ^ r], rw.at[r]
        if r == 0:
            return pltpu.make_async_copy(src, dst, lsem.at[1])
        return pltpu.make_async_remote_copy(
            src, dst, wsend.at[r - 1], wrecv.at[r - 1], device_id={"tensor": t ^ r}
        )

    mine_out = d // cut == c

    def out_piece(r):
        to = d if r == 0 else others[r - 1]
        src, dst = osum.at[rows_of(lax.rem(to, cut))], ro.at[r]
        if r == 0:
            return pltpu.make_async_copy(src, dst, lsem.at[2])
        return pltpu.make_async_remote_copy(
            src, dst, osend.at[r - 1], orecv.at[r - 1], device_id={"dp": to}
        )

    def start_all(core):
        for r in range(1, n):
            qkv_piece(r, core).start()
        qkv_piece(0, core).start()

    greeted(peers)
    each_core(start_all)
    for r in range(1, 4):
        up_piece(r).start()
    up_piece(0).start()
    for r in range(1, n):

        @pl.when(others[r - 1] // cut == c)
        def _():
            out_piece(r).start()

    @pl.when(mine_out)
    def _():
        out_piece(0).start()

    for copy in loads:
        copy.wait()
    @pl.loop(0, tokens.shape[0] // QB)
    def _(m):
        rows = pl.ds(pl.multiple_of(m * QB, QB), QB)
        r = tn(dqkv[:, rows], w_all[...])
        v = tokens[rows, :].astype(full)
        inv = lax.rsqrt(jnp.mean(v * v, axis=-1, keepdims=True) + epsilon)
        rg_ = r * gains[0:1, :]
        grad = inv * (rg_ - v * (inv * inv * jnp.mean(rg_ * v, axis=-1, keepdims=True)))
        grad_in[rows, :] = (middle[rows, :] + grad).astype(low)

    def halves(j):
        half = pl.ds(pl.multiple_of(c * hidden, hidden), hidden)
        src, dst = (
            (mine.at[0], g_qkv.at[:, half]),
            (mine.at[1], g_up.at[:, half]),
            (down_n, g_down.at[:, half]),
            (out_t, g_out),
        )[j]
        return (
            pltpu.make_async_copy(src, dst, clocal.at[j]),
            pltpu.make_async_remote_copy(
                src, dst, csend.at[j], crecv.at[j], device_id={"context": 1 - c}
            ),
        )

    def deliver(j):
        for copy in halves(j):
            copy.start()

    up_piece(0).wait()
    for r in range(1, 4):
        up_piece(r).wait_recv()
    main = hidden - SIDE
    mine[1, :, :main] = sum(rw[r, :, :main].astype(full) for r in range(4))
    mine[1, :, main:] = ssum[...]
    down_n[...] = sum(rw[r, :, main:].astype(full) for r in range(4))
    deliver(1)
    deliver(2)

    @pl.when(mine_out)
    def _():
        out_piece(0).wait()
        for r in range(1, n):
            out_piece(r).wait_recv()
        out_t[...] = sum(ro[r].astype(full) for r in range(n)).T
        deliver(3)

    def take(core):
        qkv_piece(0, core).wait()
        for r in range(1, n):
            qkv_piece(r, core).wait_recv()
        if core:
            mine[0, :, narrow] = sum(rg[r, :, narrow].astype(full) for r in range(n))
            mine[0, :, 256:] = jnp.zeros((shard, hidden - 256), full)
        else:
            mine[0] = sum(rg[r].astype(full) for r in range(n))

    each_core(take)
    deliver(0)
    lane = lax.broadcasted_iota(jnp.int32, (shard, 128), 1)
    halves_of = [jnp.concatenate([w_own[0], w_own[1]], axis=1), jnp.pad(w_own[2], ((0, 0), (0, osum.shape[1])))]
    w_mine = jnp.where(c == 0, halves_of[0].astype(full), halves_of[1].astype(full))
    up_mine = up_own[:, pl.ds(pl.multiple_of(c * hidden, hidden), hidden)].astype(full)
    first = jnp.sum(w_mine * mine[0], axis=1, keepdims=True)
    second = jnp.sum(up_mine * mine[1], axis=1, keepdims=True)
    sums[0] = jnp.where(lane == 0, first, jnp.where(lane == 1, second, 0.0)).T[:8]

    def gain_piece(i):
        dc, r = PEERS[i]
        return pltpu.make_async_remote_copy(
            sums.at[0], sums.at[i], ssend.at[i - 1], srecv.at[i - 1], device_id=at_peer(c, t, dc, r)
        )

    for i in range(1, len(PEERS)):
        gain_piece(i).start()
    for i in range(1, len(PEERS)):
        gain_piece(i).wait()
    total = sum(sums[i] for i in range(len(PEERS)))
    g_one[...] = total[0:1, :] / gain_one[...].astype(full)
    g_two[...] = total[1:2, :] / gain_two[...].astype(full)

    for j in range(3):
        for copy in halves(j):
            copy.wait()

    @pl.when(mine_out)
    def _():
        local, away = halves(3)
        local.wait()
        away.wait_send()

    @pl.when(jnp.logical_not(mine_out))
    def _():
        halves(3)[1].wait_recv()

    for r in range(1, 4):
        up_piece(r).wait_send()

    def sent(core):
        for r in range(1, n):
            qkv_piece(r, core).wait_send()

    each_core(sent)
    for r in range(1, n):

        @pl.when(others[r - 1] // cut == c)
        def _():
            out_piece(r).wait_send()


def last(n, dqkv, w_all, tokens, middle, gains, w_own, up_own, gain_one, gain_two, ssum, gw_sum, zsum, osum):
    rows, width = tokens.shape
    shard, hidden = zsum.shape[1], gw_sum.shape[1]
    local = osum.shape[1]
    return pl.pallas_call(
        functools.partial(last_kernel, n),
        in_specs=[HBM] * 4 + [VMEM] * 6 + [ANY] * 3,
        out_specs=[VMEM] + [ANY] * 4 + [VMEM] * 2,
        out_shape=[
            shape((rows, width), low),
            shape((shard, 2 * hidden), full),
            shape((shard, 2 * hidden), full),
            shape((shard, 2 * hidden), full),
            shape((local, shard), full),
            shape((1, shard), full),
            shape((1, shard), full),
        ],
        scratch_shapes=[
            pltpu.VMEM((n, shard, hidden), low),
            pltpu.VMEM((4, shard, 2 * hidden - SIDE), low),
            pltpu.VMEM((n, shard, local), low),
            pltpu.VMEM((shard, hidden), full),
            pltpu.VMEM((local, shard), full),
            pltpu.VMEM((2, shard, hidden), full),
            pltpu.VMEM((8, 8, shard), full),
            pltpu.VMEM(dqkv.shape, low), pltpu.VMEM(w_all.shape, low),
            pltpu.VMEM((rows, width), low), pltpu.VMEM((rows, width), full),
            dma((n - 1,)), dma((n - 1,)), dma((3,)), dma((3,)), dma((n - 1,)), dma((n - 1,)), dma((3,)),
            dma((4,)), dma((4,)), dma((7,)), dma((7,)), dma((4,)), dma((4,)),
        ],
        compiler_params=pltpu.CompilerParams(
            vmem_limit_bytes=63 << 20, collective_id=4, has_side_effects=True
        ),
        name="last",
    )(dqkv, w_all, tokens, middle, gains, w_own, up_own, gain_one, gain_two, ssum, gw_sum, zsum, osum)


def close_kernel(*refs):
    count = len(refs) // 2
    for i, (src, dst) in enumerate(zip(refs[:count], refs[count:])):
        if i == 2:
            local = dst.shape[2]
            for p in range(3):
                dst[p] = src[:, p * local : (p + 1) * local]
        else:
            dst[...] = src[...]


def close(result, grad_input, own_attn, *others):
    arrays = (result, grad_input, own_attn, *others)
    rows = lambda a: pl.BlockSpec((a.shape[0] // 2, a.shape[1]), lambda i: (i, 0))
    shard, local = own_attn.shape[0], others[0].shape[0]
    parts = pl.BlockSpec((3, shard // 2, local), lambda i: (0, i, 0))
    outs = [shape(a.shape, a.dtype) for a in arrays]
    outs[2] = shape((3, shard, local), full)
    return pl.pallas_call(
        close_kernel,
        grid=(2,),
        in_specs=[rows(a) for a in arrays],
        out_specs=[parts if i == 2 else rows(a) for i, a in enumerate(arrays)],
        out_shape=outs,
        compiler_params=pltpu.CompilerParams(vmem_limit_bytes=63 << 20),
        name="close",
    )(*arrays)


def gelu_and_slope(v):
    k0 = math.sqrt(2.0 / math.pi)
    square = v * v
    th = jnp.tanh(v * (k0 + (k0 * 0.044715) * square))
    half = 0.5 + 0.5 * th
    slope = half + (v * half) * ((1.0 - th) * (k0 + (3.0 * 0.044715 * k0) * square))
    return v * half, slope


def feed_kernel(
    dp, att, proj, tokens, cot, gains, w_t, up_ref, down_ref,
    result, middle, gout, gud, side, part_sum, units, w_all,
    x, g, x_t, g_t, up, down, act, gh, out, back, proj_w, sent, got, gbuf, sbuf, gatt,
    xsend, xrecv, wsend, wrecv, wlocal, zsend, zrecv, glocal, usend, urecv, ulocal, load,
):
    c, t = place()
    d = lax.axis_index("dp")
    rows, width = tokens.shape
    own = rows // 3
    shard = width // dp
    n = up_ref.shape[2]
    local = proj.shape[2]
    other = {"context": 1 - c}
    peers = [at_peer(c, t, dc, r) for dc, r in PEERS[1:]]
    mine, theirs = slice(0, rows), slice(rows, 2 * rows)
    block = rows // 3

    def cross(k):
        src, dst = (
            (cot, g.at[theirs]),
            (x.at[mine], x.at[theirs]),
            (sent.at[0], got.at[0]),
            (sent.at[1], got.at[1]),
        )[k]
        return pltpu.make_async_remote_copy(src, dst, xsend.at[k], xrecv.at[k], device_id=other)

    half = pl.ds(pl.multiple_of(c * (w_t.shape[0] // 2), 8), w_t.shape[0] // 2)

    def over_tensor(r):
        if r == 4:
            ref = w_all.at[:, half]
            return pltpu.make_async_remote_copy(ref, ref, wsend.at[3], wrecv.at[3], device_id=other)
        src, dst = w_t.at[half], w_all.at[t, half]
        if r == 0:
            return pltpu.make_async_copy(src, dst, wlocal)
        return pltpu.make_async_remote_copy(
            src, dst, wsend.at[r - 1], wrecv.at[r - 1], device_id={"tensor": t ^ r}
        )

    def rows_of(i):
        return pl.ds(pl.multiple_of(i * shard, shard), shard)

    line = Line(
        dp,
        lambda i: gbuf.at[0, :, rows_of(i)],
        lambda k, step: part_sum.at[k],
        zsend,
        zrecv,
    )

    def keep(j):
        if j == 2:
            return pltpu.make_async_copy(sbuf, side, glocal.at[2])
        return pltpu.make_async_copy(gbuf.at[j], gud.at[pl.ds(2 * j, 2)], glocal.at[j])

    def leave(whole, i):
        dc, r = PEERS[i]
        to_c, to_t = c ^ dc, t ^ r
        head = to_t * 3 + (0 if whole else to_c)
        count, first = (3, 0) if whole else (2, 3)
        seq = 2 * to_c if whole else 1
        src = gatt.at[pl.ds(head, count), :, pl.ds(pl.multiple_of(seq * own, own), own)]
        dst = units.at[pl.ds(first, count), :, pl.ds(pl.multiple_of((c * 4 + t) * own, own), own)]
        k = 0 if whole else 1
        if i == 0:
            return pltpu.make_async_copy(src, dst, ulocal.at[k])
        return pltpu.make_async_remote_copy(
            src, dst, usend.at[k, i - 1], urecv.at[k, i - 1], device_id=at_peer(c, t, dc, r)
        )

    loads = [
        pltpu.make_async_copy(ref.at[p], dst.at[p // 2, :, pl.ds((p % 2) * n, n)], load.at[i, p])
        for i, (ref, dst) in enumerate(((up_ref, up), (down_ref, down)))
        for p in range(4)
    ]
    greet(peers)
    greet_line(dp, d)
    for copy in loads:
        copy.start()
    for p in range(4):
        proj_w[:, p * local : (p + 1) * local] = proj[p]
    greeted_line(dp, d, peers)
    cross(0).start()
    for r in range(1, 4):
        over_tensor(r).start()
    over_tensor(0).start()
    for m in range(0, rows, block):
        part = slice(m, m + block)
        v = tokens[part, :].astype(full) + nn(proj_w[...], att[:, part]).T
        middle[part, :] = v
        inv = lax.rsqrt(jnp.mean(v * v, axis=-1, keepdims=True) + epsilon)
        x[part, :] = (v * inv * gains[1:2, :]).astype(low)
    cross(1).start()
    g[mine, :] = cot[...]
    g_t[:, mine] = cot[...].T
    x_t[:, mine] = x[mine, :].T
    for copy in loads:
        copy.wait()

    def hidden(side):
        @pl.loop(0, 6)
        def _(i):
            j = i // 3
            part = pl.ds(pl.multiple_of((side * 3 + i % 3) * block, block), block)
            pre = nn(x[part, :], up[j])
            ga = nn(g[part, :], down[j])
            a, slope = gelu_and_slope(pre)
            act[j, part, :] = a.astype(low)
            gh[j, part, :] = (ga * slope).astype(low)

    def branch(left, right, part):
        return nt(left[0, part, :], right[0]) + nt(left[1, part, :], right[1])

    hidden(0)
    cross(0).wait_recv()
    cross(1).wait_recv()
    hidden(1)

    def cut(side, left, right, put):
        @pl.loop(0, 3)
        def _(i):
            here = pl.ds(pl.multiple_of(i * block, block), block)
            part = pl.ds(pl.multiple_of(side * rows + i * block, block), block)
            put(here, branch(left, right, part))

    def put_sent(k):
        def put(here, value):
            sent[k, here, :] = value.astype(low)

        return put

    def put_own(ref):
        def put(here, value):
            ref[here, :] = value

        return put

    cut(1, gh, up, put_sent(0))
    cross(2).start()
    cut(0, gh, up, put_own(back))
    over_tensor(0).wait()
    for r in range(1, 4):
        over_tensor(r).wait_recv()
    over_tensor(4).start()
    x_t[:, theirs] = x[theirs, :].T
    g_t[:, theirs] = g[theirs, :].T
    cross(1).wait_send()
    cross(2).wait_recv()
    gain = gains[1:2, :]
    low_t = x
    for m in range(0, rows, block):
        part = slice(m, m + block)
        r = (back[part, :] + got[0, part, :].astype(full)) * gain
        v = middle[part, :]
        inv = lax.rsqrt(jnp.mean(v * v, axis=-1, keepdims=True) + epsilon)
        grad = inv * (r - v * (inv * inv * jnp.mean(r * v, axis=-1, keepdims=True)))
        back[part, :] = cot[part, :].astype(full) + grad
        x[part, :] = back[part, :].astype(low)
        low_t[rows : rows + width, part] = x[part, :].T
        grad = tn(proj_w[...], low_t[rows : rows + width, part]).astype(low)
        gatt[:, :, part] = grad.reshape(gatt.shape[0], HD, block)
    for whole in (True, False):
        for i in range(1, len(PEERS)):
            leave(whole, i).start()
        leave(whole, 0).start()

    def weight_grad(j, a, left_t, right):
        @pl.loop(0, 3)
        def _(i):
            part = pl.ds(pl.multiple_of(i * (width // 3), width // 3), width // 3)
            grad = nn(left_t[part, :], right[j]).astype(low)
            main = n - SIDE
            for p in range(2):
                if a:
                    gbuf[j, p, part, main:] = grad[:, p * n : (p + 1) * n]
                else:
                    gbuf[j, p, part, :main] = grad[:, p * n : p * n + main]
                    sbuf[2 * j + p, part, :] = grad[:, p * n + main : (p + 1) * n]

    weight_grad(0, 0, x_t, gh)
    weight_grad(0, 1, g_t, act)
    line.start(1, None)
    keep(0).start()
    cut(1, act, down, put_sent(1))
    cross(3).start()
    weight_grad(1, 0, x_t, gh)
    weight_grad(1, 1, g_t, act)
    keep(1).start()
    keep(2).start()
    cut(0, act, down, put_own(out))
    for p in range(4):
        gout[p] = nn(att[p * local : (p + 1) * local, :], x[mine, :]).astype(low)
    cross(3).wait_recv()
    result[...] = (middle[...] + out[...] + got[1].astype(full)).astype(low)
    middle[...] = back[...]
    for k in (0, 2, 3):
        cross(k).wait_send()
    for r in range(1, 4):
        over_tensor(r).wait_send()
    over_tensor(4).wait()
    line.received(1)
    line.sent(1)
    for j in range(3):
        keep(j).wait()
    for whole in (True, False):
        for i in range(len(PEERS)):
            leave(whole, i).wait()


def feed(dp, att, proj, tokens, cot, gains, w_t, up, down):
    rows, width = tokens.shape
    pieces, _, n = up.shape
    own = rows // 3
    assert pieces == 4 and dp > 2 and rows == width
    return pl.pallas_call(
        functools.partial(feed_kernel, dp),
        in_specs=[VMEM] * 6 + [HBM] * 2,
        out_specs=[VMEM] * 3 + [HBM] * 5,
        out_shape=[
            shape((rows, width), low),
            shape((rows, width), full),
            shape((4, proj.shape[2], width), low),
            shape((4, width, 2 * n - SIDE), low),
            shape((4, width, SIDE), low),
            shape((2, 2, width // dp, 2 * n - SIDE), low),
            shape((UNITS, HD, 8 * own), low),
            shape((4,) + w_t.shape, low),
        ],
        scratch_shapes=[pltpu.VMEM((2 * rows, width), low)] * 2
        + [pltpu.VMEM((width, 2 * rows), low)] * 2
        + [pltpu.VMEM((2, width, 2 * n), low)] * 2
        + [pltpu.VMEM((2, 2 * rows, 2 * n), low)] * 2
        + [pltpu.VMEM((rows, width), full)] * 2
        + [pltpu.VMEM((width, width), low)]
        + [pltpu.VMEM((2, rows, width), low)] * 2
        + [pltpu.VMEM((2, 2, width, 2 * n - SIDE), low), pltpu.VMEM((4, width, SIDE), low)]
        + [pltpu.VMEM((12, HD, rows), low)]
        + [dma((4,)), dma((4,)), dma((4,)), dma((4,)), dma]
        + [dma((2, 1)), dma((2, 1)), dma((3,)), dma((2, 7)), dma((2, 7)), dma((2,)), dma((2, 4))],
        compiler_params=pltpu.CompilerParams(
            vmem_limit_bytes=63 << 20, collective_id=5, has_side_effects=True
        ),
        name="feed",
    )(att, proj, tokens, cot, gains, w_t, up, down)


def per_device(tokens, segments, w_qkv, w_out, w_in, w_back, gain_attn, gain_mlp, cotangent):
    sequences, own, width = tokens.shape
    assert lax.axis_size("tensor") == 4 and lax.axis_size("context") == 2 and sequences == 3
    n = lax.axis_size("dp")
    length = segments.shape[1]
    shard = w_qkv.shape[0]
    local = w_qkv.shape[2]
    rows = sequences * own
    parts = w_qkv.transpose(1, 0, 2)
    gain_one, gain_two = gain_attn.reshape(1, shard), gain_mlp.reshape(1, shard)
    qkv, normed_units, w_t, up_part, out_part, gains, lo = project(
        n, tokens, segments, parts, w_in, w_out, gain_one, gain_two
    )
    attended, log_totals, out_full, w_up, w_down, w_proj = attend(
        n, qkv, lo, out_part, up_part, w_back.T
    )
    flat = tokens.reshape(rows, width)
    result, grad_middle, grad_out, grad_up_down, side, part_sum, grad_units, w_all = feed(
        n, attended, w_proj, flat, cotangent.reshape(rows, width), gains, w_t, w_up, w_down
    )
    grad_projected, gw_sum, zsum, osum, ssum = attend_back(
        n, qkv, grad_units, lo, log_totals, out_full, normed_units, grad_out, grad_up_down, side, part_sum
    )
    grad_input, own_attn, own_up, own_down, own_proj, own_one, own_two = last(
        n,
        grad_projected.reshape(12 * local, rows),
        w_all.reshape(12 * local, width),
        flat,
        grad_middle,
        gains,
        parts,
        w_in,
        gain_one,
        gain_two,
        ssum,
        gw_sum,
        zsum,
        osum,
    )
    result, grad_input, own_attn, own_proj, own_up, own_down = close(
        result, grad_input, own_attn, own_proj, own_up, own_down
    )
    return (
        result.reshape(sequences, own, width),
        grad_input.reshape(sequences, own, width),
        own_attn.transpose(1, 0, 2),
        own_proj,
        own_up,
        own_down.T,
        own_one.reshape(shard),
        own_two.reshape(shard),
    )


def solution(mesh):
    return jax.shard_map(
        per_device,
        mesh=mesh,
        in_specs=(
            P("dp", ("context", "tensor"), None),
            P("dp", None),
            P("dp", None, "tensor"),
            P("tensor", "dp"),
            P("dp", "tensor"),
            P("tensor", "dp"),
            P("dp"),
            P("dp"),
            P("dp", ("context", "tensor"), None),
        ),
        out_specs=(
            P("dp", ("context", "tensor"), None),
            P("dp", ("context", "tensor"), None),
            P("dp", None, "tensor"),
            P("tensor", "dp"),
            P("dp", "tensor"),
            P("tensor", "dp"),
            P("dp"),
            P("dp"),
        ),
        check_vma=False,
    )
```

```python
import functools
import math

import jax
import jax.numpy as jnp
from jax import lax
from jax.experimental import pallas as pl
from jax.experimental.pallas import tpu as pltpu
from jax.sharding import PartitionSpec as P

HD = 64
WIN = 1536
QB = 256
CHUNK = 128
NEG = -1e30
epsilon = 1e-06
low = jnp.bfloat16
full = jnp.float32


def dot(left, right, dims):
    return lax.dot_general(left, right, (dims, ((), ())), preferred_element_type=full)


def nn(left, right):
    return dot(left, right, ((1,), (0,)))


def nt(left, right):
    return dot(left, right, ((1,), (1,)))


def tn(left, right):
    return dot(left, right, ((0,), (0,)))


PEERS = [(dc, r) for dc in range(2) for r in range(4)]


def place():
    return lax.axis_index("context"), lax.axis_index("tensor")


def at_peer(c, t, dc, r):
    return {"context": c ^ dc, "tensor": t ^ r}


def greet(peers):
    for peer in peers:
        pl.semaphore_signal(pltpu.get_barrier_semaphore(), inc=1, device_id=peer)


def greeted(peers):
    pl.semaphore_wait(pltpu.get_barrier_semaphore(), len(peers))


def unit_place(u, c):
    return jnp.where(u < 3, u, c + u - 3), jnp.where(u < 3, 2 * c, 1)


def sends(u, c):
    return (u != 3) | (c == 0)


dma = pltpu.SemaphoreType.DMA
ANY = pl.BlockSpec(memory_space=pl.ANY)
VMEM = pl.BlockSpec(memory_space=pltpu.VMEM)
HBM = pl.BlockSpec(memory_space=pltpu.HBM)
shape = jax.ShapeDtypeStruct

SIDE = 128


class Line:
    def __init__(self, n, own, slot, send, recv):
        self.n, self.own, self.slot, self.sems = n, own, slot, (send, recv)
        self.d = lax.axis_index("dp")

    def along(self, k):
        m = self.d if k == 0 else self.n - 1 - self.d
        to = {"dp": jnp.clip(self.d + 1 if k == 0 else self.d - 1, 0, self.n - 1)}
        return m, to

    def target(self, k, step):
        m, _ = self.along(k)
        return jnp.clip(self.n - step + m if k == 0 else step - 1 - m, 0, self.n - 1)

    def copy(self, k, step, src):
        send, recv = self.sems
        _, to = self.along(k)
        return pltpu.make_async_remote_copy(
            src, self.slot(k, step), send.at[k, step - 1], recv.at[k, step - 1], device_id=to
        )

    def arrive(self, k, step):
        self.copy(k, step, self.slot(k, step)).wait_recv()

    def start(self, step, add):
        for k in range(2):
            m, _ = self.along(k)
            if step > 1:

                @pl.when((m >= 1) & (m < self.n - 1) & (step >= m + 1))
                def _():
                    add(k, self.target(k, step))
                    self.copy(k, step, self.slot(k, step - 1)).start()

            @pl.when(m == 0)
            def _():
                self.copy(k, step, self.own(self.target(k, step))).start()

    def received(self, step):
        for k in range(2):
            m, _ = self.along(k)

            @pl.when((m >= 1) & (step >= m))
            def _():
                self.arrive(k, step)

    def sent(self, step):
        for k in range(2):
            m, _ = self.along(k)

            @pl.when((m < self.n - 1) & (step >= m + 1))
            def _():
                self.copy(k, step, self.slot(k, step)).wait_send()


def greet_line(n, d):
    barrier = pltpu.get_barrier_semaphore()

    @pl.when(d > 0)
    def _():
        pl.semaphore_signal(barrier, inc=1, device_id={"dp": jnp.maximum(d - 1, 0)})

    @pl.when(d < n - 1)
    def _():
        pl.semaphore_signal(barrier, inc=1, device_id={"dp": jnp.minimum(d + 1, n - 1)})


def greeted_line(n, d, peers):
    ends = jnp.where(d > 0, 1, 0) + jnp.where(d < n - 1, 1, 0)
    pl.semaphore_wait(pltpu.get_barrier_semaphore(), len(peers) + ends)


def project_kernel(
    n, tokens, segments, w_qkv, up, out_own, gain_one, gain_two, qkv, norm, w_t, up_all, out_all, gain_ref, lo_ref,
    tok, x, w, proj, out_w, gain, own_gain, tsend, trecv, tlocal, wsend, wrecv, wlocal, osend, orecv, olocal, xsend, xrecv,
):
    c, t = place()
    d = lax.axis_index("dp")
    own = tokens.shape[1]
    width = tokens.shape[2]
    span = 4 * own
    shard = up.shape[0]
    half = own // 2
    hidden = up_all.shape[1]
    cut = n // 2
    to_x, to_y, to_core = {"tensor": t ^ 1}, {"tensor": t ^ 2}, {"context": 1 - c}
    others = [{"dp": lax.rem(d + r, n)} for r in range(1, n)]
    peers = [to_x, to_y, to_core] + others
    greet(peers)

    def local(i, s):
        return pltpu.make_async_copy(tokens.at[s], tok.at[s, t], tlocal.at[i])

    def weights(j, r):
        rows = pl.ds(pl.multiple_of(d * shard, shard), shard)
        source, target = (
            (w_qkv, w.at[:, rows]),
            (out_w, out_all.at[rows]),
            (up.at[:, pl.ds(pl.multiple_of(c * hidden, hidden), hidden)], up_all.at[rows]),
            (own_gain, gain.at[d]),
        )[j]
        if r == 0:
            return pltpu.make_async_copy(source, target, wlocal.at[j])
        return pltpu.make_async_remote_copy(
            source, target, wsend.at[j, r - 1], wrecv.at[j, r - 1], device_id=others[r - 1]
        )

    def gives(j, r):
        return lax.rem(d + n - r, n) // cut == c if j < 2 else True

    def weights_do(j, r, what, source=False):
        @pl.when(gives(j, 0 if source else r))
        def _():
            getattr(weights(j, r), what)()

    def to_other(j):
        rows = pl.ds(pl.multiple_of(c * cut * shard, shard), cut * shard)
        ref = w.at[:, rows]
        return pltpu.make_async_remote_copy(ref, ref, xsend, xrecv, device_id=to_core)

    order = (2 * (1 - c), 1, 2 * c)
    for i, s in enumerate(order):
        local(i, s).start()
    out_w[...] = out_own[...].T
    own_gain[...] = jnp.zeros_like(own_gain)
    own_gain[0:1, :] = gain_one[...]
    own_gain[1:2, :] = gain_two[...]
    for j in range(4):
        weights_do(j, 0, "start")
    greeted(peers)
    for j in (0, 3, 1, 2):
        for r in range(1, n):
            weights_do(j, r, "start", True)

    def hop(k, i):
        s = order[i]
        origin, rows, peer = (
            (t, slice(0, half), to_x),
            (t, slice(half, own), to_y),
            (t, slice(0, half), to_y),
            (t, slice(half, own), to_x),
            (t ^ 1, slice(0, half), to_y),
            (t ^ 2, slice(half, own), to_x),
        )[k]
        there = tok.at[s, origin, rows]
        here = tokens.at[s, rows] if k < 4 else there
        return pltpu.make_async_remote_copy(
            here, there, tsend.at[k, i], trecv.at[k, i], device_id=peer
        )

    def straight(i):
        for k in range(4):
            hop(k, i).start()

    def forward(i):
        for k in range(2):
            hop(k, i).wait_recv()
            hop(k + 4, i).start()

    units = proj.shape[1]

    def leave(i):
        out = []
        lanes = pl.ds(pl.multiple_of(c * span, span), span)
        if i != 0:
            out.append((x.at[i], norm.at[2 - i, lanes], False))
        if i != 2:
            out.append((x.at[i], norm.at[i, lanes], True))
        if i == 0:
            out.append((proj.at[0], qkv.at[pl.ds(0, units), :, lanes], True))
        if i == 2:
            out.append((proj.at[2], qkv.at[pl.ds(0, units), :, lanes], False))
        if i == 1:
            for away in (True, False):
                core = 1 - c if away else c
                for p in range(3):
                    src = proj.at[1, pl.ds(p * 3 + core, 2)]
                    out.append((src, qkv.at[pl.ds(units + 2 * p, 2), :, lanes], away))
        copies = []
        for j, (src, dst, away) in enumerate(out):
            if away:
                copies.append(
                    (away, pltpu.make_async_remote_copy(src, dst, osend.at[i, j], orecv.at[i, j], device_id=to_core))
                )
            else:
                copies.append((away, pltpu.make_async_copy(src, dst, olocal.at[i, j])))
        return copies

    def work(i):
        s = order[i]
        local(i, s).wait()
        for k in range(2, 6):
            hop(k, i).wait_recv()

        @pl.loop(0, 4)
        def _(p):
            rows = pl.ds(pl.multiple_of(p * own, own), own)
            v = tok[s, p].astype(full)
            inv = lax.rsqrt(jnp.mean(v * v, axis=-1, keepdims=True) + epsilon)
            normed = (v * inv * gain_ref[0:1, :]).astype(low)
            x[i, rows, :] = normed
            proj[i, :, :, rows] = nt(w_t[...], normed).astype(low).reshape(units, HD, own)

        for _, copy in leave(i):
            copy.start()

    straight(0)
    straight(1)
    forward(0)
    straight(2)
    seg = segments[...]
    first = jnp.zeros(seg.shape, jnp.int32)
    for value in range(8):
        before = jnp.sum((seg < value).astype(jnp.int32), axis=1, keepdims=True)
        first = jnp.where(seg == value, before, first)
    first = jnp.maximum(first, lax.broadcasted_iota(jnp.int32, seg.shape, 1) - (WIN - 1))
    lo_ref[0] = jnp.where(c == 0, first[0:1], first[2:3])
    lo_ref[1] = first[1:2]
    weights_do(0, 0, "wait")
    for r in range(1, n):
        weights_do(0, r, "wait_recv")
    to_other(0).start()
    weights(3, 0).wait()
    for r in range(1, n):
        weights(3, r).wait_recv()
    gain_ref[...] = jnp.concatenate([gain[i].astype(full) for i in range(n)], axis=1)[:8]
    to_other(0).wait_recv()
    for p in range(3):
        w_t[p * 3 * HD : (p + 1) * 3 * HD, :] = w[p].T
    forward(1)
    work(0)
    forward(2)
    work(1)
    work(2)
    to_other(0).wait_send()
    for j in range(4):
        if j in (1, 2):
            weights_do(j, 0, "wait")
        for r in range(1, n):
            weights_do(j, r, "wait_send", True)
            if j in (1, 2):
                weights_do(j, r, "wait_recv")
    for i in range(3):
        for k in range(6):
            hop(k, i).wait_send()
        for away, copy in leave(i):
            copy.wait()


def project(n, tokens, segments, w_qkv, up, out_own, gain_one, gain_two):
    sequences, own, width = tokens.shape
    shard, hidden = up.shape[0], up.shape[1] // 2
    local = out_own.shape[0]
    span = 4 * own
    return pl.pallas_call(
        functools.partial(project_kernel, n),
        in_specs=[HBM, VMEM, HBM, HBM, VMEM, VMEM, VMEM],
        out_specs=[HBM] * 2 + [VMEM] + [HBM] * 2 + [VMEM] * 2,
        out_shape=[
            shape((15, HD, 2 * span), low),
            shape((2, 2 * span, width), low),
            shape((9 * HD, n * shard), low),
            shape((n * shard, hidden), low),
            shape((n * shard, local), low),
            shape((8, n * shard), full),
            shape((2, 1, segments.shape[1]), jnp.int32),
        ],
        scratch_shapes=[
            pltpu.VMEM((sequences, 4, own, width), low),
            pltpu.VMEM((sequences, span, width), low),
            pltpu.VMEM((3, n * shard, local), low),
            pltpu.VMEM((sequences, 9, HD, span), low),
            pltpu.VMEM((shard, local), low),
            pltpu.VMEM((n, 16, shard), low),
            pltpu.VMEM((16, shard), low),
            dma((6, 3)), dma((6, 3)), dma((3,)),
            dma((4, n - 1)), dma((4, n - 1)), dma((4,)),
            dma((3, 8)), dma((3, 8)), dma((3, 8)), dma, dma,
        ],
        compiler_params=pltpu.CompilerParams(
            vmem_limit_bytes=63 << 20, collective_id=3, has_side_effects=True
        ),
        name="project",
    )(tokens, segments, w_qkv, up, out_own, gain_one, gain_two)


UNITS = 5
def unit_block(part):
    return lambda u: (jnp.where(u < 3, part * 3 + u, 9 + part * 2 + (u - 3)), 0, 0)


def attend_kernel(
    n, q_ref, k_ref, v_ref, lo_ref, out_part, up_part, down_own, att, lse_ref, of_ref, up, down, out_w,
    qs, ks, ss, obuf, ssem, rsem, lsem, wsend, wrecv, wlocal, zsend, zrecv, fsend, frecv,
):
    u = pl.program_id(0)
    c, t = place()
    d = lax.axis_index("dp")
    shard = down_own.shape[0]
    hidden = down.shape[2]
    peers = [at_peer(c, t, dc, r) for dc, r in PEERS[1:]]

    part = out_part.shape[0] // 2
    mine = pl.ds(pl.multiple_of(c * part, part), part)

    def weight(j, r):
        rows = pl.ds(pl.multiple_of(d * shard, shard), shard)
        src, dst = (
            (down_own.at[:, pl.ds(pl.multiple_of(c * hidden, hidden), hidden)], down.at[t, rows]),
            (up_part, up.at[t]),
            (out_part.at[mine], out_w.at[t, mine]),
        )[j]
        if r == 0:
            return pltpu.make_async_copy(src, dst, wlocal.at[j])
        return pltpu.make_async_remote_copy(
            src, dst, wsend.at[j, r - 1], wrecv.at[j, r - 1], device_id={"tensor": t ^ r}
        )

    def onward(k):
        if k == 2:
            ref, peer = out_w.at[:, mine], {"context": 1 - c}
        else:
            rows = pl.ds(k * part, part)
            ref, peer = up.at[t ^ (1 + k), rows], {"tensor": t ^ (2 - k)}
        return pltpu.make_async_remote_copy(
            ref, ref, fsend.at[k], frecv.at[k], device_id=peer
        )

    def shards(step, up_line):
        src = d - step if up_line else d + step
        rows = pl.ds(pl.multiple_of(jnp.clip(src, 0, n - 1) * shard, shard), shard)
        to = jnp.clip(d + 1 if up_line else d - 1, 0, n - 1)
        k = 0 if up_line else 1
        return pltpu.make_async_remote_copy(
            down.at[:, rows], down.at[:, rows], zsend.at[k, step], zrecv.at[k, step], device_id={"dp": to}
        )

    def line(step, what):
        for up_line in (True, False):
            inside = (d < n - 1) if up_line else (d > 0)
            has = (d >= step) if up_line else (d <= n - 1 - step)
            comes = (d >= step + 1) if up_line else (d <= n - 2 - step)
            if what == "recv":

                @pl.when(comes)
                def _():
                    shards(step, up_line).wait_recv()
            else:

                @pl.when(inside & has)
                def _():
                    if what == "start":
                        shards(step, up_line).start()
                    else:
                        shards(step, up_line).wait_send()
    length = lo_ref.shape[2]
    half = length // 2
    own = half // 4

    @pl.when(u == 0)
    def _():
        greet(peers)
        greet_line(n, d)
        for j in range(3):
            weight(j, 0).start()
        greeted_line(n, d, peers)
        for r in range(1, 4):
            weight(0, r).start()
        for r in range(1, 3):
            weight(1, r).start()

    qs[...] = q_ref[0] * low(0.125)
    ks[...] = k_ref[0].T
    for start in range(0, length, QB):
        stop = start + QB
        q = qs[:, start:stop]
        lo = lo_ref[0, :, start:stop]
        first = max(0, start - WIN)
        most = jnp.full((8, QB), NEG, full)
        for at in range(first, stop, CHUNK):
            s = nn(ks[at : at + CHUNK, :], q)
            key_pos = at + lax.broadcasted_iota(jnp.int32, (CHUNK, QB), 0)
            allowed = key_pos >= lo
            if at + CHUNK - 1 > start:
                allowed &= key_pos <= start + lax.broadcasted_iota(jnp.int32, (CHUNK, QB), 1)
            s = jnp.where(allowed, s, NEG)
            ss[at - first : at - first + CHUNK, :] = s
            most = jnp.maximum(most, jnp.max(s.reshape(CHUNK // 8, 8, QB), axis=0))
        most = jnp.max(most, axis=0, keepdims=True)
        total = jnp.zeros((8, QB), full)
        acc = jnp.zeros((HD, QB), full)
        for at in range(first, stop, CHUNK):
            p = jnp.exp(ss[at - first : at - first + CHUNK, :] - most)
            total += jnp.sum(p.reshape(CHUNK // 8, 8, QB), axis=0)
            acc += nn(v_ref[0, :, at : at + CHUNK], p.astype(low))
        total = jnp.sum(total, axis=0, keepdims=True)
        lse_ref[0, :, start:stop] = most + jnp.log(total)
        o = acc * (1.0 / total)
        of_ref[0, :, start:stop] = o
        obuf[u, :, start:stop] = o.astype(low)

    @pl.when(u == 0)
    def _():
        weight(0, 0).wait()
        for r in range(1, 4):
            weight(0, r).wait_recv()
        line(0, "start")
        for r in range(1, 4):
            weight(2, r).start()

    @pl.when(u == 3)
    def _():
        if n > 2:
            line(0, "recv")
            line(1, "start")
        for k in range(2):
            weight(1, 1 + k).wait_recv()
            onward(k).start()
        weight(2, 0).wait()
        for r in range(1, 4):
            weight(2, r).wait_recv()
        onward(2).start()

    def move(unit, i, source_core):
        dc, r = PEERS[i]
        h, seq = unit_place(unit, source_core)
        dest = pl.multiple_of(((c ^ dc) * 4 + (t ^ r)) * own, own)
        src = obuf.at[unit, :, pl.ds(dest, own)]
        dst = att.at[
            pl.ds(pl.multiple_of((t * 3 + h) * HD, HD), HD), pl.ds(pl.multiple_of(seq * own, own), own)
        ]
        if i == 0:
            return pltpu.make_async_copy(src, dst, lsem.at[unit])
        return pltpu.make_async_remote_copy(
            src, dst, ssem.at[i - 1, unit], rsem.at[i - 1, unit], device_id=at_peer(c, t, dc, r)
        )

    @pl.when(sends(u, c))
    def _():
        for i in range(1, len(PEERS)):
            move(u, i, c).start()
        move(u, 0, c).start()

    @pl.when(u == pl.num_programs(0) - 1)
    def _():
        for step in range(2, n - 1):
            line(step - 1, "recv")
            line(step, "start")
        line(n - 2, "recv")
        for step in range(n - 1):
            line(step, "sent")
        weight(1, 0).wait()
        for j in range(3):
            for r in range(1, 3 if j == 1 else 4):
                weight(j, r).wait_send()
        for k in range(3):
            onward(k).wait()
        for unit in range(UNITS):
            for i, (dc, r) in enumerate(PEERS):

                @pl.when(sends(unit, c))
                def _():
                    if i:
                        move(unit, i, c).wait_send()
                    else:
                        move(unit, i, c).wait()

                if i:

                    @pl.when(sends(unit, c ^ dc))
                    def _():
                        move(unit, i, c ^ dc).wait_recv()


def attend(n, qkv, lo, out_part, up_part, down_own):
    length = lo.shape[2]
    half = length // 2
    own = half // 4
    width, hidden = up_part.shape
    part = lambda p: pl.BlockSpec((1, HD, length), unit_block(p))
    unit = lambda rows, n: pl.BlockSpec((1, rows, n), lambda u: (u, 0, 0))
    heads = 4 * 3 * HD
    return pl.pallas_call(
        functools.partial(attend_kernel, n),
        grid=(UNITS,),
        in_specs=[part(0), part(1), part(2)]
        + [pl.BlockSpec((1, 1, length), lambda u: (u // 3, 0, 0))]
        + [
            pl.BlockSpec(a.shape, lambda u: (0, 0), pipeline_mode=pl.Buffered(1))
            for a in (out_part, up_part, down_own)
        ],
        out_specs=[HBM, unit(1, length), unit(HD, length)] + [HBM] * 3,
        scratch_shapes=[
            pltpu.VMEM((HD, length), low),
            pltpu.VMEM((length, HD), low),
            pltpu.VMEM((WIN + QB, QB), full),
            pltpu.VMEM((UNITS, HD, length), low),
            dma((7, UNITS)),
            dma((7, UNITS)),
            dma((UNITS,)),
            dma((3, 3)),
            dma((3, 3)),
            dma((3,)),
            dma((2, n - 1)),
            dma((2, n - 1)),
            dma((3,)),
            dma((3,)),
        ],
        out_shape=[
            jax.ShapeDtypeStruct((heads, 3 * own), low),
            jax.ShapeDtypeStruct((UNITS, 1, length), full),
            jax.ShapeDtypeStruct((UNITS, HD, length), full),
            shape((4, width, hidden), low),
            shape((4, width, hidden), low),
            shape((4,) + out_part.shape, low),
        ],
        compiler_params=pltpu.CompilerParams(
            vmem_limit_bytes=63 << 20, collective_id=1, has_side_effects=True
        ),
        cost_estimate=pl.CostEstimate(
            flops=UNITS * 18 * 2 * 256 * 1024 * 128, bytes_accessed=20 << 20, transcendentals=0
        ),
        name="attend",
    )(qkv, qkv, qkv, lo, out_part, up_part, down_own)


def add_to(ref, terms):
    for p in range(ref.shape[0]):
        ref[p] = (ref[p].astype(full) + terms(p).astype(full)).astype(low)


def attend_back_kernel(
    n, q_ref, k_ref, v_ref, lo_ref, lse_ref, of_ref, norm, g_ref, gout, gud, side, part_sum,
    dall, gw_sum, zsum, osum, ssum,
    qs, ks, vs, grow, qrow, delta, dqs, soft, dscore, norm_v, dbuf, gw, gwx, gwr, zr, gud_v, obuf, ogot, sgot, stot, sdp, ssem, rsem, lsem,
    zsend, zrecv, xsend, xrecv, osend, orecv, olocal, vlocal, nlocal, s_send, s_recv, s_local, dsend, drecv,
):
    u = pl.program_id(0)
    c, t = place()
    d = lax.axis_index("dp")
    shard = gud.shape[1] // n
    length = lo_ref.shape[2]
    own = length // 8
    others = [lax.rem(d + r, n) for r in range(1, n)]
    peers = [at_peer(c, t, dc, r) for dc, r in PEERS[1:]] + [{"dp": o} for o in others]

    def rows_of(j):
        return pl.ds(pl.multiple_of(j * shard, shard), shard)

    def side_tensor(r):
        if r == 0:
            return pltpu.make_async_copy(side.at[t], sgot.at[0], s_local)
        return pltpu.make_async_remote_copy(
            side.at[t ^ r], sgot.at[r], s_send.at[r - 1], s_recv.at[r - 1], device_id={"tensor": t ^ r}
        )

    def side_dp(r):
        return pltpu.make_async_remote_copy(
            stot.at[rows_of(others[r - 1])],
            sdp.at[r - 1],
            dsend.at[r - 1],
            drecv.at[r - 1],
            device_id={"dp": others[r - 1]},
        )

    def line_of(h):
        pair = pl.ds(2 * h, 2)
        return Line(
            n,
            lambda j: gud.at[pair, rows_of(j)],
            lambda k, step: zr.at[h, k, step - 1],
            zsend.at[h],
            zrecv.at[h],
        )

    lines = [line_of(0), line_of(1)]

    def step_of(h, step, arrived=True):
        if arrived and step > 1:
            lines[h].received(step - 1)

        def add(k, j):
            rows = rows_of(j)
            add_to(zr.at[h, k, step - 2], lambda p: gud_v[2 * h + p, rows])

        lines[h].start(step, add)

    def finish(h):
        lines[h].received(n - 1)
        for step in range(2 if h == 0 else 1, n):
            lines[h].sent(step)
        for p in range(2):
            total = gud_v[2 * h + p, rows_of(d)].astype(full)
            up, down = (zr[h, k, n - 2, p].astype(full) for k in range(2))
            total += jnp.where(d > 0, up, 0.0) + jnp.where(d < n - 1, down, 0.0)
            zsum[2 * h + p] = total.astype(low)

    part_rows = gout.shape[2] // 2
    own_half = pl.ds(pl.multiple_of(c * part_rows, part_rows), part_rows)
    other_half = pl.ds(pl.multiple_of((1 - c) * part_rows, part_rows), part_rows)

    def out_grad(r):
        if r == 4:
            return pltpu.make_async_remote_copy(
                gout.at[:, :, other_half], ogot, osend.at[3], orecv.at[3], device_id={"context": 1 - c}
            )
        src, dst = ogot.at[t ^ r], obuf.at[r]
        if r == 0:
            return pltpu.make_async_copy(src, dst, olocal)
        return pltpu.make_async_remote_copy(
            src, dst, osend.at[r - 1], orecv.at[r - 1], device_id={"tensor": t ^ r}
        )

    def other_core():
        return pltpu.make_async_remote_copy(
            gwx.at[1 - c], gwr, xsend, xrecv, device_id={"context": 1 - c}
        )

    def load(i):
        if i == 2:
            return pltpu.make_async_copy(gud, gud_v, vlocal.at[2])
        return pltpu.make_async_copy(part_sum.at[i], zr.at[0, i, 0], vlocal.at[i])

    def normed(i):
        return pltpu.make_async_copy(norm.at[i], norm_v.at[i], nlocal.at[i])

    @pl.when(u == 0)
    def _():
        greet(peers)
        for i in range(3):
            load(i).start()
        for i in range(2):
            normed(i).start()
        gw[...] = jnp.zeros_like(gw)
        greeted(peers)
        out_grad(4).start()
        for r in range(1, 4):
            side_tensor(r).start()
        side_tensor(0).start()
        step_of(1, 1)
        for i in range(3):
            load(i).wait()
        step_of(0, 2, False)

    @pl.when(u == 1)
    def _():
        out_grad(4).wait()
        for p in range(4):
            ogot[p] = (ogot[p].astype(full) + gout[p, :, own_half].astype(full)).astype(low)
        for r in range(1, 4):
            out_grad(r).start()
        out_grad(0).start()
        step_of(1, 2)

    @pl.when(u == 2)
    def _():
        side_tensor(0).wait()
        for r in range(1, 4):
            side_tensor(r).wait_recv()
        stot[...] = sum(sgot[r].astype(full) for r in range(4)).astype(low)
        for r in range(1, n):
            side_dp(r).start()

    @pl.when(u == 3)
    def _():
        step_of(0, 3)

    @pl.when(u == 4)
    def _():
        step_of(1, 3)

    qs[...] = q_ref[0] * low(0.125)
    ks[...] = k_ref[0].T
    vs[...] = v_ref[0].T
    grow[...] = g_ref[0].T
    qrow[...] = qs[...].T
    delta[...] = jnp.sum(g_ref[0].astype(full) * of_ref[0], axis=0, keepdims=True)
    dqs[...] = jnp.zeros_like(dqs)
    for key_start in range(0, length, QB):
        rows = slice(key_start, key_start + QB)
        k, v, key_t = ks[rows, :], vs[rows, :], k_ref[0, :, rows]
        stop = min(key_start + WIN + QB, length)
        key_pos = key_start + lax.broadcasted_iota(jnp.int32, (QB, QB), 0)
        for start in range(key_start, stop, QB):
            cols = slice(start, start + QB)
            held = slice(start - key_start, start - key_start + QB)
            s = nn(k, qs[:, cols]) - lse_ref[0, :, cols]
            allowed = key_pos >= lo_ref[0, :, cols]
            if start == key_start:
                allowed &= key_pos <= start + lax.broadcasted_iota(jnp.int32, (QB, QB), 1)
            p = jnp.exp(jnp.where(allowed, s, NEG))
            dp = nn(v, g_ref[0, :, cols])
            soft[:, held] = p.astype(low)
            dscore[:, held] = (p * (dp - delta[:, cols])).astype(low)
        cols, held = slice(key_start, stop), slice(0, stop - key_start)
        dv = nn(soft[:, held], grow[cols, :])
        dk = nn(dscore[:, held], qrow[cols, :])
        dqs[:, cols] += nn(key_t, dscore[:, held])
        dbuf[u, 1, :, rows] = dk.T.astype(low)
        dbuf[u, 2, :, rows] = dv.T.astype(low)
    dbuf[u, 0] = (dqs[...] * 0.125).astype(low)

    def move(unit, i, source_core):
        dc, r = PEERS[i]
        h, seq = unit_place(unit, source_core)
        dest = pl.multiple_of(((c ^ dc) * 4 + (t ^ r)) * own, own)
        src = dbuf.at[unit, :, :, pl.ds(dest, own)]
        dst = dall.at[t, :, h, :, pl.ds(pl.multiple_of(seq * own, own), own)]
        if i == 0:
            return pltpu.make_async_copy(src, dst, lsem.at[unit])
        return pltpu.make_async_remote_copy(
            src, dst, ssem.at[i - 1, unit], rsem.at[i - 1, unit], device_id=at_peer(c, t, dc, r)
        )

    for i, at in enumerate((0, 3)):

        @pl.when(u == at)
        def _():
            normed(i).wait()

    @pl.when(sends(u, c))
    def _():
        for i in range(1, len(PEERS)):
            move(u, i, c).start()
        move(u, 0, c).start()
        h, _ = unit_place(u, c)
        gw[h] += nn(dbuf[u].reshape(3 * HD, length), norm_v[u // 3])

    @pl.when(u == pl.num_programs(0) - 1)
    def _():
        wide_rows = [gw[h, p * HD : (p + 1) * HD, :] for p in range(3) for h in range(3)]
        gwx[0] = jnp.concatenate(wide_rows[:6], axis=0).T.astype(low)
        empty = jnp.zeros((3 * HD, gw.shape[2]), full)
        gwx[1] = jnp.concatenate(wide_rows[6:] + [empty], axis=0).T.astype(low)
        other_core().start()
        out_grad(0).wait()
        for r in range(1, 4):
            out_grad(r).wait()
        osum[...] = sum(obuf[r].astype(full) for r in range(4)).T.astype(low)
        other_core().wait()
        gw_sum[...] = (gwx[c].astype(full) + gwr[...].astype(full)).astype(low)
        for step in range(4, n):
            step_of(0, step)
            step_of(1, step)
        finish(0)
        finish(1)
        total = stot[rows_of(d)].astype(full)
        for r in range(1, n):
            side_tensor(r).wait_send() if r < 4 else None
            side_dp(r).wait()
            total += sdp[r - 1].astype(full)
        ssum[...] = total
        for unit in range(UNITS):
            for i, (dc, r) in enumerate(PEERS):

                @pl.when(sends(unit, c))
                def _():
                    if i:
                        move(unit, i, c).wait_send()
                    else:
                        move(unit, i, c).wait()

                if i:

                    @pl.when(sends(unit, c ^ dc))
                    def _():
                        move(unit, i, c ^ dc).wait_recv()


def attend_back(n, qkv, grad_units, lo, lse, attended, normed, grad_out, grad_up_down, side, part_sum):
    length = lo.shape[2]
    own = length // 8
    width = normed.shape[2]
    shard, columns = grad_up_down.shape[1] // n, grad_up_down.shape[2]
    out_rows, local = grad_out.shape[2] // 2, grad_out.shape[1]
    part = lambda p: pl.BlockSpec((1, HD, length), unit_block(p))
    unit = lambda rows, m: pl.BlockSpec((1, rows, m), lambda u: (u, 0, 0))
    once = lambda dims: pl.BlockSpec(dims, lambda u: (0,) * len(dims), pipeline_mode=pl.Buffered(1))
    wide, tall = pltpu.VMEM((HD, length), low), pltpu.VMEM((length, HD), low)
    results = [(width, 2 * 3 * HD), (4, shard, columns), (out_rows, local)]
    return pl.pallas_call(
        functools.partial(attend_back_kernel, n),
        grid=(UNITS,),
        in_specs=[part(0), part(1), part(2)]
        + [
            pl.BlockSpec((1, 1, length), lambda u: (u // 3, 0, 0)),
            unit(1, length),
            unit(HD, length),
            HBM,
            unit(HD, length),
            once(grad_out.shape),
        ]
        + [HBM] * 3,
        out_specs=[HBM] + [once(r) for r in results] + [once((shard, SIDE))],
        scratch_shapes=[
            wide, tall, tall, tall, tall,
            pltpu.VMEM((1, length), full), pltpu.VMEM((HD, length), full),
            pltpu.VMEM((QB, WIN + QB), low), pltpu.VMEM((QB, WIN + QB), low), pltpu.VMEM(normed.shape, low),
            pltpu.VMEM((UNITS, 3, HD, length), low), pltpu.VMEM((3, 3 * HD, width), full),
            pltpu.VMEM((2, width, 6 * HD), low), pltpu.VMEM((width, 6 * HD), low),
            pltpu.VMEM((2, 2, n - 1, 2, shard, columns), low), pltpu.VMEM(grad_up_down.shape, low),
            pltpu.VMEM((4, local, out_rows), low), pltpu.VMEM((4, local, out_rows), low),
            pltpu.VMEM((4, width, SIDE), low), pltpu.VMEM((width, SIDE), low), pltpu.VMEM((n - 1, shard, SIDE), low),
            dma((7, UNITS)), dma((7, UNITS)), dma((UNITS,)),
            dma((2, 2, n - 1)), dma((2, 2, n - 1)), dma, dma, dma((4,)), dma((4,)), dma, dma((3,)), dma((2,)),
            dma((3,)), dma((3,)), dma, dma((n - 1,)), dma((n - 1,)),
        ],
        out_shape=[shape((4, 3, 3, HD, 3 * own), low)]
        + [shape(r, low) for r in results]
        + [shape((shard, SIDE), full)],
        compiler_params=pltpu.CompilerParams(
            vmem_limit_bytes=63 << 20, collective_id=2, has_side_effects=True
        ),
        name="attend_back",
    )(qkv, qkv, qkv, lo, lse, attended, normed, grad_units, grad_out, grad_up_down, side, part_sum)


def last_kernel(
    n, dqkv_ref, w_ref, tokens_ref, middle_ref, gains, w_own, up_own, gain_one, gain_two, ssum, gw_sum, zsum, osum,
    grad_in, g_qkv, g_up, g_down, g_out, g_one, g_two,
    rg, rw, ro, down_n, out_t, mine, sums, dqkv, w_all, tokens, middle,
    gsend, grecv, wsend, wrecv, osend, orecv, lsem, csend, crecv, ssend, srecv, clocal, fetch,
):
    c, t = place()
    d = lax.axis_index("dp")
    shard, hidden = rg.shape[1], rg.shape[2]
    cut = n // 2
    group = [at_peer(c, t, dc, r) for dc, r in PEERS[1:]]
    others = [lax.rem(d + r, n) for r in range(1, n)]
    peers = group + [{"dp": o} for o in others]
    greet(peers)
    loads = [
        pltpu.make_async_copy(src, dst, fetch.at[i])
        for i, (src, dst) in enumerate(
            ((tokens_ref, tokens), (w_ref, w_all), (dqkv_ref, dqkv), (middle_ref, middle))
        )
    ]
    for copy in loads:
        copy.start()

    def rows_of(j):
        return pl.ds(pl.multiple_of(j * shard, shard), shard)

    narrow = slice(0, 256)

    def qkv_piece(r, core):
        src, dst = gw_sum.at[rows_of(d if r == 0 else others[r - 1])], rg.at[r]
        if core:
            src, dst = src.at[:, narrow], dst.at[:, narrow]
        if r == 0:
            return pltpu.make_async_copy(src, dst, lsem.at[0])
        return pltpu.make_async_remote_copy(
            src, dst, gsend.at[r - 1], grecv.at[r - 1], device_id={"dp": others[r - 1]}
        )

    def each_core(what):
        for core in range(2):

            @pl.when(c == core)
            def _():
                what(core)

    def up_piece(r):
        src, dst = zsum.at[t ^ r], rw.at[r]
        if r == 0:
            return pltpu.make_async_copy(src, dst, lsem.at[1])
        return pltpu.make_async_remote_copy(
            src, dst, wsend.at[r - 1], wrecv.at[r - 1], device_id={"tensor": t ^ r}
        )

    mine_out = d // cut == c

    def out_piece(r):
        to = d if r == 0 else others[r - 1]
        src, dst = osum.at[rows_of(lax.rem(to, cut))], ro.at[r]
        if r == 0:
            return pltpu.make_async_copy(src, dst, lsem.at[2])
        return pltpu.make_async_remote_copy(
            src, dst, osend.at[r - 1], orecv.at[r - 1], device_id={"dp": to}
        )

    def start_all(core):
        for r in range(1, n):
            qkv_piece(r, core).start()
        qkv_piece(0, core).start()

    greeted(peers)
    each_core(start_all)
    for r in range(1, 4):
        up_piece(r).start()
    up_piece(0).start()
    for r in range(1, n):

        @pl.when(others[r - 1] // cut == c)
        def _():
            out_piece(r).start()

    @pl.when(mine_out)
    def _():
        out_piece(0).start()

    for copy in loads:
        copy.wait()
    @pl.loop(0, tokens.shape[0] // QB)
    def _(m):
        rows = pl.ds(pl.multiple_of(m * QB, QB), QB)
        r = tn(dqkv[:, rows], w_all[...])
        v = tokens[rows, :].astype(full)
        inv = lax.rsqrt(jnp.mean(v * v, axis=-1, keepdims=True) + epsilon)
        rg_ = r * gains[0:1, :]
        grad = inv * (rg_ - v * (inv * inv * jnp.mean(rg_ * v, axis=-1, keepdims=True)))
        grad_in[rows, :] = (middle[rows, :] + grad).astype(low)

    def halves(j):
        half = pl.ds(pl.multiple_of(c * hidden, hidden), hidden)
        src, dst = (
            (mine.at[0], g_qkv.at[:, half]),
            (mine.at[1], g_up.at[:, half]),
            (down_n, g_down.at[:, half]),
            (out_t, g_out),
        )[j]
        return (
            pltpu.make_async_copy(src, dst, clocal.at[j]),
            pltpu.make_async_remote_copy(
                src, dst, csend.at[j], crecv.at[j], device_id={"context": 1 - c}
            ),
        )

    def deliver(j):
        for copy in halves(j):
            copy.start()

    up_piece(0).wait()
    for r in range(1, 4):
        up_piece(r).wait_recv()
    main = hidden - SIDE
    mine[1, :, :main] = sum(rw[r, :, :main].astype(full) for r in range(4))
    mine[1, :, main:] = ssum[...]
    down_n[...] = sum(rw[r, :, main:].astype(full) for r in range(4))
    deliver(1)
    deliver(2)

    @pl.when(mine_out)
    def _():
        out_piece(0).wait()
        for r in range(1, n):
            out_piece(r).wait_recv()
        out_t[...] = sum(ro[r].astype(full) for r in range(n)).T
        deliver(3)

    def take(core):
        qkv_piece(0, core).wait()
        for r in range(1, n):
            qkv_piece(r, core).wait_recv()
        if core:
            mine[0, :, narrow] = sum(rg[r, :, narrow].astype(full) for r in range(n))
            mine[0, :, 256:] = jnp.zeros((shard, hidden - 256), full)
        else:
            mine[0] = sum(rg[r].astype(full) for r in range(n))

    each_core(take)
    deliver(0)
    lane = lax.broadcasted_iota(jnp.int32, (shard, 128), 1)
    halves_of = [jnp.concatenate([w_own[0], w_own[1]], axis=1), jnp.pad(w_own[2], ((0, 0), (0, osum.shape[1])))]
    w_mine = jnp.where(c == 0, halves_of[0].astype(full), halves_of[1].astype(full))
    up_mine = up_own[:, pl.ds(pl.multiple_of(c * hidden, hidden), hidden)].astype(full)
    first = jnp.sum(w_mine * mine[0], axis=1, keepdims=True)
    second = jnp.sum(up_mine * mine[1], axis=1, keepdims=True)
    sums[0] = jnp.where(lane == 0, first, jnp.where(lane == 1, second, 0.0)).T[:8]

    def gain_piece(i):
        dc, r = PEERS[i]
        return pltpu.make_async_remote_copy(
            sums.at[0], sums.at[i], ssend.at[i - 1], srecv.at[i - 1], device_id=at_peer(c, t, dc, r)
        )

    for i in range(1, len(PEERS)):
        gain_piece(i).start()
    for i in range(1, len(PEERS)):
        gain_piece(i).wait()
    total = sum(sums[i] for i in range(len(PEERS)))
    g_one[...] = total[0:1, :] / gain_one[...].astype(full)
    g_two[...] = total[1:2, :] / gain_two[...].astype(full)

    for j in range(3):
        for copy in halves(j):
            copy.wait()

    @pl.when(mine_out)
    def _():
        local, away = halves(3)
        local.wait()
        away.wait_send()

    @pl.when(jnp.logical_not(mine_out))
    def _():
        halves(3)[1].wait_recv()

    for r in range(1, 4):
        up_piece(r).wait_send()

    def sent(core):
        for r in range(1, n):
            qkv_piece(r, core).wait_send()

    each_core(sent)
    for r in range(1, n):

        @pl.when(others[r - 1] // cut == c)
        def _():
            out_piece(r).wait_send()


def last(n, dqkv, w_all, tokens, middle, gains, w_own, up_own, gain_one, gain_two, ssum, gw_sum, zsum, osum):
    rows, width = tokens.shape
    shard, hidden = zsum.shape[1], gw_sum.shape[1]
    local = osum.shape[1]
    return pl.pallas_call(
        functools.partial(last_kernel, n),
        in_specs=[HBM] * 4 + [VMEM] * 6 + [ANY] * 3,
        out_specs=[VMEM] + [ANY] * 4 + [VMEM] * 2,
        out_shape=[
            shape((rows, width), low),
            shape((shard, 2 * hidden), full),
            shape((shard, 2 * hidden), full),
            shape((shard, 2 * hidden), full),
            shape((local, shard), full),
            shape((1, shard), full),
            shape((1, shard), full),
        ],
        scratch_shapes=[
            pltpu.VMEM((n, shard, hidden), low),
            pltpu.VMEM((4, shard, 2 * hidden - SIDE), low),
            pltpu.VMEM((n, shard, local), low),
            pltpu.VMEM((shard, hidden), full),
            pltpu.VMEM((local, shard), full),
            pltpu.VMEM((2, shard, hidden), full),
            pltpu.VMEM((8, 8, shard), full),
            pltpu.VMEM(dqkv.shape, low), pltpu.VMEM(w_all.shape, low),
            pltpu.VMEM((rows, width), low), pltpu.VMEM((rows, width), full),
            dma((n - 1,)), dma((n - 1,)), dma((3,)), dma((3,)), dma((n - 1,)), dma((n - 1,)), dma((3,)),
            dma((4,)), dma((4,)), dma((7,)), dma((7,)), dma((4,)), dma((4,)),
        ],
        compiler_params=pltpu.CompilerParams(
            vmem_limit_bytes=63 << 20, collective_id=4, has_side_effects=True
        ),
        name="last",
    )(dqkv, w_all, tokens, middle, gains, w_own, up_own, gain_one, gain_two, ssum, gw_sum, zsum, osum)


def close_kernel(*refs):
    count = len(refs) // 2
    for i, (src, dst) in enumerate(zip(refs[:count], refs[count:])):
        if i == 2:
            local = dst.shape[2]
            for p in range(3):
                dst[p] = src[:, p * local : (p + 1) * local]
        else:
            dst[...] = src[...]


def close(result, grad_input, own_attn, *others):
    arrays = (result, grad_input, own_attn, *others)
    rows = lambda a: pl.BlockSpec((a.shape[0] // 2, a.shape[1]), lambda i: (i, 0))
    shard, local = own_attn.shape[0], others[0].shape[0]
    parts = pl.BlockSpec((3, shard // 2, local), lambda i: (0, i, 0))
    outs = [shape(a.shape, a.dtype) for a in arrays]
    outs[2] = shape((3, shard, local), full)
    return pl.pallas_call(
        close_kernel,
        grid=(2,),
        in_specs=[rows(a) for a in arrays],
        out_specs=[parts if i == 2 else rows(a) for i, a in enumerate(arrays)],
        out_shape=outs,
        compiler_params=pltpu.CompilerParams(vmem_limit_bytes=63 << 20),
        name="close",
    )(*arrays)


def gelu_and_slope(v):
    k0 = math.sqrt(2.0 / math.pi)
    square = v * v
    th = jnp.tanh(v * (k0 + (k0 * 0.044715) * square))
    half = 0.5 + 0.5 * th
    slope = half + (v * half) * ((1.0 - th) * (k0 + (3.0 * 0.044715 * k0) * square))
    return v * half, slope


def feed_kernel(
    dp, att_ref, proj_ref, tokens_ref, cot_ref, gains, w_t_ref, up_ref, down_ref,
    result, grad_middle, gout, gud, side, part_sum, units, w_all,
    x, g, x_t, g_t, up, down, act, gh, out, back, proj_w, sent, got, gbuf, sbuf, gatt,
    att, proj, tokens, cot, w_t, middle,
    xsend, xrecv, wsend, wrecv, wlocal, zsend, zrecv, glocal, usend, urecv, ulocal, load, first_load, mlocal,
):
    c, t = place()
    d = lax.axis_index("dp")
    rows, width = tokens.shape
    own = rows // 3
    shard = width // dp
    n = up_ref.shape[2]
    local = proj.shape[2]
    other = {"context": 1 - c}
    peers = [at_peer(c, t, dc, r) for dc, r in PEERS[1:]]
    mine, theirs = slice(0, rows), slice(rows, 2 * rows)
    block = rows // 3

    def cross(k):
        src, dst = (
            (cot, g.at[theirs]),
            (x.at[mine], x.at[theirs]),
            (sent.at[0], got.at[0]),
            (sent.at[1], got.at[1]),
        )[k]
        return pltpu.make_async_remote_copy(src, dst, xsend.at[k], xrecv.at[k], device_id=other)

    half = pl.ds(pl.multiple_of(c * (w_t.shape[0] // 2), 8), w_t.shape[0] // 2)

    def over_tensor(r):
        if r == 4:
            ref = w_all.at[:, half]
            return pltpu.make_async_remote_copy(ref, ref, wsend.at[3], wrecv.at[3], device_id=other)
        src, dst = w_t.at[half], w_all.at[t, half]
        if r == 0:
            return pltpu.make_async_copy(src, dst, wlocal)
        return pltpu.make_async_remote_copy(
            src, dst, wsend.at[r - 1], wrecv.at[r - 1], device_id={"tensor": t ^ r}
        )

    def rows_of(i):
        return pl.ds(pl.multiple_of(i * shard, shard), shard)

    line = Line(
        dp,
        lambda i: gbuf.at[0, :, rows_of(i)],
        lambda k, step: part_sum.at[k],
        zsend,
        zrecv,
    )

    def keep(j):
        if j == 2:
            return pltpu.make_async_copy(sbuf, side, glocal.at[2])
        return pltpu.make_async_copy(gbuf.at[j], gud.at[pl.ds(2 * j, 2)], glocal.at[j])

    def leave(whole, i):
        dc, r = PEERS[i]
        to_c, to_t = c ^ dc, t ^ r
        head = to_t * 3 + (0 if whole else to_c)
        count, first = (3, 0) if whole else (2, 3)
        seq = 2 * to_c if whole else 1
        src = gatt.at[pl.ds(head, count), :, pl.ds(pl.multiple_of(seq * own, own), own)]
        dst = units.at[pl.ds(first, count), :, pl.ds(pl.multiple_of((c * 4 + t) * own, own), own)]
        k = 0 if whole else 1
        if i == 0:
            return pltpu.make_async_copy(src, dst, ulocal.at[k])
        return pltpu.make_async_remote_copy(
            src, dst, usend.at[k, i - 1], urecv.at[k, i - 1], device_id=at_peer(c, t, dc, r)
        )

    loads = [
        pltpu.make_async_copy(ref.at[p], dst.at[p // 2, :, pl.ds((p % 2) * n, n)], load.at[i, p])
        for i, (ref, dst) in enumerate(((up_ref, up), (down_ref, down)))
        for p in range(4)
    ]
    greet(peers)
    greet_line(dp, d)
    firsts = [
        pltpu.make_async_copy(src, dst, first_load.at[i])
        for i, (src, dst) in enumerate(
            ((cot_ref, cot), (proj_ref, proj), (w_t_ref, w_t), (att_ref, att), (tokens_ref, tokens))
        )
    ]
    for copy in firsts + loads:
        copy.start()
    for copy in firsts[:2]:
        copy.wait()
    for p in range(4):
        proj_w[:, p * local : (p + 1) * local] = proj[p]
    firsts[2].wait()
    greeted_line(dp, d, peers)
    cross(0).start()
    for r in range(1, 4):
        over_tensor(r).start()
    over_tensor(0).start()
    for copy in firsts[3:]:
        copy.wait()
    for m in range(0, rows, block):
        part = slice(m, m + block)
        v = tokens[part, :].astype(full) + nn(proj_w[...], att[:, part]).T
        middle[part, :] = v
        inv = lax.rsqrt(jnp.mean(v * v, axis=-1, keepdims=True) + epsilon)
        x[part, :] = (v * inv * gains[1:2, :]).astype(low)
    cross(1).start()
    g[mine, :] = cot[...]
    g_t[:, mine] = cot[...].T
    x_t[:, mine] = x[mine, :].T
    for copy in loads:
        copy.wait()

    def hidden(side):
        @pl.loop(0, 6)
        def _(i):
            j = i // 3
            part = pl.ds(pl.multiple_of((side * 3 + i % 3) * block, block), block)
            pre = nn(x[part, :], up[j])
            ga = nn(g[part, :], down[j])
            a, slope = gelu_and_slope(pre)
            act[j, part, :] = a.astype(low)
            gh[j, part, :] = (ga * slope).astype(low)

    def branch(left, right, part):
        return nt(left[0, part, :], right[0]) + nt(left[1, part, :], right[1])

    hidden(0)
    cross(0).wait_recv()
    cross(1).wait_recv()
    hidden(1)

    def cut(side, left, right, put):
        @pl.loop(0, 3)
        def _(i):
            here = pl.ds(pl.multiple_of(i * block, block), block)
            part = pl.ds(pl.multiple_of(side * rows + i * block, block), block)
            put(here, branch(left, right, part))

    def put_sent(k):
        def put(here, value):
            sent[k, here, :] = value.astype(low)

        return put

    def put_own(ref):
        def put(here, value):
            ref[here, :] = value

        return put

    cut(1, gh, up, put_sent(0))
    cross(2).start()
    cut(0, gh, up, put_own(back))
    over_tensor(0).wait()
    for r in range(1, 4):
        over_tensor(r).wait_recv()
    over_tensor(4).start()
    x_t[:, theirs] = x[theirs, :].T
    g_t[:, theirs] = g[theirs, :].T
    cross(1).wait_send()
    cross(2).wait_recv()
    gain = gains[1:2, :]
    low_t = x
    for m in range(0, rows, block):
        part = slice(m, m + block)
        r = (back[part, :] + got[0, part, :].astype(full)) * gain
        v = middle[part, :]
        inv = lax.rsqrt(jnp.mean(v * v, axis=-1, keepdims=True) + epsilon)
        grad = inv * (r - v * (inv * inv * jnp.mean(r * v, axis=-1, keepdims=True)))
        back[part, :] = cot[part, :].astype(full) + grad
        x[part, :] = back[part, :].astype(low)
        low_t[rows : rows + width, part] = x[part, :].T
        grad = tn(proj_w[...], low_t[rows : rows + width, part]).astype(low)
        gatt[:, :, part] = grad.reshape(gatt.shape[0], HD, block)
    for whole in (True, False):
        for i in range(1, len(PEERS)):
            leave(whole, i).start()
        leave(whole, 0).start()
    keep_middle = pltpu.make_async_copy(back, grad_middle, mlocal)
    keep_middle.start()

    def weight_grad(j, a, left_t, right):
        @pl.loop(0, 3)
        def _(i):
            part = pl.ds(pl.multiple_of(i * (width // 3), width // 3), width // 3)
            grad = nn(left_t[part, :], right[j]).astype(low)
            main = n - SIDE
            for p in range(2):
                if a:
                    gbuf[j, p, part, main:] = grad[:, p * n : (p + 1) * n]
                else:
                    gbuf[j, p, part, :main] = grad[:, p * n : p * n + main]
                    sbuf[2 * j + p, part, :] = grad[:, p * n + main : (p + 1) * n]

    weight_grad(0, 0, x_t, gh)
    weight_grad(0, 1, g_t, act)
    line.start(1, None)
    keep(0).start()
    cut(1, act, down, put_sent(1))
    cross(3).start()
    weight_grad(1, 0, x_t, gh)
    weight_grad(1, 1, g_t, act)
    keep(1).start()
    keep(2).start()
    cut(0, act, down, put_own(out))
    for p in range(4):
        gout[p] = nn(att[p * local : (p + 1) * local, :], x[mine, :]).astype(low)
    cross(3).wait_recv()
    result[...] = (middle[...] + out[...] + got[1].astype(full)).astype(low)
    keep_middle.wait()
    for k in (0, 2, 3):
        cross(k).wait_send()
    for r in range(1, 4):
        over_tensor(r).wait_send()
    over_tensor(4).wait()
    line.received(1)
    line.sent(1)
    for j in range(3):
        keep(j).wait()
    for whole in (True, False):
        for i in range(len(PEERS)):
            leave(whole, i).wait()


def feed(dp, att, proj, tokens, cot, gains, w_t, up, down):
    rows, width = tokens.shape
    pieces, _, n = up.shape
    own = rows // 3
    assert pieces == 4 and dp > 2 and rows == width
    return pl.pallas_call(
        functools.partial(feed_kernel, dp),
        in_specs=[HBM] * 4 + [VMEM] + [HBM] * 3,
        out_specs=[VMEM, HBM, VMEM] + [HBM] * 5,
        out_shape=[
            shape((rows, width), low),
            shape((rows, width), full),
            shape((4, proj.shape[2], width), low),
            shape((4, width, 2 * n - SIDE), low),
            shape((4, width, SIDE), low),
            shape((2, 2, width // dp, 2 * n - SIDE), low),
            shape((UNITS, HD, 8 * own), low),
            shape((4,) + w_t.shape, low),
        ],
        scratch_shapes=[pltpu.VMEM((2 * rows, width), low)] * 2
        + [pltpu.VMEM((width, 2 * rows), low)] * 2
        + [pltpu.VMEM((2, width, 2 * n), low)] * 2
        + [pltpu.VMEM((2, 2 * rows, 2 * n), low)] * 2
        + [pltpu.VMEM((rows, width), full)] * 2
        + [pltpu.VMEM((width, width), low)]
        + [pltpu.VMEM((2, rows, width), low)] * 2
        + [pltpu.VMEM((2, 2, width, 2 * n - SIDE), low), pltpu.VMEM((4, width, SIDE), low)]
        + [pltpu.VMEM((12, HD, rows), low)]
        + [pltpu.VMEM(a.shape, low) for a in (att, proj, tokens, cot, w_t)]
        + [pltpu.VMEM((rows, width), full)]
        + [dma((4,)), dma((4,)), dma((4,)), dma((4,)), dma]
        + [dma((2, 1)), dma((2, 1)), dma((3,)), dma((2, 7)), dma((2, 7)), dma((2,)), dma((2, 4)), dma((5,)), dma],
        compiler_params=pltpu.CompilerParams(
            vmem_limit_bytes=63 << 20, collective_id=5, has_side_effects=True
        ),
        name="feed",
    )(att, proj, tokens, cot, gains, w_t, up, down)


def per_device(tokens, segments, w_qkv, w_out, w_in, w_back, gain_attn, gain_mlp, cotangent):
    sequences, own, width = tokens.shape
    assert lax.axis_size("tensor") == 4 and lax.axis_size("context") == 2 and sequences == 3
    n = lax.axis_size("dp")
    length = segments.shape[1]
    shard = w_qkv.shape[0]
    local = w_qkv.shape[2]
    rows = sequences * own
    parts = w_qkv.transpose(1, 0, 2)
    gain_one, gain_two = gain_attn.reshape(1, shard), gain_mlp.reshape(1, shard)
    qkv, normed_units, w_t, up_part, out_part, gains, lo = project(
        n, tokens, segments, parts, w_in, w_out, gain_one, gain_two
    )
    attended, log_totals, out_full, w_up, w_down, w_proj = attend(
        n, qkv, lo, out_part, up_part, w_back.T
    )
    flat = tokens.reshape(rows, width)
    result, grad_middle, grad_out, grad_up_down, side, part_sum, grad_units, w_all = feed(
        n, attended, w_proj, flat, cotangent.reshape(rows, width), gains, w_t, w_up, w_down
    )
    grad_projected, gw_sum, zsum, osum, ssum = attend_back(
        n, qkv, grad_units, lo, log_totals, out_full, normed_units, grad_out, grad_up_down, side, part_sum
    )
    grad_input, own_attn, own_up, own_down, own_proj, own_one, own_two = last(
        n,
        grad_projected.reshape(12 * local, rows),
        w_all.reshape(12 * local, width),
        flat,
        grad_middle,
        gains,
        parts,
        w_in,
        gain_one,
        gain_two,
        ssum,
        gw_sum,
        zsum,
        osum,
    )
    result, grad_input, own_attn, own_proj, own_up, own_down = close(
        result, grad_input, own_attn, own_proj, own_up, own_down
    )
    return (
        result.reshape(sequences, own, width),
        grad_input.reshape(sequences, own, width),
        own_attn.transpose(1, 0, 2),
        own_proj,
        own_up,
        own_down.T,
        own_one.reshape(shard),
        own_two.reshape(shard),
    )


def solution(mesh):
    return jax.shard_map(
        per_device,
        mesh=mesh,
        in_specs=(
            P("dp", ("context", "tensor"), None),
            P("dp", None),
            P("dp", None, "tensor"),
            P("tensor", "dp"),
            P("dp", "tensor"),
            P("tensor", "dp"),
            P("dp"),
            P("dp"),
            P("dp", ("context", "tensor"), None),
        ),
        out_specs=(
            P("dp", ("context", "tensor"), None),
            P("dp", ("context", "tensor"), None),
            P("dp", None, "tensor"),
            P("tensor", "dp"),
            P("dp", "tensor"),
            P("tensor", "dp"),
            P("dp"),
            P("dp"),
        ),
        check_vma=False,
    )
```

```python
import functools
import math

import jax
import jax.numpy as jnp
from jax import lax
from jax.experimental import pallas as pl
from jax.experimental.pallas import tpu as pltpu
from jax.sharding import PartitionSpec as P

HD = 64
WIN = 1536
QB = 256
CHUNK = 128
NEG = -1e30
epsilon = 1e-06
low = jnp.bfloat16
full = jnp.float32


def dot(left, right, dims):
    return lax.dot_general(left, right, (dims, ((), ())), preferred_element_type=full)


def nn(left, right):
    return dot(left, right, ((1,), (0,)))


def nt(left, right):
    return dot(left, right, ((1,), (1,)))


def tn(left, right):
    return dot(left, right, ((0,), (0,)))


PEERS = [(dc, r) for dc in range(2) for r in range(4)]


def place():
    return lax.axis_index("context"), lax.axis_index("tensor")


def at_peer(c, t, dc, r):
    return {"context": c ^ dc, "tensor": t ^ r}


def greet(peers):
    for peer in peers:
        pl.semaphore_signal(pltpu.get_barrier_semaphore(), inc=1, device_id=peer)


def greeted(peers):
    pl.semaphore_wait(pltpu.get_barrier_semaphore(), len(peers))


def unit_place(u, c):
    return jnp.where(u < 3, u, c + u - 3), jnp.where(u < 3, 2 * c, 1)


def sends(u, c):
    return (u != 3) | (c == 0)


dma = pltpu.SemaphoreType.DMA
ANY = pl.BlockSpec(memory_space=pl.ANY)
VMEM = pl.BlockSpec(memory_space=pltpu.VMEM)
HBM = pl.BlockSpec(memory_space=pltpu.HBM)
shape = jax.ShapeDtypeStruct

SIDE = 128


class Line:
    def __init__(self, n, own, slot, send, recv):
        self.n, self.own, self.slot, self.sems = n, own, slot, (send, recv)
        self.d = lax.axis_index("dp")

    def along(self, k):
        m = self.d if k == 0 else self.n - 1 - self.d
        to = {"dp": jnp.clip(self.d + 1 if k == 0 else self.d - 1, 0, self.n - 1)}
        return m, to

    def target(self, k, step):
        m, _ = self.along(k)
        return jnp.clip(self.n - step + m if k == 0 else step - 1 - m, 0, self.n - 1)

    def copy(self, k, step, src):
        send, recv = self.sems
        _, to = self.along(k)
        return pltpu.make_async_remote_copy(
            src, self.slot(k, step), send.at[k, step - 1], recv.at[k, step - 1], device_id=to
        )

    def arrive(self, k, step):
        self.copy(k, step, self.slot(k, step)).wait_recv()

    def start(self, step, add):
        for k in range(2):
            m, _ = self.along(k)
            if step > 1:

                @pl.when((m >= 1) & (m < self.n - 1) & (step >= m + 1))
                def _():
                    add(k, self.target(k, step))
                    self.copy(k, step, self.slot(k, step - 1)).start()

            @pl.when(m == 0)
            def _():
                self.copy(k, step, self.own(self.target(k, step))).start()

    def received(self, step):
        for k in range(2):
            m, _ = self.along(k)

            @pl.when((m >= 1) & (step >= m))
            def _():
                self.arrive(k, step)

    def sent(self, step):
        for k in range(2):
            m, _ = self.along(k)

            @pl.when((m < self.n - 1) & (step >= m + 1))
            def _():
                self.copy(k, step, self.slot(k, step)).wait_send()


def greet_line(n, d):
    barrier = pltpu.get_barrier_semaphore()

    @pl.when(d > 0)
    def _():
        pl.semaphore_signal(barrier, inc=1, device_id={"dp": jnp.maximum(d - 1, 0)})

    @pl.when(d < n - 1)
    def _():
        pl.semaphore_signal(barrier, inc=1, device_id={"dp": jnp.minimum(d + 1, n - 1)})


def greeted_line(n, d, peers):
    ends = jnp.where(d > 0, 1, 0) + jnp.where(d < n - 1, 1, 0)
    pl.semaphore_wait(pltpu.get_barrier_semaphore(), len(peers) + ends)


def project_kernel(
    n, tokens, segments, w_qkv, up, out_own, gain_one, gain_two, qkv, norm, w_t, up_all, out_all, gain_ref, lo_ref,
    tok, x, w, proj, out_w, gain, own_gain, tsend, trecv, tlocal, wsend, wrecv, wlocal, osend, orecv, olocal, xsend, xrecv,
):
    c, t = place()
    d = lax.axis_index("dp")
    own = tokens.shape[1]
    width = tokens.shape[2]
    span = 4 * own
    shard = up.shape[0]
    half = own // 2
    hidden = up_all.shape[1]
    cut = n // 2
    to_x, to_y, to_core = {"tensor": t ^ 1}, {"tensor": t ^ 2}, {"context": 1 - c}
    others = [{"dp": lax.rem(d + r, n)} for r in range(1, n)]
    peers = [to_x, to_y, to_core] + others
    greet(peers)

    def local(i, s):
        return pltpu.make_async_copy(tokens.at[s], tok.at[s, t], tlocal.at[i])

    def weights(j, r):
        rows = pl.ds(pl.multiple_of(d * shard, shard), shard)
        source, target = (
            (w_qkv, w.at[:, rows]),
            (out_w, out_all.at[rows]),
            (up.at[:, pl.ds(pl.multiple_of(c * hidden, hidden), hidden)], up_all.at[rows]),
            (own_gain, gain.at[d]),
        )[j]
        if r == 0:
            return pltpu.make_async_copy(source, target, wlocal.at[j])
        return pltpu.make_async_remote_copy(
            source, target, wsend.at[j, r - 1], wrecv.at[j, r - 1], device_id=others[r - 1]
        )

    def gives(j, r):
        return lax.rem(d + n - r, n) // cut == c if j < 2 else True

    def weights_do(j, r, what, source=False):
        @pl.when(gives(j, 0 if source else r))
        def _():
            getattr(weights(j, r), what)()

    def to_other(j):
        rows = pl.ds(pl.multiple_of(c * cut * shard, shard), cut * shard)
        ref = w.at[:, rows]
        return pltpu.make_async_remote_copy(ref, ref, xsend, xrecv, device_id=to_core)

    order = (2 * (1 - c), 1, 2 * c)
    for i, s in enumerate(order):
        local(i, s).start()
    out_w[...] = out_own[...].T
    own_gain[...] = jnp.zeros_like(own_gain)
    own_gain[0:1, :] = gain_one[...]
    own_gain[1:2, :] = gain_two[...]
    for j in range(4):
        weights_do(j, 0, "start")
    greeted(peers)
    for j in (0, 3, 1, 2):
        for r in range(1, n):
            weights_do(j, r, "start", True)

    def hop(k, i):
        s = order[i]
        origin, rows, peer = (
            (t, slice(0, half), to_x),
            (t, slice(half, own), to_y),
            (t, slice(0, half), to_y),
            (t, slice(half, own), to_x),
            (t ^ 1, slice(0, half), to_y),
            (t ^ 2, slice(half, own), to_x),
        )[k]
        there = tok.at[s, origin, rows]
        here = tokens.at[s, rows] if k < 4 else there
        return pltpu.make_async_remote_copy(
            here, there, tsend.at[k, i], trecv.at[k, i], device_id=peer
        )

    def straight(i):
        for k in range(4):
            hop(k, i).start()

    def forward(i):
        for k in range(2):
            hop(k, i).wait_recv()
            hop(k + 4, i).start()

    units = proj.shape[1]

    def leave(i):
        out = []
        lanes = pl.ds(pl.multiple_of(c * span, span), span)
        if i != 0:
            out.append((x.at[i], norm.at[2 - i, lanes], False))
        if i != 2:
            out.append((x.at[i], norm.at[i, lanes], True))
        if i == 0:
            out.append((proj.at[0], qkv.at[pl.ds(0, units), :, lanes], True))
        if i == 2:
            out.append((proj.at[2], qkv.at[pl.ds(0, units), :, lanes], False))
        if i == 1:
            for away in (True, False):
                core = 1 - c if away else c
                for p in range(3):
                    src = proj.at[1, pl.ds(p * 3 + core, 2)]
                    out.append((src, qkv.at[pl.ds(units + 2 * p, 2), :, lanes], away))
        copies = []
        for j, (src, dst, away) in enumerate(out):
            if away:
                copies.append(
                    (away, pltpu.make_async_remote_copy(src, dst, osend.at[i, j], orecv.at[i, j], device_id=to_core))
                )
            else:
                copies.append((away, pltpu.make_async_copy(src, dst, olocal.at[i, j])))
        return copies

    def work(i):
        s = order[i]
        local(i, s).wait()
        for k in range(2, 6):
            hop(k, i).wait_recv()

        @pl.loop(0, 4)
        def _(p):
            rows = pl.ds(pl.multiple_of(p * own, own), own)
            v = tok[s, p].astype(full)
            inv = lax.rsqrt(jnp.mean(v * v, axis=-1, keepdims=True) + epsilon)
            normed = (v * inv * gain_ref[0:1, :]).astype(low)
            x[i, rows, :] = normed
            proj[i, :, :, rows] = nt(w_t[...], normed).astype(low).reshape(units, HD, own)

        for _, copy in leave(i):
            copy.start()

    straight(0)
    straight(1)
    forward(0)
    straight(2)
    seg = segments[...]
    first = jnp.zeros(seg.shape, jnp.int32)
    for value in range(8):
        before = jnp.sum((seg < value).astype(jnp.int32), axis=1, keepdims=True)
        first = jnp.where(seg == value, before, first)
    first = jnp.maximum(first, lax.broadcasted_iota(jnp.int32, seg.shape, 1) - (WIN - 1))
    lo_ref[0] = jnp.where(c == 0, first[0:1], first[2:3])
    lo_ref[1] = first[1:2]
    weights_do(0, 0, "wait")
    for r in range(1, n):
        weights_do(0, r, "wait_recv")
    to_other(0).start()
    weights(3, 0).wait()
    for r in range(1, n):
        weights(3, r).wait_recv()
    gain_ref[...] = jnp.concatenate([gain[i].astype(full) for i in range(n)], axis=1)[:8]
    to_other(0).wait_recv()
    for p in range(3):
        w_t[p * 3 * HD : (p + 1) * 3 * HD, :] = w[p].T
    forward(1)
    work(0)
    forward(2)
    work(1)
    work(2)
    to_other(0).wait_send()
    for j in range(4):
        if j in (1, 2):
            weights_do(j, 0, "wait")
        for r in range(1, n):
            weights_do(j, r, "wait_send", True)
            if j in (1, 2):
                weights_do(j, r, "wait_recv")
    for i in range(3):
        for k in range(6):
            hop(k, i).wait_send()
        for away, copy in leave(i):
            copy.wait()


def project(n, tokens, segments, w_qkv, up, out_own, gain_one, gain_two):
    sequences, own, width = tokens.shape
    shard, hidden = up.shape[0], up.shape[1] // 2
    local = out_own.shape[0]
    span = 4 * own
    return pl.pallas_call(
        functools.partial(project_kernel, n),
        in_specs=[HBM, VMEM, HBM, HBM, VMEM, VMEM, VMEM],
        out_specs=[HBM] * 2 + [VMEM] + [HBM] * 2 + [VMEM] * 2,
        out_shape=[
            shape((15, HD, 2 * span), low),
            shape((2, 2 * span, width), low),
            shape((9 * HD, n * shard), low),
            shape((n * shard, hidden), low),
            shape((n * shard, local), low),
            shape((8, n * shard), full),
            shape((2, 1, segments.shape[1]), jnp.int32),
        ],
        scratch_shapes=[
            pltpu.VMEM((sequences, 4, own, width), low),
            pltpu.VMEM((sequences, span, width), low),
            pltpu.VMEM((3, n * shard, local), low),
            pltpu.VMEM((sequences, 9, HD, span), low),
            pltpu.VMEM((shard, local), low),
            pltpu.VMEM((n, 16, shard), low),
            pltpu.VMEM((16, shard), low),
            dma((6, 3)), dma((6, 3)), dma((3,)),
            dma((4, n - 1)), dma((4, n - 1)), dma((4,)),
            dma((3, 8)), dma((3, 8)), dma((3, 8)), dma, dma,
        ],
        compiler_params=pltpu.CompilerParams(
            vmem_limit_bytes=63 << 20, collective_id=3, has_side_effects=True
        ),
        name="project",
    )(tokens, segments, w_qkv, up, out_own, gain_one, gain_two)


UNITS = 5
def unit_block(part):
    return lambda u: (jnp.where(u < 3, part * 3 + u, 9 + part * 2 + (u - 3)), 0, 0)


def attend_kernel(
    n, q_ref, k_ref, v_ref, lo_ref, out_part, up_part, down_own, att, lse_ref, of_ref, up, down, out_w,
    qs, ks, ss, obuf, ssem, rsem, lsem, wsend, wrecv, wlocal, zsend, zrecv, fsend, frecv,
):
    u = pl.program_id(0)
    c, t = place()
    d = lax.axis_index("dp")
    shard = down_own.shape[0]
    hidden = down.shape[2]
    peers = [at_peer(c, t, dc, r) for dc, r in PEERS[1:]]

    part = out_part.shape[0] // 2
    mine = pl.ds(pl.multiple_of(c * part, part), part)

    def weight(j, r):
        rows = pl.ds(pl.multiple_of(d * shard, shard), shard)
        src, dst = (
            (down_own.at[:, pl.ds(pl.multiple_of(c * hidden, hidden), hidden)], down.at[t, rows]),
            (up_part, up.at[t]),
            (out_part.at[mine], out_w.at[t, mine]),
        )[j]
        if r == 0:
            return pltpu.make_async_copy(src, dst, wlocal.at[j])
        return pltpu.make_async_remote_copy(
            src, dst, wsend.at[j, r - 1], wrecv.at[j, r - 1], device_id={"tensor": t ^ r}
        )

    def onward(k):
        if k == 2:
            ref, peer = out_w.at[:, mine], {"context": 1 - c}
        else:
            rows = pl.ds(k * part, part)
            ref, peer = up.at[t ^ (1 + k), rows], {"tensor": t ^ (2 - k)}
        return pltpu.make_async_remote_copy(
            ref, ref, fsend.at[k], frecv.at[k], device_id=peer
        )

    def shards(step, up_line):
        src = d - step if up_line else d + step
        rows = pl.ds(pl.multiple_of(jnp.clip(src, 0, n - 1) * shard, shard), shard)
        to = jnp.clip(d + 1 if up_line else d - 1, 0, n - 1)
        k = 0 if up_line else 1
        return pltpu.make_async_remote_copy(
            down.at[:, rows], down.at[:, rows], zsend.at[k, step], zrecv.at[k, step], device_id={"dp": to}
        )

    def line(step, what):
        for up_line in (True, False):
            inside = (d < n - 1) if up_line else (d > 0)
            has = (d >= step) if up_line else (d <= n - 1 - step)
            comes = (d >= step + 1) if up_line else (d <= n - 2 - step)
            if what == "recv":

                @pl.when(comes)
                def _():
                    shards(step, up_line).wait_recv()
            else:

                @pl.when(inside & has)
                def _():
                    if what == "start":
                        shards(step, up_line).start()
                    else:
                        shards(step, up_line).wait_send()
    length = lo_ref.shape[2]
    half = length // 2
    own = half // 4

    @pl.when(u == 0)
    def _():
        greet(peers)
        greet_line(n, d)
        for j in range(3):
            weight(j, 0).start()
        greeted_line(n, d, peers)
        for r in range(1, 4):
            weight(0, r).start()
        for r in range(1, 3):
            weight(1, r).start()

    qs[...] = q_ref[0] * low(0.125)
    ks[...] = k_ref[0].T
    for start in range(0, length, QB):
        stop = start + QB
        q = qs[:, start:stop]
        lo = lo_ref[0, :, start:stop]
        first = max(0, start - WIN)
        most = jnp.full((8, QB), NEG, full)
        for at in range(first, stop, CHUNK):
            s = nn(ks[at : at + CHUNK, :], q)
            key_pos = at + lax.broadcasted_iota(jnp.int32, (CHUNK, QB), 0)
            allowed = key_pos >= lo
            if at + CHUNK - 1 > start:
                allowed &= key_pos <= start + lax.broadcasted_iota(jnp.int32, (CHUNK, QB), 1)
            s = jnp.where(allowed, s, NEG)
            ss[at - first : at - first + CHUNK, :] = s
            most = jnp.maximum(most, jnp.max(s.reshape(CHUNK // 8, 8, QB), axis=0))
        most = jnp.max(most, axis=0, keepdims=True)
        total = jnp.zeros((8, QB), full)
        acc = jnp.zeros((HD, QB), full)
        for at in range(first, stop, CHUNK):
            p = jnp.exp(ss[at - first : at - first + CHUNK, :] - most)
            total += jnp.sum(p.reshape(CHUNK // 8, 8, QB), axis=0)
            acc += nn(v_ref[0, :, at : at + CHUNK], p.astype(low))
        total = jnp.sum(total, axis=0, keepdims=True)
        lse_ref[0, :, start:stop] = most + jnp.log(total)
        o = acc * (1.0 / total)
        of_ref[0, :, start:stop] = o
        obuf[u, :, start:stop] = o.astype(low)

    @pl.when(u == 0)
    def _():
        weight(0, 0).wait()
        for r in range(1, 4):
            weight(0, r).wait_recv()
        line(0, "start")
        for r in range(1, 4):
            weight(2, r).start()

    @pl.when(u == 3)
    def _():
        if n > 2:
            line(0, "recv")
            line(1, "start")
        for k in range(2):
            weight(1, 1 + k).wait_recv()
            onward(k).start()
        weight(2, 0).wait()
        for r in range(1, 4):
            weight(2, r).wait_recv()
        onward(2).start()

    def move(unit, i, source_core):
        dc, r = PEERS[i]
        h, seq = unit_place(unit, source_core)
        dest = pl.multiple_of(((c ^ dc) * 4 + (t ^ r)) * own, own)
        src = obuf.at[unit, :, pl.ds(dest, own)]
        dst = att.at[
            pl.ds(pl.multiple_of((t * 3 + h) * HD, HD), HD), pl.ds(pl.multiple_of(seq * own, own), own)
        ]
        if i == 0:
            return pltpu.make_async_copy(src, dst, lsem.at[unit])
        return pltpu.make_async_remote_copy(
            src, dst, ssem.at[i - 1, unit], rsem.at[i - 1, unit], device_id=at_peer(c, t, dc, r)
        )

    @pl.when(sends(u, c))
    def _():
        for i in range(1, len(PEERS)):
            move(u, i, c).start()
        move(u, 0, c).start()

    @pl.when(u == pl.num_programs(0) - 1)
    def _():
        for step in range(2, n - 1):
            line(step - 1, "recv")
            line(step, "start")
        line(n - 2, "recv")
        for step in range(n - 1):
            line(step, "sent")
        weight(1, 0).wait()
        for j in range(3):
            for r in range(1, 3 if j == 1 else 4):
                weight(j, r).wait_send()
        for k in range(3):
            onward(k).wait()
        for unit in range(UNITS):
            for i, (dc, r) in enumerate(PEERS):

                @pl.when(sends(unit, c))
                def _():
                    if i:
                        move(unit, i, c).wait_send()
                    else:
                        move(unit, i, c).wait()

                if i:

                    @pl.when(sends(unit, c ^ dc))
                    def _():
                        move(unit, i, c ^ dc).wait_recv()


def attend(n, qkv, lo, out_part, up_part, down_own):
    length = lo.shape[2]
    half = length // 2
    own = half // 4
    width, hidden = up_part.shape
    part = lambda p: pl.BlockSpec((1, HD, length), unit_block(p))
    unit = lambda rows, n: pl.BlockSpec((1, rows, n), lambda u: (u, 0, 0))
    heads = 4 * 3 * HD
    return pl.pallas_call(
        functools.partial(attend_kernel, n),
        grid=(UNITS,),
        in_specs=[part(0), part(1), part(2)]
        + [pl.BlockSpec((1, 1, length), lambda u: (u // 3, 0, 0))]
        + [
            pl.BlockSpec(a.shape, lambda u: (0, 0), pipeline_mode=pl.Buffered(1))
            for a in (out_part, up_part, down_own)
        ],
        out_specs=[HBM, unit(1, length), unit(HD, length)] + [HBM] * 3,
        scratch_shapes=[
            pltpu.VMEM((HD, length), low),
            pltpu.VMEM((length, HD), low),
            pltpu.VMEM((WIN + QB, QB), full),
            pltpu.VMEM((UNITS, HD, length), low),
            dma((7, UNITS)),
            dma((7, UNITS)),
            dma((UNITS,)),
            dma((3, 3)),
            dma((3, 3)),
            dma((3,)),
            dma((2, n - 1)),
            dma((2, n - 1)),
            dma((3,)),
            dma((3,)),
        ],
        out_shape=[
            jax.ShapeDtypeStruct((heads, 3 * own), low),
            jax.ShapeDtypeStruct((UNITS, 1, length), full),
            jax.ShapeDtypeStruct((UNITS, HD, length), full),
            shape((4, width, hidden), low),
            shape((4, width, hidden), low),
            shape((4,) + out_part.shape, low),
        ],
        compiler_params=pltpu.CompilerParams(
            vmem_limit_bytes=63 << 20, collective_id=1, has_side_effects=True
        ),
        cost_estimate=pl.CostEstimate(
            flops=UNITS * 18 * 2 * 256 * 1024 * 128, bytes_accessed=20 << 20, transcendentals=0
        ),
        name="attend",
    )(qkv, qkv, qkv, lo, out_part, up_part, down_own)


def add_to(ref, terms):
    for p in range(ref.shape[0]):
        ref[p] = (ref[p].astype(full) + terms(p).astype(full)).astype(low)


def attend_back_kernel(
    n, q_ref, k_ref, v_ref, lo_ref, lse_ref, of_ref, norm, g_ref, gout, gud, side, part_sum,
    dall, gw_sum, zsum, osum, ssum,
    qs, ks, vs, grow, qrow, delta, dqs, soft, dscore, norm_v, dbuf, gw, gwx, gwr, zr, gud_v, obuf, ogot, sgot, stot, sdp, ssem, rsem, lsem,
    zsend, zrecv, xsend, xrecv, osend, orecv, olocal, vlocal, nlocal, s_send, s_recv, s_local, dsend, drecv,
):
    u = pl.program_id(0)
    c, t = place()
    d = lax.axis_index("dp")
    shard = gud.shape[1] // n
    length = lo_ref.shape[2]
    own = length // 8
    others = [lax.rem(d + r, n) for r in range(1, n)]
    peers = [at_peer(c, t, dc, r) for dc, r in PEERS[1:]] + [{"dp": o} for o in others]

    def rows_of(j):
        return pl.ds(pl.multiple_of(j * shard, shard), shard)

    def side_tensor(r):
        if r == 0:
            return pltpu.make_async_copy(side.at[t], sgot.at[0], s_local)
        return pltpu.make_async_remote_copy(
            side.at[t ^ r], sgot.at[r], s_send.at[r - 1], s_recv.at[r - 1], device_id={"tensor": t ^ r}
        )

    def side_dp(r):
        return pltpu.make_async_remote_copy(
            stot.at[rows_of(others[r - 1])],
            sdp.at[r - 1],
            dsend.at[r - 1],
            drecv.at[r - 1],
            device_id={"dp": others[r - 1]},
        )

    def line_of(h):
        pair = pl.ds(2 * h, 2)
        return Line(
            n,
            lambda j: gud.at[pair, rows_of(j)],
            lambda k, step: zr.at[h, k, step - 1],
            zsend.at[h],
            zrecv.at[h],
        )

    lines = [line_of(0), line_of(1)]

    def step_of(h, step, arrived=True):
        if arrived and step > 1:
            lines[h].received(step - 1)

        def add(k, j):
            rows = rows_of(j)
            add_to(zr.at[h, k, step - 2], lambda p: gud_v[2 * h + p, rows])

        lines[h].start(step, add)

    def finish(h):
        lines[h].received(n - 1)
        for step in range(2 if h == 0 else 1, n):
            lines[h].sent(step)
        for p in range(2):
            total = gud_v[2 * h + p, rows_of(d)].astype(full)
            up, down = (zr[h, k, n - 2, p].astype(full) for k in range(2))
            total += jnp.where(d > 0, up, 0.0) + jnp.where(d < n - 1, down, 0.0)
            zsum[2 * h + p] = total.astype(low)

    part_rows = gout.shape[2] // 2
    own_half = pl.ds(pl.multiple_of(c * part_rows, part_rows), part_rows)
    other_half = pl.ds(pl.multiple_of((1 - c) * part_rows, part_rows), part_rows)

    def out_grad(r):
        if r == 4:
            return pltpu.make_async_remote_copy(
                gout.at[:, :, other_half], ogot, osend.at[3], orecv.at[3], device_id={"context": 1 - c}
            )
        src, dst = ogot.at[t ^ r], obuf.at[r]
        if r == 0:
            return pltpu.make_async_copy(src, dst, olocal)
        return pltpu.make_async_remote_copy(
            src, dst, osend.at[r - 1], orecv.at[r - 1], device_id={"tensor": t ^ r}
        )

    def other_core():
        return pltpu.make_async_remote_copy(
            gwx.at[1 - c], gwr, xsend, xrecv, device_id={"context": 1 - c}
        )

    def load(i):
        if i == 2:
            return pltpu.make_async_copy(gud, gud_v, vlocal.at[2])
        return pltpu.make_async_copy(part_sum.at[i], zr.at[0, i, 0], vlocal.at[i])

    def normed(i):
        return pltpu.make_async_copy(norm.at[i], norm_v.at[i], nlocal.at[i])

    @pl.when(u == 0)
    def _():
        greet(peers)
        for i in range(3):
            load(i).start()
        for i in range(2):
            normed(i).start()
        gw[...] = jnp.zeros_like(gw)
        greeted(peers)
        out_grad(4).start()
        for r in range(1, 4):
            side_tensor(r).start()
        side_tensor(0).start()
        step_of(1, 1)
        for i in range(3):
            load(i).wait()
        step_of(0, 2, False)

    @pl.when(u == 1)
    def _():
        out_grad(4).wait()
        for p in range(4):
            ogot[p] = (ogot[p].astype(full) + gout[p, :, own_half].astype(full)).astype(low)
        for r in range(1, 4):
            out_grad(r).start()
        out_grad(0).start()
        step_of(1, 2)

    @pl.when(u == 2)
    def _():
        side_tensor(0).wait()
        for r in range(1, 4):
            side_tensor(r).wait_recv()
        stot[...] = sum(sgot[r].astype(full) for r in range(4)).astype(low)
        for r in range(1, n):
            side_dp(r).start()

    @pl.when(u == 3)
    def _():
        step_of(0, 3)

    @pl.when(u == 4)
    def _():
        step_of(1, 3)

    qs[...] = q_ref[0] * low(0.125)
    ks[...] = k_ref[0].T
    vs[...] = v_ref[0].T
    grow[...] = g_ref[0].T
    qrow[...] = qs[...].T
    delta[...] = jnp.sum(g_ref[0].astype(full) * of_ref[0], axis=0, keepdims=True)
    dqs[...] = jnp.zeros_like(dqs)
    for key_start in range(0, length, QB):
        rows = slice(key_start, key_start + QB)
        k, v, key_t = ks[rows, :], vs[rows, :], k_ref[0, :, rows]
        stop = min(key_start + WIN + QB, length)
        key_pos = key_start + lax.broadcasted_iota(jnp.int32, (QB, QB), 0)
        for start in range(key_start, stop, QB):
            cols = slice(start, start + QB)
            held = slice(start - key_start, start - key_start + QB)
            s = nn(k, qs[:, cols]) - lse_ref[0, :, cols]
            allowed = key_pos >= lo_ref[0, :, cols]
            if start == key_start:
                allowed &= key_pos <= start + lax.broadcasted_iota(jnp.int32, (QB, QB), 1)
            p = jnp.exp(jnp.where(allowed, s, NEG))
            dp = nn(v, g_ref[0, :, cols])
            soft[:, held] = p.astype(low)
            dscore[:, held] = (p * (dp - delta[:, cols])).astype(low)
        cols, held = slice(key_start, stop), slice(0, stop - key_start)
        dv = nn(soft[:, held], grow[cols, :])
        dk = nn(dscore[:, held], qrow[cols, :])
        dqs[:, cols] += nn(key_t, dscore[:, held])
        dbuf[u, 1, :, rows] = dk.T.astype(low)
        dbuf[u, 2, :, rows] = dv.T.astype(low)
    dbuf[u, 0] = (dqs[...] * 0.125).astype(low)

    def move(unit, i, source_core):
        dc, r = PEERS[i]
        h, seq = unit_place(unit, source_core)
        dest = pl.multiple_of(((c ^ dc) * 4 + (t ^ r)) * own, own)
        src = dbuf.at[unit, :, :, pl.ds(dest, own)]
        dst = dall.at[t, :, h, :, pl.ds(pl.multiple_of(seq * own, own), own)]
        if i == 0:
            return pltpu.make_async_copy(src, dst, lsem.at[unit])
        return pltpu.make_async_remote_copy(
            src, dst, ssem.at[i - 1, unit], rsem.at[i - 1, unit], device_id=at_peer(c, t, dc, r)
        )

    for i, at in enumerate((0, 3)):

        @pl.when(u == at)
        def _():
            normed(i).wait()

    @pl.when(sends(u, c))
    def _():
        for i in range(1, len(PEERS)):
            move(u, i, c).start()
        move(u, 0, c).start()
        h, _ = unit_place(u, c)
        gw[h] += nn(dbuf[u].reshape(3 * HD, length), norm_v[u // 3])

    @pl.when(u == pl.num_programs(0) - 1)
    def _():
        wide_rows = [gw[h, p * HD : (p + 1) * HD, :] for p in range(3) for h in range(3)]
        gwx[0] = jnp.concatenate(wide_rows[:6], axis=0).T.astype(low)
        empty = jnp.zeros((3 * HD, gw.shape[2]), full)
        gwx[1] = jnp.concatenate(wide_rows[6:] + [empty], axis=0).T.astype(low)
        other_core().start()
        out_grad(0).wait()
        for r in range(1, 4):
            out_grad(r).wait()
        osum[...] = sum(obuf[r].astype(full) for r in range(4)).T.astype(low)
        other_core().wait()
        gw_sum[...] = (gwx[c].astype(full) + gwr[...].astype(full)).astype(low)
        for step in range(4, n):
            step_of(0, step)
            step_of(1, step)
        finish(0)
        finish(1)
        total = stot[rows_of(d)].astype(full)
        for r in range(1, n):
            side_tensor(r).wait_send() if r < 4 else None
            side_dp(r).wait()
            total += sdp[r - 1].astype(full)
        ssum[...] = total
        for unit in range(UNITS):
            for i, (dc, r) in enumerate(PEERS):

                @pl.when(sends(unit, c))
                def _():
                    if i:
                        move(unit, i, c).wait_send()
                    else:
                        move(unit, i, c).wait()

                if i:

                    @pl.when(sends(unit, c ^ dc))
                    def _():
                        move(unit, i, c ^ dc).wait_recv()


def attend_back(n, qkv, grad_units, lo, lse, attended, normed, grad_out, grad_up_down, side, part_sum):
    length = lo.shape[2]
    own = length // 8
    width = normed.shape[2]
    shard, columns = grad_up_down.shape[1] // n, grad_up_down.shape[2]
    out_rows, local = grad_out.shape[2] // 2, grad_out.shape[1]
    part = lambda p: pl.BlockSpec((1, HD, length), unit_block(p))
    unit = lambda rows, m: pl.BlockSpec((1, rows, m), lambda u: (u, 0, 0))
    once = lambda dims: pl.BlockSpec(dims, lambda u: (0,) * len(dims), pipeline_mode=pl.Buffered(1))
    wide, tall = pltpu.VMEM((HD, length), low), pltpu.VMEM((length, HD), low)
    results = [(width, 2 * 3 * HD), (4, shard, columns), (out_rows, local)]
    return pl.pallas_call(
        functools.partial(attend_back_kernel, n),
        grid=(UNITS,),
        in_specs=[part(0), part(1), part(2)]
        + [
            pl.BlockSpec((1, 1, length), lambda u: (u // 3, 0, 0)),
            unit(1, length),
            unit(HD, length),
            HBM,
            unit(HD, length),
            once(grad_out.shape),
        ]
        + [HBM] * 3,
        out_specs=[HBM] + [once(r) for r in results] + [once((shard, SIDE))],
        scratch_shapes=[
            wide, tall, tall, tall, tall,
            pltpu.VMEM((1, length), full), pltpu.VMEM((HD, length), full),
            pltpu.VMEM((QB, WIN + QB), low), pltpu.VMEM((QB, WIN + QB), low), pltpu.VMEM(normed.shape, low),
            pltpu.VMEM((UNITS, 3, HD, length), low), pltpu.VMEM((3, 3 * HD, width), full),
            pltpu.VMEM((2, width, 6 * HD), low), pltpu.VMEM((width, 6 * HD), low),
            pltpu.VMEM((2, 2, n - 1, 2, shard, columns), low), pltpu.VMEM(grad_up_down.shape, low),
            pltpu.VMEM((4, local, out_rows), low), pltpu.VMEM((4, local, out_rows), low),
            pltpu.VMEM((4, width, SIDE), low), pltpu.VMEM((width, SIDE), low), pltpu.VMEM((n - 1, shard, SIDE), low),
            dma((7, UNITS)), dma((7, UNITS)), dma((UNITS,)),
            dma((2, 2, n - 1)), dma((2, 2, n - 1)), dma, dma, dma((4,)), dma((4,)), dma, dma((3,)), dma((2,)),
            dma((3,)), dma((3,)), dma, dma((n - 1,)), dma((n - 1,)),
        ],
        out_shape=[shape((4, 3, 3, HD, 3 * own), low)]
        + [shape(r, low) for r in results]
        + [shape((shard, SIDE), full)],
        compiler_params=pltpu.CompilerParams(
            vmem_limit_bytes=63 << 20, collective_id=2, has_side_effects=True
        ),
        name="attend_back",
    )(qkv, qkv, qkv, lo, lse, attended, normed, grad_units, grad_out, grad_up_down, side, part_sum)


def last_kernel(
    n, dqkv_ref, w_ref, tokens_ref, middle_ref, gains, w_own, up_own, gain_one, gain_two, ssum, gw_sum, zsum, osum,
    grad_in, g_qkv, g_up, g_down, g_out, g_one, g_two,
    rg, rw, ro, down_n, out_t, mine, sums, dqkv, w_all, tokens, middle,
    gsend, grecv, wsend, wrecv, osend, orecv, lsem, csend, crecv, ssend, srecv, clocal, fetch,
):
    c, t = place()
    d = lax.axis_index("dp")
    shard, hidden = rg.shape[1], rg.shape[2]
    cut = n // 2
    group = [at_peer(c, t, dc, r) for dc, r in PEERS[1:]]
    others = [lax.rem(d + r, n) for r in range(1, n)]
    peers = group + [{"dp": o} for o in others]
    greet(peers)
    loads = [
        pltpu.make_async_copy(src, dst, fetch.at[i])
        for i, (src, dst) in enumerate(
            ((tokens_ref, tokens), (w_ref, w_all), (dqkv_ref, dqkv), (middle_ref, middle))
        )
    ]
    for copy in loads:
        copy.start()

    def rows_of(j):
        return pl.ds(pl.multiple_of(j * shard, shard), shard)

    narrow = slice(0, 256)

    def qkv_piece(r, core):
        src, dst = gw_sum.at[rows_of(d if r == 0 else others[r - 1])], rg.at[r]
        if core:
            src, dst = src.at[:, narrow], dst.at[:, narrow]
        if r == 0:
            return pltpu.make_async_copy(src, dst, lsem.at[0])
        return pltpu.make_async_remote_copy(
            src, dst, gsend.at[r - 1], grecv.at[r - 1], device_id={"dp": others[r - 1]}
        )

    def each_core(what):
        for core in range(2):

            @pl.when(c == core)
            def _():
                what(core)

    def up_piece(r):
        src, dst = zsum.at[t ^ r], rw.at[r]
        if r == 0:
            return pltpu.make_async_copy(src, dst, lsem.at[1])
        return pltpu.make_async_remote_copy(
            src, dst, wsend.at[r - 1], wrecv.at[r - 1], device_id={"tensor": t ^ r}
        )

    mine_out = d // cut == c

    def out_piece(r):
        to = d if r == 0 else others[r - 1]
        src, dst = osum.at[rows_of(lax.rem(to, cut))], ro.at[r]
        if r == 0:
            return pltpu.make_async_copy(src, dst, lsem.at[2])
        return pltpu.make_async_remote_copy(
            src, dst, osend.at[r - 1], orecv.at[r - 1], device_id={"dp": to}
        )

    def start_all(core):
        for r in range(1, n):
            qkv_piece(r, core).start()
        qkv_piece(0, core).start()

    greeted(peers)
    each_core(start_all)
    for r in range(1, 4):
        up_piece(r).start()
    up_piece(0).start()
    for r in range(1, n):

        @pl.when(others[r - 1] // cut == c)
        def _():
            out_piece(r).start()

    @pl.when(mine_out)
    def _():
        out_piece(0).start()

    for copy in loads:
        copy.wait()
    @pl.loop(0, tokens.shape[0] // QB)
    def _(m):
        rows = pl.ds(pl.multiple_of(m * QB, QB), QB)
        r = tn(dqkv[:, rows], w_all[...])
        v = tokens[rows, :].astype(full)
        inv = lax.rsqrt(jnp.mean(v * v, axis=-1, keepdims=True) + epsilon)
        rg_ = r * gains[0:1, :]
        grad = inv * (rg_ - v * (inv * inv * jnp.mean(rg_ * v, axis=-1, keepdims=True)))
        grad_in[rows, :] = (middle[rows, :] + grad).astype(low)

    def halves(j):
        half = pl.ds(pl.multiple_of(c * hidden, hidden), hidden)
        src, dst = (
            (mine.at[0], g_qkv.at[:, half]),
            (mine.at[1], g_up.at[:, half]),
            (down_n, g_down.at[:, half]),
            (out_t, g_out),
        )[j]
        return (
            pltpu.make_async_copy(src, dst, clocal.at[j]),
            pltpu.make_async_remote_copy(
                src, dst, csend.at[j], crecv.at[j], device_id={"context": 1 - c}
            ),
        )

    def deliver(j):
        for copy in halves(j):
            copy.start()

    up_piece(0).wait()
    for r in range(1, 4):
        up_piece(r).wait_recv()
    main = hidden - SIDE
    mine[1, :, :main] = sum(rw[r, :, :main].astype(full) for r in range(4))
    mine[1, :, main:] = ssum[...]
    down_n[...] = sum(rw[r, :, main:].astype(full) for r in range(4))
    deliver(1)
    deliver(2)

    @pl.when(mine_out)
    def _():
        out_piece(0).wait()
        for r in range(1, n):
            out_piece(r).wait_recv()
        out_t[...] = sum(ro[r].astype(full) for r in range(n)).T
        deliver(3)

    def take(core):
        qkv_piece(0, core).wait()
        for r in range(1, n):
            qkv_piece(r, core).wait_recv()
        if core:
            mine[0, :, narrow] = sum(rg[r, :, narrow].astype(full) for r in range(n))
            mine[0, :, 256:] = jnp.zeros((shard, hidden - 256), full)
        else:
            mine[0] = sum(rg[r].astype(full) for r in range(n))

    each_core(take)
    deliver(0)
    lane = lax.broadcasted_iota(jnp.int32, (shard, 128), 1)
    halves_of = [jnp.concatenate([w_own[0], w_own[1]], axis=1), jnp.pad(w_own[2], ((0, 0), (0, osum.shape[1])))]
    w_mine = jnp.where(c == 0, halves_of[0].astype(full), halves_of[1].astype(full))
    up_mine = up_own[:, pl.ds(pl.multiple_of(c * hidden, hidden), hidden)].astype(full)
    first = jnp.sum(w_mine * mine[0], axis=1, keepdims=True)
    second = jnp.sum(up_mine * mine[1], axis=1, keepdims=True)
    sums[0] = jnp.where(lane == 0, first, jnp.where(lane == 1, second, 0.0)).T[:8]

    def gain_piece(i):
        dc, r = PEERS[i]
        return pltpu.make_async_remote_copy(
            sums.at[0], sums.at[i], ssend.at[i - 1], srecv.at[i - 1], device_id=at_peer(c, t, dc, r)
        )

    for i in range(1, len(PEERS)):
        gain_piece(i).start()
    for i in range(1, len(PEERS)):
        gain_piece(i).wait()
    total = sum(sums[i] for i in range(len(PEERS)))
    g_one[...] = total[0:1, :] / gain_one[...].astype(full)
    g_two[...] = total[1:2, :] / gain_two[...].astype(full)

    for j in range(3):
        for copy in halves(j):
            copy.wait()

    @pl.when(mine_out)
    def _():
        local, away = halves(3)
        local.wait()
        away.wait_send()

    @pl.when(jnp.logical_not(mine_out))
    def _():
        halves(3)[1].wait_recv()

    for r in range(1, 4):
        up_piece(r).wait_send()

    def sent(core):
        for r in range(1, n):
            qkv_piece(r, core).wait_send()

    each_core(sent)
    for r in range(1, n):

        @pl.when(others[r - 1] // cut == c)
        def _():
            out_piece(r).wait_send()


def last(n, dqkv, w_all, tokens, middle, gains, w_own, up_own, gain_one, gain_two, ssum, gw_sum, zsum, osum):
    rows, width = tokens.shape
    shard, hidden = zsum.shape[1], gw_sum.shape[1]
    local = osum.shape[1]
    return pl.pallas_call(
        functools.partial(last_kernel, n),
        in_specs=[HBM] * 4 + [VMEM] * 6 + [ANY] * 3,
        out_specs=[VMEM] + [ANY] * 4 + [VMEM] * 2,
        out_shape=[
            shape((rows, width), low),
            shape((shard, 2 * hidden), full),
            shape((shard, 2 * hidden), full),
            shape((shard, 2 * hidden), full),
            shape((local, shard), full),
            shape((1, shard), full),
            shape((1, shard), full),
        ],
        scratch_shapes=[
            pltpu.VMEM((n, shard, hidden), low),
            pltpu.VMEM((4, shard, 2 * hidden - SIDE), low),
            pltpu.VMEM((n, shard, local), low),
            pltpu.VMEM((shard, hidden), full),
            pltpu.VMEM((local, shard), full),
            pltpu.VMEM((2, shard, hidden), full),
            pltpu.VMEM((8, 8, shard), full),
            pltpu.VMEM(dqkv.shape, low), pltpu.VMEM(w_all.shape, low),
            pltpu.VMEM((rows, width), low), pltpu.VMEM((rows, width), full),
            dma((n - 1,)), dma((n - 1,)), dma((3,)), dma((3,)), dma((n - 1,)), dma((n - 1,)), dma((3,)),
            dma((4,)), dma((4,)), dma((7,)), dma((7,)), dma((4,)), dma((4,)),
        ],
        compiler_params=pltpu.CompilerParams(
            vmem_limit_bytes=63 << 20, collective_id=4, has_side_effects=True
        ),
        name="last",
    )(dqkv, w_all, tokens, middle, gains, w_own, up_own, gain_one, gain_two, ssum, gw_sum, zsum, osum)


def close_kernel(*refs):
    count = (len(refs) - 3) // 3
    sources, targets, held = refs[:count], refs[count : 2 * count], refs[2 * count : 3 * count]
    parts, into, out = refs[3 * count :]
    loads = [
        pltpu.make_async_copy(src, dst, into.at[i]) for i, (src, dst) in enumerate(zip(sources, held))
    ]
    stores = [
        pltpu.make_async_copy(parts if i == 2 else src, dst, out.at[i])
        for i, (src, dst) in enumerate(zip(held, targets))
    ]
    for copy in loads:
        copy.start()
    local = parts.shape[2]
    for i in range(count):
        loads[i].wait()
        if i == 2:
            for p in range(3):
                parts[p] = held[2][:, p * local : (p + 1) * local]
        stores[i].start()
    for copy in stores:
        copy.wait()


def close(result, grad_input, own_attn, *others):
    arrays = (result, grad_input, own_attn, *others)
    shard, local = own_attn.shape[0], others[0].shape[0]
    outs = [shape(a.shape, a.dtype) for a in arrays]
    outs[2] = shape((3, shard, local), full)
    return pl.pallas_call(
        close_kernel,
        in_specs=[HBM] * len(arrays),
        out_specs=[HBM] * len(arrays),
        out_shape=outs,
        scratch_shapes=[pltpu.VMEM(a.shape, a.dtype) for a in arrays]
        + [pltpu.VMEM((3, shard, local), full), dma((len(arrays),)), dma((len(arrays),))],
        compiler_params=pltpu.CompilerParams(vmem_limit_bytes=63 << 20),
        name="close",
    )(*arrays)


def gelu_and_slope(v):
    k0 = math.sqrt(2.0 / math.pi)
    square = v * v
    th = jnp.tanh(v * (k0 + (k0 * 0.044715) * square))
    half = 0.5 + 0.5 * th
    slope = half + (v * half) * ((1.0 - th) * (k0 + (3.0 * 0.044715 * k0) * square))
    return v * half, slope


def feed_kernel(
    dp, att_ref, proj_ref, tokens_ref, cot_ref, gains, w_t_ref, up_ref, down_ref,
    result, grad_middle, gout, gud, side, part_sum, units, w_all,
    x, g, x_t, g_t, up, down, act, gh, out, back, proj_w, sent, got, gbuf, sbuf, gatt,
    att, proj, tokens, cot, w_t, middle,
    xsend, xrecv, wsend, wrecv, wlocal, zsend, zrecv, glocal, usend, urecv, ulocal, load, first_load, mlocal,
):
    c, t = place()
    d = lax.axis_index("dp")
    rows, width = tokens.shape
    own = rows // 3
    shard = width // dp
    n = up_ref.shape[2]
    local = proj.shape[2]
    other = {"context": 1 - c}
    peers = [at_peer(c, t, dc, r) for dc, r in PEERS[1:]]
    mine, theirs = slice(0, rows), slice(rows, 2 * rows)
    block = rows // 3

    def cross(k):
        src, dst = (
            (cot, g.at[theirs]),
            (x.at[mine], x.at[theirs]),
            (sent.at[0], got.at[0]),
            (sent.at[1], got.at[1]),
        )[k]
        return pltpu.make_async_remote_copy(src, dst, xsend.at[k], xrecv.at[k], device_id=other)

    half = pl.ds(pl.multiple_of(c * (w_t.shape[0] // 2), 8), w_t.shape[0] // 2)

    def over_tensor(r):
        if r == 4:
            ref = w_all.at[:, half]
            return pltpu.make_async_remote_copy(ref, ref, wsend.at[3], wrecv.at[3], device_id=other)
        src, dst = w_t.at[half], w_all.at[t, half]
        if r == 0:
            return pltpu.make_async_copy(src, dst, wlocal)
        return pltpu.make_async_remote_copy(
            src, dst, wsend.at[r - 1], wrecv.at[r - 1], device_id={"tensor": t ^ r}
        )

    def rows_of(i):
        return pl.ds(pl.multiple_of(i * shard, shard), shard)

    line = Line(
        dp,
        lambda i: gbuf.at[0, :, rows_of(i)],
        lambda k, step: part_sum.at[k],
        zsend,
        zrecv,
    )

    def keep(j):
        if j == 2:
            return pltpu.make_async_copy(sbuf, side, glocal.at[2])
        return pltpu.make_async_copy(gbuf.at[j], gud.at[pl.ds(2 * j, 2)], glocal.at[j])

    def leave(whole, i):
        dc, r = PEERS[i]
        to_c, to_t = c ^ dc, t ^ r
        head = to_t * 3 + (0 if whole else to_c)
        count, first = (3, 0) if whole else (2, 3)
        seq = 2 * to_c if whole else 1
        src = gatt.at[pl.ds(head, count), :, pl.ds(pl.multiple_of(seq * own, own), own)]
        dst = units.at[pl.ds(first, count), :, pl.ds(pl.multiple_of((c * 4 + t) * own, own), own)]
        k = 0 if whole else 1
        if i == 0:
            return pltpu.make_async_copy(src, dst, ulocal.at[k])
        return pltpu.make_async_remote_copy(
            src, dst, usend.at[k, i - 1], urecv.at[k, i - 1], device_id=at_peer(c, t, dc, r)
        )

    loads = [
        pltpu.make_async_copy(ref.at[p], dst.at[p // 2, :, pl.ds((p % 2) * n, n)], load.at[i, p])
        for i, (ref, dst) in enumerate(((up_ref, up), (down_ref, down)))
        for p in range(4)
    ]
    greet(peers)
    greet_line(dp, d)
    firsts = [
        pltpu.make_async_copy(src, dst, first_load.at[i])
        for i, (src, dst) in enumerate(
            ((cot_ref, cot), (proj_ref, proj), (w_t_ref, w_t), (att_ref, att), (tokens_ref, tokens))
        )
    ]
    for copy in firsts + loads:
        copy.start()
    for copy in firsts[:2]:
        copy.wait()
    for p in range(4):
        proj_w[:, p * local : (p + 1) * local] = proj[p]
    firsts[2].wait()
    greeted_line(dp, d, peers)
    cross(0).start()
    for r in range(1, 4):
        over_tensor(r).start()
    over_tensor(0).start()
    for copy in firsts[3:]:
        copy.wait()
    for m in range(0, rows, block):
        part = slice(m, m + block)
        v = tokens[part, :].astype(full) + nn(proj_w[...], att[:, part]).T
        middle[part, :] = v
        inv = lax.rsqrt(jnp.mean(v * v, axis=-1, keepdims=True) + epsilon)
        x[part, :] = (v * inv * gains[1:2, :]).astype(low)
    cross(1).start()
    g[mine, :] = cot[...]
    g_t[:, mine] = cot[...].T
    x_t[:, mine] = x[mine, :].T
    for copy in loads:
        copy.wait()

    def hidden(side):
        @pl.loop(0, 6)
        def _(i):
            j = i // 3
            part = pl.ds(pl.multiple_of((side * 3 + i % 3) * block, block), block)
            pre = nn(x[part, :], up[j])
            ga = nn(g[part, :], down[j])
            a, slope = gelu_and_slope(pre)
            act[j, part, :] = a.astype(low)
            gh[j, part, :] = (ga * slope).astype(low)

    def branch(left, right, part):
        return nt(left[0, part, :], right[0]) + nt(left[1, part, :], right[1])

    hidden(0)
    cross(0).wait_recv()
    cross(1).wait_recv()
    hidden(1)

    def cut(side, left, right, put):
        @pl.loop(0, 3)
        def _(i):
            here = pl.ds(pl.multiple_of(i * block, block), block)
            part = pl.ds(pl.multiple_of(side * rows + i * block, block), block)
            put(here, branch(left, right, part))

    def put_sent(k):
        def put(here, value):
            sent[k, here, :] = value.astype(low)

        return put

    def put_own(ref):
        def put(here, value):
            ref[here, :] = value

        return put

    cut(1, gh, up, put_sent(0))
    cross(2).start()
    cut(0, gh, up, put_own(back))
    over_tensor(0).wait()
    for r in range(1, 4):
        over_tensor(r).wait_recv()
    over_tensor(4).start()
    x_t[:, theirs] = x[theirs, :].T
    g_t[:, theirs] = g[theirs, :].T
    cross(1).wait_send()
    cross(2).wait_recv()
    gain = gains[1:2, :]
    low_t = x
    for m in range(0, rows, block):
        part = slice(m, m + block)
        r = (back[part, :] + got[0, part, :].astype(full)) * gain
        v = middle[part, :]
        inv = lax.rsqrt(jnp.mean(v * v, axis=-1, keepdims=True) + epsilon)
        grad = inv * (r - v * (inv * inv * jnp.mean(r * v, axis=-1, keepdims=True)))
        back[part, :] = cot[part, :].astype(full) + grad
        x[part, :] = back[part, :].astype(low)
        low_t[rows : rows + width, part] = x[part, :].T
        grad = tn(proj_w[...], low_t[rows : rows + width, part]).astype(low)
        gatt[:, :, part] = grad.reshape(gatt.shape[0], HD, block)
    for whole in (True, False):
        for i in range(1, len(PEERS)):
            leave(whole, i).start()
        leave(whole, 0).start()
    keep_middle = pltpu.make_async_copy(back, grad_middle, mlocal)
    keep_middle.start()

    def weight_grad(j, a, left_t, right):
        @pl.loop(0, 3)
        def _(i):
            part = pl.ds(pl.multiple_of(i * (width // 3), width // 3), width // 3)
            grad = nn(left_t[part, :], right[j]).astype(low)
            main = n - SIDE
            for p in range(2):
                if a:
                    gbuf[j, p, part, main:] = grad[:, p * n : (p + 1) * n]
                else:
                    gbuf[j, p, part, :main] = grad[:, p * n : p * n + main]
                    sbuf[2 * j + p, part, :] = grad[:, p * n + main : (p + 1) * n]

    weight_grad(0, 0, x_t, gh)
    weight_grad(0, 1, g_t, act)
    line.start(1, None)
    keep(0).start()
    cut(1, act, down, put_sent(1))
    cross(3).start()
    weight_grad(1, 0, x_t, gh)
    weight_grad(1, 1, g_t, act)
    keep(1).start()
    keep(2).start()
    cut(0, act, down, put_own(out))
    for p in range(4):
        gout[p] = nn(att[p * local : (p + 1) * local, :], x[mine, :]).astype(low)
    cross(3).wait_recv()
    result[...] = (middle[...] + out[...] + got[1].astype(full)).astype(low)
    keep_middle.wait()
    for k in (0, 2, 3):
        cross(k).wait_send()
    for r in range(1, 4):
        over_tensor(r).wait_send()
    over_tensor(4).wait()
    line.received(1)
    line.sent(1)
    for j in range(3):
        keep(j).wait()
    for whole in (True, False):
        for i in range(len(PEERS)):
            leave(whole, i).wait()


def feed(dp, att, proj, tokens, cot, gains, w_t, up, down):
    rows, width = tokens.shape
    pieces, _, n = up.shape
    own = rows // 3
    assert pieces == 4 and dp > 2 and rows == width
    return pl.pallas_call(
        functools.partial(feed_kernel, dp),
        in_specs=[HBM] * 4 + [VMEM] + [HBM] * 3,
        out_specs=[VMEM, HBM, VMEM] + [HBM] * 5,
        out_shape=[
            shape((rows, width), low),
            shape((rows, width), full),
            shape((4, proj.shape[2], width), low),
            shape((4, width, 2 * n - SIDE), low),
            shape((4, width, SIDE), low),
            shape((2, 2, width // dp, 2 * n - SIDE), low),
            shape((UNITS, HD, 8 * own), low),
            shape((4,) + w_t.shape, low),
        ],
        scratch_shapes=[pltpu.VMEM((2 * rows, width), low)] * 2
        + [pltpu.VMEM((width, 2 * rows), low)] * 2
        + [pltpu.VMEM((2, width, 2 * n), low)] * 2
        + [pltpu.VMEM((2, 2 * rows, 2 * n), low)] * 2
        + [pltpu.VMEM((rows, width), full)] * 2
        + [pltpu.VMEM((width, width), low)]
        + [pltpu.VMEM((2, rows, width), low)] * 2
        + [pltpu.VMEM((2, 2, width, 2 * n - SIDE), low), pltpu.VMEM((4, width, SIDE), low)]
        + [pltpu.VMEM((12, HD, rows), low)]
        + [pltpu.VMEM(a.shape, low) for a in (att, proj, tokens, cot, w_t)]
        + [pltpu.VMEM((rows, width), full)]
        + [dma((4,)), dma((4,)), dma((4,)), dma((4,)), dma]
        + [dma((2, 1)), dma((2, 1)), dma((3,)), dma((2, 7)), dma((2, 7)), dma((2,)), dma((2, 4)), dma((5,)), dma],
        compiler_params=pltpu.CompilerParams(
            vmem_limit_bytes=63 << 20, collective_id=5, has_side_effects=True
        ),
        name="feed",
    )(att, proj, tokens, cot, gains, w_t, up, down)


def per_device(tokens, segments, w_qkv, w_out, w_in, w_back, gain_attn, gain_mlp, cotangent):
    sequences, own, width = tokens.shape
    assert lax.axis_size("tensor") == 4 and lax.axis_size("context") == 2 and sequences == 3
    n = lax.axis_size("dp")
    length = segments.shape[1]
    shard = w_qkv.shape[0]
    local = w_qkv.shape[2]
    rows = sequences * own
    parts = w_qkv.transpose(1, 0, 2)
    gain_one, gain_two = gain_attn.reshape(1, shard), gain_mlp.reshape(1, shard)
    qkv, normed_units, w_t, up_part, out_part, gains, lo = project(
        n, tokens, segments, parts, w_in, w_out, gain_one, gain_two
    )
    attended, log_totals, out_full, w_up, w_down, w_proj = attend(
        n, qkv, lo, out_part, up_part, w_back.T
    )
    flat = tokens.reshape(rows, width)
    result, grad_middle, grad_out, grad_up_down, side, part_sum, grad_units, w_all = feed(
        n, attended, w_proj, flat, cotangent.reshape(rows, width), gains, w_t, w_up, w_down
    )
    grad_projected, gw_sum, zsum, osum, ssum = attend_back(
        n, qkv, grad_units, lo, log_totals, out_full, normed_units, grad_out, grad_up_down, side, part_sum
    )
    grad_input, own_attn, own_up, own_down, own_proj, own_one, own_two = last(
        n,
        grad_projected.reshape(12 * local, rows),
        w_all.reshape(12 * local, width),
        flat,
        grad_middle,
        gains,
        parts,
        w_in,
        gain_one,
        gain_two,
        ssum,
        gw_sum,
        zsum,
        osum,
    )
    result, grad_input, own_attn, own_proj, own_up, own_down = close(
        result, grad_input, own_attn, own_proj, own_up, own_down
    )
    return (
        result.reshape(sequences, own, width),
        grad_input.reshape(sequences, own, width),
        own_attn.transpose(1, 0, 2),
        own_proj,
        own_up,
        own_down.T,
        own_one.reshape(shard),
        own_two.reshape(shard),
    )


def solution(mesh):
    return jax.shard_map(
        per_device,
        mesh=mesh,
        in_specs=(
            P("dp", ("context", "tensor"), None),
            P("dp", None),
            P("dp", None, "tensor"),
            P("tensor", "dp"),
            P("dp", "tensor"),
            P("tensor", "dp"),
            P("dp"),
            P("dp"),
            P("dp", ("context", "tensor"), None),
        ),
        out_specs=(
            P("dp", ("context", "tensor"), None),
            P("dp", ("context", "tensor"), None),
            P("dp", None, "tensor"),
            P("tensor", "dp"),
            P("dp", "tensor"),
            P("tensor", "dp"),
            P("dp"),
            P("dp"),
        ),
        check_vma=False,
    )
```
